32 devices in a mesh: dp: 32 (over z, y, x, core).
Axes of the slice: x: 2, y: 2, z: 4, core: 2. Of those that a mesh axis runs over, the one named last changes fastest.
Arguments:
- tokens: bfloat16 [8192, 1024], P('dp'), may hold values from -6 to 6
- w_query: bfloat16 [1024, 1024], P('dp'), may hold values from -0.1875 to 0.1875
- key_weight: bfloat16 [1024, 512], P('dp'), may hold values from -0.1875 to 0.1875
- w_value: bfloat16 [1024, 512], P('dp'), may hold values from -0.1875 to 0.1875
- w_out: bfloat16 [1024, 1024], P('dp'), may hold values from -3 to 3
- w_gate: bfloat16 [1024, 4608], P('dp'), may hold values from -0.1875 to 0.1875
- w_up: bfloat16 [1024, 4608], P('dp'), may hold values from -0.1875 to 0.1875
- w_down: bfloat16 [4608, 1024], P('dp'), may hold values from -0.09375 to 0.09375
- norm_gains: bfloat16 [2176], P('dp'), may hold values from 0.099609375 to 1.8984375
- seq_lengths: int32 [4, 4], replicated, may hold values from 1 to 1024, 2048 in all within a row
- slot_order: int32 [4, 16], replicated, may hold values from 0 to 15, each once within a row
- out_grad: bfloat16 [8192, 1024], P('dp'), may hold values from -6 to 6
Outputs:
- result: bfloat16 [8192, 1024], P('dp')
- grad_tokens: float32 [8192, 1024], P('dp')
- grad_w_query: float32 [1024, 1024], P('dp')
- grad_w_key: float32 [1024, 512], P('dp')
- grad_w_value: float32 [1024, 512], P('dp')
- grad_w_out: float32 [1024, 1024], P('dp')
- grad_w_gate: float32 [1024, 4608], P('dp')
- grad_w_up: float32 [1024, 4608], P('dp')
- grad_w_down: float32 [4608, 1024], P('dp')
- grad_norm_gains: float32 [2176], P('dp')
The draws below stay inside these ranges and needn't reach their ends.
Inputs may be any that keep to these rules, and one draw needn't show every extreme that they name: Each row of seq_lengths sums to 2048, and its largest entry is 1024. Each row of slot_order is a permutation of the group's 16 slots.
All inputs are finite; a program needn't handle non-finite values.
Results may differ from the reference program's by a relative error of at most 0.014.
Values may be sent and summed in bfloat16 or wider, within the bound.
A program may use at most 192 MiB of HBM per device.

```python
import math
import jax
import jax.numpy as jnp
import numpy as np
from jax import lax

D = 1024
FF = 4608
QUERY_HEADS = 16
KEY_VALUE_HEADS = 8
HEAD_SIZE = 64
SLOT = 128
SEQS = 4
DQ = 1024
KEY_VALUE_DIMS = 512
GROUP_TOKENS = 2048
GSLOTS = 16
MAXLEN = 1024
GROUP_COUNT = 4
TOKEN_TOTAL = 8192
GAINS = 2176


def steps_of(own_key, shape, pieces, low, largest):
    def one(dim, shards_of):
        steps = jax.random.uniform(jax.random.fold_in(jax.random.fold_in(own_key, 6), dim), (shards_of,), jnp.float32, low / len(pieces), largest / len(pieces))
        return jnp.repeat(jnp.exp(steps), shape[dim] // shards_of).reshape((-1,) + (1,) * (len(shape) - dim - 1))

    loudness = one(*pieces[0])
    for cut in pieces[1:]:
        loudness = loudness * one(*cut)
    return loudness


def profile(count, total, most, lean):
    loads = [(1 << 20) // math.isqrt(rank ** lean) + 1 for rank in range(2, count + 1)]
    surplus, given = total - most - (count - 1), [1] * (count - 1)
    while surplus > 0:
        free = [i for i in range(count - 1) if given[i] < most]
        pool, remaining = sum([loads[i] for i in free]), surplus
        for i in free:
            addition = min(most - given[i], max(1, remaining * loads[i] // pool), surplus)
            given[i] = given[i] + addition
            surplus = surplus - addition
    return np.array([most] + given)


def uneven_parts(own_key, count, total, reach, lean):
    if count == 2:
        one = jax.random.randint(own_key, (), max(1, total - reach), min(reach, total - 1) + 1)
        return jnp.stack([one, total - one])
    lengths = jnp.asarray(profile(count, total, reach, lean), jnp.int32)
    twos = (count - 1) // 2
    giver, taker = lengths[1:1 + 2 * twos:2], lengths[2:2 + 2 * twos:2]
    margin = jnp.minimum(giver - 1, reach - taker)
    passed = jax.random.randint(jax.random.fold_in(own_key, 1), (twos,), 0, 1 << 20) % (margin + 1)
    lengths = lengths.at[1:1 + 2 * twos:2].set(giver - passed).at[2:2 + 2 * twos:2].set(taker + passed)
    return lengths[jax.random.permutation(jax.random.fold_in(own_key, 2), count)]


def centred(own_key, shape, deviation, limit, shards=(), held_as=jnp.bfloat16):
    level = steps_of(own_key, shape, shards, -0.22, 0.18) if shards else 1.0
    values = jax.random.normal(own_key, shape, jnp.float32) * deviation * level
    return jnp.minimum(jnp.maximum(values, -limit), limit).astype(held_as)


def setup_inputs(seed: int = 0) -> dict:
    keys = jax.random.split(jax.random.key(seed), 13)
    return {
        "tokens": centred(keys[0], (TOKEN_TOTAL, D), 1.0, 6.0, ((0, 32),)),
        "w_query": centred(keys[1], (D, DQ), D ** -0.5, 0.1875, ((0, 32),)),
        "key_weight": centred(keys[2], (D, KEY_VALUE_DIMS), D ** -0.5, 0.1875, ((0, 32),)),
        "w_value": centred(keys[3], (D, KEY_VALUE_DIMS), D ** -0.5, 0.1875, ((0, 32),)),
        "w_out": centred(keys[4], (DQ, D), 4 ** -0.5, 3.0, ((0, 32),)),
        "w_gate": centred(keys[5], (D, FF), D ** -0.5, 0.1875, ((0, 32),)),
        "w_up": centred(keys[6], (D, FF), D ** -0.5, 0.1875, ((0, 32),)),
        "w_down": centred(keys[7], (FF, D), FF ** -0.5, 0.09375, ((0, 32),)),
        "norm_gains": jnp.clip(1.0 + 0.18 * jax.random.normal(keys[8], (GAINS,), jnp.float32), 0.099609375, 1.8984375).astype(jnp.bfloat16),
        "seq_lengths": jax.vmap(lambda own: uneven_parts(own, SEQS, GROUP_TOKENS, MAXLEN, 2))(jax.random.split(keys[9], GROUP_COUNT)).reshape((GROUP_COUNT, SEQS)).astype(jnp.int32),
        "slot_order": jax.vmap(lambda own: jax.random.permutation(own, GSLOTS))(jax.random.split(keys[10], GROUP_COUNT)).reshape((GROUP_COUNT, GSLOTS)).astype(jnp.int32),
        "out_grad": centred(keys[11], (TOKEN_TOTAL, D), 1.0, 6.0, ((0, 32),)),
    }


EPSILON = 1e-05
ROPE_THETA = 1000000.0
MASKED = -1e+30
TOP_PRECISION = lax.Precision.HIGHEST

@jax.custom_vjp
def low(v):
    return lax.optimization_barrier(v.astype(jnp.bfloat16)).astype(jnp.float32)

@jax.custom_vjp
def low_back(v):
    return v

def low_keep(v):
    return (low(v), None)

def low_pass(kept, grad):
    return (grad,)

def back_keep(v):
    return (v, None)

def back_low(kept, grad):
    return (low(grad),)
low.defvjp(low_keep, low_pass)
low_back.defvjp(back_keep, back_low)

def norm_rows(value_rows, gain_vec):
    return value_rows * lax.rsqrt(lax.optimization_barrier(jnp.mean(value_rows * value_rows, axis=-1, keepdims=True)) + EPSILON) * gain_vec

def rotate(value_rows, angles):
    half_width = value_rows.shape[-1] // 2
    cosine = jnp.cos(angles)[:, None, :]
    sine_part = jnp.sin(angles)[:, None, :]
    front_half = value_rows[..., :half_width]
    back_half = value_rows[..., half_width:]
    return jnp.concatenate([front_half * cosine - back_half * sine_part, back_half * cosine + front_half * sine_part], axis=-1)

def rotary_angles(position, head_width):
    frequency = jnp.exp(jnp.arange(head_width // 2, dtype=jnp.float32) * (-2.0 * math.log(ROPE_THETA) / head_width))
    return position.astype(jnp.float32)[:, None] * frequency[None, :]

def token_info(order_row, length_row, slot_ids, slot_len):
    offsets = jnp.arange(slot_len, dtype=jnp.int32)
    group_positions = (order_row[slot_ids][:, None] * slot_len + offsets[None, :]).reshape(-1)
    seq_ends = jnp.cumsum(length_row, dtype=jnp.int32)
    starts = seq_ends - length_row
    inside = (group_positions[:, None] >= starts[None, :]) & (group_positions[:, None] < seq_ends[None, :])
    labels = jnp.arange(length_row.shape[0], dtype=jnp.int32)
    sequence_ids = lax.optimization_barrier(jnp.sum(jnp.where(inside, labels[None, :], 0), axis=-1, dtype=jnp.int32))
    position = group_positions - lax.optimization_barrier(jnp.sum(jnp.where(inside, starts[None, :], 0), axis=-1, dtype=jnp.int32))
    return (group_positions, sequence_ids, position)

def reorder_slots(rows, slot_index):
    width = rows.shape[-1]
    grouped = rows.reshape(GROUP_COUNT, GSLOTS, SLOT * width)
    moved = jnp.take_along_axis(grouped, slot_index[:, :, None], axis=1)
    return moved.reshape(TOKEN_TOTAL, width)

def attend_block(query_block, grouped_keys, grouped_values, pos_block, seq_block, group_positions, sequence_ids):
    scores = jnp.einsum('qgrd,kgd->qgrk', query_block, grouped_keys, precision=TOP_PRECISION) * (1.0 / math.sqrt(HEAD_SIZE))
    scores = low_back(scores)
    allowed = (seq_block[:, None] == sequence_ids[None, :]) & (group_positions[None, :] <= pos_block[:, None])
    scores = jnp.where(allowed[:, None, None, :], scores, MASKED)
    row_top = lax.optimization_barrier(jnp.max(scores, axis=-1, keepdims=True))
    exponent = jnp.exp(scores - row_top)
    prob_rows = exponent / lax.optimization_barrier(jnp.sum(exponent, axis=-1, keepdims=True))
    return jnp.einsum('qgrk,kgd->qgrd', low(prob_rows), grouped_values, precision=TOP_PRECISION)

def attention_per_group(group_item):
    grouped_queries, grouped_keys, grouped_values, group_positions, sequence_ids = group_item
    block_length = min(512, GROUP_TOKENS)
    count_of_blocks = GROUP_TOKENS // block_length
    heads_per_key = QUERY_HEADS // KEY_VALUE_HEADS
    checked = jax.checkpoint(attend_block)

    def single_block(block_item):
        query_block, pos_block, seq_block = block_item
        return checked(query_block, grouped_keys, grouped_values, pos_block, seq_block, group_positions, sequence_ids)
    blocks_mixed = lax.map(single_block, (grouped_queries.reshape(count_of_blocks, block_length, KEY_VALUE_HEADS, heads_per_key, HEAD_SIZE), group_positions.reshape(count_of_blocks, block_length), sequence_ids.reshape(count_of_blocks, block_length)))
    return blocks_mixed.reshape(GROUP_TOKENS, KEY_VALUE_HEADS, heads_per_key, HEAD_SIZE)

def block_forward(tokens32, w_query, key_weight, w_value, w_out, w_gate, w_up, w_down, norm_gains, angles, positions_every, sequence_every):
    gain_attn = norm_gains[:D]
    gain_ffn = norm_gains[D:2 * D]
    gain_query = norm_gains[2 * D:2 * D + HEAD_SIZE]
    gain_key = norm_gains[2 * D + HEAD_SIZE:]
    normalized_rows = low(norm_rows(tokens32, gain_attn))
    query_raw = low_back(jnp.dot(normalized_rows, w_query, precision=TOP_PRECISION)).reshape(TOKEN_TOTAL, QUERY_HEADS, HEAD_SIZE)
    unrotated_key = low_back(jnp.dot(normalized_rows, key_weight, precision=TOP_PRECISION)).reshape(TOKEN_TOTAL, KEY_VALUE_HEADS, HEAD_SIZE)
    value_rows = low(low_back(jnp.dot(normalized_rows, w_value, precision=TOP_PRECISION)))
    rotated_query = low(rotate(norm_rows(query_raw, gain_query), angles))
    rotated_key = low(rotate(norm_rows(unrotated_key, gain_key), angles))
    heads_per_key = QUERY_HEADS // KEY_VALUE_HEADS
    attention_mixed = lax.map(attention_per_group, (rotated_query.reshape(GROUP_COUNT, GROUP_TOKENS, KEY_VALUE_HEADS, heads_per_key, HEAD_SIZE), rotated_key.reshape(GROUP_COUNT, GROUP_TOKENS, KEY_VALUE_HEADS, HEAD_SIZE), value_rows.reshape(GROUP_COUNT, GROUP_TOKENS, KEY_VALUE_HEADS, HEAD_SIZE), positions_every, sequence_every))
    mixed_low = low(low_back(attention_mixed.reshape(TOKEN_TOTAL, DQ)))
    residual_mid = tokens32 + low_back(jnp.dot(mixed_low, w_out, precision=TOP_PRECISION))
    normed_ffn = low(norm_rows(residual_mid, gain_ffn))
    gate_pre = low_back(jnp.dot(normed_ffn, w_gate, precision=TOP_PRECISION))
    up_pre = low_back(jnp.dot(normed_ffn, w_up, precision=TOP_PRECISION))
    act_low = low(jax.nn.silu(gate_pre) * up_pre)
    return residual_mid + low_back(jnp.dot(act_low, w_down, precision=TOP_PRECISION))

def reference(tokens, w_query, key_weight, w_value, w_out, w_gate, w_up, w_down, norm_gains, seq_lengths, slot_order, out_grad):
    slot_ids = jnp.arange(GSLOTS, dtype=jnp.int32)
    positions_every, sequence_every, position_all = jax.vmap(lambda order_row, length_row: token_info(order_row, length_row, slot_ids, SLOT))(slot_order, seq_lengths)
    angles = rotary_angles(position_all.reshape(-1), HEAD_SIZE)
    inverse_order = jnp.argsort(slot_order, axis=1).astype(jnp.int32)
    dealt_tokens = reorder_slots(tokens.astype(jnp.float32), slot_order)
    dealt_grad = out_grad.astype(jnp.float32)
    primals = (dealt_tokens,) + tuple((array_in.astype(jnp.float32) for array_in in (w_query, key_weight, w_value, w_out, w_gate, w_up, w_down, norm_gains)))

    def forward_only(*inputs):
        return block_forward(*inputs, angles, positions_every, sequence_every)
    dealt_result, pull_back = jax.vjp(forward_only, *primals)
    grads = pull_back(dealt_grad)
    result = reorder_slots(dealt_result, inverse_order)
    grad_tokens = reorder_slots(grads[0], inverse_order)
    return (result.astype(jnp.bfloat16), grad_tokens, grads[1], grads[2], grads[3], grads[4], grads[5], grads[6], grads[7], grads[8])
```

```python
import functools
import math

import jax
import jax.numpy as jnp
from jax import lax
from jax.experimental import pallas as pl
from jax.experimental.pallas import tpu as pltpu
from jax.sharding import PartitionSpec as P

D = 1024
FF = 4608
QUERY_HEADS = 16
KEY_VALUE_HEADS = 8
HEAD = 64
SLOT = 128
GROUP = 8
ROWS = 2048
BLOCK = 256
QKV = 256
EPSILON = 1e-05
ROPE_THETA = 1000000.0
SCALE = 1.0 / math.sqrt(HEAD)
LOG2E = math.log2(math.e)
F32 = jnp.float32
BF16 = jnp.bfloat16
MESH = pl.DeviceIdType.MESH
DMA = pltpu.SemaphoreType.DMA
VM = pl.BlockSpec(memory_space=pltpu.VMEM)
ANY = pl.BlockSpec(memory_space=pl.ANY)
SM = pl.BlockSpec(memory_space=pltpu.SMEM)
SDS = jax.ShapeDtypeStruct


def nn(a, b):
    return lax.dot_general(a, b, (((1,), (0,)), ((), ())), preferred_element_type=F32)


def nt(a, b):
    return lax.dot_general(a, b, (((1,), (1,)), ((), ())), preferred_element_type=F32)


def tn(a, b):
    return lax.dot_general(a, b, (((0,), (0,)), ((), ())), preferred_element_type=F32)


def rcopy(src, dst, send, recv, dev):
    return pltpu.make_async_remote_copy(
        src_ref=src, dst_ref=dst, send_sem=send, recv_sem=recv, device_id=(dev,), device_id_type=MESH
    )


def barrier(peers):
    sem = pltpu.get_barrier_semaphore()
    for q in peers:
        pl.semaphore_signal(sem, inc=1, device_id=(q,), device_id_type=MESH)
    pl.semaphore_wait(sem, len(peers))


def places(n):
    me = lax.axis_index("dp")
    p = lax.rem(me, GROUP)
    g = me // GROUP
    groups = n // GROUP
    zq = [lax.rem(g + s, groups) * GROUP + p for s in range(1, groups)]
    zg = [lax.rem(g + s, groups) for s in range(1, groups)]
    return me, p, g, groups, zq, zg


def start_all(copies):
    for c in copies:
        c.start()
    return copies


def wait_all(copies):
    for c in copies:
        c.wait()


def gather_plane(me, p, src, out, ss, rs):
    half = src.shape[0] // 2
    h = [pl.ds(0, half), pl.ds(half, half)]
    sib, xn, yn = me ^ 1, me ^ 2, me ^ 4

    def cp(a, blk, i, dev):
        return rcopy(a, out.at[blk] if isinstance(blk, jax.Array) else blk, ss.at[i], rs.at[i], dev)

    x0 = cp(src.at[h[0]], out.at[p, h[0]], 0, xn)
    y1 = cp(src.at[h[1]], out.at[p, h[1]], 1, yn)
    x1 = cp(src.at[h[1]], out.at[p, h[1]], 2, xn)
    y0 = cp(src.at[h[0]], out.at[p, h[0]], 3, yn)
    own = cp(src, out.at[p], 4, sib)
    first = start_all([x0, y1, x1, y0, own])

    def middle():
        x0.wait_recv()
        r0 = cp(out.at[p ^ 2, h[0]], out.at[p ^ 2, h[0]], 5, yn)
        f0 = cp(out.at[p ^ 2, h[0]], out.at[p ^ 2, h[0]], 6, sib)
        start_all([r0, f0])
        y1.wait_recv()
        r1 = cp(out.at[p ^ 4, h[1]], out.at[p ^ 4, h[1]], 7, xn)
        f1 = cp(out.at[p ^ 4, h[1]], out.at[p ^ 4, h[1]], 8, sib)
        start_all([r1, f1])
        x1.wait_recv()
        f2 = cp(out.at[p ^ 2, h[1]], out.at[p ^ 2, h[1]], 9, sib)
        f2.start()
        y0.wait_recv()
        f3 = cp(out.at[p ^ 4, h[0]], out.at[p ^ 4, h[0]], 10, sib)
        f3.start()
        r0.wait_recv()
        f4 = cp(out.at[p ^ 6, h[0]], out.at[p ^ 6, h[0]], 11, sib)
        f4.start()
        r1.wait_recv()
        f5 = cp(out.at[p ^ 6, h[1]], out.at[p ^ 6, h[1]], 12, sib)
        f5.start()
        own.wait_recv()
        for c in first + [r0, r1]:
            c.wait_send()
        for c in (f0, f1, f2, f3, f4, f5):
            c.wait()

    return middle


ORDER = (6, 2, 4, 0)


def reduce_plane(me, part, sibbuf, sendbuf, rbuf, s1, r1, s2, r2):
    p = lax.rem(me, GROUP)
    first = start_all(
        [
            rcopy(part(p ^ (m ^ 1)), sibbuf.at[i], s1.at[i], r1.at[i], me ^ 1)
            for i, m in enumerate(ORDER)
        ]
    )

    def middle():
        second = []
        own = None
        for i, m in enumerate(ORDER):
            first[i].wait_recv()
            val = part(p ^ m)[...].astype(F32) + sibbuf[i].astype(F32)
            if m:
                sendbuf[i] = val.astype(BF16)
                c = rcopy(sendbuf.at[i], rbuf.at[i], s2.at[i], r2.at[i], me ^ m)
                c.start()
                second.append(c)
            else:
                own = val
        for i, c in enumerate(second):
            c.wait_recv()
            own = own + rbuf[i].astype(F32)
        for c in first + second:
            c.wait_send()
        return own

    return middle


def gather_kernel(n, x, dy, a1, a2, wo, wd, gt, xo, dyo, a1o, a2o, woo, wdo, gto, ls, xs, xr, ds_, dr, ps, pr, zs, zr):
    me, p, g, groups, zq, zg = places(n)
    barrier([me ^ m for m in range(1, GROUP)] + zq)
    nz = groups - 1
    local = [
        pltpu.make_async_copy(a1.at[p], a1o.at[g, p], ls.at[0]),
        pltpu.make_async_copy(gt, gto.at[g, p], ls.at[1]),
        pltpu.make_async_copy(wo, woo.at[g, p], ls.at[2]),
        pltpu.make_async_copy(a2.at[p], a2o.at[g, p], ls.at[3]),
        pltpu.make_async_copy(wd, wdo.at[g], ls.at[4]),
        pltpu.make_async_copy(x, xo.at[p], ls.at[5]),
        pltpu.make_async_copy(dy, dyo.at[p], ls.at[6]),
    ]
    start_all(local)
    pc = {}
    for k, (src, dst) in enumerate(((a1, a1o), (gt, gto))):
        for m in range(1, GROUP):
            block = src.at[p ^ m] if k == 0 else src
            pc[k, m] = rcopy(block, dst.at[g, p], ps.at[k, m - 1], pr.at[k, m - 1], me ^ m)
            pc[k, m].start()
    xmid = gather_plane(me, p, x, xo, xs, xr)
    for k, (src, dst) in ((2, (wo, woo)), (3, (a2, a2o))):
        for m in range(1, GROUP):
            block = src.at[p ^ m] if k == 3 else src
            pc[k, m] = rcopy(block, dst.at[g, p], ps.at[k, m - 1], pr.at[k, m - 1], me ^ m)
            pc[k, m].start()
    zc = start_all([rcopy(wd, wdo.at[g], zs.at[4, s], zr.at[4, s], zq[s]) for s in range(nz)])
    for k, dst in enumerate((a1o, gto)):
        for m in range(1, GROUP):
            pc[k, m].wait_recv()
        local[k].wait()
        zc += start_all([rcopy(dst.at[g], dst.at[g], zs.at[k, s], zr.at[k, s], zq[s]) for s in range(nz)])
    for k, dst in ((2, woo), (3, a2o)):
        for m in range(1, GROUP):
            pc[k, m].wait_recv()
        local[k].wait()
        zc += start_all([rcopy(dst.at[g], dst.at[g], zs.at[k, s], zr.at[k, s], zq[s]) for s in range(nz)])
    dmid = gather_plane(me, p, dy, dyo, ds_, dr)
    xmid()
    dmid()
    for c in pc.values():
        c.wait_send()
    for c in local[4:]:
        c.wait()
    wait_all(zc)


def gather_all(n, x, dy, a1, a2, wo, wd, gt):
    groups = n // GROUP
    r = wo.shape[0]
    ffc = wd.shape[0]
    return pl.pallas_call(
        functools.partial(gather_kernel, n),
        out_shape=(
            SDS((GROUP, BLOCK, D), BF16),
            SDS((GROUP, BLOCK, D), BF16),
            SDS((groups, GROUP, r, a1.shape[-1]), BF16),
            SDS((groups, GROUP, r, a2.shape[-1]), BF16),
            SDS((groups, GROUP, r, D), BF16),
            SDS((groups, ffc, D), BF16),
            SDS((groups, GROUP, 8, 128), F32),
        ),
        in_specs=[ANY] * 7,
        out_specs=(ANY,) * 7,
        scratch_shapes=[
            DMA((7,)),
            DMA((13,)),
            DMA((13,)),
            DMA((13,)),
            DMA((13,)),
            DMA((4, 7)),
            DMA((4, 7)),
            DMA((5, groups - 1)),
            DMA((5, groups - 1)),
        ],
        compiler_params=pltpu.CompilerParams(collective_id=1, has_side_effects=True),
        name="gather_all",
    )(x, dy, a1, a2, wo, wd, gt)


def swap_halves(v):
    lane = lax.broadcasted_iota(jnp.int32, v.shape, 1)
    low = lax.rem(lane, HEAD) < HEAD // 2
    width = v.shape[1]
    return jnp.where(low, pltpu.roll(v, width - HEAD // 2, 1), pltpu.roll(v, HEAD // 2, 1))


def head_mean(v):
    lane = lax.broadcasted_iota(jnp.int32, v.shape, 1)
    low = lane < HEAD
    a = jnp.sum(jnp.where(low, v, 0.0), axis=-1, keepdims=True)
    b = jnp.sum(jnp.where(low, 0.0, v), axis=-1, keepdims=True)
    return jnp.where(low, a, b) * (1.0 / HEAD)


def seq_start(row, len_ref, g):
    e1 = len_ref[g, 0]
    e2 = e1 + len_ref[g, 1]
    e3 = e2 + len_ref[g, 2]
    zero = row * 0
    s = jnp.where(row >= e1, zero + e1, zero)
    s = jnp.where(row >= e2, zero + e2, s)
    return jnp.where(row >= e3, zero + e3, s)


def tables(cs_ref):
    t = cs_ref[...].T
    c, s = t[:, : HEAD // 2], t[:, HEAD // 2 :]
    return jnp.concatenate([c, c, c, c], axis=1), jnp.concatenate([-s, s, -s, s], axis=1)


def attn_fwd_kernel(len_ref, x_ref, w_ref, ga_ref, gqk_ref, cs_ref, h_ref, raw_ref, q_ref, kv_ref, mix_ref, mixf_ref, lse_ref, k_s, v_s, acc):
    i = pl.program_id(0)
    g = lax.axis_index("dp") // GROUP
    xb = x_ref[0].astype(F32)
    r = lax.rsqrt(jnp.mean(xb * xb, axis=-1, keepdims=True) + EPSILON)
    h = (xb * r * ga_ref[...]).astype(BF16)
    h_ref[0] = h
    raw = nn(h, w_ref[...])
    raw_ref[0] = raw
    ct, st = tables(cs_ref)
    qraw, kvraw = raw[:, :128], raw[:, 128:]
    qn = qraw * lax.rsqrt(head_mean(qraw * qraw) + EPSILON) * gqk_ref[0:1, :]
    q = (qn * ct + swap_halves(qn) * st).astype(BF16)
    kn = kvraw * lax.rsqrt(head_mean(kvraw * kvraw) + EPSILON) * gqk_ref[1:2, :]
    k = (kn * ct + swap_halves(kn) * st).astype(BF16)
    lane = lax.broadcasted_iota(jnp.int32, (BLOCK, 128), 1)
    kv = jnp.where(lane < HEAD, k.astype(F32), kvraw).astype(BF16)
    q_ref[0] = q
    kv_ref[0] = kv
    k_s[pl.ds(i * BLOCK, BLOCK), :] = kv[:, :HEAD]
    v_s[pl.ds(i * BLOCK, BLOCK), :] = jnp.where(lane < HEAD, pltpu.roll(kvraw, HEAD, 1), 1.0).astype(BF16)
    q2 = jnp.concatenate([q[:, :HEAD], q[:, HEAD:]], axis=0)
    acc[...] = jnp.zeros_like(acc)
    row = lax.broadcasted_iota(jnp.int32, (2 * BLOCK, 1), 0)
    qrow = i * BLOCK + jnp.where(row >= BLOCK, row - BLOCK, row)
    qstart = seq_start(qrow, len_ref, g)
    first = seq_start(i * BLOCK, len_ref, g) // BLOCK
    col = lax.broadcasted_iota(jnp.int32, (2 * BLOCK, BLOCK), 1)

    def step(j, carry):
        kb = k_s[pl.ds(pl.multiple_of(j * BLOCK, BLOCK), BLOCK), :]
        vb = v_s[pl.ds(pl.multiple_of(j * BLOCK, BLOCK), BLOCK), :]
        s = nt(q2, kb)
        kc = col + j * BLOCK
        ok = (kc >= qstart) & (kc <= qrow)
        e = jnp.where(ok, jnp.exp2(s * (SCALE * LOG2E)), 0.0).astype(BF16)
        acc[...] += nn(e, vb)
        return carry

    lax.fori_loop(first, i + 1, step, 0)
    total = acc[:, HEAD:]
    m = acc[:, :HEAD] / total
    both = jnp.concatenate([m[:BLOCK], m[BLOCK:]], axis=1)
    mixf_ref[0] = both
    mix_ref[0] = both.astype(BF16)
    lse_ref[0] = jnp.log2(total.T)[:8, :]


def attn_fwd(lengths, x_all, wqkv, ga, gqk, cs):
    blk = lambda c: pl.BlockSpec((1, BLOCK, c), lambda i: (i, 0, 0))
    whole = lambda s: pl.BlockSpec(s, lambda i: (0,) * len(s), pipeline_mode=pl.Buffered(1))
    nb = ROWS // BLOCK
    return pl.pallas_call(
        attn_fwd_kernel,
        grid=(nb,),
        in_specs=[
            SM,
            blk(D),
            whole((D, QKV)),
            whole((1, D)),
            whole((2, 128)),
            pl.BlockSpec((HEAD, BLOCK), lambda i: (0, i)),
        ],
        out_specs=(blk(D), blk(QKV), blk(128), blk(128), blk(128), blk(128), pl.BlockSpec((1, 8, 2 * BLOCK), lambda i: (i, 0, 0))),
        out_shape=(
            SDS((nb, BLOCK, D), BF16),
            SDS((nb, BLOCK, QKV), F32),
            SDS((nb, BLOCK, 128), BF16),
            SDS((nb, BLOCK, 128), BF16),
            SDS((nb, BLOCK, 128), BF16),
            SDS((nb, BLOCK, 128), F32),
            SDS((nb, 8, 2 * BLOCK), F32),
        ),
        scratch_shapes=[
            pltpu.VMEM((ROWS, HEAD), BF16),
            pltpu.VMEM((ROWS, 128), BF16),
            pltpu.VMEM((2 * BLOCK, 128), F32),
        ],
        compiler_params=pltpu.CompilerParams(dimension_semantics=("arbitrary",), vmem_limit_bytes=48 << 20),
        cost_estimate=pl.CostEstimate(flops=4 * 10**9, bytes_accessed=16 << 20, transcendentals=4 * 10**6),
        name="attn_fwd",
    )(lengths, x_all, wqkv, ga, gqk, cs)


def mid_kernel(n, mix, x, wo, gf, res, mown, h2, h2all, mbuf, ps, pr, hs, hr, ls):
    me, p, g, groups, zq, zg = places(n)
    barrier([me ^ m for m in range(1, GROUP)])
    pc = start_all(
        [rcopy(mix.at[p ^ m], mbuf.at[p], ps.at[m - 1], pr.at[m - 1], me ^ m) for m in range(1, GROUP)]
    )
    mbuf[p] = mix[p]
    for c in pc:
        c.wait_recv()
    m = jnp.concatenate([mbuf[b] for b in range(GROUP)], axis=1)
    mown[...] = m
    z = x[...].astype(F32) + nn(m, wo[...])
    res[...] = z
    r = lax.rsqrt(jnp.mean(z * z, axis=-1, keepdims=True) + EPSILON)
    h2[...] = (z * r * gf[...]).astype(BF16)
    done = gather_plane(me, p, h2, h2all, hs, hr)
    cl = pltpu.make_async_copy(h2, h2all.at[p], ls)
    cl.start()
    done()
    cl.wait()
    for c in pc:
        c.wait_send()


def mid(n, mix, x, wo, gf):
    return pl.pallas_call(
        functools.partial(mid_kernel, n),
        out_shape=(SDS((BLOCK, D), F32), SDS((BLOCK, D), BF16), SDS((BLOCK, D), BF16), SDS((GROUP, BLOCK, D), BF16)),
        in_specs=[VM] * 4,
        out_specs=(VM, VM, VM, ANY),
        scratch_shapes=[
            pltpu.VMEM((GROUP, BLOCK, 128), BF16),
            DMA((7,)),
            DMA((7,)),
            DMA((13,)),
            DMA((13,)),
            DMA,
        ],
        compiler_params=pltpu.CompilerParams(collective_id=2, has_side_effects=True, vmem_limit_bytes=48 << 20),
        name="mid",
    )(mix, x, wo, gf)


def ffn_kernel(inv_ref, h_ref, da_ref, db_ref, wgu_ref, wd_ref, po_ref, dh_ref, dwgu_ref, dwd_ref, agu, ad):
    i = pl.program_id(0)
    fl = wd_ref.shape[0]

    @pl.when(i == 0)
    def _():
        agu[...] = jnp.zeros_like(agu)
        ad[...] = jnp.zeros_like(ad)

    h = h_ref[0]
    dy = jnp.concatenate([da_ref[0], db_ref[0]], axis=0)
    gp = nn(h, wgu_ref[:, :fl])
    up = nn(h, wgu_ref[:, fl:])
    sig = 1.0 / (1.0 + jnp.exp(-gp))
    sg = gp * sig
    act = (sg * up).astype(BF16)
    po_ref[0] = nn(act, wd_ref[...]).astype(BF16)
    da = nt(dy, wd_ref[...])
    dg = (da * up * (sig * (1.0 + gp * (1.0 - sig)))).astype(BF16)
    du = (da * sg).astype(BF16)
    dh_ref[0] = (nt(dg, wgu_ref[:, :fl]) + nt(du, wgu_ref[:, fl:])).astype(BF16)
    ad[...] += tn(act, dy)
    agu[:, :fl] += tn(h, dg)
    agu[:, fl:] += tn(h, du)

    @pl.when(i == pl.num_programs(0) - 1)
    def _():
        dwgu_ref[...] = agu[...].astype(BF16)
        dwd_ref[...] = ad[...].astype(BF16)


def ffn(inv, h2all, dyall, wgu, wd):
    nb = ROWS // BLOCK
    fl = wd.shape[0]
    blk = pl.BlockSpec((1, BLOCK, D), lambda i, inv: (i, 0, 0))
    one = pl.Buffered(1)
    slots = dyall.reshape(ROWS // SLOT, SLOT, D)
    return pl.pallas_call(
        ffn_kernel,
        grid_spec=pltpu.PrefetchScalarGridSpec(
            num_scalar_prefetch=1,
            grid=(nb,),
            in_specs=[
                blk,
                pl.BlockSpec((1, SLOT, D), lambda i, inv: (inv[2 * i], 0, 0)),
                pl.BlockSpec((1, SLOT, D), lambda i, inv: (inv[2 * i + 1], 0, 0)),
                pl.BlockSpec((D, 2 * fl), lambda i, inv: (0, 0), pipeline_mode=one),
                pl.BlockSpec((fl, D), lambda i, inv: (0, 0), pipeline_mode=one),
            ],
            out_specs=(
                blk,
                blk,
                pl.BlockSpec((D, 2 * fl), lambda i, inv: (0, 0), pipeline_mode=one),
                pl.BlockSpec((fl, D), lambda i, inv: (0, 0), pipeline_mode=one),
            ),
            scratch_shapes=[pltpu.VMEM((D, 2 * fl), F32), pltpu.VMEM((fl, D), F32)],
        ),
        out_shape=(
            SDS((nb, BLOCK, D), BF16),
            SDS((nb, BLOCK, D), BF16),
            SDS((D, 2 * fl), BF16),
            SDS((fl, D), BF16),
        ),
        compiler_params=pltpu.CompilerParams(dimension_semantics=("arbitrary",), vmem_limit_bytes=56 << 20),
        cost_estimate=pl.CostEstimate(flops=24 * 10**9, bytes_accessed=24 << 20, transcendentals=10**6),
        name="ffn",
    )(inv, h2all, slots, slots, wgu, wd)


def norm_back(dyv, xv, gain):
    r = lax.rsqrt(jnp.mean(xv * xv, axis=-1, keepdims=True) + EPSILON)
    xr = xv * r
    gy = dyv * gain
    dx = r * (gy - xr * jnp.mean(gy * xr, axis=-1, keepdims=True))
    return dx, jnp.sum(dyv * xr, axis=0, keepdims=True)


def back_mid_kernel(n, dh, po, dyo, res, mown, wo, gf, result, gmid, dgf, dwo, dmh, sib1, send1, rb1, sib2, send2, rb2, dmix, sem, ps, pr):
    me, p, g, groups, zq, zg = places(n)
    barrier([me ^ m for m in range(1, GROUP)])
    part = lambda ref: (lambda b: ref.at[b])
    mid1 = reduce_plane(me, part(dh), sib1, send1, rb1, sem.at[0], sem.at[1], sem.at[2], sem.at[3])
    dh2 = mid1()
    mid2 = reduce_plane(me, part(po), sib2, send2, rb2, sem.at[4], sem.at[5], sem.at[6], sem.at[7])
    dx, dgain = norm_back(dh2, res[...], gf[...])
    gm = dyo[...].astype(F32) + dx
    gmid[...] = gm
    dgf[...] = dgain
    gl = gm.astype(BF16)
    dm = nt(gl, wo[...]).astype(BF16)
    for b in range(GROUP):
        dmix[b] = dm[:, 128 * b : 128 * (b + 1)]
    pc = start_all(
        [rcopy(dmix.at[p ^ m], dmh.at[p], ps.at[m - 1], pr.at[m - 1], me ^ m) for m in range(1, GROUP)]
    )
    dmh[p] = dmix[p]
    dwo[...] = tn(mown[...], gl).astype(BF16)
    result[...] = (mid2() + res[...]).astype(BF16)
    wait_all(pc)


def back_mid(n, dh, po, dyo, res, mown, wo, gf):
    rb = lambda k: pltpu.VMEM((k, BLOCK, D), BF16)
    return pl.pallas_call(
        functools.partial(back_mid_kernel, n),
        out_shape=(
            SDS((BLOCK, D), BF16),
            SDS((BLOCK, D), F32),
            SDS((1, D), F32),
            SDS((D, D), BF16),
            SDS((GROUP, BLOCK, 128), BF16),
        ),
        in_specs=[VM] * 7,
        out_specs=(VM,) * 5,
        scratch_shapes=[
            rb(4),
            rb(3),
            rb(3),
            rb(4),
            rb(3),
            rb(3),
            pltpu.VMEM((GROUP, BLOCK, 128), BF16),
            DMA((8, 4)),
            DMA((7,)),
            DMA((7,)),
        ],
        compiler_params=pltpu.CompilerParams(collective_id=3, has_side_effects=True, vmem_limit_bytes=58 << 20),
        name="back_mid",
    )(dh, po, dyo, res, mown, wo, gf)


def attn_bwd_kernel(len_ref, dm_ref, q_ref, kvall_ref, lse_ref, mixf_ref, h_ref, raw_ref, w_ref, gqk_ref, cs_ref, dh_ref, dw_ref, dg_ref, k_s, v_s, dkv, dqt, dws):
    step_id = pl.program_id(0)
    nb = pl.num_programs(0)
    i = nb - 1 - step_id
    g = lax.axis_index("dp") // GROUP

    @pl.when(step_id == 0)
    def _():
        dkv[...] = jnp.zeros_like(dkv)
        dws[...] = jnp.zeros_like(dws)
        dg_ref[...] = jnp.zeros_like(dg_ref)
        for b in range(ROWS // BLOCK):
            kvb = kvall_ref[b]
            k_s[pl.ds(b * BLOCK, BLOCK), :] = kvb[:, :HEAD]
            v_s[pl.ds(b * BLOCK, BLOCK), :] = kvb[:, HEAD:]

    q, do, mf = q_ref[0], dm_ref[0], mixf_ref[0]
    q2 = jnp.concatenate([q[:, :HEAD], q[:, HEAD:]], axis=0)
    do2 = jnp.concatenate([do[:, :HEAD], do[:, HEAD:]], axis=0)
    prod = (do.astype(F32) * mf).T
    delta = jnp.concatenate(
        [jnp.sum(prod[:HEAD], axis=0, keepdims=True), jnp.sum(prod[HEAD:], axis=0, keepdims=True)], axis=1
    )
    lse = lse_ref[0, 0:1, :]
    colq = lax.broadcasted_iota(jnp.int32, (1, 2 * BLOCK), 1)
    qrow = i * BLOCK + jnp.where(colq >= BLOCK, colq - BLOCK, colq)
    qstart = seq_start(qrow, len_ref, g)
    first = seq_start(i * BLOCK, len_ref, g) // BLOCK
    rowk = lax.broadcasted_iota(jnp.int32, (BLOCK, 2 * BLOCK), 0)
    dqt[...] = jnp.zeros_like(dqt)

    def step(j, carry):
        at = pl.ds(pl.multiple_of(j * BLOCK, BLOCK), BLOCK)
        kb, vb = k_s[at, :], v_s[at, :]
        s = nt(kb, q2)
        kc = rowk + j * BLOCK
        ok = (kc >= qstart) & (kc <= qrow)
        pr = jnp.where(ok, jnp.exp2(s * (SCALE * LOG2E) - lse), 0.0)
        dp = nt(vb, do2)
        dsc = (pr * (dp - delta)).astype(BF16)
        dkv[at, :HEAD] += nn(dsc, q2)
        dkv[at, HEAD:] += nn(pr.astype(BF16), do2)
        dqt[...] += tn(dsc, kb)
        return carry

    lax.fori_loop(first, i + 1, step, 0)
    ct, st = tables(cs_ref)
    raw = raw_ref[0]
    dq = jnp.concatenate([dqt[:BLOCK], dqt[BLOCK:]], axis=1) * SCALE
    dkvb = dkv[pl.ds(pl.multiple_of(i * BLOCK, BLOCK), BLOCK), :]
    lane = lax.broadcasted_iota(jnp.int32, (BLOCK, 128), 1)

    def pull(d, v, gain):
        dn = d * ct - swap_halves(d) * st
        r = lax.rsqrt(head_mean(v * v) + EPSILON)
        vr = v * r
        gy = dn * gain
        return r * (gy - vr * head_mean(gy * vr)), jnp.sum(dn * vr, axis=0, keepdims=True)

    dqr, dgq = pull(dq, raw[:, :128], gqk_ref[0:1, :])
    dkr, dgk = pull(dkvb * SCALE, raw[:, 128:], gqk_ref[1:2, :])
    dg_ref[0:1, :] += dgq
    dg_ref[1:2, :] += dgk
    dqkv = jnp.concatenate([dqr, jnp.where(lane < HEAD, dkr, dkvb)], axis=1).astype(BF16)
    dh_ref[0] = nt(dqkv, w_ref[...]).astype(BF16)
    dws[...] += tn(h_ref[0], dqkv)

    @pl.when(step_id == nb - 1)
    def _():
        dw_ref[...] = dws[...].astype(BF16)


def attn_bwd(lengths, dmh, q, kv, lse, mixf, h, raw, wqkv, gqk, cs):
    nb = ROWS // BLOCK
    blk = lambda c: pl.BlockSpec((1, BLOCK, c), lambda i: (nb - 1 - i, 0, 0))
    whole = lambda s: pl.BlockSpec(s, lambda i: (0,) * len(s), pipeline_mode=pl.Buffered(1))
    return pl.pallas_call(
        attn_bwd_kernel,
        grid=(nb,),
        in_specs=[
            SM,
            blk(128),
            blk(128),
            whole((nb, BLOCK, 128)),
            pl.BlockSpec((1, 8, 2 * BLOCK), lambda i: (nb - 1 - i, 0, 0)),
            blk(128),
            blk(D),
            blk(QKV),
            whole((D, QKV)),
            whole((2, 128)),
            pl.BlockSpec((HEAD, BLOCK), lambda i: (0, nb - 1 - i)),
        ],
        out_specs=(blk(D), whole((D, QKV)), whole((8, 128))),
        out_shape=(SDS((nb, BLOCK, D), BF16), SDS((D, QKV), BF16), SDS((8, 128), F32)),
        scratch_shapes=[
            pltpu.VMEM((ROWS, HEAD), BF16),
            pltpu.VMEM((ROWS, HEAD), BF16),
            pltpu.VMEM((ROWS, 128), F32),
            pltpu.VMEM((2 * BLOCK, HEAD), F32),
            pltpu.VMEM((D, QKV), F32),
        ],
        compiler_params=pltpu.CompilerParams(dimension_semantics=("arbitrary",), vmem_limit_bytes=48 << 20),
        cost_estimate=pl.CostEstimate(flops=8 * 10**9, bytes_accessed=16 << 20, transcendentals=4 * 10**6),
        name="attn_bwd",
    )(lengths, dmh, q, kv, lse, mixf, h, raw, wqkv, gqk, cs)


def final_kernel(n, dh, x, gmid, ga, dgf, dgqk, dw1, dw2, dwd, dwo, gtok, o1, o2, od, oo, og, sib1, send1, rb1, z1, z2, zd, zo, t1, t2, wsib, wsend, wrb, wsum, gpart, gin, gsum, gz, sem, wsem, zs, zr, ps, pr, gs, gr):
    me, p, g, groups, zq, zg = places(n)
    nz = groups - 1
    barrier([me ^ m for m in range(1, GROUP)] + zq)
    mid1 = reduce_plane(me, lambda b: dh.at[b], sib1, send1, rb1, sem.at[0], sem.at[1], sem.at[2], sem.at[3])
    zc = {}
    for k, (src, dst) in enumerate(((dw1, z1), (dw2, z2), (dwd, zd))):
        for s in range(nz):
            zc[k, s] = rcopy(src.at[zg[s]], dst.at[s], zs.at[k, s], zr.at[k, s], zq[s])
            zc[k, s].start()
    first = start_all(
        [rcopy(dwo.at[:, p ^ (m ^ 1)], wsib.at[i], wsem.at[0, i], wsem.at[1, i], me ^ 1) for i, m in enumerate(ORDER)]
    )
    dh1 = mid1()
    dx, dga = norm_back(dh1, x[...].astype(F32), ga[...])
    gtok[...] = gmid[...] + dx
    gpart[...] = jnp.zeros_like(gpart)
    for b in range(8):
        gpart[b : b + 1, :] = dga[:, 128 * b : 128 * (b + 1)]
        gpart[8 + b : 9 + b, :] = dgf[:, 128 * b : 128 * (b + 1)]
    lane = lax.broadcasted_iota(jnp.int32, (1, 128), 1)
    dgq = dgqk[0:1, :]
    dgq = dgq + pltpu.roll(jnp.broadcast_to(dgq, (8, 128)), HEAD, 1)[0:1, :]
    dgk = pltpu.roll(jnp.broadcast_to(dgqk[1:2, :], (8, 128)), HEAD, 1)[0:1, :]
    gpart[16:17, :] = jnp.where(lane < HEAD, dgq, dgk)
    gc = start_all([rcopy(gpart, gin.at[m - 1], gs.at[m - 1], gr.at[m - 1], me ^ m) for m in range(1, GROUP)])
    second = []
    own = None
    for i, m in enumerate(ORDER):
        first[i].wait_recv()
        val = dwo[:, p ^ m].astype(F32) + wsib[i].astype(F32)
        if m:
            wsend[i] = val.astype(BF16)
            c = rcopy(wsend.at[i], wrb.at[i], wsem.at[2, i], wsem.at[3, i], me ^ m)
            c.start()
            second.append(c)
        else:
            own = val
    tot = gpart[...]
    for m in range(1, GROUP):
        gc[m - 1].wait_recv()
        tot = tot + gin[m - 1]
    gsum[...] = tot
    gzc = start_all([rcopy(gsum, gz.at[s], gs.at[7 + s], gr.at[7 + s], zq[s]) for s in range(nz)])
    for i, c in enumerate(second):
        c.wait_recv()
        own = own + wrb[i].astype(F32)
    wsum[...] = own.astype(BF16)
    for s in range(nz):
        zc[3, s] = rcopy(wsum.at[zg[s]], zo.at[s], zs.at[3, s], zr.at[3, s], zq[s])
        zc[3, s].start()
    pc = []
    for k, (src, dst, tmp, out) in enumerate(((dw1, z1, t1, o1), (dw2, z2, t2, o2))):
        acc = src[g].astype(F32)
        for s in range(nz):
            zc[k, s].wait_recv()
            acc = acc + dst[s].astype(F32)
        tmp[...] = acc.astype(BF16)
        for m in range(1, GROUP):
            c = rcopy(tmp.at[p ^ m], out.at[p], ps.at[k, m - 1], pr.at[k, m - 1], me ^ m)
            c.start()
            pc.append(c)
        out[p] = tmp[p]
    for k, (mine, dst, out) in ((2, (dwd[g], zd, od)), (3, (wsum[g], zo, oo))):
        acc = mine.astype(F32)
        for s in range(nz):
            zc[k, s].wait_recv()
            acc = acc + dst[s].astype(F32)
        out[...] = acc
    tot = gsum[...]
    for s in range(nz):
        gzc[s].wait_recv()
        tot = tot + gz[s]
    og[...] = tot
    wait_all(pc)
    for c in gc + gzc + first + second + list(zc.values()):
        c.wait_send()


def final(n, dh, x, gmid, ga, dgf, dgqk, dw1, dw2, dwd, dwo):
    groups = n // GROUP
    nz = groups - 1
    r, c1, c2, ffc = dw1.shape[2], dw1.shape[3], dw2.shape[3], dwd.shape[1]
    rb = lambda k: pltpu.VMEM((k, BLOCK, D), BF16)
    return pl.pallas_call(
        functools.partial(final_kernel, n),
        out_shape=(
            SDS((BLOCK, D), F32),
            SDS((GROUP, r, c1), BF16),
            SDS((GROUP, r, c2), BF16),
            SDS((ffc, D), F32),
            SDS((r, D), F32),
            SDS((24, 128), F32),
        ),
        in_specs=[VM] * 10,
        out_specs=(VM,) * 6,
        scratch_shapes=[
            rb(4),
            rb(3),
            rb(3),
            pltpu.VMEM((nz, GROUP, r, c1), BF16),
            pltpu.VMEM((nz, GROUP, r, c2), BF16),
            pltpu.VMEM((nz, ffc, D), BF16),
            pltpu.VMEM((nz, r, D), BF16),
            pltpu.VMEM((GROUP, r, c1), BF16),
            pltpu.VMEM((GROUP, r, c2), BF16),
            pltpu.VMEM((4, groups, r, D), BF16),
            pltpu.VMEM((3, groups, r, D), BF16),
            pltpu.VMEM((3, groups, r, D), BF16),
            pltpu.VMEM((groups, r, D), BF16),
            pltpu.VMEM((24, 128), F32),
            pltpu.VMEM((7, 24, 128), F32),
            pltpu.VMEM((24, 128), F32),
            pltpu.VMEM((nz, 24, 128), F32),
            DMA((4, 4)),
            DMA((4, 4)),
            DMA((4, nz)),
            DMA((4, nz)),
            DMA((2, 7)),
            DMA((2, 7)),
            DMA((7 + nz,)),
            DMA((7 + nz,)),
        ],
        compiler_params=pltpu.CompilerParams(collective_id=4, has_side_effects=True, vmem_limit_bytes=58 << 20),
        name="final",
    )(dh, x, gmid, ga, dgf, dgqk, dw1, dw2, dwd, dwo)


def body(n, tokens, w_query, key_weight, w_value, w_out, w_gate, w_up, w_down, norm_gains, seq_lengths, slot_order, out_grad):
    groups = n // GROUP
    r = w_query.shape[0]
    ffc = w_down.shape[0]
    device = lax.axis_index("dp")
    g, p = device // GROUP, device % GROUP
    lengths = seq_lengths
    a1 = jnp.concatenate(
        [
            w_query.reshape(r, GROUP, 128),
            key_weight.reshape(r, GROUP, HEAD),
            w_value.reshape(r, GROUP, HEAD),
        ],
        axis=2,
    ).transpose(1, 0, 2)
    wgu = jnp.stack([w_gate, w_up], axis=1).reshape(r, 2, groups, GROUP, ffc)
    a2 = wgu.transpose(3, 0, 1, 2, 4).reshape(GROUP, r, 2 * groups * ffc)
    share = norm_gains.shape[0]
    gt = jnp.pad(norm_gains.astype(F32)[None, :], ((0, 7), (0, 128 - share)))
    x_all, dy_all, w1, w2, wo, wd, gains = gather_all(n, tokens, out_grad, a1, a2, w_out, w_down, gt)
    gains = gains[:, :, 0, :share].reshape(1, -1)
    ga, gf = gains[:, :D], gains[:, D : 2 * D]
    gq = gains[:, 2 * D : 2 * D + HEAD]
    gk = gains[:, 2 * D + HEAD :]
    gqk = jnp.concatenate([jnp.concatenate([gq, gq], axis=1), jnp.concatenate([gk, gk], axis=1)], axis=0)
    wqkv = w1.reshape(D, QKV)
    wgu = w2.reshape(D, -1)
    wo = wo.reshape(D, D)
    wd = wd.reshape(-1, D)
    row = jnp.arange(ROWS, dtype=jnp.int32)
    length_row = lax.dynamic_index_in_dim(seq_lengths, g, 0, keepdims=False)
    order_row = lax.dynamic_index_in_dim(slot_order, g, 0, keepdims=False)
    ends = jnp.cumsum(length_row)
    start = jnp.max(jnp.where(row[:, None] >= ends[None, :], ends[None, :], 0), axis=1)
    frequency = jnp.exp(jnp.arange(HEAD // 2, dtype=F32) * (-2.0 * math.log(ROPE_THETA) / HEAD))
    angles = frequency[:, None] * (row - start).astype(F32)[None, :]
    cs = jnp.concatenate([jnp.cos(angles), jnp.sin(angles)], axis=0)
    slots = jnp.arange(ROWS // SLOT, dtype=jnp.int32)
    inv = jnp.sum(jnp.where(order_row[None, :] == slots[:, None], slots[None, :], 0), axis=1)

    h, raw, q, kv, mix, mixf, lse = attn_fwd(lengths, x_all, wqkv, ga, gqk, cs)
    res, mown, _, h2_all = mid(n, mix, tokens, wo, gf)
    po, dh2, dwgu, dwd = ffn(inv, h2_all, dy_all, wgu, wd)
    dslots = dy_all.reshape(ROWS // SLOT, SLOT, D)
    dy_own = jnp.concatenate(
        [lax.dynamic_index_in_dim(dslots, inv[2 * p + k], 0, keepdims=False) for k in range(2)], axis=0
    )
    result, gmid, dgf, dwo, dmh = back_mid(n, dh2, po, dy_own, res, mown, wo, gf)
    dh1, dwqkv, dgqk = attn_bwd(lengths, dmh, q, kv, lse, mixf, h, raw, wqkv, gqk, cs)
    gtok, o1, o2, od, oo, og = final(
        n,
        dh1,
        tokens,
        gmid,
        ga,
        dgf,
        dgqk,
        dwqkv.reshape(groups, GROUP, r, QKV),
        dwgu.reshape(groups, GROUP, r, -1),
        dwd.reshape(groups, ffc, D),
        dwo.reshape(groups, GROUP, r, D),
    )
    o1 = o1.transpose(1, 0, 2).astype(F32)
    gwq = o1[:, :, :128].reshape(r, -1)
    gwk = o1[:, :, 128 : 128 + HEAD].reshape(r, -1)
    gwv = o1[:, :, 128 + HEAD :].reshape(r, -1)
    o2 = o2.reshape(GROUP, r, 2, groups, ffc).transpose(2, 1, 3, 0, 4).reshape(2, r, -1).astype(F32)
    gains_out = lax.dynamic_slice(og.reshape(-1), (device * share,), (share,))
    return result, gtok, gwq, gwk, gwv, oo, o2[0], o2[1], od, gains_out


def solution(mesh):
    n = mesh.shape["dp"]
    row = P("dp", None)
    return jax.shard_map(
        functools.partial(body, n),
        mesh=mesh,
        in_specs=(row,) * 8 + (P("dp"), P(), P(), row),
        out_specs=(row,) * 9 + (P("dp"),),
        check_vma=False,
    )
```

```python
import functools
import math

import jax
import jax.numpy as jnp
from jax import lax
from jax.experimental import pallas as pl
from jax.experimental.pallas import tpu as pltpu
from jax.sharding import PartitionSpec as P

D = 1024
FF = 4608
QUERY_HEADS = 16
KEY_VALUE_HEADS = 8
HEAD = 64
SLOT = 128
GROUP = 8
ROWS = 2048
BLOCK = 256
QKV = 256
WINDOW = 4
EPSILON = 1e-05
ROPE_THETA = 1000000.0
SCALE = 1.0 / math.sqrt(HEAD)
LOG2E = math.log2(math.e)
F32 = jnp.float32
BF16 = jnp.bfloat16
MESH = pl.DeviceIdType.MESH
DMA = pltpu.SemaphoreType.DMA
VM = pl.BlockSpec(memory_space=pltpu.VMEM)
ANY = pl.BlockSpec(memory_space=pl.ANY)
SM = pl.BlockSpec(memory_space=pltpu.SMEM)
SDS = jax.ShapeDtypeStruct


def nn(a, b):
    return lax.dot_general(a, b, (((1,), (0,)), ((), ())), preferred_element_type=F32)


def nt(a, b):
    return lax.dot_general(a, b, (((1,), (1,)), ((), ())), preferred_element_type=F32)


def tn(a, b):
    return lax.dot_general(a, b, (((0,), (0,)), ((), ())), preferred_element_type=F32)


def rcopy(src, dst, send, recv, dev):
    return pltpu.make_async_remote_copy(
        src_ref=src, dst_ref=dst, send_sem=send, recv_sem=recv, device_id=(dev,), device_id_type=MESH
    )


def barrier(peers):
    sem = pltpu.get_barrier_semaphore()
    for q in peers:
        pl.semaphore_signal(sem, inc=1, device_id=(q,), device_id_type=MESH)
    pl.semaphore_wait(sem, len(peers))


def places(n):
    me = lax.axis_index("dp")
    p = lax.rem(me, GROUP)
    g = me // GROUP
    groups = n // GROUP
    zq = [lax.rem(g + s, groups) * GROUP + p for s in range(1, groups)]
    zg = [lax.rem(g + s, groups) for s in range(1, groups)]
    return me, p, g, groups, zq, zg


def start_all(copies):
    for c in copies:
        c.start()
    return copies


def wait_all(copies):
    for c in copies:
        c.wait()


class PlaneGather:
    COPIES = 14

    def __init__(self, me, p, src, dst, ss, rs, ls=None):
        sib, xn, yn = me ^ 1, me ^ 2, me ^ 4

        def cp(a, b, i, dev):
            return rcopy(a, b, ss.at[i], rs.at[i], dev)

        def own(i, dev):
            return [cp(src(h), dst(p, h), i + h, dev) for h in range(2)]

        def on(m, h, i, dev):
            return cp(dst(p ^ m, h), dst(p ^ m, h), i, dev)

        self.x, self.y, self.o = own(0, xn), own(2, yn), own(4, sib)
        self.r = [on(2, 0, 6, yn), on(4, 1, 7, xn)]
        self.fx = [on(2, h, 8 + h, sib) for h in range(2)]
        self.fy = [on(4, h, 10 + h, sib) for h in range(2)]
        self.fd = [on(6, h, 12 + h, sib) for h in range(2)]
        self.local = [] if ls is None else [
            pltpu.make_async_copy(src(h), dst(p, h), ls.at[h]) for h in range(2)
        ]

    def start(self):
        start_all([self.x[0], self.y[1], self.x[1], self.y[0]] + self.o + self.local)

    def relay1(self):
        self.x[0].wait_recv()
        start_all([self.r[0], self.fx[0]])
        self.y[1].wait_recv()
        start_all([self.r[1], self.fy[1]])

    def relay2(self):
        self.x[1].wait_recv()
        self.fx[1].start()
        self.y[0].wait_recv()
        self.fy[0].start()

    def relay3(self):
        for h in range(2):
            self.r[h].wait_recv()
            self.fd[h].start()

    def finish(self):
        wait_all(self.o + self.fx + self.fy + self.fd + self.local)
        for c in self.x + self.y + self.r:
            c.wait_send()


class Ring:
    def __init__(self, n, p, g, src, dst, ss, rs, ls=None):
        groups = n // GROUP
        to = lambda s: lax.rem(g + s, groups) * GROUP + p
        at = lambda s: lax.rem(g + s, groups)

        def cp(a, b, i, dev):
            return rcopy(a, b, ss.at[i], rs.at[i], dev)

        self.relays = []
        if groups == 4:
            self.up = [cp(src(h), dst(g, h), h, to(1)) for h in range(2)]
            self.down = [cp(src(h), dst(g, h), 2 + h, to(3)) for h in range(2)]
            self.first = [self.up[0], self.down[1], self.up[1], self.down[0]]
            below, above = at(3), at(1)
            self.relays = [cp(dst(below, 0), dst(below, 0), 4, to(1)), cp(dst(above, 1), dst(above, 1), 5, to(3))]
        else:
            self.first = [cp(src(None), dst(g, None), s - 1, to(s)) for s in range(1, groups)]
        self.local = [] if ls is None else [pltpu.make_async_copy(src(None), dst(g, None), ls)]

    def start(self):
        start_all(self.first + self.local)

    def relay(self):
        if self.relays:
            self.up[0].wait_recv()
            self.relays[0].start()
            self.down[1].wait_recv()
            self.relays[1].start()

    def finish(self):
        if self.relays:
            self.up[1].wait_recv()
            self.down[0].wait_recv()
            for c in self.first:
                c.wait_send()
        else:
            wait_all(self.first)
        wait_all(self.relays + self.local)


def ring_count(n):
    return max(6, n // GROUP - 1)


def halves(length):
    cut = length // 2
    part = (pl.ds(0, cut), pl.ds(cut, length - cut))
    return lambda h: slice(None) if h is None else part[h]


class RingReduce:
    def __init__(self, n, p, g, part, low, high, send, fin, ss, rs):
        groups = n // GROUP
        to = lambda s: lax.rem(g + s, groups) * GROUP + p
        at = lambda s: lax.rem(g + s, groups)
        hs = halves(part.shape[1])
        self.part, self.fin, self.send, self.g, self.hs = part, fin, send, g, hs

        def cp(a, b, i, dev):
            return rcopy(a, b, ss.at[i], rs.at[i], dev)

        self.ring = groups == 4
        if self.ring:
            self.above, self.below = at(1), at(3)
            self.low, self.high = low, high
            far = at(2)
            self.a = cp(part.at[far, hs(0)], low, 0, to(1))
            self.b = cp(part.at[far, hs(1)], high, 1, to(3))
            self.c = cp(part.at[self.above, hs(1)], fin.at[0, hs(1)], 2, to(1))
            self.d = cp(part.at[self.below, hs(0)], fin.at[1, hs(0)], 3, to(3))
            self.e = cp(send.at[hs(0)], fin.at[0, hs(0)], 4, to(1))
            self.f = cp(send.at[hs(1)], fin.at[1, hs(1)], 5, to(3))
            self.all = [self.a, self.b, self.c, self.d, self.e, self.f]
        else:
            self.all = [cp(part.at[at(s)], fin.at[s - 1], s - 1, to(s)) for s in range(1, groups)]
        self.count = groups - 1

    def start(self):
        start_all(self.all[:4] if self.ring else self.all)

    def relay(self):
        if self.ring:
            for got, buf, h, b, out in (
                (self.a, self.low, 0, self.above, self.e),
                (self.b, self.high, 1, self.below, self.f),
            ):
                got.wait_recv()
                at = self.hs(h)
                self.send[at] = (self.part[b, at].astype(F32) + buf[...].astype(F32)).astype(BF16)
                out.start()

    def finish(self):
        for c in self.all[2:] if self.ring else self.all:
            c.wait_recv()
        val = self.part[self.g].astype(F32)
        for s in range(2 if self.ring else self.count):
            val = val + self.fin[s].astype(F32)
        for c in self.all:
            c.wait_send()
        return val


def ring_scratch(n, shape):
    cut = shape[0] // 2
    groups = n // GROUP
    count = 2 if groups == 4 else groups - 1
    tail = tuple(shape[1:])
    vm = lambda s: pltpu.VMEM(s, BF16)
    return [
        vm((max(cut, 1),) + tail),
        vm((shape[0] - cut,) + tail),
        vm(tuple(shape)),
        vm((count,) + tuple(shape)),
        DMA((ring_count(n),)),
        DMA((ring_count(n),)),
    ]


ORDER = (6, 2, 4, 0)


class PlaneReduce:
    def __init__(self, me, part, sib, send, relay, fx, fy, ss, rs):
        p = lax.rem(me, GROUP)
        xn, yn = me ^ 2, me ^ 4
        hs = halves(sib.shape[1])
        self.hs, self.p, self.part = hs, p, part
        self.sib, self.send, self.relay, self.fx, self.fy = sib, send, relay, fx, fy

        def cp(a, b, i, dev):
            return rcopy(a, b, ss.at[i], rs.at[i], dev)

        self.first = [cp(part(p ^ (m ^ 1)), sib.at[i], i, me ^ 1) for i, m in enumerate(ORDER)]
        self.diag = [cp(send.at[0, hs(0)], relay.at[0], 4, xn), cp(send.at[0, hs(1)], relay.at[1], 5, yn)]
        self.toy = [cp(send.at[2, hs(h)], fy.at[hs(h)], 6 + h, yn) for h in range(2)]
        self.tox = [cp(send.at[1, hs(h)], fx.at[hs(h)], 8 + h, xn) for h in range(2)]

    def start(self):
        start_all(self.first)

    def chip(self, i):
        self.first[i].wait_recv()
        return self.part(self.p ^ ORDER[i])[...].astype(F32) + self.sib[i].astype(F32)

    def phase1(self):
        self.send[0] = self.chip(0).astype(BF16)
        start_all(self.diag)
        self.send[1] = self.chip(1).astype(BF16)
        self.tox[0].start()
        self.send[2] = self.chip(2).astype(BF16)
        self.toy[1].start()

    def phase2(self):
        self.diag[0].wait_recv()
        at = self.hs(0)
        self.send[2, at] = (self.send[2, at].astype(F32) + self.relay[0].astype(F32)).astype(BF16)
        self.toy[0].start()
        self.diag[1].wait_recv()
        at = self.hs(1)
        self.send[1, at] = (self.send[1, at].astype(F32) + self.relay[1].astype(F32)).astype(BF16)
        self.tox[1].start()

    def phase3(self):
        own = self.chip(3)
        for c in self.toy + self.tox:
            c.wait_recv()
        own = own + self.fx[...].astype(F32) + self.fy[...].astype(F32)
        for c in self.first + self.diag + self.toy + self.tox:
            c.wait_send()
        return own


def plane_scratch(shape):
    tail = tuple(shape[1:])
    vm = lambda *s: pltpu.VMEM(s + tail, BF16)
    return [
        vm(4, shape[0]),
        vm(3, shape[0]),
        vm(2, shape[0] // 2),
        vm(shape[0]),
        vm(shape[0]),
        DMA((10,)),
        DMA((10,)),
    ]


def gather_kernel(n, x, a1, a2, wo, wd, gt, xo, a1o, a2o, woo, wdo, gto, ls, xs, xr, ps, pr, zs, zr):
    me, p, g, groups, zq, zg = places(n)
    barrier([me ^ m for m in range(1, GROUP)] + zq)
    local = [
        pltpu.make_async_copy(a1.at[p], a1o.at[g, p], ls.at[0]),
        pltpu.make_async_copy(gt, gto.at[g, p], ls.at[1]),
        pltpu.make_async_copy(a2.at[p], a2o.at[p], ls.at[2]),
    ]
    start_all(local)
    pc = {}

    def exchange(k, src, dst):
        for m in range(1, GROUP):
            pc[k, m] = rcopy(src(p ^ m), dst, ps.at[k, m - 1], pr.at[k, m - 1], me ^ m)
            pc[k, m].start()

    exchange(0, lambda b: a1.at[b], a1o.at[g, p])
    exchange(1, lambda b: gt, gto.at[g, p])
    hx = halves(BLOCK)
    xg = PlaneGather(me, p, lambda h: x.at[hx(h)], lambda b, h: xo.at[b, hx(h)], xs, xr, ls.at[pl.ds(5, 2)])
    xg.start()

    def ring(k, src, dst, local=None):
        hk = halves(dst.shape[1])
        return Ring(n, p, g, lambda h: src.at[hk(h)], lambda b, h: dst.at[b, hk(h)], zs.at[k], zr.at[k], local)

    rings = [
        ring(0, a1o.at[g], a1o),
        ring(1, gto.at[g], gto),
        ring(2, wd, wdo, ls.at[3]),
        ring(3, wo, woo, ls.at[4]),
    ]
    rings[2].start()
    rings[3].start()
    exchange(2, lambda b: a2.at[b], a2o.at[p])
    for k in range(2):
        for m in range(1, GROUP):
            pc[k, m].wait_recv()
        local[k].wait()
        rings[k].start()
    xg.relay1()
    for k in (3, 0, 1, 2):
        rings[k].relay()
    xg.relay2()
    xg.relay3()
    for m in range(1, GROUP):
        pc[2, m].wait_recv()
    local[2].wait()
    for c in pc.values():
        c.wait_send()
    for k in range(4):
        rings[k].finish()
    xg.finish()


def gather_all(n, x, a1, a2, wo, wd, gt):
    groups = n // GROUP
    r = a1.shape[1]
    return pl.pallas_call(
        functools.partial(gather_kernel, n),
        out_shape=(
            SDS((GROUP, BLOCK, D), BF16),
            SDS((groups, GROUP, r, a1.shape[-1]), BF16),
            SDS((GROUP, r, a2.shape[-1]), BF16),
            SDS((groups,) + wo.shape, BF16),
            SDS((groups,) + wd.shape, BF16),
            SDS((groups, GROUP, 8, 128), F32),
        ),
        in_specs=[ANY] * 6,
        out_specs=(ANY,) * 6,
        scratch_shapes=[
            DMA((7,)),
            DMA((14,)),
            DMA((14,)),
            DMA((3, 7)),
            DMA((3, 7)),
            DMA((4, ring_count(n))),
            DMA((4, ring_count(n))),
        ],
        compiler_params=pltpu.CompilerParams(collective_id=1, has_side_effects=True),
        name="gather_all",
    )(x, a1, a2, wo, wd, gt)


def swap_halves(v):
    lane = lax.broadcasted_iota(jnp.int32, v.shape, 1)
    low = lax.rem(lane, HEAD) < HEAD // 2
    width = v.shape[1]
    return jnp.where(low, pltpu.roll(v, width - HEAD // 2, 1), pltpu.roll(v, HEAD // 2, 1))


def head_mean(v):
    lane = lax.broadcasted_iota(jnp.int32, v.shape, 1)
    low = lane < HEAD
    a = jnp.sum(jnp.where(low, v, 0.0), axis=-1, keepdims=True)
    b = jnp.sum(jnp.where(low, 0.0, v), axis=-1, keepdims=True)
    return jnp.where(low, a, b) * (1.0 / HEAD)


def seq_start(row, len_ref, g):
    e1 = len_ref[g, 0]
    e2 = e1 + len_ref[g, 1]
    e3 = e2 + len_ref[g, 2]
    zero = row * 0
    s = jnp.where(row >= e1, zero + e1, zero)
    s = jnp.where(row >= e2, zero + e2, s)
    return jnp.where(row >= e3, zero + e3, s)


def tables(cs_ref):
    t = cs_ref[...].T
    c, s = t[:, : HEAD // 2], t[:, HEAD // 2 :]
    return jnp.concatenate([c, c, c, c], axis=1), jnp.concatenate([-s, s, -s, s], axis=1)


def attn_fwd_kernel(n, len_ref, x_ref, w_ref, ga_ref, gqk_ref, cs_ref, dy, w2, wo, h_ref, raw_ref, q_ref, kv_ref, mix_ref, mixf_ref, lse_ref, dyo, w2o, woo, k_s, v_s, acc, ls, ds_, dr, os_, orr, zs, zr):
    i = pl.program_id(0)
    me, p, g, groups, zq, zg = places(n)
    hd, hw, ho = halves(BLOCK), halves(w2.shape[0]), halves(wo.shape[0])
    dg = PlaneGather(me, p, lambda h: dy.at[hd(h)], lambda b, h: dyo.at[b, hd(h)], ds_, dr, ls.at[pl.ds(0, 2)])
    og = PlaneGather(me, p, lambda h: wo.at[ho(h)], lambda b, h: woo.at[ho(h), b], os_, orr, ls.at[pl.ds(2, 2)])
    zg_ = Ring(n, p, g, lambda h: w2.at[hw(h)], lambda b, h: w2o.at[b, hw(h)], zs, zr, ls.at[4])

    @pl.when(i == 0)
    def _():
        barrier([me ^ m for m in (1, 2, 4)] + zq)
        dg.start()
        zg_.start()
        og.start()

    @pl.when(i == 3)
    def _():
        dg.relay1()

    @pl.when(i == 5)
    def _():
        zg_.relay()
        dg.relay2()

    @pl.when(i == 6)
    def _():
        og.relay1()
        dg.relay3()

    @pl.when(i == 7)
    def _():
        og.relay2()

    xb = x_ref[0].astype(F32)
    r = lax.rsqrt(jnp.mean(xb * xb, axis=-1, keepdims=True) + EPSILON)
    h = (xb * r * ga_ref[...]).astype(BF16)
    h_ref[0] = h
    raw = nn(h, w_ref[...])
    raw_ref[0] = raw
    ct, st = tables(cs_ref)
    qraw, kvraw = raw[:, :128], raw[:, 128:]
    qn = qraw * lax.rsqrt(head_mean(qraw * qraw) + EPSILON) * gqk_ref[0:1, :]
    q = (qn * ct + swap_halves(qn) * st).astype(BF16)
    kn = kvraw * lax.rsqrt(head_mean(kvraw * kvraw) + EPSILON) * gqk_ref[1:2, :]
    k = (kn * ct + swap_halves(kn) * st).astype(BF16)
    lane = lax.broadcasted_iota(jnp.int32, (BLOCK, 128), 1)
    kv = jnp.where(lane < HEAD, k.astype(F32), kvraw).astype(BF16)
    q_ref[0] = q
    kv_ref[0] = kv
    k_s[pl.ds(i * BLOCK, BLOCK), :] = kv[:, :HEAD]
    v_s[pl.ds(i * BLOCK, BLOCK), :] = jnp.where(lane < HEAD, pltpu.roll(kvraw, HEAD, 1), 1.0).astype(BF16)
    q2 = jnp.concatenate([q[:, :HEAD], q[:, HEAD:]], axis=0)
    acc[...] = jnp.zeros_like(acc)
    row = lax.broadcasted_iota(jnp.int32, (2 * BLOCK, 1), 0)
    qrow = i * BLOCK + jnp.where(row >= BLOCK, row - BLOCK, row)
    qstart = seq_start(qrow, len_ref, g)
    first = jnp.maximum(i - WINDOW, 0)
    col = lax.broadcasted_iota(jnp.int32, (2 * BLOCK, BLOCK), 1)

    def step(j, carry):
        kb = k_s[pl.ds(pl.multiple_of(j * BLOCK, BLOCK), BLOCK), :]
        vb = v_s[pl.ds(pl.multiple_of(j * BLOCK, BLOCK), BLOCK), :]
        s = nt(q2, kb)
        kc = col + j * BLOCK
        ok = (kc >= qstart) & (kc <= qrow)
        e = jnp.where(ok, jnp.exp2(s * (SCALE * LOG2E)), 0.0).astype(BF16)
        acc[...] += nn(e, vb)
        return carry

    lax.fori_loop(first, i + 1, step, 0)
    total = acc[:, HEAD:]
    m = acc[:, :HEAD] / total
    both = jnp.concatenate([m[:BLOCK], m[BLOCK:]], axis=1)
    mixf_ref[0] = both
    mix_ref[0] = both.astype(BF16)
    lse_ref[0] = jnp.log2(total.T)[:8, :]

    @pl.when(i == 7)
    def _():
        og.relay3()
        dg.finish()
        zg_.finish()
        og.finish()


def attn_fwd(n, lengths, x_all, wqkv, ga, gqk, cs, dy, w2, wo):
    groups = n // GROUP
    blk = lambda c: pl.BlockSpec((1, BLOCK, c), lambda i: (i, 0, 0))
    whole = lambda s: pl.BlockSpec(s, lambda i: (0,) * len(s), pipeline_mode=pl.Buffered(1))
    nb = ROWS // BLOCK
    return pl.pallas_call(
        functools.partial(attn_fwd_kernel, n),
        grid=(nb,),
        in_specs=[
            SM,
            blk(D),
            whole((D, QKV)),
            whole((1, D)),
            whole((2, 128)),
            pl.BlockSpec((HEAD, BLOCK), lambda i: (0, i)),
            ANY,
            ANY,
            ANY,
        ],
        out_specs=(blk(D), blk(QKV), blk(128), blk(128), blk(128), blk(128), pl.BlockSpec((1, 8, 2 * BLOCK), lambda i: (i, 0, 0)), ANY, ANY, ANY),
        out_shape=(
            SDS((nb, BLOCK, D), BF16),
            SDS((nb, BLOCK, QKV), F32),
            SDS((nb, BLOCK, 128), BF16),
            SDS((nb, BLOCK, 128), BF16),
            SDS((nb, BLOCK, 128), BF16),
            SDS((nb, BLOCK, 128), F32),
            SDS((nb, 8, 2 * BLOCK), F32),
            SDS((GROUP, BLOCK, D), BF16),
            SDS((groups,) + w2.shape, BF16),
            SDS((groups, GROUP) + wo.shape[1:], BF16),
        ),
        scratch_shapes=[
            pltpu.VMEM((ROWS, HEAD), BF16),
            pltpu.VMEM((ROWS, 128), BF16),
            pltpu.VMEM((2 * BLOCK, 128), F32),
            DMA((5,)),
            DMA((14,)),
            DMA((14,)),
            DMA((14,)),
            DMA((14,)),
            DMA((ring_count(n),)),
            DMA((ring_count(n),)),
        ],
        compiler_params=pltpu.CompilerParams(
            collective_id=5, has_side_effects=True, dimension_semantics=("arbitrary",), vmem_limit_bytes=48 << 20
        ),
        cost_estimate=pl.CostEstimate(flops=4 * 10**9, bytes_accessed=16 << 20, transcendentals=4 * 10**6),
        name="attn_fwd",
    )(lengths, x_all, wqkv, ga, gqk, cs, dy, w2, wo)


def mid_kernel(n, mix, x, wo, gf, res, mown, h2, h2all, mbuf, ps, pr, hs, hr, ls):
    me, p, g, groups, zq, zg = places(n)
    barrier([me ^ m for m in range(1, GROUP)])
    pc = start_all(
        [rcopy(mix.at[p ^ m], mbuf.at[p], ps.at[m - 1], pr.at[m - 1], me ^ m) for m in range(1, GROUP)]
    )
    mbuf[p] = mix[p]
    for c in pc:
        c.wait_recv()
    m = jnp.concatenate([mbuf[b] for b in range(GROUP)], axis=1)
    mown[...] = m
    z = x[...].astype(F32) + nn(m, wo[...])
    res[...] = z
    r = lax.rsqrt(jnp.mean(z * z, axis=-1, keepdims=True) + EPSILON)
    h2[...] = (z * r * gf[...]).astype(BF16)
    hb = halves(BLOCK)
    hg = PlaneGather(me, p, lambda h: h2.at[hb(h)], lambda b, h: h2all.at[b, hb(h)], hs, hr, ls)
    hg.start()
    hg.relay1()
    hg.relay2()
    hg.relay3()
    hg.finish()
    for c in pc:
        c.wait_send()


def mid(n, mix, x, wo, gf):
    return pl.pallas_call(
        functools.partial(mid_kernel, n),
        out_shape=(SDS((BLOCK, D), F32), SDS((BLOCK, D), BF16), SDS((BLOCK, D), BF16), SDS((GROUP, BLOCK, D), BF16)),
        in_specs=[VM] * 4,
        out_specs=(VM, VM, VM, ANY),
        scratch_shapes=[
            pltpu.VMEM((GROUP, BLOCK, 128), BF16),
            DMA((7,)),
            DMA((7,)),
            DMA((14,)),
            DMA((14,)),
            DMA((2,)),
        ],
        compiler_params=pltpu.CompilerParams(collective_id=2, has_side_effects=True, vmem_limit_bytes=48 << 20),
        name="mid",
    )(mix, x, wo, gf)


def ffn_kernel(inv_ref, h_ref, da_ref, db_ref, wgu_ref, wd_ref, po_ref, dh_ref, dwgu_ref, dwd_ref, agu, ad):
    i = pl.program_id(0)
    fl = wd_ref.shape[0]

    @pl.when(i == 0)
    def _():
        agu[...] = jnp.zeros_like(agu)
        ad[...] = jnp.zeros_like(ad)

    h = h_ref[0]
    dy = jnp.concatenate([da_ref[0], db_ref[0]], axis=0)
    gp = nn(h, wgu_ref[:, :fl])
    up = nn(h, wgu_ref[:, fl:])
    sig = 1.0 / (1.0 + jnp.exp(-gp))
    sg = gp * sig
    act = (sg * up).astype(BF16)
    po_ref[0] = nn(act, wd_ref[...]).astype(BF16)
    da = nt(dy, wd_ref[...])
    dg = (da * up * (sig * (1.0 + gp * (1.0 - sig)))).astype(BF16)
    du = (da * sg).astype(BF16)
    dh_ref[0] = (nt(dg, wgu_ref[:, :fl]) + nt(du, wgu_ref[:, fl:])).astype(BF16)
    ad[...] += tn(act, dy)
    agu[:, :fl] += tn(h, dg)
    agu[:, fl:] += tn(h, du)

    @pl.when(i == pl.num_programs(0) - 1)
    def _():
        dwgu_ref[...] = agu[...].astype(BF16)
        dwd_ref[...] = ad[...].astype(BF16)


def ffn(inv, h2all, dyall, wgu, wd):
    nb = ROWS // BLOCK
    fl = wd.shape[0]
    blk = pl.BlockSpec((1, BLOCK, D), lambda i, inv: (i, 0, 0))
    one = pl.Buffered(1)
    slots = dyall.reshape(ROWS // SLOT, SLOT, D)
    return pl.pallas_call(
        ffn_kernel,
        grid_spec=pltpu.PrefetchScalarGridSpec(
            num_scalar_prefetch=1,
            grid=(nb,),
            in_specs=[
                blk,
                pl.BlockSpec((1, SLOT, D), lambda i, inv: (inv[2 * i], 0, 0)),
                pl.BlockSpec((1, SLOT, D), lambda i, inv: (inv[2 * i + 1], 0, 0)),
                pl.BlockSpec((D, 2 * fl), lambda i, inv: (0, 0), pipeline_mode=one),
                pl.BlockSpec((fl, D), lambda i, inv: (0, 0), pipeline_mode=one),
            ],
            out_specs=(
                blk,
                blk,
                pl.BlockSpec((D, 2 * fl), lambda i, inv: (0, 0), pipeline_mode=one),
                pl.BlockSpec((fl, D), lambda i, inv: (0, 0), pipeline_mode=one),
            ),
            scratch_shapes=[pltpu.VMEM((D, 2 * fl), F32), pltpu.VMEM((fl, D), F32)],
        ),
        out_shape=(
            SDS((nb, BLOCK, D), BF16),
            SDS((nb, BLOCK, D), BF16),
            SDS((D, 2 * fl), BF16),
            SDS((fl, D), BF16),
        ),
        compiler_params=pltpu.CompilerParams(dimension_semantics=("arbitrary",), vmem_limit_bytes=56 << 20),
        cost_estimate=pl.CostEstimate(flops=24 * 10**9, bytes_accessed=24 << 20, transcendentals=10**6),
        name="ffn",
    )(inv, h2all, slots, slots, wgu, wd)


def norm_back(dyv, xv, gain):
    r = lax.rsqrt(jnp.mean(xv * xv, axis=-1, keepdims=True) + EPSILON)
    xr = xv * r
    gy = dyv * gain
    dx = r * (gy - xr * jnp.mean(gy * xr, axis=-1, keepdims=True))
    return dx, jnp.sum(dyv * xr, axis=0, keepdims=True)


def back_mid_kernel(n, dh, dyo, res, mown, wo, gf, gmid, dgf, dwo, dmh, sib, send, rel, fx, fy, ss, rs, dmix, ps, pr):
    me, p, g, groups, zq, zg = places(n)
    barrier([me ^ m for m in range(1, GROUP)])
    red = PlaneReduce(me, lambda b: dh.at[b], sib, send, rel, fx, fy, ss, rs)
    red.start()
    red.phase1()
    red.phase2()
    dx, dgain = norm_back(red.phase3(), res[...], gf[...])
    gm = dyo[...].astype(F32) + dx
    gmid[...] = gm
    dgf[...] = dgain
    gl = gm.astype(BF16)
    dm = nt(gl, wo[...]).astype(BF16)
    for b in range(GROUP):
        dmix[b] = dm[:, 128 * b : 128 * (b + 1)]
    pc = start_all(
        [rcopy(dmix.at[p ^ m], dmh.at[p], ps.at[m - 1], pr.at[m - 1], me ^ m) for m in range(1, GROUP)]
    )
    dmh[p] = dmix[p]
    dwo[...] = tn(mown[...], gl).astype(BF16)
    wait_all(pc)


def back_mid(n, dh, dyo, res, mown, wo, gf):
    return pl.pallas_call(
        functools.partial(back_mid_kernel, n),
        out_shape=(
            SDS((BLOCK, D), F32),
            SDS((1, D), F32),
            SDS((D, D), BF16),
            SDS((GROUP, BLOCK, 128), BF16),
        ),
        in_specs=[VM] * 6,
        out_specs=(VM,) * 4,
        scratch_shapes=plane_scratch((BLOCK, D))
        + [
            pltpu.VMEM((GROUP, BLOCK, 128), BF16),
            DMA((7,)),
            DMA((7,)),
        ],
        compiler_params=pltpu.CompilerParams(collective_id=3, has_side_effects=True, vmem_limit_bytes=58 << 20),
        name="back_mid",
    )(dh, dyo, res, mown, wo, gf)


def attn_bwd_kernel(n, len_ref, dm_ref, q_ref, kvall_ref, lse_ref, mixf_ref, h_ref, raw_ref, w_ref, gqk_ref, cs_ref, po, res, dwo, dw2, dwd, dh_ref, dw_ref, dg_ref, result, two, t2, od, k_s, v_s, dkv, dqt, dws, *rest):
    step_id = pl.program_id(0)
    nb = ROWS // BLOCK
    i = nb - 1 - step_id
    me, p, g, groups, zq, zg = places(n)
    ored = PlaneReduce(me, lambda b: po.at[b], *rest[:7])
    wred = PlaneReduce(me, lambda b: dwo.at[:, b], *rest[7:14])
    ring2 = RingReduce(n, p, g, dw2, *rest[14:20])
    ringd = RingReduce(n, p, g, dwd, *rest[20:26])

    @pl.when(step_id == 0)
    def _():
        barrier([me ^ m for m in (1, 2, 4)] + zq)
        ored.start()
        ring2.start()
        wred.start()
        ringd.start()

    @pl.when(step_id == 1)
    def _():
        ored.phase1()
        wred.phase1()

    @pl.when(step_id == 3)
    def _():
        ring2.relay()
        ored.phase2()

    @pl.when(step_id == 4)
    def _():
        ringd.relay()
        wred.phase2()


    @pl.when(step_id == 0)
    def _():
        dkv[...] = jnp.zeros_like(dkv)
        dws[...] = jnp.zeros_like(dws)
        dg_ref[...] = jnp.zeros_like(dg_ref)
        for b in range(ROWS // BLOCK):
            kvb = kvall_ref[b]
            k_s[pl.ds(b * BLOCK, BLOCK), :] = kvb[:, :HEAD]
            v_s[pl.ds(b * BLOCK, BLOCK), :] = kvb[:, HEAD:]

    q, do, mf = q_ref[0], dm_ref[0], mixf_ref[0]
    q2 = jnp.concatenate([q[:, :HEAD], q[:, HEAD:]], axis=0)
    do2 = jnp.concatenate([do[:, :HEAD], do[:, HEAD:]], axis=0)
    prod = (do.astype(F32) * mf).T
    delta = jnp.concatenate(
        [jnp.sum(prod[:HEAD], axis=0, keepdims=True), jnp.sum(prod[HEAD:], axis=0, keepdims=True)], axis=1
    )
    lse = lse_ref[0, 0:1, :]
    colq = lax.broadcasted_iota(jnp.int32, (1, 2 * BLOCK), 1)
    qrow = i * BLOCK + jnp.where(colq >= BLOCK, colq - BLOCK, colq)
    qstart = seq_start(qrow, len_ref, g)
    first = jnp.maximum(i - WINDOW, 0)
    rowk = lax.broadcasted_iota(jnp.int32, (BLOCK, 2 * BLOCK), 0)
    dqt[...] = jnp.zeros_like(dqt)

    def step(j, carry):
        at = pl.ds(pl.multiple_of(j * BLOCK, BLOCK), BLOCK)
        kb, vb = k_s[at, :], v_s[at, :]
        s = nt(kb, q2)
        kc = rowk + j * BLOCK
        ok = (kc >= qstart) & (kc <= qrow)
        pr = jnp.where(ok, jnp.exp2(s * (SCALE * LOG2E) - lse), 0.0)
        dp = nt(vb, do2)
        dsc = (pr * (dp - delta)).astype(BF16)
        dkv[at, :HEAD] += nn(dsc, q2)
        dkv[at, HEAD:] += nn(pr.astype(BF16), do2)
        dqt[...] += tn(dsc, kb)
        return carry

    lax.fori_loop(first, i + 1, step, 0)
    ct, st = tables(cs_ref)
    raw = raw_ref[0]
    dq = jnp.concatenate([dqt[:BLOCK], dqt[BLOCK:]], axis=1) * SCALE
    dkvb = dkv[pl.ds(pl.multiple_of(i * BLOCK, BLOCK), BLOCK), :]
    lane = lax.broadcasted_iota(jnp.int32, (BLOCK, 128), 1)

    def pull(d, v, gain):
        dn = d * ct - swap_halves(d) * st
        r = lax.rsqrt(head_mean(v * v) + EPSILON)
        vr = v * r
        gy = dn * gain
        return r * (gy - vr * head_mean(gy * vr)), jnp.sum(dn * vr, axis=0, keepdims=True)

    dqr, dgq = pull(dq, raw[:, :128], gqk_ref[0:1, :])
    dkr, dgk = pull(dkvb * SCALE, raw[:, 128:], gqk_ref[1:2, :])
    dg_ref[0:1, :] += dgq
    dg_ref[1:2, :] += dgk
    dqkv = jnp.concatenate([dqr, jnp.where(lane < HEAD, dkr, dkvb)], axis=1).astype(BF16)
    dh_ref[0] = nt(dqkv, w_ref[...]).astype(BF16)
    dws[...] += tn(h_ref[0], dqkv)

    @pl.when(step_id == nb - 1)
    def _():
        dw_ref[...] = dws[...].astype(BF16)
        result[...] = (ored.phase3() + res[...]).astype(BF16)
        two[...] = wred.phase3().astype(BF16)
        t2[...] = ring2.finish().astype(BF16)
        od[...] = ringd.finish()


def attn_bwd(n, lengths, dmh, q, kv, lse, mixf, h, raw, wqkv, gqk, cs, po, res, dwo, dw2, dwd):
    nb = ROWS // BLOCK
    groups = n // GROUP
    blk = lambda c: pl.BlockSpec((1, BLOCK, c), lambda i: (nb - 1 - i, 0, 0))
    whole = lambda s: pl.BlockSpec(s, lambda i: (0,) * len(s), pipeline_mode=pl.Buffered(1))
    return pl.pallas_call(
        functools.partial(attn_bwd_kernel, n),
        grid=(nb,),
        in_specs=[
            SM,
            blk(128),
            blk(128),
            whole((nb, BLOCK, 128)),
            pl.BlockSpec((1, 8, 2 * BLOCK), lambda i: (nb - 1 - i, 0, 0)),
            blk(128),
            blk(D),
            blk(QKV),
            whole((D, QKV)),
            whole((2, 128)),
            pl.BlockSpec((HEAD, BLOCK), lambda i: (0, nb - 1 - i)),
            whole(po.shape),
            whole(res.shape),
            whole(dwo.shape),
            whole(dw2.shape),
            whole(dwd.shape),
        ],
        out_specs=(
            blk(D),
            whole((D, QKV)),
            whole((8, 128)),
            whole((BLOCK, D)),
            whole((groups,) + dwo.shape[2:]),
            whole(dw2.shape[1:]),
            whole(dwd.shape[1:]),
        ),
        out_shape=(
            SDS((nb, BLOCK, D), BF16),
            SDS((D, QKV), BF16),
            SDS((8, 128), F32),
            SDS((BLOCK, D), BF16),
            SDS((groups,) + dwo.shape[2:], BF16),
            SDS(dw2.shape[1:], BF16),
            SDS(dwd.shape[1:], F32),
        ),
        scratch_shapes=[
            pltpu.VMEM((ROWS, HEAD), BF16),
            pltpu.VMEM((ROWS, HEAD), BF16),
            pltpu.VMEM((ROWS, 128), F32),
            pltpu.VMEM((2 * BLOCK, HEAD), F32),
            pltpu.VMEM((D, QKV), F32),
        ]
        + plane_scratch((BLOCK, D))
        + plane_scratch((groups,) + dwo.shape[2:])
        + ring_scratch(n, dw2.shape[1:])
        + ring_scratch(n, dwd.shape[1:]),
        compiler_params=pltpu.CompilerParams(
            collective_id=6, has_side_effects=True, dimension_semantics=("arbitrary",), vmem_limit_bytes=60 << 20
        ),
        cost_estimate=pl.CostEstimate(flops=8 * 10**9, bytes_accessed=16 << 20, transcendentals=4 * 10**6),
        name="attn_bwd",
    )(lengths, dmh, q, kv, lse, mixf, h, raw, wqkv, gqk, cs, po, res, dwo, dw2, dwd)


def final_kernel(n, dh, x, gmid, ga, dgf, dgqk, dw1, two, t2, gtok, o1, o2, oo, og, t1, gpart, gin, gsum, gz, ps, pr, gs, gr, *rest):
    me, p, g, groups, zq, zg = places(n)
    nz = groups - 1
    barrier([me ^ m for m in range(1, GROUP)] + zq)
    red = PlaneReduce(me, lambda b: dh.at[b], *rest[:7])
    ring1 = RingReduce(n, p, g, dw1, *rest[7:13])
    ringo = RingReduce(n, p, g, two, *rest[13:19])
    red.start()
    ring1.start()
    ringo.start()
    pc = []

    def exchange(k, src, out):
        for m in range(1, GROUP):
            c = rcopy(src.at[p ^ m], out.at[p], ps.at[k, m - 1], pr.at[k, m - 1], me ^ m)
            c.start()
            pc.append(c)
        out[p] = src[p]

    red.phase1()
    exchange(1, t2, o2)
    ring1.relay()
    ringo.relay()
    red.phase2()
    t1[...] = ring1.finish().astype(BF16)
    exchange(0, t1, o1)
    dx, dga = norm_back(red.phase3(), x[...].astype(F32), ga[...])
    gtok[...] = gmid[...] + dx
    gpart[...] = jnp.zeros_like(gpart)
    for b in range(8):
        gpart[b : b + 1, :] = dga[:, 128 * b : 128 * (b + 1)]
        gpart[8 + b : 9 + b, :] = dgf[:, 128 * b : 128 * (b + 1)]
    lane = lax.broadcasted_iota(jnp.int32, (1, 128), 1)
    dgq = dgqk[0:1, :]
    dgq = dgq + pltpu.roll(jnp.broadcast_to(dgq, (8, 128)), HEAD, 1)[0:1, :]
    dgk = pltpu.roll(jnp.broadcast_to(dgqk[1:2, :], (8, 128)), HEAD, 1)[0:1, :]
    gpart[16:17, :] = jnp.where(lane < HEAD, dgq, dgk)
    gc = start_all([rcopy(gpart, gin.at[m - 1], gs.at[m - 1], gr.at[m - 1], me ^ m) for m in range(1, GROUP)])
    oo[...] = ringo.finish()
    tot = gpart[...]
    for m in range(1, GROUP):
        gc[m - 1].wait_recv()
        tot = tot + gin[m - 1]
    gsum[...] = tot
    gzc = start_all([rcopy(gsum, gz.at[s], gs.at[7 + s], gr.at[7 + s], zq[s]) for s in range(nz)])
    for s in range(nz):
        gzc[s].wait_recv()
        tot = tot + gz[s]
    og[...] = tot
    wait_all(pc)
    for c in gc + gzc:
        c.wait_send()


def final(n, dh, x, gmid, ga, dgf, dgqk, dw1, two, t2):
    groups = n // GROUP
    nz = groups - 1
    return pl.pallas_call(
        functools.partial(final_kernel, n),
        out_shape=(
            SDS((BLOCK, D), F32),
            SDS(dw1.shape[1:], BF16),
            SDS(t2.shape, BF16),
            SDS(two.shape[1:], F32),
            SDS((24, 128), F32),
        ),
        in_specs=[VM] * 9,
        out_specs=(VM,) * 5,
        scratch_shapes=[
            pltpu.VMEM(dw1.shape[1:], BF16),
            pltpu.VMEM((24, 128), F32),
            pltpu.VMEM((7, 24, 128), F32),
            pltpu.VMEM((24, 128), F32),
            pltpu.VMEM((nz, 24, 128), F32),
            DMA((2, 7)),
            DMA((2, 7)),
            DMA((7 + nz,)),
            DMA((7 + nz,)),
        ]
        + plane_scratch((BLOCK, D))
        + ring_scratch(n, dw1.shape[1:])
        + ring_scratch(n, two.shape[1:]),
        compiler_params=pltpu.CompilerParams(collective_id=4, has_side_effects=True, vmem_limit_bytes=58 << 20),
        name="final",
    )(dh, x, gmid, ga, dgf, dgqk, dw1, two, t2)


def body(n, tokens, w_query, key_weight, w_value, w_out, w_gate, w_up, w_down, norm_gains, seq_lengths, slot_order, out_grad):
    groups = n // GROUP
    r = w_query.shape[0]
    ffc = w_down.shape[0]
    device = lax.axis_index("dp")
    g, p = device // GROUP, device % GROUP
    lengths = seq_lengths
    a1 = jnp.concatenate(
        [
            w_query.reshape(r, GROUP, 128),
            key_weight.reshape(r, GROUP, HEAD),
            w_value.reshape(r, GROUP, HEAD),
        ],
        axis=2,
    ).transpose(1, 0, 2)
    wgu = jnp.stack([w_gate, w_up], axis=1).reshape(r, 2, groups, GROUP, ffc)
    a2 = wgu.transpose(3, 0, 1, 2, 4).reshape(GROUP, r, 2 * groups * ffc)
    share = norm_gains.shape[0]
    gt = jnp.pad(norm_gains.astype(F32)[None, :], ((0, 7), (0, 128 - share)))
    wok = r // 16 if r % 16 == 0 else 1
    wdk = ffc // 16 if ffc % 16 == 0 else 1
    x_all, w1, w2, wo, wd, gains = gather_all(
        n, tokens, a1, a2, w_out.reshape(wok, r // wok, D), w_down.reshape(wdk, ffc // wdk, D), gt
    )
    gains = gains[:, :, 0, :share].reshape(1, -1)
    ga, gf = gains[:, :D], gains[:, D : 2 * D]
    gq = gains[:, 2 * D : 2 * D + HEAD]
    gk = gains[:, 2 * D + HEAD :]
    gqk = jnp.concatenate([jnp.concatenate([gq, gq], axis=1), jnp.concatenate([gk, gk], axis=1)], axis=0)
    wqkv = w1.reshape(D, QKV)
    wd = wd.reshape(-1, D)
    row = jnp.arange(ROWS, dtype=jnp.int32)
    length_row = lax.dynamic_index_in_dim(seq_lengths, g, 0, keepdims=False)
    order_row = lax.dynamic_index_in_dim(slot_order, g, 0, keepdims=False)
    ends = jnp.cumsum(length_row)
    start = jnp.max(jnp.where(row[:, None] >= ends[None, :], ends[None, :], 0), axis=1)
    frequency = jnp.exp(jnp.arange(HEAD // 2, dtype=F32) * (-2.0 * math.log(ROPE_THETA) / HEAD))
    angles = frequency[:, None] * (row - start).astype(F32)[None, :]
    cs = jnp.concatenate([jnp.cos(angles), jnp.sin(angles)], axis=0)
    slots = jnp.arange(ROWS // SLOT, dtype=jnp.int32)
    inv = jnp.sum(jnp.where(order_row[None, :] == slots[:, None], slots[None, :], 0), axis=1)

    h, raw, q, kv, mix, mixf, lse, dy_all, w2, wo = attn_fwd(
        n, lengths, x_all, wqkv, ga, gqk, cs, out_grad, w2, wo.reshape(groups, r, D)
    )
    wgu = w2.reshape(D, -1)
    wo = wo.reshape(D, D)
    res, mown, _, h2_all = mid(n, mix, tokens, wo, gf)
    po, dh2, dwgu, dwd = ffn(inv, h2_all, dy_all, wgu, wd)
    dslots = dy_all.reshape(ROWS // SLOT, SLOT, D)
    dy_own = jnp.concatenate(
        [lax.dynamic_index_in_dim(dslots, inv[2 * p + k], 0, keepdims=False) for k in range(2)], axis=0
    )
    gmid, dgf, dwo, dmh = back_mid(n, dh2, dy_own, res, mown, wo, gf)
    dh1, dwqkv, dgqk, result, two, t2, od = attn_bwd(
        n,
        lengths,
        dmh,
        q,
        kv,
        lse,
        mixf,
        h,
        raw,
        wqkv,
        gqk,
        cs,
        po,
        res,
        dwo.reshape(groups, GROUP, r, D),
        dwgu.reshape(groups, GROUP, r, -1),
        dwd.reshape(groups, wdk, ffc // wdk, D),
    )
    gtok, o1, o2, oo, og = final(
        n,
        dh1,
        tokens,
        gmid,
        ga,
        dgf,
        dgqk,
        dwqkv.reshape(groups, GROUP, r, QKV),
        two.reshape(groups, wok, r // wok, D),
        t2,
    )
    oo = oo.reshape(r, D)
    od = od.reshape(ffc, D)
    o1 = o1.transpose(1, 0, 2).astype(F32)
    gwq = o1[:, :, :128].reshape(r, -1)
    gwk = o1[:, :, 128 : 128 + HEAD].reshape(r, -1)
    gwv = o1[:, :, 128 + HEAD :].reshape(r, -1)
    o2 = o2.reshape(GROUP, r, 2, groups, ffc).transpose(2, 1, 3, 0, 4).reshape(2, r, -1).astype(F32)
    gains_out = lax.dynamic_slice(og.reshape(-1), (device * share,), (share,))
    return result, gtok, gwq, gwk, gwv, oo, o2[0], o2[1], od, gains_out


def solution(mesh):
    n = mesh.shape["dp"]
    row = P("dp", None)
    return jax.shard_map(
        functools.partial(body, n),
        mesh=mesh,
        in_specs=(row,) * 8 + (P("dp"), P(), P(), row),
        out_specs=(row,) * 9 + (P("dp"),),
        check_vma=False,
    )
```

```python
import functools
import math

import jax
import jax.numpy as jnp
from jax import lax
from jax.experimental import pallas as pl
from jax.experimental.pallas import tpu as pltpu
from jax.sharding import PartitionSpec as P

D = 1024
FF = 4608
QUERY_HEADS = 16
KEY_VALUE_HEADS = 8
HEAD = 64
SLOT = 128
GROUP = 8
ROWS = 2048
BLOCK = 256
QKV = 256
WINDOW = 4
EPSILON = 1e-05
ROPE_THETA = 1000000.0
SCALE = 1.0 / math.sqrt(HEAD)
LOG2E = math.log2(math.e)
F32 = jnp.float32
BF16 = jnp.bfloat16
MESH = pl.DeviceIdType.MESH
DMA = pltpu.SemaphoreType.DMA
VM = pl.BlockSpec(memory_space=pltpu.VMEM)
ANY = pl.BlockSpec(memory_space=pl.ANY)
SM = pl.BlockSpec(memory_space=pltpu.SMEM)
SDS = jax.ShapeDtypeStruct


def nn(a, b):
    return lax.dot_general(a, b, (((1,), (0,)), ((), ())), preferred_element_type=F32)


def nt(a, b):
    return lax.dot_general(a, b, (((1,), (1,)), ((), ())), preferred_element_type=F32)


def tn(a, b):
    return lax.dot_general(a, b, (((0,), (0,)), ((), ())), preferred_element_type=F32)


def rcopy(src, dst, send, recv, dev):
    return pltpu.make_async_remote_copy(
        src_ref=src, dst_ref=dst, send_sem=send, recv_sem=recv, device_id=(dev,), device_id_type=MESH
    )


def barrier(peers):
    sem = pltpu.get_barrier_semaphore()
    for q in peers:
        pl.semaphore_signal(sem, inc=1, device_id=(q,), device_id_type=MESH)
    pl.semaphore_wait(sem, len(peers))


def places(n):
    me = lax.axis_index("dp")
    p = lax.rem(me, GROUP)
    g = me // GROUP
    groups = n // GROUP
    zq = [lax.rem(g + s, groups) * GROUP + p for s in range(1, groups)]
    zg = [lax.rem(g + s, groups) for s in range(1, groups)]
    return me, p, g, groups, zq, zg


def start_all(copies):
    for c in copies:
        c.start()
    return copies


def wait_all(copies):
    for c in copies:
        c.wait()


class PlaneGather:
    COPIES = 14

    def __init__(self, me, p, src, dst, ss, rs, ls=None):
        sib, xn, yn = me ^ 1, me ^ 2, me ^ 4

        def cp(a, b, i, dev):
            return rcopy(a, b, ss.at[i], rs.at[i], dev)

        def own(i, dev):
            return [cp(src(h), dst(p, h), i + h, dev) for h in range(2)]

        def on(m, h, i, dev):
            return cp(dst(p ^ m, h), dst(p ^ m, h), i, dev)

        self.x, self.y, self.o = own(0, xn), own(2, yn), own(4, sib)
        self.r = [on(2, 0, 6, yn), on(4, 1, 7, xn)]
        self.fx = [on(2, h, 8 + h, sib) for h in range(2)]
        self.fy = [on(4, h, 10 + h, sib) for h in range(2)]
        self.fd = [on(6, h, 12 + h, sib) for h in range(2)]
        self.local = [] if ls is None else [
            pltpu.make_async_copy(src(h), dst(p, h), ls.at[h]) for h in range(2)
        ]

    def start(self):
        self.start_first()
        self.start_second()

    def start_first(self):
        start_all([self.x[0], self.y[1]] + self.o + self.local)

    def start_second(self):
        start_all([self.x[1], self.y[0]])

    def relay1(self):
        self.x[0].wait_recv()
        start_all([self.r[0], self.fx[0]])
        self.y[1].wait_recv()
        start_all([self.r[1], self.fy[1]])

    def relay2(self):
        self.x[1].wait_recv()
        self.fx[1].start()
        self.y[0].wait_recv()
        self.fy[0].start()

    def relay3(self):
        for h in range(2):
            self.r[h].wait_recv()
            self.fd[h].start()

    def arrive(self, copies):
        for c in copies:
            c.wait_recv()

    def sent(self):
        for c in self.x + self.y + self.r + self.o + self.fx + self.fy + self.fd:
            c.wait_send()
        wait_all(self.local)

    def finish(self):
        self.arrive(self.o + self.fx + self.fy + self.fd)
        self.sent()


class Ring:
    def __init__(self, n, p, g, src, dst, ss, rs, ls=None):
        groups = n // GROUP
        to = lambda s: lax.rem(g + s, groups) * GROUP + p
        at = lambda s: lax.rem(g + s, groups)

        def cp(a, b, i, dev):
            return rcopy(a, b, ss.at[i], rs.at[i], dev)

        self.relays = []
        if groups == 4:
            self.up = [cp(src(h), dst(g, h), h, to(1)) for h in range(2)]
            self.down = [cp(src(h), dst(g, h), 2 + h, to(3)) for h in range(2)]
            self.first = [self.up[0], self.down[1], self.up[1], self.down[0]]
            below, above = at(3), at(1)
            self.relays = [cp(dst(below, 0), dst(below, 0), 4, to(1)), cp(dst(above, 1), dst(above, 1), 5, to(3))]
        else:
            self.first = [cp(src(None), dst(g, None), s - 1, to(s)) for s in range(1, groups)]
        self.local = [] if ls is None else [pltpu.make_async_copy(src(None), dst(g, None), ls)]

    def start(self):
        start_all(self.first + self.local)

    def relay(self):
        if self.relays:
            self.up[0].wait_recv()
            self.relays[0].start()
            self.down[1].wait_recv()
            self.relays[1].start()

    def finish(self):
        if self.relays:
            self.up[1].wait_recv()
            self.down[0].wait_recv()
            for c in self.first:
                c.wait_send()
        else:
            wait_all(self.first)
        wait_all(self.relays + self.local)


def ring_count(n):
    return max(6, n // GROUP - 1)


def halves(length):
    cut = length // 2
    part = (pl.ds(0, cut), pl.ds(cut, length - cut))
    return lambda h: slice(None) if h is None else part[h]


class RingReduce:
    def __init__(self, n, p, g, part, low, high, send, fin, ss, rs):
        groups = n // GROUP
        to = lambda s: lax.rem(g + s, groups) * GROUP + p
        at = lambda s: lax.rem(g + s, groups)
        hs = halves(part.shape[1])
        self.part, self.fin, self.send, self.g, self.hs = part, fin, send, g, hs

        def cp(a, b, i, dev):
            return rcopy(a, b, ss.at[i], rs.at[i], dev)

        self.ring = groups == 4
        if self.ring:
            self.above, self.below = at(1), at(3)
            self.low, self.high = low, high
            far = at(2)
            self.a = cp(part.at[far, hs(0)], low, 0, to(1))
            self.b = cp(part.at[far, hs(1)], high, 1, to(3))
            self.c = cp(part.at[self.above, hs(1)], fin.at[0, hs(1)], 2, to(1))
            self.d = cp(part.at[self.below, hs(0)], fin.at[1, hs(0)], 3, to(3))
            self.e = cp(send.at[hs(0)], fin.at[0, hs(0)], 4, to(1))
            self.f = cp(send.at[hs(1)], fin.at[1, hs(1)], 5, to(3))
            self.all = [self.a, self.b, self.c, self.d, self.e, self.f]
        else:
            self.all = [cp(part.at[at(s)], fin.at[s - 1], s - 1, to(s)) for s in range(1, groups)]
        self.count = groups - 1

    def start(self):
        start_all(self.all[:4] if self.ring else self.all)

    def relay(self):
        if self.ring:
            for got, buf, h, b, out in (
                (self.a, self.low, 0, self.above, self.e),
                (self.b, self.high, 1, self.below, self.f),
            ):
                got.wait_recv()
                at = self.hs(h)
                self.send[at] = (self.part[b, at].astype(F32) + buf[...].astype(F32)).astype(BF16)
                out.start()

    def finish(self):
        for c in self.all[2:] if self.ring else self.all:
            c.wait_recv()
        val = self.part[self.g].astype(F32)
        for s in range(2 if self.ring else self.count):
            val = val + self.fin[s].astype(F32)
        for c in self.all:
            c.wait_send()
        return val


def ring_scratch(n, shape):
    cut = shape[0] // 2
    groups = n // GROUP
    count = 2 if groups == 4 else groups - 1
    tail = tuple(shape[1:])
    vm = lambda s: pltpu.VMEM(s, BF16)
    return [
        vm((max(cut, 1),) + tail),
        vm((shape[0] - cut,) + tail),
        vm(tuple(shape)),
        vm((count,) + tuple(shape)),
        DMA((ring_count(n),)),
        DMA((ring_count(n),)),
    ]


class PlaneReduce:
    def __init__(self, me, part, sib, send, relay, fx, fy, ss, rs):
        p = lax.rem(me, GROUP)
        xn, yn = me ^ 2, me ^ 4
        hs = halves(sib.shape[1])
        self.hs, self.p, self.part = hs, p, part
        self.sib, self.send, self.relay, self.fx, self.fy = sib, send, relay, fx, fy

        def cp(a, b, i, dev):
            return rcopy(a, b, ss.at[i], rs.at[i], dev)

        self.first = [cp(part(p ^ (2 * i + 1)), sib.at[i], i, me ^ 1) for i in range(4)]
        self.diag = [cp(send.at[0, hs(0)], relay.at[0], 4, xn), cp(send.at[0, hs(1)], relay.at[1], 5, yn)]
        self.toy = [cp(send.at[2, hs(h)], fy.at[hs(h)], 6 + h, yn) for h in range(2)]
        self.tox = [cp(send.at[1, hs(h)], fx.at[hs(h)], 8 + h, xn) for h in range(2)]

    def start(self):
        start_all([self.first[i] for i in (3, 1, 2, 0)])

    def chip(self, i):
        self.first[i].wait_recv()
        return self.part(self.p ^ (2 * i))[...].astype(F32) + self.sib[i].astype(F32)

    def chip_d(self):
        self.send[0] = self.chip(3).astype(BF16)
        start_all(self.diag)

    def chip_x(self):
        self.send[1] = self.chip(1).astype(BF16)
        self.tox[0].start()

    def chip_y(self):
        self.send[2] = self.chip(2).astype(BF16)
        self.toy[1].start()

    def phase1(self):
        self.chip_d()
        self.chip_x()
        self.chip_y()

    def phase2(self):
        self.diag[0].wait_recv()
        at = self.hs(0)
        self.send[2, at] = (self.send[2, at].astype(F32) + self.relay[0].astype(F32)).astype(BF16)
        self.toy[0].start()
        self.diag[1].wait_recv()
        at = self.hs(1)
        self.send[1, at] = (self.send[1, at].astype(F32) + self.relay[1].astype(F32)).astype(BF16)
        self.tox[1].start()

    def phase3(self):
        own = self.chip(0)
        for c in self.toy + self.tox:
            c.wait_recv()
        own = own + self.fx[...].astype(F32) + self.fy[...].astype(F32)
        for c in self.first + self.diag + self.toy + self.tox:
            c.wait_send()
        return own


def plane_scratch(shape):
    tail = tuple(shape[1:])
    vm = lambda *s: pltpu.VMEM(s + tail, BF16)
    return [
        vm(4, shape[0]),
        vm(3, shape[0]),
        vm(2, shape[0] // 2),
        vm(shape[0]),
        vm(shape[0]),
        DMA((10,)),
        DMA((10,)),
    ]


def gather_kernel(n, x, a1, a2, wo, wd, gt, xo, a1o, a2o, woo, wdo, gto, ls, xs, xr, ps, pr, zs, zr):
    me, p, g, groups, zq, zg = places(n)
    barrier([me ^ m for m in range(1, GROUP)] + zq)
    local = [
        pltpu.make_async_copy(a1.at[p], a1o.at[g, p], ls.at[0]),
        pltpu.make_async_copy(gt, gto.at[g, p], ls.at[1]),
        pltpu.make_async_copy(a2.at[p], a2o.at[p], ls.at[2]),
    ]
    start_all(local)
    pc = {}

    def exchange(k, src, dst):
        for m in range(1, GROUP):
            pc[k, m] = rcopy(src(p ^ m), dst, ps.at[k, m - 1], pr.at[k, m - 1], me ^ m)
            pc[k, m].start()

    exchange(0, lambda b: a1.at[b], a1o.at[g, p])
    exchange(1, lambda b: gt, gto.at[g, p])
    hx = halves(BLOCK)
    xg = PlaneGather(me, p, lambda h: x.at[hx(h)], lambda b, h: xo.at[b, hx(h)], xs, xr, ls.at[pl.ds(5, 2)])
    xg.start()

    def ring(k, src, dst, local=None):
        hk = halves(dst.shape[1])
        return Ring(n, p, g, lambda h: src.at[hk(h)], lambda b, h: dst.at[b, hk(h)], zs.at[k], zr.at[k], local)

    rings = [
        ring(0, a1o.at[g], a1o),
        ring(1, gto.at[g], gto),
        ring(2, wd, wdo, ls.at[3]),
        ring(3, wo, woo, ls.at[4]),
    ]
    rings[2].start()
    rings[3].start()
    exchange(2, lambda b: a2.at[b], a2o.at[p])
    for k in range(2):
        for m in range(1, GROUP):
            pc[k, m].wait_recv()
        local[k].wait()
        rings[k].start()
    xg.relay1()
    for k in (3, 0, 1, 2):
        rings[k].relay()
    xg.relay2()
    xg.relay3()
    for m in range(1, GROUP):
        pc[2, m].wait_recv()
    local[2].wait()
    for c in pc.values():
        c.wait_send()
    for k in range(4):
        rings[k].finish()
    xg.finish()


def gather_all(n, x, a1, a2, wo, wd, gt):
    groups = n // GROUP
    r = a1.shape[1]
    return pl.pallas_call(
        functools.partial(gather_kernel, n),
        out_shape=(
            SDS((GROUP, BLOCK, D), BF16),
            SDS((groups, GROUP, r, a1.shape[-1]), BF16),
            SDS((GROUP, r, a2.shape[-1]), BF16),
            SDS((groups,) + wo.shape, BF16),
            SDS((groups,) + wd.shape, BF16),
            SDS((groups, GROUP, 8, 128), F32),
        ),
        in_specs=[ANY] * 6,
        out_specs=(ANY,) * 6,
        scratch_shapes=[
            DMA((7,)),
            DMA((14,)),
            DMA((14,)),
            DMA((3, 7)),
            DMA((3, 7)),
            DMA((4, ring_count(n))),
            DMA((4, ring_count(n))),
        ],
        compiler_params=pltpu.CompilerParams(collective_id=1, has_side_effects=True),
        name="gather_all",
    )(x, a1, a2, wo, wd, gt)


def swap_halves(v):
    lane = lax.broadcasted_iota(jnp.int32, v.shape, 1)
    low = lax.rem(lane, HEAD) < HEAD // 2
    width = v.shape[1]
    return jnp.where(low, pltpu.roll(v, width - HEAD // 2, 1), pltpu.roll(v, HEAD // 2, 1))


def head_mean(v):
    lane = lax.broadcasted_iota(jnp.int32, v.shape, 1)
    low = lane < HEAD
    a = jnp.sum(jnp.where(low, v, 0.0), axis=-1, keepdims=True)
    b = jnp.sum(jnp.where(low, 0.0, v), axis=-1, keepdims=True)
    return jnp.where(low, a, b) * (1.0 / HEAD)


def seq_start(row, len_ref, g):
    e1 = len_ref[g, 0]
    e2 = e1 + len_ref[g, 1]
    e3 = e2 + len_ref[g, 2]
    zero = row * 0
    s = jnp.where(row >= e1, zero + e1, zero)
    s = jnp.where(row >= e2, zero + e2, s)
    return jnp.where(row >= e3, zero + e3, s)


def tables(cs_ref):
    t = cs_ref[...].T
    c, s = t[:, : HEAD // 2], t[:, HEAD // 2 :]
    return jnp.concatenate([c, c, c, c], axis=1), jnp.concatenate([-s, s, -s, s], axis=1)


def attn_fwd_kernel(n, len_ref, x_ref, w_ref, ga_ref, gqk_ref, cs_ref, dy, w2, wo, h_ref, raw_ref, q_ref, kv_ref, mix_ref, mixf_ref, lse_ref, dyo, w2o, woo, k_s, v_s, acc, ls, ds_, dr, os_, orr, zs, zr):
    i = pl.program_id(0)
    me, p, g, groups, zq, zg = places(n)
    hd, hw, ho = halves(BLOCK), halves(w2.shape[0]), halves(wo.shape[0])
    dg = PlaneGather(me, p, lambda h: dy.at[hd(h)], lambda b, h: dyo.at[b, hd(h)], ds_, dr, ls.at[pl.ds(0, 2)])
    og = PlaneGather(me, p, lambda h: wo.at[ho(h)], lambda b, h: woo.at[ho(h), b], os_, orr, ls.at[pl.ds(2, 2)])
    zg_ = Ring(n, p, g, lambda h: w2.at[hw(h)], lambda b, h: w2o.at[b, hw(h)], zs, zr, ls.at[4])

    @pl.when(i == 0)
    def _():
        barrier([me ^ m for m in (1, 2, 4)] + zq)
        dg.start()
        zg_.start()
        og.start()

    @pl.when(i == 3)
    def _():
        dg.relay1()

    @pl.when(i == 5)
    def _():
        zg_.relay()
        dg.relay2()

    @pl.when(i == 6)
    def _():
        og.relay1()
        dg.relay3()

    @pl.when(i == 7)
    def _():
        og.relay2()

    xb = x_ref[0].astype(F32)
    r = lax.rsqrt(jnp.mean(xb * xb, axis=-1, keepdims=True) + EPSILON)
    h = (xb * r * ga_ref[...]).astype(BF16)
    h_ref[0] = h
    raw = nn(h, w_ref[...])
    raw_ref[0] = raw
    ct, st = tables(cs_ref)
    qraw, kvraw = raw[:, :128], raw[:, 128:]
    qn = qraw * lax.rsqrt(head_mean(qraw * qraw) + EPSILON) * gqk_ref[0:1, :]
    q = (qn * ct + swap_halves(qn) * st).astype(BF16)
    kn = kvraw * lax.rsqrt(head_mean(kvraw * kvraw) + EPSILON) * gqk_ref[1:2, :]
    k = (kn * ct + swap_halves(kn) * st).astype(BF16)
    lane = lax.broadcasted_iota(jnp.int32, (BLOCK, 128), 1)
    kv = jnp.where(lane < HEAD, k.astype(F32), kvraw).astype(BF16)
    q_ref[0] = q
    kv_ref[0] = kv
    k_s[pl.ds(i * BLOCK, BLOCK), :] = kv[:, :HEAD]
    v_s[pl.ds(i * BLOCK, BLOCK), :] = jnp.where(lane < HEAD, pltpu.roll(kvraw, HEAD, 1), 1.0).astype(BF16)
    q2 = jnp.concatenate([q[:, :HEAD], q[:, HEAD:]], axis=0)
    acc[...] = jnp.zeros_like(acc)
    row = lax.broadcasted_iota(jnp.int32, (2 * BLOCK, 1), 0)
    qrow = i * BLOCK + jnp.where(row >= BLOCK, row - BLOCK, row)
    qstart = seq_start(qrow, len_ref, g)
    first = jnp.maximum(i - WINDOW, 0)
    col = lax.broadcasted_iota(jnp.int32, (2 * BLOCK, BLOCK), 1)

    def step(j, carry):
        kb = k_s[pl.ds(pl.multiple_of(j * BLOCK, BLOCK), BLOCK), :]
        vb = v_s[pl.ds(pl.multiple_of(j * BLOCK, BLOCK), BLOCK), :]
        s = nt(q2, kb)
        kc = col + j * BLOCK
        ok = (kc >= qstart) & (kc <= qrow)
        e = jnp.where(ok, jnp.exp2(s * (SCALE * LOG2E)), 0.0).astype(BF16)
        acc[...] += nn(e, vb)
        return carry

    lax.fori_loop(first, i + 1, step, 0)
    total = acc[:, HEAD:]
    m = acc[:, :HEAD] / total
    both = jnp.concatenate([m[:BLOCK], m[BLOCK:]], axis=1)
    mixf_ref[0] = both
    mix_ref[0] = both.astype(BF16)
    lse_ref[0] = jnp.log2(total.T)[:8, :]

    @pl.when(i == 7)
    def _():
        og.relay3()
        dg.finish()
        zg_.finish()
        og.finish()


def attn_fwd(n, lengths, x_all, wqkv, ga, gqk, cs, dy, w2, wo):
    groups = n // GROUP
    blk = lambda c: pl.BlockSpec((1, BLOCK, c), lambda i: (i, 0, 0))
    whole = lambda s: pl.BlockSpec(s, lambda i: (0,) * len(s), pipeline_mode=pl.Buffered(1))
    nb = ROWS // BLOCK
    return pl.pallas_call(
        functools.partial(attn_fwd_kernel, n),
        grid=(nb,),
        in_specs=[
            SM,
            blk(D),
            whole((D, QKV)),
            whole((1, D)),
            whole((2, 128)),
            pl.BlockSpec((HEAD, BLOCK), lambda i: (0, i)),
            ANY,
            ANY,
            ANY,
        ],
        out_specs=(blk(D), blk(QKV), blk(128), blk(128), blk(128), blk(128), pl.BlockSpec((1, 8, 2 * BLOCK), lambda i: (i, 0, 0)), ANY, ANY, ANY),
        out_shape=(
            SDS((nb, BLOCK, D), BF16),
            SDS((nb, BLOCK, QKV), F32),
            SDS((nb, BLOCK, 128), BF16),
            SDS((nb, BLOCK, 128), BF16),
            SDS((nb, BLOCK, 128), BF16),
            SDS((nb, BLOCK, 128), F32),
            SDS((nb, 8, 2 * BLOCK), F32),
            SDS((GROUP, BLOCK, D), BF16),
            SDS((groups,) + w2.shape, BF16),
            SDS((groups, GROUP) + wo.shape[1:], BF16),
        ),
        scratch_shapes=[
            pltpu.VMEM((ROWS, HEAD), BF16),
            pltpu.VMEM((ROWS, 128), BF16),
            pltpu.VMEM((2 * BLOCK, 128), F32),
            DMA((5,)),
            DMA((14,)),
            DMA((14,)),
            DMA((14,)),
            DMA((14,)),
            DMA((ring_count(n),)),
            DMA((ring_count(n),)),
        ],
        compiler_params=pltpu.CompilerParams(
            collective_id=5, has_side_effects=True, dimension_semantics=("arbitrary",), vmem_limit_bytes=48 << 20
        ),
        cost_estimate=pl.CostEstimate(flops=4 * 10**9, bytes_accessed=16 << 20, transcendentals=4 * 10**6),
        name="attn_fwd",
    )(lengths, x_all, wqkv, ga, gqk, cs, dy, w2, wo)


def norm_back(dyv, xv, gain):
    r = lax.rsqrt(jnp.mean(xv * xv, axis=-1, keepdims=True) + EPSILON)
    xr = xv * r
    gy = dyv * gain
    dx = r * (gy - xr * jnp.mean(gy * xr, axis=-1, keepdims=True))
    return dx, jnp.sum(dyv * xr, axis=0, keepdims=True)


def ffn_block_kernel(n, inv, mix, x, wo, gf, w2, wd, dy, res, gmid, dgf, dwo, dmh, po, dw2, dwd, mbuf, h2, wgs, wds, dys, acts, dgus, part, mown, stage, ps, pr, hs, hr, os_, qs, qr, *red_refs):
    me, p, g, groups, zq, zg = places(n)
    barrier([me ^ m for m in range(1, GROUP)])
    fl = wd.shape[0]
    fp = wds.shape[0]
    pc = start_all(
        [rcopy(mix.at[p ^ m], mbuf.at[p], ps.at[m - 1], pr.at[m - 1], me ^ m) for m in range(1, GROUP)]
    )
    mbuf[p] = mix[p]
    gap = jnp.zeros((D, fp - fl), BF16)
    wgs[:, :fl] = w2[:, :fl]
    wgs[:, fl:fp] = gap
    wgs[:, fp : fp + fl] = w2[:, fl:]
    wgs[:, fp + fl :] = gap
    wds[:fl] = wd[...]
    wds[fl:] = jnp.zeros((fp - fl, D), BF16)
    for c in pc:
        c.wait_recv()
    m = jnp.concatenate([mbuf[b] for b in range(GROUP)], axis=1)
    mown[...] = m
    z = x[...].astype(F32) + nn(m, wo[...])
    res[...] = z
    r = lax.rsqrt(jnp.mean(z * z, axis=-1, keepdims=True) + EPSILON)
    h2[p] = (z * r * gf[...]).astype(BF16)
    hb = halves(BLOCK)
    hg = PlaneGather(me, p, lambda h: h2.at[p, hb(h)], lambda b, h: h2.at[b, hb(h)], hs, hr)
    red = PlaneReduce(me, lambda b: part.at[b], *red_refs)
    hg.start_first()

    def block(t, carry):
        @pl.when(t == 1)
        def _():
            hg.start_second()
            hg.arrive(hg.o)

        @pl.when(t == 2)
        def _():
            red.first[0].start()
            hg.relay1()
            hg.relay2()

        @pl.when(t == 3)
        def _():
            hg.arrive(hg.fx)

        @pl.when(t == 4)
        def _():
            red.first[1].start()

        @pl.when(t == 5)
        def _():
            hg.arrive(hg.fy)
            red.chip_x()

        @pl.when(t == 6)
        def _():
            red.first[2].start()
            hg.relay3()

        @pl.when(t == 7)
        def _():
            red.chip_y()
            hg.arrive(hg.fd)

        b = p ^ t
        h = h2[b]
        dyb = jnp.concatenate([dy[inv[2 * b]], dy[inv[2 * b + 1]]], axis=0)
        dys[b] = dyb
        gu = nn(h, wgs[...])
        da = nt(dyb, wds[...])
        gp, up = gu[:, :fp], gu[:, fp:]
        sig = 1.0 / (1.0 + jnp.exp(-gp))
        sg = gp * sig
        acts[b] = (sg * up).astype(BF16)
        dgu = jnp.concatenate(
            [(da * up * (sig * (1.0 + gp * (1.0 - sig)))).astype(BF16), (da * sg).astype(BF16)], axis=1
        )
        dgus[b] = dgu
        part[b] = nt(dgu, wgs[...]).astype(BF16)
        return carry

    lax.fori_loop(0, GROUP, block, 0)
    red.first[3].start()
    a_all = acts[...].reshape(ROWS, fp)
    dwd[...] = tn(a_all, dys[...].reshape(ROWS, D))[:fl].astype(BF16)
    red.chip_d()

    def out(b, carry):
        slot = lax.rem(b, 2)

        @pl.when(b > 1)
        def _():
            pltpu.make_async_copy(stage.at[slot], po.at[b - 2], os_.at[slot]).wait()

        stage[slot] = nn(acts[b], wds[...]).astype(BF16)
        pltpu.make_async_copy(stage.at[slot], po.at[b], os_.at[slot]).start()
        return carry

    lax.fori_loop(0, GROUP, out, 0)
    for b in range(GROUP - 2, GROUP):
        pltpu.make_async_copy(stage.at[b % 2], po.at[b], os_.at[b % 2]).wait()
    red.phase2()
    h_all = h2[...].reshape(ROWS, D)
    dg_all = dgus[...].reshape(ROWS, 2 * fp)
    dw2[:, :fl] = tn(h_all, dg_all[:, :fp])[:, :fl].astype(BF16)
    dw2[:, fl:] = tn(h_all, dg_all[:, fp:])[:, :fl].astype(BF16)
    dx, dgain = norm_back(red.phase3(), res[...], gf[...])
    dyo = dys[p].astype(F32)
    gm = dyo + dx
    gmid[...] = gm
    dgf[...] = dgain
    gl = gm.astype(BF16)
    dm = nt(gl, wo[...]).astype(BF16)
    for b in range(GROUP):
        mbuf[b] = dm[:, 128 * b : 128 * (b + 1)]
    for c in pc:
        c.wait_send()
    qc = start_all(
        [rcopy(mbuf.at[p ^ m], dmh.at[p], qs.at[m - 1], qr.at[m - 1], me ^ m) for m in range(1, GROUP)]
    )
    dmh[p] = mbuf[p]
    dwo[...] = tn(mown[...], gl).astype(BF16)
    wait_all(qc)
    hg.sent()


def ffn_block(n, inv, mix, x, wo, gf, w2, wd, dy):
    fl = wd.shape[0]
    fp = -(-fl // 128) * 128
    vm = lambda *s: pltpu.VMEM(s, BF16)
    return pl.pallas_call(
        functools.partial(ffn_block_kernel, n),
        out_shape=(
            SDS((BLOCK, D), F32),
            SDS((BLOCK, D), F32),
            SDS((1, D), F32),
            SDS((D, D), BF16),
            SDS((GROUP, BLOCK, 128), BF16),
            SDS((GROUP, BLOCK, D), BF16),
            SDS((D, 2 * fl), BF16),
            SDS((fl, D), BF16),
        ),
        in_specs=[SM] + [VM] * 7,
        out_specs=(VM, VM, VM, VM, VM, ANY, VM, VM),
        scratch_shapes=[
            vm(GROUP, BLOCK, 128),
            vm(GROUP, BLOCK, D),
            vm(D, 2 * fp),
            vm(fp, D),
            vm(GROUP, BLOCK, D),
            vm(GROUP, BLOCK, fp),
            vm(GROUP, BLOCK, 2 * fp),
            vm(GROUP, BLOCK, D),
            vm(BLOCK, D),
            vm(2, BLOCK, D),
            DMA((7,)),
            DMA((7,)),
            DMA((14,)),
            DMA((14,)),
            DMA((2,)),
            DMA((7,)),
            DMA((7,)),
        ]
        + plane_scratch((BLOCK, D)),
        compiler_params=pltpu.CompilerParams(collective_id=2, has_side_effects=True, vmem_limit_bytes=62 << 20),
        name="ffn_block",
    )(inv, mix, x, wo, gf, w2, wd, dy.reshape(ROWS // SLOT, SLOT, D))


def attn_bwd_kernel(n, len_ref, dm_ref, q_ref, kvall_ref, lse_ref, mixf_ref, h_ref, raw_ref, w_ref, gqk_ref, cs_ref, po, res, dwo, dw2, dwd, dh_ref, dw_ref, dg_ref, result, two, t2, od, k_s, v_s, dkv, dqt, dws, *rest):
    step_id = pl.program_id(0)
    nb = ROWS // BLOCK
    i = nb - 1 - step_id
    me, p, g, groups, zq, zg = places(n)
    ored = PlaneReduce(me, lambda b: po.at[b], *rest[:7])
    wred = PlaneReduce(me, lambda b: dwo.at[:, b], *rest[7:14])
    ring2 = RingReduce(n, p, g, dw2, *rest[14:20])
    ringd = RingReduce(n, p, g, dwd, *rest[20:26])

    @pl.when(step_id == 0)
    def _():
        barrier([me ^ m for m in (1, 2, 4)] + zq)
        ored.start()
        ring2.start()
        wred.start()
        ringd.start()

    @pl.when(step_id == 1)
    def _():
        ored.phase1()
        wred.phase1()

    @pl.when(step_id == 3)
    def _():
        ring2.relay()
        ored.phase2()

    @pl.when(step_id == 4)
    def _():
        ringd.relay()
        wred.phase2()


    @pl.when(step_id == 0)
    def _():
        dkv[...] = jnp.zeros_like(dkv)
        dws[...] = jnp.zeros_like(dws)
        dg_ref[...] = jnp.zeros_like(dg_ref)
        for b in range(ROWS // BLOCK):
            kvb = kvall_ref[b]
            k_s[pl.ds(b * BLOCK, BLOCK), :] = kvb[:, :HEAD]
            v_s[pl.ds(b * BLOCK, BLOCK), :] = kvb[:, HEAD:]

    q, do, mf = q_ref[0], dm_ref[0], mixf_ref[0]
    q2 = jnp.concatenate([q[:, :HEAD], q[:, HEAD:]], axis=0)
    do2 = jnp.concatenate([do[:, :HEAD], do[:, HEAD:]], axis=0)
    prod = (do.astype(F32) * mf).T
    delta = jnp.concatenate(
        [jnp.sum(prod[:HEAD], axis=0, keepdims=True), jnp.sum(prod[HEAD:], axis=0, keepdims=True)], axis=1
    )
    lse = lse_ref[0, 0:1, :]
    colq = lax.broadcasted_iota(jnp.int32, (1, 2 * BLOCK), 1)
    qrow = i * BLOCK + jnp.where(colq >= BLOCK, colq - BLOCK, colq)
    qstart = seq_start(qrow, len_ref, g)
    first = jnp.maximum(i - WINDOW, 0)
    rowk = lax.broadcasted_iota(jnp.int32, (BLOCK, 2 * BLOCK), 0)
    dqt[...] = jnp.zeros_like(dqt)

    def step(j, carry):
        at = pl.ds(pl.multiple_of(j * BLOCK, BLOCK), BLOCK)
        kb, vb = k_s[at, :], v_s[at, :]
        s = nt(kb, q2)
        kc = rowk + j * BLOCK
        ok = (kc >= qstart) & (kc <= qrow)
        pr = jnp.where(ok, jnp.exp2(s * (SCALE * LOG2E) - lse), 0.0)
        dp = nt(vb, do2)
        dsc = (pr * (dp - delta)).astype(BF16)
        dkv[at, :HEAD] += nn(dsc, q2)
        dkv[at, HEAD:] += nn(pr.astype(BF16), do2)
        dqt[...] += tn(dsc, kb)
        return carry

    lax.fori_loop(first, i + 1, step, 0)
    ct, st = tables(cs_ref)
    raw = raw_ref[0]
    dq = jnp.concatenate([dqt[:BLOCK], dqt[BLOCK:]], axis=1) * SCALE
    dkvb = dkv[pl.ds(pl.multiple_of(i * BLOCK, BLOCK), BLOCK), :]
    lane = lax.broadcasted_iota(jnp.int32, (BLOCK, 128), 1)

    def pull(d, v, gain):
        dn = d * ct - swap_halves(d) * st
        r = lax.rsqrt(head_mean(v * v) + EPSILON)
        vr = v * r
        gy = dn * gain
        return r * (gy - vr * head_mean(gy * vr)), jnp.sum(dn * vr, axis=0, keepdims=True)

    dqr, dgq = pull(dq, raw[:, :128], gqk_ref[0:1, :])
    dkr, dgk = pull(dkvb * SCALE, raw[:, 128:], gqk_ref[1:2, :])
    dg_ref[0:1, :] += dgq
    dg_ref[1:2, :] += dgk
    dqkv = jnp.concatenate([dqr, jnp.where(lane < HEAD, dkr, dkvb)], axis=1).astype(BF16)
    dh_ref[0] = nt(dqkv, w_ref[...]).astype(BF16)
    dws[...] += tn(h_ref[0], dqkv)

    @pl.when(step_id == nb - 1)
    def _():
        dw_ref[...] = dws[...].astype(BF16)
        result[...] = (ored.phase3() + res[...]).astype(BF16)
        two[...] = wred.phase3().astype(BF16)
        t2[...] = ring2.finish().astype(BF16)
        od[...] = ringd.finish()


def attn_bwd(n, lengths, dmh, q, kv, lse, mixf, h, raw, wqkv, gqk, cs, po, res, dwo, dw2, dwd):
    nb = ROWS // BLOCK
    groups = n // GROUP
    blk = lambda c: pl.BlockSpec((1, BLOCK, c), lambda i: (nb - 1 - i, 0, 0))
    whole = lambda s: pl.BlockSpec(s, lambda i: (0,) * len(s), pipeline_mode=pl.Buffered(1))
    return pl.pallas_call(
        functools.partial(attn_bwd_kernel, n),
        grid=(nb,),
        in_specs=[
            SM,
            blk(128),
            blk(128),
            whole((nb, BLOCK, 128)),
            pl.BlockSpec((1, 8, 2 * BLOCK), lambda i: (nb - 1 - i, 0, 0)),
            blk(128),
            blk(D),
            blk(QKV),
            whole((D, QKV)),
            whole((2, 128)),
            pl.BlockSpec((HEAD, BLOCK), lambda i: (0, nb - 1 - i)),
            whole(po.shape),
            whole(res.shape),
            whole(dwo.shape),
            whole(dw2.shape),
            whole(dwd.shape),
        ],
        out_specs=(
            blk(D),
            whole((D, QKV)),
            whole((8, 128)),
            whole((BLOCK, D)),
            whole((groups,) + dwo.shape[2:]),
            whole(dw2.shape[1:]),
            whole(dwd.shape[1:]),
        ),
        out_shape=(
            SDS((nb, BLOCK, D), BF16),
            SDS((D, QKV), BF16),
            SDS((8, 128), F32),
            SDS((BLOCK, D), BF16),
            SDS((groups,) + dwo.shape[2:], BF16),
            SDS(dw2.shape[1:], BF16),
            SDS(dwd.shape[1:], F32),
        ),
        scratch_shapes=[
            pltpu.VMEM((ROWS, HEAD), BF16),
            pltpu.VMEM((ROWS, HEAD), BF16),
            pltpu.VMEM((ROWS, 128), F32),
            pltpu.VMEM((2 * BLOCK, HEAD), F32),
            pltpu.VMEM((D, QKV), F32),
        ]
        + plane_scratch((BLOCK, D))
        + plane_scratch((groups,) + dwo.shape[2:])
        + ring_scratch(n, dw2.shape[1:])
        + ring_scratch(n, dwd.shape[1:]),
        compiler_params=pltpu.CompilerParams(
            collective_id=6, has_side_effects=True, dimension_semantics=("arbitrary",), vmem_limit_bytes=60 << 20
        ),
        cost_estimate=pl.CostEstimate(flops=8 * 10**9, bytes_accessed=16 << 20, transcendentals=4 * 10**6),
        name="attn_bwd",
    )(lengths, dmh, q, kv, lse, mixf, h, raw, wqkv, gqk, cs, po, res, dwo, dw2, dwd)


def final_kernel(n, dh, x, gmid, ga, dgf, dgqk, dw1, two, t2, gtok, o1, o2, oo, og, t1, gpart, gin, gsum, gz, ps, pr, gs, gr, *rest):
    me, p, g, groups, zq, zg = places(n)
    nz = groups - 1
    barrier([me ^ m for m in range(1, GROUP)] + zq)
    red = PlaneReduce(me, lambda b: dh.at[b], *rest[:7])
    ring1 = RingReduce(n, p, g, dw1, *rest[7:13])
    ringo = RingReduce(n, p, g, two, *rest[13:19])
    red.start()
    ring1.start()
    ringo.start()
    pc = []

    def exchange(k, src, out):
        for m in range(1, GROUP):
            c = rcopy(src.at[p ^ m], out.at[p], ps.at[k, m - 1], pr.at[k, m - 1], me ^ m)
            c.start()
            pc.append(c)
        out[p] = src[p]

    red.phase1()
    exchange(1, t2, o2)
    ring1.relay()
    ringo.relay()
    red.phase2()
    t1[...] = ring1.finish().astype(BF16)
    exchange(0, t1, o1)
    dx, dga = norm_back(red.phase3(), x[...].astype(F32), ga[...])
    gtok[...] = gmid[...] + dx
    gpart[...] = jnp.zeros_like(gpart)
    for b in range(8):
        gpart[b : b + 1, :] = dga[:, 128 * b : 128 * (b + 1)]
        gpart[8 + b : 9 + b, :] = dgf[:, 128 * b : 128 * (b + 1)]
    lane = lax.broadcasted_iota(jnp.int32, (1, 128), 1)
    dgq = dgqk[0:1, :]
    dgq = dgq + pltpu.roll(jnp.broadcast_to(dgq, (8, 128)), HEAD, 1)[0:1, :]
    dgk = pltpu.roll(jnp.broadcast_to(dgqk[1:2, :], (8, 128)), HEAD, 1)[0:1, :]
    gpart[16:17, :] = jnp.where(lane < HEAD, dgq, dgk)
    gc = start_all([rcopy(gpart, gin.at[m - 1], gs.at[m - 1], gr.at[m - 1], me ^ m) for m in range(1, GROUP)])
    oo[...] = ringo.finish()
    tot = gpart[...]
    for m in range(1, GROUP):
        gc[m - 1].wait_recv()
        tot = tot + gin[m - 1]
    gsum[...] = tot
    gzc = start_all([rcopy(gsum, gz.at[s], gs.at[7 + s], gr.at[7 + s], zq[s]) for s in range(nz)])
    for s in range(nz):
        gzc[s].wait_recv()
        tot = tot + gz[s]
    og[...] = tot
    wait_all(pc)
    for c in gc + gzc:
        c.wait_send()


def final(n, dh, x, gmid, ga, dgf, dgqk, dw1, two, t2):
    groups = n // GROUP
    nz = groups - 1
    return pl.pallas_call(
        functools.partial(final_kernel, n),
        out_shape=(
            SDS((BLOCK, D), F32),
            SDS(dw1.shape[1:], BF16),
            SDS(t2.shape, BF16),
            SDS(two.shape[1:], F32),
            SDS((24, 128), F32),
        ),
        in_specs=[VM] * 9,
        out_specs=(VM,) * 5,
        scratch_shapes=[
            pltpu.VMEM(dw1.shape[1:], BF16),
            pltpu.VMEM((24, 128), F32),
            pltpu.VMEM((7, 24, 128), F32),
            pltpu.VMEM((24, 128), F32),
            pltpu.VMEM((nz, 24, 128), F32),
            DMA((2, 7)),
            DMA((2, 7)),
            DMA((7 + nz,)),
            DMA((7 + nz,)),
        ]
        + plane_scratch((BLOCK, D))
        + ring_scratch(n, dw1.shape[1:])
        + ring_scratch(n, two.shape[1:]),
        compiler_params=pltpu.CompilerParams(collective_id=4, has_side_effects=True, vmem_limit_bytes=58 << 20),
        name="final",
    )(dh, x, gmid, ga, dgf, dgqk, dw1, two, t2)


def body(n, tokens, w_query, key_weight, w_value, w_out, w_gate, w_up, w_down, norm_gains, seq_lengths, slot_order, out_grad):
    groups = n // GROUP
    r = w_query.shape[0]
    ffc = w_down.shape[0]
    device = lax.axis_index("dp")
    g, p = device // GROUP, device % GROUP
    lengths = seq_lengths
    a1 = jnp.concatenate(
        [
            w_query.reshape(r, GROUP, 128),
            key_weight.reshape(r, GROUP, HEAD),
            w_value.reshape(r, GROUP, HEAD),
        ],
        axis=2,
    ).transpose(1, 0, 2)
    wgu = jnp.stack([w_gate, w_up], axis=1).reshape(r, 2, groups, GROUP, ffc)
    a2 = wgu.transpose(3, 0, 1, 2, 4).reshape(GROUP, r, 2 * groups * ffc)
    share = norm_gains.shape[0]
    gt = jnp.pad(norm_gains.astype(F32)[None, :], ((0, 7), (0, 128 - share)))
    wok = r // 16 if r % 16 == 0 else 1
    wdk = ffc // 16 if ffc % 16 == 0 else 1
    x_all, w1, w2, wo, wd, gains = gather_all(
        n, tokens, a1, a2, w_out.reshape(wok, r // wok, D), w_down.reshape(wdk, ffc // wdk, D), gt
    )
    gains = gains[:, :, 0, :share].reshape(1, -1)
    ga, gf = gains[:, :D], gains[:, D : 2 * D]
    gq = gains[:, 2 * D : 2 * D + HEAD]
    gk = gains[:, 2 * D + HEAD :]
    gqk = jnp.concatenate([jnp.concatenate([gq, gq], axis=1), jnp.concatenate([gk, gk], axis=1)], axis=0)
    wqkv = w1.reshape(D, QKV)
    wd = wd.reshape(-1, D)
    row = jnp.arange(ROWS, dtype=jnp.int32)
    length_row = lax.dynamic_index_in_dim(seq_lengths, g, 0, keepdims=False)
    order_row = lax.dynamic_index_in_dim(slot_order, g, 0, keepdims=False)
    ends = jnp.cumsum(length_row)
    start = jnp.max(jnp.where(row[:, None] >= ends[None, :], ends[None, :], 0), axis=1)
    frequency = jnp.exp(jnp.arange(HEAD // 2, dtype=F32) * (-2.0 * math.log(ROPE_THETA) / HEAD))
    angles = frequency[:, None] * (row - start).astype(F32)[None, :]
    cs = jnp.concatenate([jnp.cos(angles), jnp.sin(angles)], axis=0)
    slots = jnp.arange(ROWS // SLOT, dtype=jnp.int32)
    inv = jnp.sum(jnp.where(order_row[None, :] == slots[:, None], slots[None, :], 0), axis=1)

    h, raw, q, kv, mix, mixf, lse, dy_all, w2, wo = attn_fwd(
        n, lengths, x_all, wqkv, ga, gqk, cs, out_grad, w2, wo.reshape(groups, r, D)
    )
    wgu = w2.reshape(D, -1)
    wo = wo.reshape(D, D)
    res, gmid, dgf, dwo, dmh, po, dwgu, dwd = ffn_block(n, inv, mix, tokens, wo, gf, wgu, wd, dy_all)
    dh1, dwqkv, dgqk, result, two, t2, od = attn_bwd(
        n,
        lengths,
        dmh,
        q,
        kv,
        lse,
        mixf,
        h,
        raw,
        wqkv,
        gqk,
        cs,
        po,
        res,
        dwo.reshape(groups, GROUP, r, D),
        dwgu.reshape(groups, GROUP, r, -1),
        dwd.reshape(groups, wdk, ffc // wdk, D),
    )
    gtok, o1, o2, oo, og = final(
        n,
        dh1,
        tokens,
        gmid,
        ga,
        dgf,
        dgqk,
        dwqkv.reshape(groups, GROUP, r, QKV),
        two.reshape(groups, wok, r // wok, D),
        t2,
    )
    oo = oo.reshape(r, D)
    od = od.reshape(ffc, D)
    o1 = o1.transpose(1, 0, 2).astype(F32)
    gwq = o1[:, :, :128].reshape(r, -1)
    gwk = o1[:, :, 128 : 128 + HEAD].reshape(r, -1)
    gwv = o1[:, :, 128 + HEAD :].reshape(r, -1)
    o2 = o2.reshape(GROUP, r, 2, groups, ffc).transpose(2, 1, 3, 0, 4).reshape(2, r, -1).astype(F32)
    gains_out = lax.dynamic_slice(og.reshape(-1), (device * share,), (share,))
    return result, gtok, gwq, gwk, gwv, oo, o2[0], o2[1], od, gains_out


def solution(mesh):
    n = mesh.shape["dp"]
    row = P("dp", None)
    return jax.shard_map(
        functools.partial(body, n),
        mesh=mesh,
        in_specs=(row,) * 8 + (P("dp"), P(), P(), row),
        out_specs=(row,) * 9 + (P("dp"),),
        check_vma=False,
    )
```

```python
import functools
import math

import jax
import jax.numpy as jnp
from jax import lax
from jax.experimental import pallas as pl
from jax.experimental.pallas import tpu as pltpu
from jax.sharding import PartitionSpec as P

D = 1024
FF = 4608
QUERY_HEADS = 16
KEY_VALUE_HEADS = 8
HEAD = 64
SLOT = 128
GROUP = 8
ROWS = 2048
BLOCK = 256
QKV = 256
WINDOW = 4
VMEM_LIMIT = 62 << 20
EPSILON = 1e-05
ROPE_THETA = 1000000.0
SCALE = 1.0 / math.sqrt(HEAD)
LOG2E = math.log2(math.e)
F32 = jnp.float32
BF16 = jnp.bfloat16
MESH = pl.DeviceIdType.MESH
DMA = pltpu.SemaphoreType.DMA
VM = pl.BlockSpec(memory_space=pltpu.VMEM)
ANY = pl.BlockSpec(memory_space=pl.ANY)
HB = pl.BlockSpec(memory_space=pltpu.HBM)
SM = pl.BlockSpec(memory_space=pltpu.SMEM)
SDS = jax.ShapeDtypeStruct


def nn(a, b):
    return lax.dot_general(a, b, (((1,), (0,)), ((), ())), preferred_element_type=F32)


def nt(a, b):
    return lax.dot_general(a, b, (((1,), (1,)), ((), ())), preferred_element_type=F32)


def tn(a, b):
    return lax.dot_general(a, b, (((0,), (0,)), ((), ())), preferred_element_type=F32)


def rcopy(src, dst, send, recv, dev):
    return pltpu.make_async_remote_copy(
        src_ref=src, dst_ref=dst, send_sem=send, recv_sem=recv, device_id=(dev,), device_id_type=MESH
    )


def barrier(peers):
    sem = pltpu.get_barrier_semaphore()
    for q in peers:
        pl.semaphore_signal(sem, inc=1, device_id=(q,), device_id_type=MESH)
    pl.semaphore_wait(sem, len(peers))


def places(n):
    me = lax.axis_index("dp")
    p = lax.rem(me, GROUP)
    g = me // GROUP
    groups = n // GROUP
    zq = [lax.rem(g + s, groups) * GROUP + p for s in range(1, groups)]
    zg = [lax.rem(g + s, groups) for s in range(1, groups)]
    return me, p, g, groups, zq, zg


def start_all(copies):
    for c in copies:
        c.start()
    return copies


def bring(pairs, sem):
    return start_all([pltpu.make_async_copy(a, b, sem.at[i]) for i, (a, b) in enumerate(pairs)])


def in_hbm(*arrays):
    return [pltpu.with_memory_space_constraint(a, pltpu.HBM) for a in arrays]


def wait_all(copies):
    for c in copies:
        c.wait()


class PlaneGather:
    COPIES = 14

    def __init__(self, me, p, src, dst, ss, rs, ls=None):
        sib, xn, yn = me ^ 1, me ^ 2, me ^ 4

        def cp(a, b, i, dev):
            return rcopy(a, b, ss.at[i], rs.at[i], dev)

        def own(i, dev):
            return [cp(src(h), dst(p, h), i + h, dev) for h in range(2)]

        def on(m, h, i, dev):
            return cp(dst(p ^ m, h), dst(p ^ m, h), i, dev)

        self.x, self.y, self.o = own(0, xn), own(2, yn), own(4, sib)
        self.r = [on(2, 0, 6, yn), on(4, 1, 7, xn)]
        self.fx = [on(2, h, 8 + h, sib) for h in range(2)]
        self.fy = [on(4, h, 10 + h, sib) for h in range(2)]
        self.fd = [on(6, h, 12 + h, sib) for h in range(2)]
        self.local = [] if ls is None else [
            pltpu.make_async_copy(src(h), dst(p, h), ls.at[h]) for h in range(2)
        ]

    def start(self):
        self.start_first()
        self.start_second()

    def start_first(self):
        start_all([self.x[0], self.y[1]] + self.o + self.local)

    def start_second(self):
        start_all([self.x[1], self.y[0]])

    def relay1(self):
        self.x[0].wait_recv()
        start_all([self.r[0], self.fx[0]])
        self.y[1].wait_recv()
        start_all([self.r[1], self.fy[1]])

    def relay2(self):
        self.x[1].wait_recv()
        self.fx[1].start()
        self.y[0].wait_recv()
        self.fy[0].start()

    def relay3(self):
        for h in range(2):
            self.r[h].wait_recv()
            self.fd[h].start()

    def arrive(self, copies):
        for c in copies:
            c.wait_recv()

    def sent(self):
        for c in self.x + self.y + self.r + self.o + self.fx + self.fy + self.fd:
            c.wait_send()
        wait_all(self.local)

    def finish(self):
        self.arrive(self.o + self.fx + self.fy + self.fd)
        self.sent()


class Ring:
    def __init__(self, n, p, g, src, dst, ss, rs, ls=None):
        groups = n // GROUP
        to = lambda s: lax.rem(g + s, groups) * GROUP + p
        at = lambda s: lax.rem(g + s, groups)

        def cp(a, b, i, dev):
            return rcopy(a, b, ss.at[i], rs.at[i], dev)

        self.relays = []
        if groups == 4:
            self.up = [cp(src(h), dst(g, h), h, to(1)) for h in range(2)]
            self.down = [cp(src(h), dst(g, h), 2 + h, to(3)) for h in range(2)]
            self.first = [self.up[0], self.down[1], self.up[1], self.down[0]]
            below, above = at(3), at(1)
            self.relays = [cp(dst(below, 0), dst(below, 0), 4, to(1)), cp(dst(above, 1), dst(above, 1), 5, to(3))]
        else:
            self.first = [cp(src(None), dst(g, None), s - 1, to(s)) for s in range(1, groups)]
        self.local = [] if ls is None else [pltpu.make_async_copy(src(None), dst(g, None), ls)]

    def start(self):
        start_all(self.first + self.local)

    def relay(self):
        if self.relays:
            self.up[0].wait_recv()
            self.relays[0].start()
            self.down[1].wait_recv()
            self.relays[1].start()

    def finish(self):
        if self.relays:
            self.up[1].wait_recv()
            self.down[0].wait_recv()
            for c in self.first:
                c.wait_send()
        else:
            wait_all(self.first)
        wait_all(self.relays + self.local)


def ring_count(n):
    return max(6, n // GROUP - 1)


def halves(length):
    cut = length // 2
    part = (pl.ds(0, cut), pl.ds(cut, length - cut))
    return lambda h: slice(None) if h is None else part[h]


class RingReduce:
    def __init__(self, n, p, g, part, low, high, send, fin, ss, rs):
        groups = n // GROUP
        to = lambda s: lax.rem(g + s, groups) * GROUP + p
        at = lambda s: lax.rem(g + s, groups)
        hs = halves(part.shape[1])
        self.part, self.fin, self.send, self.g, self.hs = part, fin, send, g, hs

        def cp(a, b, i, dev):
            return rcopy(a, b, ss.at[i], rs.at[i], dev)

        self.ring = groups == 4
        if self.ring:
            self.above, self.below = at(1), at(3)
            self.low, self.high = low, high
            far = at(2)
            self.a = cp(part.at[far, hs(0)], low, 0, to(1))
            self.b = cp(part.at[far, hs(1)], high, 1, to(3))
            self.c = cp(part.at[self.above, hs(1)], fin.at[0, hs(1)], 2, to(1))
            self.d = cp(part.at[self.below, hs(0)], fin.at[1, hs(0)], 3, to(3))
            self.e = cp(send.at[hs(0)], fin.at[0, hs(0)], 4, to(1))
            self.f = cp(send.at[hs(1)], fin.at[1, hs(1)], 5, to(3))
            self.all = [self.a, self.b, self.c, self.d, self.e, self.f]
        else:
            self.all = [cp(part.at[at(s)], fin.at[s - 1], s - 1, to(s)) for s in range(1, groups)]
        self.count = groups - 1

    def start(self):
        start_all(self.all[:4] if self.ring else self.all)

    def relay(self):
        if self.ring:
            for got, buf, h, b, out in (
                (self.a, self.low, 0, self.above, self.e),
                (self.b, self.high, 1, self.below, self.f),
            ):
                got.wait_recv()
                at = self.hs(h)
                self.send[at] = (self.part[b, at].astype(F32) + buf[...].astype(F32)).astype(BF16)
                out.start()

    def finish(self):
        for c in self.all[2:] if self.ring else self.all:
            c.wait_recv()
        val = self.part[self.g].astype(F32)
        for s in range(2 if self.ring else self.count):
            val = val + self.fin[s].astype(F32)
        for c in self.all:
            c.wait_send()
        return val


def ring_scratch(n, shape):
    cut = shape[0] // 2
    groups = n // GROUP
    count = 2 if groups == 4 else groups - 1
    tail = tuple(shape[1:])
    vm = lambda s: pltpu.VMEM(s, BF16)
    return [
        vm((max(cut, 1),) + tail),
        vm((shape[0] - cut,) + tail),
        vm(tuple(shape)),
        vm((count,) + tuple(shape)),
        DMA((ring_count(n),)),
        DMA((ring_count(n),)),
    ]


class PlaneReduce:
    def __init__(self, me, part, sib, send, relay, fx, fy, ss, rs):
        p = lax.rem(me, GROUP)
        xn, yn = me ^ 2, me ^ 4
        hs = halves(sib.shape[1])
        self.hs, self.p, self.part = hs, p, part
        self.sib, self.send, self.relay, self.fx, self.fy = sib, send, relay, fx, fy

        def cp(a, b, i, dev):
            return rcopy(a, b, ss.at[i], rs.at[i], dev)

        self.first = [cp(part(p ^ (2 * i + 1)), sib.at[i], i, me ^ 1) for i in range(4)]
        self.diag = [cp(send.at[0, hs(0)], relay.at[0], 4, xn), cp(send.at[0, hs(1)], relay.at[1], 5, yn)]
        self.toy = [cp(send.at[2, hs(h)], fy.at[hs(h)], 6 + h, yn) for h in range(2)]
        self.tox = [cp(send.at[1, hs(h)], fx.at[hs(h)], 8 + h, xn) for h in range(2)]

    def start(self):
        start_all([self.first[i] for i in (3, 1, 2, 0)])

    def chip(self, i):
        self.first[i].wait_recv()
        return self.part(self.p ^ (2 * i))[...].astype(F32) + self.sib[i].astype(F32)

    def chip_d(self):
        self.send[0] = self.chip(3).astype(BF16)
        start_all(self.diag)

    def chip_x(self):
        self.send[1] = self.chip(1).astype(BF16)
        self.tox[0].start()

    def chip_y(self):
        self.send[2] = self.chip(2).astype(BF16)
        self.toy[1].start()

    def phase1(self):
        self.chip_d()
        self.chip_x()
        self.chip_y()

    def phase2(self):
        self.diag[0].wait_recv()
        at = self.hs(0)
        self.send[2, at] = (self.send[2, at].astype(F32) + self.relay[0].astype(F32)).astype(BF16)
        self.toy[0].start()
        self.diag[1].wait_recv()
        at = self.hs(1)
        self.send[1, at] = (self.send[1, at].astype(F32) + self.relay[1].astype(F32)).astype(BF16)
        self.tox[1].start()

    def phase3(self):
        own = self.chip(0)
        for c in self.toy + self.tox:
            c.wait_recv()
        own = own + self.fx[...].astype(F32) + self.fy[...].astype(F32)
        for c in self.first + self.diag + self.toy + self.tox:
            c.wait_send()
        return own


def plane_scratch(shape):
    tail = tuple(shape[1:])
    vm = lambda *s: pltpu.VMEM(s + tail, BF16)
    return [
        vm(4, shape[0]),
        vm(3, shape[0]),
        vm(2, shape[0] // 2),
        vm(shape[0]),
        vm(shape[0]),
        DMA((10,)),
        DMA((10,)),
    ]


def gather_kernel(n, len_ref, x_, wq_, wk_, wv_, wg_, wu_, wo_, wd_, gn_, xo, a1o, a2o, woo, wdo, gvec, cs, x, gn, wq, wk, wv, wo, wd, wg, wu, a1, a2, gt, gto, fs, ls, xs, xr, ps, pr, zs, zr):
    me, p, g, groups, zq, zg = places(n)
    fetch = bring(
        (
            (x_, x),
            (gn_, gn),
            (wq_, wq),
            (wk_, wk),
            (wv_, wv),
            (wo_, wo),
            (wd_, wd),
            (wg_, wg),
            (wu_, wu),
        ),
        fs,
    )
    share = gn.shape[1]
    ffc = wg.shape[1] // (groups * GROUP)
    barrier([me ^ m for m in range(1, GROUP)] + zq)
    hx = halves(BLOCK)
    xg = PlaneGather(me, p, lambda h: x.at[hx(h)], lambda b, h: xo.at[b, hx(h)], xs, xr, ls.at[pl.ds(5, 2)])
    fetch[0].wait()
    xg.start_first()

    def ring(k, src, dst, local=None):
        hk = halves(dst.shape[1])
        return Ring(n, p, g, lambda h: src.at[hk(h)], lambda b, h: dst.at[b, hk(h)], zs.at[k], zr.at[k], local)

    rings = [
        ring(0, a1o.at[g], a1o),
        ring(1, gto.at[g], gto),
        ring(2, wd, wdo, ls.at[3]),
        ring(3, wo, woo, ls.at[4]),
    ]
    pc = {}

    def exchange(k, src, dst):
        for m in range(1, GROUP):
            pc[k, m] = rcopy(src(p ^ m), dst, ps.at[k, m - 1], pr.at[k, m - 1], me ^ m)
            pc[k, m].start()

    fetch[1].wait()
    gt[...] = jnp.zeros_like(gt)
    gt[0:1, :share] = gn[...].astype(F32)
    exchange(1, lambda b: gt, gto.at[g, p])
    gto[g, p] = gt[...]
    wait_all(fetch[2:5])
    for b in range(GROUP):
        a1[b, :, :128] = wq[:, 128 * b : 128 * (b + 1)]
        at = slice(HEAD * b, HEAD * (b + 1))
        a1[b, :, 128:] = jnp.concatenate([wk[:, at], wv[:, at]], axis=1)
    exchange(0, lambda b: a1.at[b], a1o.at[g, p])
    wait_all(fetch[5:7])
    rings[3].start()
    rings[2].start()
    wait_all(fetch[7:])
    for b in range(GROUP):
        at = [slice((GROUP * k + b) * ffc, (GROUP * k + b + 1) * ffc) for k in range(groups)]
        a2[b] = jnp.concatenate([wg[:, k] for k in at] + [wu[:, k] for k in at], axis=1)
    exchange(2, lambda b: a2.at[b], a2o.at[p])
    xg.start_second()
    local = [
        pltpu.make_async_copy(a1.at[p], a1o.at[g, p], ls.at[0]),
        pltpu.make_async_copy(a2.at[p], a2o.at[p], ls.at[2]),
    ]
    start_all(local)
    local[0].wait()
    for k in range(2):
        for m in range(1, GROUP):
            pc[k, m].wait_recv()
        rings[k].start()
    xg.relay1()
    row = lax.broadcasted_iota(jnp.int32, (1, ROWS), 1)
    position = (row - seq_start(row, len_ref, g)).astype(F32)
    index = lax.broadcasted_iota(jnp.int32, (HEAD // 2, 1), 0).astype(F32)
    angles = jnp.exp(index * (-2.0 * math.log(ROPE_THETA) / HEAD)) * position
    cs[: HEAD // 2] = jnp.cos(angles)
    cs[HEAD // 2 :] = jnp.sin(angles)
    xg.relay2()
    for k in (3, 0, 1, 2):
        rings[k].relay()
    xg.relay3()
    for m in range(1, GROUP):
        pc[2, m].wait_recv()
    local[1].wait()
    for c in pc.values():
        c.wait_send()
    for k in range(4):
        rings[k].finish()
    gvec[...] = jnp.concatenate(
        [gto[k, b, 0:1, :share] for k in range(groups) for b in range(GROUP)], axis=1
    )
    xg.finish()


def gather_all(n, lengths, x, wq, wk, wv, wg, wu, wo, wd, gn):
    groups = n // GROUP
    r = wq.shape[0]
    wide = 2 * wg.shape[1] // GROUP
    return pl.pallas_call(
        functools.partial(gather_kernel, n),
        out_shape=(
            SDS((GROUP, BLOCK, D), BF16),
            SDS((groups, GROUP, r, QKV), BF16),
            SDS((GROUP, r, wide), BF16),
            SDS((groups,) + wo.shape, BF16),
            SDS((groups,) + wd.shape, BF16),
            SDS((1, gn.shape[1] * n), F32),
            SDS((HEAD, ROWS), F32),
        ),
        in_specs=[SM] + [HB] * 9,
        out_specs=(HB,) * 5 + (VM, VM),
        scratch_shapes=[pltpu.VMEM(w.shape, BF16) for w in (x, gn, wq, wk, wv, wo, wd, wg, wu)]
        + [
            pltpu.VMEM((GROUP, r, QKV), BF16),
            pltpu.VMEM((GROUP, r, wide), BF16),
            pltpu.VMEM((8, 128), F32),
            pltpu.VMEM((groups, GROUP, 8, 128), F32),
            DMA((9,)),
            DMA((7,)),
            DMA((14,)),
            DMA((14,)),
            DMA((3, 7)),
            DMA((3, 7)),
            DMA((4, ring_count(n))),
            DMA((4, ring_count(n))),
        ],
        compiler_params=pltpu.CompilerParams(collective_id=1, has_side_effects=True, vmem_limit_bytes=VMEM_LIMIT),
        name="gather_all",
    )(lengths, x, wq, wk, wv, wg, wu, wo, wd, gn)


def swap_halves(v):
    lane = lax.broadcasted_iota(jnp.int32, v.shape, 1)
    low = lax.rem(lane, HEAD) < HEAD // 2
    width = v.shape[1]
    return jnp.where(low, pltpu.roll(v, width - HEAD // 2, 1), pltpu.roll(v, HEAD // 2, 1))


def head_mean(v):
    lane = lax.broadcasted_iota(jnp.int32, v.shape, 1)
    low = lane < HEAD
    a = jnp.sum(jnp.where(low, v, 0.0), axis=-1, keepdims=True)
    b = jnp.sum(jnp.where(low, 0.0, v), axis=-1, keepdims=True)
    return jnp.where(low, a, b) * (1.0 / HEAD)


def head_gains(g_ref):
    t = g_ref[:, 2 * D :]
    t = jnp.broadcast_to(t, (8, 128))
    lane = lax.broadcasted_iota(jnp.int32, (8, 128), 1)
    other = pltpu.roll(t, HEAD, 1)
    return jnp.where(lane < HEAD, t, other)[0:1, :], jnp.where(lane < HEAD, other, t)[0:1, :]


def seq_start(row, len_ref, g):
    e1 = len_ref[g, 0]
    e2 = e1 + len_ref[g, 1]
    e3 = e2 + len_ref[g, 2]
    zero = row * 0
    s = jnp.where(row >= e1, zero + e1, zero)
    s = jnp.where(row >= e2, zero + e2, s)
    return jnp.where(row >= e3, zero + e3, s)


def tables(cs_ref):
    t = cs_ref[...].T
    c, s = t[:, : HEAD // 2], t[:, HEAD // 2 :]
    return jnp.concatenate([c, c, c, c], axis=1), jnp.concatenate([-s, s, -s, s], axis=1)


def attn_fwd_kernel(n, len_ref, x_ref, w_ref, g_ref, cs_ref, dy_, w2_, wo_, h_ref, raw_ref, q_ref, kv_ref, mix_ref, mixf_ref, lse_ref, dyo, w2o, woo, k_s, v_s, acc, dy, w2, wo, fs, ls, ds_, dr, os_, orr, zs, zr):
    i = pl.program_id(0)
    me, p, g, groups, zq, zg = places(n)
    hd, hw, ho = halves(BLOCK), halves(w2.shape[0]), halves(wo.shape[0])
    dg = PlaneGather(me, p, lambda h: dy.at[hd(h)], lambda b, h: dyo.at[b, hd(h)], ds_, dr, ls.at[pl.ds(0, 2)])
    og = PlaneGather(me, p, lambda h: wo.at[ho(h)], lambda b, h: woo.at[ho(h), b], os_, orr, ls.at[pl.ds(2, 2)])
    zg_ = Ring(n, p, g, lambda h: w2.at[hw(h)], lambda b, h: w2o.at[b, hw(h)], zs, zr, ls.at[4])

    @pl.when(i == 0)
    def _():
        fetch = bring(((dy_, dy), (w2_, w2), (wo_, wo)), fs)
        barrier([me ^ m for m in (1, 2, 4)] + zq)
        fetch[1].wait()
        zg_.start()
        fetch[0].wait()
        dg.start()
        fetch[2].wait()
        og.start()

    @pl.when(i == 3)
    def _():
        dg.relay1()

    @pl.when(i == 5)
    def _():
        zg_.relay()
        dg.relay2()

    @pl.when(i == 6)
    def _():
        og.relay1()
        dg.relay3()

    @pl.when(i == 7)
    def _():
        og.relay2()

    xb = x_ref[0].astype(F32)
    r = lax.rsqrt(jnp.mean(xb * xb, axis=-1, keepdims=True) + EPSILON)
    h = (xb * r * g_ref[:, :D]).astype(BF16)
    gq, gk = head_gains(g_ref)
    h_ref[0] = h
    raw = nn(h, w_ref[...])
    raw_ref[0] = raw
    ct, st = tables(cs_ref)
    qraw, kvraw = raw[:, :128], raw[:, 128:]
    qn = qraw * lax.rsqrt(head_mean(qraw * qraw) + EPSILON) * gq
    q = (qn * ct + swap_halves(qn) * st).astype(BF16)
    kn = kvraw * lax.rsqrt(head_mean(kvraw * kvraw) + EPSILON) * gk
    k = (kn * ct + swap_halves(kn) * st).astype(BF16)
    lane = lax.broadcasted_iota(jnp.int32, (BLOCK, 128), 1)
    kv = jnp.where(lane < HEAD, k.astype(F32), kvraw).astype(BF16)
    q_ref[0] = q
    kv_ref[0] = kv
    k_s[pl.ds(i * BLOCK, BLOCK), :] = kv[:, :HEAD]
    v_s[pl.ds(i * BLOCK, BLOCK), :] = jnp.where(lane < HEAD, pltpu.roll(kvraw, HEAD, 1), 1.0).astype(BF16)
    q2 = jnp.concatenate([q[:, :HEAD], q[:, HEAD:]], axis=0)
    acc[...] = jnp.zeros_like(acc)
    row = lax.broadcasted_iota(jnp.int32, (2 * BLOCK, 1), 0)
    qrow = i * BLOCK + jnp.where(row >= BLOCK, row - BLOCK, row)
    qstart = seq_start(qrow, len_ref, g)
    first = jnp.maximum(i - WINDOW, 0)
    col = lax.broadcasted_iota(jnp.int32, (2 * BLOCK, BLOCK), 1)

    def step(j, carry):
        kb = k_s[pl.ds(pl.multiple_of(j * BLOCK, BLOCK), BLOCK), :]
        vb = v_s[pl.ds(pl.multiple_of(j * BLOCK, BLOCK), BLOCK), :]
        s = nt(q2, kb)
        kc = col + j * BLOCK
        ok = (kc >= qstart) & (kc <= qrow)
        e = jnp.where(ok, jnp.exp2(s * (SCALE * LOG2E)), 0.0).astype(BF16)
        acc[...] += nn(e, vb)
        return carry

    lax.fori_loop(first, i + 1, step, 0)
    total = acc[:, HEAD:]
    m = acc[:, :HEAD] / total
    both = jnp.concatenate([m[:BLOCK], m[BLOCK:]], axis=1)
    mixf_ref[0] = both
    mix_ref[0] = both.astype(BF16)
    lse_ref[0] = jnp.log2(total.T)[:8, :]

    @pl.when(i == 7)
    def _():
        og.relay3()
        dg.finish()
        zg_.finish()
        og.finish()


def attn_fwd(n, lengths, x_all, wqkv, gvec, cs, dy, w2, wo):
    groups = n // GROUP
    blk = lambda c: pl.BlockSpec((1, BLOCK, c), lambda i: (i, 0, 0))
    whole = lambda s: pl.BlockSpec(s, lambda i: (0,) * len(s), pipeline_mode=pl.Buffered(1))
    nb = ROWS // BLOCK
    return pl.pallas_call(
        functools.partial(attn_fwd_kernel, n),
        grid=(nb,),
        in_specs=[
            SM,
            blk(D),
            whole((D, QKV)),
            whole(gvec.shape),
            pl.BlockSpec((HEAD, BLOCK), lambda i: (0, i)),
            HB,
            HB,
            HB,
        ],
        out_specs=(blk(D), blk(QKV), blk(128), blk(128), blk(128), blk(128), pl.BlockSpec((1, 8, 2 * BLOCK), lambda i: (i, 0, 0)), HB, HB, HB),
        out_shape=(
            SDS((nb, BLOCK, D), BF16),
            SDS((nb, BLOCK, QKV), F32),
            SDS((nb, BLOCK, 128), BF16),
            SDS((nb, BLOCK, 128), BF16),
            SDS((nb, BLOCK, 128), BF16),
            SDS((nb, BLOCK, 128), F32),
            SDS((nb, 8, 2 * BLOCK), F32),
            SDS((GROUP, BLOCK, D), BF16),
            SDS((groups,) + w2.shape, BF16),
            SDS((groups, GROUP) + wo.shape[1:], BF16),
        ),
        scratch_shapes=[
            pltpu.VMEM((ROWS, HEAD), BF16),
            pltpu.VMEM((ROWS, 128), BF16),
            pltpu.VMEM((2 * BLOCK, 128), F32),
            pltpu.VMEM(dy.shape, BF16),
            pltpu.VMEM(w2.shape, BF16),
            pltpu.VMEM(wo.shape, BF16),
            DMA((3,)),
            DMA((5,)),
            DMA((14,)),
            DMA((14,)),
            DMA((14,)),
            DMA((14,)),
            DMA((ring_count(n),)),
            DMA((ring_count(n),)),
        ],
        compiler_params=pltpu.CompilerParams(
            collective_id=5, has_side_effects=True, dimension_semantics=("arbitrary",), vmem_limit_bytes=VMEM_LIMIT
        ),
        cost_estimate=pl.CostEstimate(flops=4 * 10**9, bytes_accessed=16 << 20, transcendentals=4 * 10**6),
        name="attn_fwd",
    )(lengths, *in_hbm(x_all, wqkv, gvec, cs), dy, w2, wo)


def norm_back(dyv, xv, gain):
    r = lax.rsqrt(jnp.mean(xv * xv, axis=-1, keepdims=True) + EPSILON)
    xr = xv * r
    gy = dyv * gain
    dx = r * (gy - xr * jnp.mean(gy * xr, axis=-1, keepdims=True))
    return dx, jnp.sum(dyv * xr, axis=0, keepdims=True)


def ffn_block_kernel(n, order, mix, x_, wo_, g_ref, w2_, wd_, dy_, res, gmid, dgf, dwo, dmh, po, dw2, od, x, wo, w2, wd, dy, fs, mbuf, h2, wgs, wds, dys, acts, dgus, part, mown, stage, dwd, ps, pr, hs, hr, os_, qs, qr, *red_refs):
    me, p, g, groups, zq, zg = places(n)
    barrier([me ^ m for m in range(1, GROUP)] + zq)
    fetch = bring(((w2_, w2), (wd_, wd), (x_, x), (wo_, wo), (mix.at[p], mbuf.at[p]), (dy_, dy)), fs)
    gf = g_ref.at[:, D : 2 * D]

    def holder(q):
        s = 0
        for k in range(ROWS // SLOT):
            s = jnp.where(order[g, k] == q, k, s)
        return s

    fl = wd.shape[0]
    fp = wds.shape[0]
    pc = start_all(
        [rcopy(mix.at[p ^ m], mbuf.at[p], ps.at[m - 1], pr.at[m - 1], me ^ m) for m in range(1, GROUP)]
    )
    wait_all(fetch[:2])
    gap = jnp.zeros((D, fp - fl), BF16)
    wgs[:, :fl] = w2[:, :fl]
    wgs[:, fl:fp] = gap
    wgs[:, fp : fp + fl] = w2[:, fl:]
    wgs[:, fp + fl :] = gap
    wds[:fl] = wd[...]
    wds[fl:] = jnp.zeros((fp - fl, D), BF16)
    for c in pc:
        c.wait_recv()
    wait_all(fetch[2:5])
    m = jnp.concatenate([mbuf[b] for b in range(GROUP)], axis=1)
    mown[...] = m
    z = x[...].astype(F32) + nn(m, wo[...])
    res[...] = z
    r = lax.rsqrt(jnp.mean(z * z, axis=-1, keepdims=True) + EPSILON)
    h2[p] = (z * r * gf[...]).astype(BF16)
    hb = halves(BLOCK)
    hg = PlaneGather(me, p, lambda h: h2.at[p, hb(h)], lambda b, h: h2.at[b, hb(h)], hs, hr)
    red = PlaneReduce(me, lambda b: part.at[b], *red_refs[:7])
    ring = RingReduce(n, p, g, dwd, *red_refs[7:])
    hg.start_first()
    fetch[5].wait()

    def block(t, carry):
        @pl.when(t == 1)
        def _():
            hg.start_second()
            hg.arrive(hg.o)

        @pl.when(t == 2)
        def _():
            red.first[0].start()
            hg.relay1()
            hg.relay2()

        @pl.when(t == 3)
        def _():
            hg.arrive(hg.fx)

        @pl.when(t == 4)
        def _():
            red.first[1].start()

        @pl.when(t == 5)
        def _():
            hg.arrive(hg.fy)
            red.chip_x()

        @pl.when(t == 6)
        def _():
            red.first[2].start()
            hg.relay3()

        @pl.when(t == 7)
        def _():
            red.chip_y()
            hg.arrive(hg.fd)

        b = p ^ t
        h = h2[b]
        dyb = jnp.concatenate([dy[holder(2 * b)], dy[holder(2 * b + 1)]], axis=0)
        dys[b] = dyb
        gu = nn(h, wgs[...])
        da = nt(dyb, wds[...])
        gp, up = gu[:, :fp], gu[:, fp:]
        sig = 1.0 / (1.0 + jnp.exp(-gp))
        sg = gp * sig
        acts[b] = (sg * up).astype(BF16)
        dgu = jnp.concatenate(
            [(da * up * (sig * (1.0 + gp * (1.0 - sig)))).astype(BF16), (da * sg).astype(BF16)], axis=1
        )
        dgus[b] = dgu
        part[b] = nt(dgu, wgs[...]).astype(BF16)
        return carry

    lax.fori_loop(0, GROUP, block, 0)
    red.first[3].start()
    a_all = acts[...].reshape(ROWS, fp)
    dw = tn(a_all, dys[...].reshape(ROWS, D))[:fl].astype(BF16)
    each = fl // groups
    for k in range(groups):
        dwd[k] = dw[k * each : (k + 1) * each].reshape(dwd.shape[1:])
    ring.start()
    red.chip_d()

    def out(b, carry):
        slot = lax.rem(b, 2)

        @pl.when(b > 1)
        def _():
            pltpu.make_async_copy(stage.at[slot], po.at[b - 2], os_.at[slot]).wait()

        stage[slot] = nn(acts[b], wds[...]).astype(BF16)
        pltpu.make_async_copy(stage.at[slot], po.at[b], os_.at[slot]).start()
        return carry

    lax.fori_loop(0, GROUP, out, 0)
    for b in range(GROUP - 2, GROUP):
        pltpu.make_async_copy(stage.at[b % 2], po.at[b], os_.at[b % 2]).wait()
    red.phase2()
    h_all = h2[...].reshape(ROWS, D)
    dg_all = dgus[...].reshape(ROWS, 2 * fp)
    dw2[:, :fl] = tn(h_all, dg_all[:, :fp])[:, :fl].astype(BF16)
    dw2[:, fl:] = tn(h_all, dg_all[:, fp:])[:, :fl].astype(BF16)
    ring.relay()
    dx, dgain = norm_back(red.phase3(), res[...], gf[...])
    dyo = dys[p].astype(F32)
    gm = dyo + dx
    gmid[...] = gm
    dgf[...] = dgain
    gl = gm.astype(BF16)
    dm = nt(gl, wo[...]).astype(BF16)
    for b in range(GROUP):
        mbuf[b] = dm[:, 128 * b : 128 * (b + 1)]
    for c in pc:
        c.wait_send()
    qc = start_all(
        [rcopy(mbuf.at[p ^ m], dmh.at[p], qs.at[m - 1], qr.at[m - 1], me ^ m) for m in range(1, GROUP)]
    )
    dmh[p] = mbuf[p]
    dwo[...] = tn(mown[...], gl).astype(BF16)
    wait_all(qc)
    hg.sent()
    od[...] = ring.finish()


def ffn_block(n, order, mix, x, wo, gvec, w2, wd, dy, blk):
    fl = wd.shape[0]
    groups = n // GROUP
    fp = -(-fl // 128) * 128
    vm = lambda *s: pltpu.VMEM(s, BF16)
    return pl.pallas_call(
        functools.partial(ffn_block_kernel, n),
        out_shape=(
            SDS((BLOCK, D), F32),
            SDS((BLOCK, D), F32),
            SDS((1, D), F32),
            SDS((D, D), BF16),
            SDS((GROUP, BLOCK, 128), BF16),
            SDS((GROUP, BLOCK, D), BF16),
            SDS((D, 2 * fl), BF16),
            SDS(blk, F32),
        ),
        in_specs=[SM, HB, HB, HB, VM, HB, HB, HB],
        out_specs=(VM, VM, VM, VM, VM, HB, VM, VM),
        scratch_shapes=[
            vm(BLOCK, D),
            vm(D, D),
            vm(D, 2 * fl),
            vm(fl, D),
            vm(ROWS // SLOT, SLOT, D),
            DMA((6,)),
            vm(GROUP, BLOCK, 128),
            vm(GROUP, BLOCK, D),
            vm(D, 2 * fp),
            vm(fp, D),
            vm(GROUP, BLOCK, D),
            vm(GROUP, BLOCK, fp),
            vm(GROUP, BLOCK, 2 * fp),
            vm(GROUP, BLOCK, D),
            vm(BLOCK, D),
            vm(2, BLOCK, D),
            vm(groups, *blk),
            DMA((7,)),
            DMA((7,)),
            DMA((14,)),
            DMA((14,)),
            DMA((2,)),
            DMA((7,)),
            DMA((7,)),
        ]
        + plane_scratch((BLOCK, D))
        + ring_scratch(n, blk),
        compiler_params=pltpu.CompilerParams(collective_id=2, has_side_effects=True, vmem_limit_bytes=VMEM_LIMIT),
        name="ffn_block",
    )(order, mix, x, wo, gvec, w2, wd, dy.reshape(ROWS // SLOT, SLOT, D))


def attn_bwd_kernel(n, len_ref, dm_ref, q_ref, kvall_ref, lse_ref, mixf_ref, h_ref, raw_ref, w_ref, g_ref, cs_ref, po, res, dwo, dw2, dgf, dh_ref, dw_ref, gpart, result, two, t2, k_s, v_s, dkv, dqt, dws, dg_ref, *rest):
    step_id = pl.program_id(0)
    nb = ROWS // BLOCK
    i = nb - 1 - step_id
    me, p, g, groups, zq, zg = places(n)
    ored = PlaneReduce(me, lambda b: po.at[b], *rest[:7])
    wred = PlaneReduce(me, lambda b: dwo.at[:, b], *rest[7:14])
    ring2 = RingReduce(n, p, g, dw2, *rest[14:20])

    @pl.when(step_id == 0)
    def _():
        barrier([me ^ m for m in (1, 2, 4)] + zq)
        ored.start()
        ring2.start()
        wred.start()

    @pl.when(step_id == 1)
    def _():
        ored.phase1()
        wred.phase1()

    @pl.when(step_id == 3)
    def _():
        ring2.relay()
        ored.phase2()

    @pl.when(step_id == 4)
    def _():
        wred.phase2()


    @pl.when(step_id == 0)
    def _():
        dkv[...] = jnp.zeros_like(dkv)
        dws[...] = jnp.zeros_like(dws)
        dg_ref[...] = jnp.zeros_like(dg_ref)
        for b in range(ROWS // BLOCK):
            kvb = kvall_ref[b]
            k_s[pl.ds(b * BLOCK, BLOCK), :] = kvb[:, :HEAD]
            v_s[pl.ds(b * BLOCK, BLOCK), :] = kvb[:, HEAD:]

    q, do, mf = q_ref[0], dm_ref[0], mixf_ref[0]
    q2 = jnp.concatenate([q[:, :HEAD], q[:, HEAD:]], axis=0)
    do2 = jnp.concatenate([do[:, :HEAD], do[:, HEAD:]], axis=0)
    prod = (do.astype(F32) * mf).T
    delta = jnp.concatenate(
        [jnp.sum(prod[:HEAD], axis=0, keepdims=True), jnp.sum(prod[HEAD:], axis=0, keepdims=True)], axis=1
    )
    lse = lse_ref[0, 0:1, :]
    colq = lax.broadcasted_iota(jnp.int32, (1, 2 * BLOCK), 1)
    qrow = i * BLOCK + jnp.where(colq >= BLOCK, colq - BLOCK, colq)
    qstart = seq_start(qrow, len_ref, g)
    first = jnp.maximum(i - WINDOW, 0)
    rowk = lax.broadcasted_iota(jnp.int32, (BLOCK, 2 * BLOCK), 0)
    dqt[...] = jnp.zeros_like(dqt)

    def step(j, carry):
        at = pl.ds(pl.multiple_of(j * BLOCK, BLOCK), BLOCK)
        kb, vb = k_s[at, :], v_s[at, :]
        s = nt(kb, q2)
        kc = rowk + j * BLOCK
        ok = (kc >= qstart) & (kc <= qrow)
        pr = jnp.where(ok, jnp.exp2(s * (SCALE * LOG2E) - lse), 0.0)
        dp = nt(vb, do2)
        dsc = (pr * (dp - delta)).astype(BF16)
        dkv[at, :HEAD] += nn(dsc, q2)
        dkv[at, HEAD:] += nn(pr.astype(BF16), do2)
        dqt[...] += tn(dsc, kb)
        return carry

    lax.fori_loop(first, i + 1, step, 0)
    ct, st = tables(cs_ref)
    raw = raw_ref[0]
    dq = jnp.concatenate([dqt[:BLOCK], dqt[BLOCK:]], axis=1) * SCALE
    dkvb = dkv[pl.ds(pl.multiple_of(i * BLOCK, BLOCK), BLOCK), :]
    lane = lax.broadcasted_iota(jnp.int32, (BLOCK, 128), 1)

    def pull(d, v, gain):
        dn = d * ct - swap_halves(d) * st
        r = lax.rsqrt(head_mean(v * v) + EPSILON)
        vr = v * r
        gy = dn * gain
        return r * (gy - vr * head_mean(gy * vr)), jnp.sum(dn * vr, axis=0, keepdims=True)

    gq, gk = head_gains(g_ref)
    dqr, dgq = pull(dq, raw[:, :128], gq)
    dkr, dgk = pull(dkvb * SCALE, raw[:, 128:], gk)
    dg_ref[0:1, :] += dgq
    dg_ref[1:2, :] += dgk
    dqkv = jnp.concatenate([dqr, jnp.where(lane < HEAD, dkr, dkvb)], axis=1).astype(BF16)
    dh_ref[0] = nt(dqkv, w_ref[...]).astype(BF16)
    dws[...] += tn(h_ref[0], dqkv)

    @pl.when(step_id == nb - 1)
    def _():
        dw_ref[...] = dws[...].astype(BF16)
        result[...] = (ored.phase3() + res[...]).astype(BF16)
        two[...] = wred.phase3().astype(BF16)
        t2[...] = ring2.finish().astype(BF16)
        dga = lax.dot_general(
            jnp.ones((8, QKV), F32),
            w_ref[...].astype(F32) * dws[...],
            (((1,), (1,)), ((), ())),
            precision=lax.Precision.HIGHEST,
            preferred_element_type=F32,
        )
        dga = dga[0:1, :] / g_ref[:, :D]
        gpart[...] = jnp.zeros_like(gpart)
        for b in range(8):
            gpart[b : b + 1, :] = dga[:, 128 * b : 128 * (b + 1)]
            gpart[8 + b : 9 + b, :] = dgf[:, 128 * b : 128 * (b + 1)]
        turned = pltpu.roll(dg_ref[...], HEAD, 1)
        low = lax.broadcasted_iota(jnp.int32, (1, 128), 1) < HEAD
        gpart[16:17, :] = jnp.where(low, dg_ref[0:1, :] + turned[0:1, :], turned[1:2, :])


def attn_bwd(n, lengths, dmh, q, kv, lse, mixf, h, raw, wqkv, gvec, cs, po, res, dwo, dw2, dgf):
    nb = ROWS // BLOCK
    groups = n // GROUP
    blk = lambda c: pl.BlockSpec((1, BLOCK, c), lambda i: (nb - 1 - i, 0, 0))
    whole = lambda s: pl.BlockSpec(s, lambda i: (0,) * len(s), pipeline_mode=pl.Buffered(1))
    return pl.pallas_call(
        functools.partial(attn_bwd_kernel, n),
        grid=(nb,),
        in_specs=[
            SM,
            blk(128),
            blk(128),
            whole((nb, BLOCK, 128)),
            pl.BlockSpec((1, 8, 2 * BLOCK), lambda i: (nb - 1 - i, 0, 0)),
            blk(128),
            blk(D),
            blk(QKV),
            whole((D, QKV)),
            whole(gvec.shape),
            pl.BlockSpec((HEAD, BLOCK), lambda i: (0, nb - 1 - i)),
            whole(po.shape),
            whole(res.shape),
            whole(dwo.shape),
            whole(dw2.shape),
            whole(dgf.shape),
        ],
        out_specs=(
            blk(D),
            whole((D, QKV)),
            whole((24, 128)),
            whole((BLOCK, D)),
            whole((groups,) + dwo.shape[2:]),
            whole(dw2.shape[1:]),
        ),
        out_shape=(
            SDS((nb, BLOCK, D), BF16),
            SDS((D, QKV), BF16),
            SDS((24, 128), F32),
            SDS((BLOCK, D), BF16),
            SDS((groups,) + dwo.shape[2:], BF16),
            SDS(dw2.shape[1:], BF16),
        ),
        scratch_shapes=[
            pltpu.VMEM((ROWS, HEAD), BF16),
            pltpu.VMEM((ROWS, HEAD), BF16),
            pltpu.VMEM((ROWS, 128), F32),
            pltpu.VMEM((2 * BLOCK, HEAD), F32),
            pltpu.VMEM((D, QKV), F32),
            pltpu.VMEM((8, 128), F32),
        ]
        + plane_scratch((BLOCK, D))
        + plane_scratch((groups,) + dwo.shape[2:])
        + ring_scratch(n, dw2.shape[1:]),
        compiler_params=pltpu.CompilerParams(
            collective_id=6, has_side_effects=True, dimension_semantics=("arbitrary",), vmem_limit_bytes=VMEM_LIMIT
        ),
        cost_estimate=pl.CostEstimate(flops=8 * 10**9, bytes_accessed=16 << 20, transcendentals=4 * 10**6),
        name="attn_bwd",
    )(lengths, dmh, q, kv, lse, mixf, h, raw, wqkv, gvec, cs, po, res, dwo, dw2, dgf)


def final_kernel(n, dh, x, gmid, g_ref, dw1, two, t2, gpart, gtok, o1, o2, oo, og, t1, gin, gsum, gz, ps, pr, gs, gr, *rest):
    me, p, g, groups, zq, zg = places(n)
    nz = groups - 1
    share = g_ref.shape[1] // n
    barrier([me ^ m for m in range(1, GROUP)] + zq)
    red = PlaneReduce(me, lambda b: dh.at[b], *rest[:7])
    ring1 = RingReduce(n, p, g, dw1, *rest[7:13])
    ringo = RingReduce(n, p, g, two, *rest[13:19])
    red.start()
    gc = start_all([rcopy(gpart, gin.at[m - 1], gs.at[m - 1], gr.at[m - 1], me ^ m) for m in range(1, GROUP)])
    ring1.start()
    ringo.start()
    pc = []

    def exchange(k, src, out):
        for m in range(1, GROUP):
            c = rcopy(src.at[p ^ m], out.at[p], ps.at[k, m - 1], pr.at[k, m - 1], me ^ m)
            c.start()
            pc.append(c)
        out[p] = src[p]

    red.phase1()
    exchange(1, t2, o2)
    tot = gpart[...]
    for m in range(1, GROUP):
        gc[m - 1].wait_recv()
        tot = tot + gin[m - 1]
    gsum[...] = tot
    gzc = start_all([rcopy(gsum, gz.at[s], gs.at[7 + s], gr.at[7 + s], zq[s]) for s in range(nz)])
    ring1.relay()
    ringo.relay()
    red.phase2()
    t1[...] = ring1.finish().astype(BF16)
    exchange(0, t1, o1)
    oo[...] = ringo.finish()
    for s in range(nz):
        gzc[s].wait_recv()
        tot = tot + gz[s]
    gsum_row = me * share
    for c in gzc:
        c.wait_send()
    gsum[...] = tot
    first = gsum_row // 128
    off = lax.rem(gsum_row, 128)
    lane = lax.broadcasted_iota(jnp.int32, (8, 128), 1)
    turn = lambda row: pltpu.roll(jnp.broadcast_to(gsum[pl.ds(row, 1), :], (8, 128)), lax.rem(128 - off, 128), 1)
    og[...] = jnp.where(lane < 128 - off, turn(first), turn(first + 1))
    dx, _ = norm_back(red.phase3(), x[...].astype(F32), g_ref[:, :D])
    gtok[...] = gmid[...] + dx
    wait_all(pc)
    for c in gc:
        c.wait_send()


def final(n, dh, x, gmid, gvec, dw1, two, t2, gpart):
    groups = n // GROUP
    nz = groups - 1
    return pl.pallas_call(
        functools.partial(final_kernel, n),
        out_shape=(
            SDS((BLOCK, D), F32),
            SDS(dw1.shape[1:], BF16),
            SDS(t2.shape, BF16),
            SDS(two.shape[1:], F32),
            SDS((8, 128), F32),
        ),
        in_specs=[VM] * 8,
        out_specs=(VM,) * 5,
        scratch_shapes=[
            pltpu.VMEM(dw1.shape[1:], BF16),
            pltpu.VMEM((7, 24, 128), F32),
            pltpu.VMEM((24, 128), F32),
            pltpu.VMEM((nz, 24, 128), F32),
            DMA((2, 7)),
            DMA((2, 7)),
            DMA((7 + nz,)),
            DMA((7 + nz,)),
        ]
        + plane_scratch((BLOCK, D))
        + ring_scratch(n, dw1.shape[1:])
        + ring_scratch(n, two.shape[1:]),
        compiler_params=pltpu.CompilerParams(collective_id=4, has_side_effects=True, vmem_limit_bytes=VMEM_LIMIT),
        name="final",
    )(dh, x, gmid, gvec, dw1, two, t2, gpart)


def unpack_kernel(groups, result, gtok, o1, o2, oo, od, og, result_o, gtok_o, gq, gk, gv, go, gg, gu, gd, gn):
    result_o[...] = result[...]
    gtok_o[...] = gtok[...]
    go[...] = oo[...]
    gd[...] = od[...]
    gn[...] = og[0:1, : gn.shape[1]]
    for b in range(GROUP):
        gq[:, 128 * b : 128 * (b + 1)] = o1[b, :, :128].astype(F32)
    for out, at in ((gk, slice(128, 128 + HEAD)), (gv, slice(128 + HEAD, 256))):
        for c in range(GROUP // 2):
            pair = [o1[2 * c + k, :, at].astype(F32) for k in range(2)]
            out[:, 128 * c : 128 * (c + 1)] = jnp.concatenate(pair, axis=1)
    ffc = gg.shape[1] // (groups * GROUP)
    for k, out in enumerate((gg, gu)):
        parts = [
            o2[b, :, (k * groups + c) * ffc : (k * groups + c + 1) * ffc].astype(F32)
            for c in range(groups)
            for b in range(GROUP)
        ]
        out[...] = jnp.concatenate(parts, axis=1)


def unpack(n, result, gtok, o1, o2, oo, od, og, share):
    r = oo.shape[0]
    return pl.pallas_call(
        functools.partial(unpack_kernel, n // GROUP),
        out_shape=(
            SDS(result.shape, BF16),
            SDS(gtok.shape, F32),
            SDS((r, D), F32),
            SDS((r, D // 2), F32),
            SDS((r, D // 2), F32),
            SDS((r, D), F32),
            SDS((r, FF), F32),
            SDS((r, FF), F32),
            SDS(od.shape, F32),
            SDS((1, share), F32),
        ),
        in_specs=[VM] * 7,
        out_specs=(VM,) * 10,
        compiler_params=pltpu.CompilerParams(vmem_limit_bytes=VMEM_LIMIT),
        name="unpack",
    )(result, gtok, o1, o2, oo, od, og)


def body(n, tokens, w_query, key_weight, w_value, w_out, w_gate, w_up, w_down, norm_gains, seq_lengths, slot_order, out_grad):
    groups = n // GROUP
    r = w_query.shape[0]
    ffc = w_down.shape[0]
    share = norm_gains.shape[0]
    wok = r // 16 if r % 16 == 0 else 1
    wdk = ffc // 16 if ffc % 16 == 0 else 1
    wo_blk, wd_blk = (wok, r // wok, D), (wdk, ffc // wdk, D)
    x_all, w1, w2, wo, wd, gvec, cs = gather_all(
        n,
        seq_lengths,
        tokens,
        w_query,
        key_weight,
        w_value,
        w_gate,
        w_up,
        w_out.reshape(wo_blk),
        w_down.reshape(wd_blk),
        norm_gains.reshape(1, share),
    )
    wqkv = w1.reshape(D, QKV)
    h, raw, q, kv, mix, mixf, lse, dy_all, w2, wo = attn_fwd(
        n, seq_lengths, x_all, wqkv, gvec, cs, out_grad, w2, wo.reshape(groups, r, D)
    )
    res, gmid, dgf, dwo, dmh, po, dwgu, od = ffn_block(
        n, slot_order, mix, tokens, wo.reshape(D, D), gvec, w2.reshape(D, -1), wd.reshape(-1, D), dy_all, wd_blk
    )
    dh1, dwqkv, gpart, result, two, t2 = attn_bwd(
        n,
        seq_lengths,
        dmh,
        q,
        kv,
        lse,
        mixf,
        h,
        raw,
        wqkv,
        gvec,
        cs,
        po,
        res,
        dwo.reshape(groups, GROUP, r, D),
        dwgu.reshape(groups, GROUP, r, -1),
        dgf,
    )
    gtok, o1, o2, oo, og = final(
        n,
        dh1,
        tokens,
        gmid,
        gvec,
        dwqkv.reshape(groups, GROUP, r, QKV),
        two.reshape((groups,) + wo_blk),
        t2,
        gpart,
    )
    outs = unpack(n, result, gtok, o1, o2, oo.reshape(r, D), od.reshape(ffc, D), og, share)
    return outs[:-1] + (outs[-1].reshape(share),)


def solution(mesh):
    n = mesh.shape["dp"]
    row = P("dp", None)
    return jax.shard_map(
        functools.partial(body, n),
        mesh=mesh,
        in_specs=(row,) * 8 + (P("dp"), P(), P(), row),
        out_specs=(row,) * 9 + (P("dp"),),
        check_vma=False,
    )
```

```python
import functools
import math

import jax
import jax.numpy as jnp
from jax import lax
from jax.experimental import pallas as pl
from jax.experimental.pallas import tpu as pltpu
from jax.sharding import PartitionSpec as P

D = 1024
FF = 4608
QUERY_HEADS = 16
KEY_VALUE_HEADS = 8
HEAD = 64
SLOT = 128
GROUP = 8
ROWS = 2048
BLOCK = 256
QKV = 256
WINDOW = 4
VMEM_LIMIT = 62 << 20
EPSILON = 1e-05
ROPE_THETA = 1000000.0
SCALE = 1.0 / math.sqrt(HEAD)
LOG2E = math.log2(math.e)
F32 = jnp.float32
BF16 = jnp.bfloat16
MESH = pl.DeviceIdType.MESH
DMA = pltpu.SemaphoreType.DMA
VM = pl.BlockSpec(memory_space=pltpu.VMEM)
ANY = pl.BlockSpec(memory_space=pl.ANY)
HB = pl.BlockSpec(memory_space=pltpu.HBM)
SM = pl.BlockSpec(memory_space=pltpu.SMEM)
SDS = jax.ShapeDtypeStruct


def nn(a, b):
    return lax.dot_general(a, b, (((1,), (0,)), ((), ())), preferred_element_type=F32)


def nt(a, b):
    return lax.dot_general(a, b, (((1,), (1,)), ((), ())), preferred_element_type=F32)


def tn(a, b):
    return lax.dot_general(a, b, (((0,), (0,)), ((), ())), preferred_element_type=F32)


def rcopy(src, dst, send, recv, dev):
    return pltpu.make_async_remote_copy(
        src_ref=src, dst_ref=dst, send_sem=send, recv_sem=recv, device_id=(dev,), device_id_type=MESH
    )


def barrier(peers):
    sem = pltpu.get_barrier_semaphore()
    for q in peers:
        pl.semaphore_signal(sem, inc=1, device_id=(q,), device_id_type=MESH)
    pl.semaphore_wait(sem, len(peers))


def places(n):
    me = lax.axis_index("dp")
    p = lax.rem(me, GROUP)
    g = me // GROUP
    groups = n // GROUP
    zq = [lax.rem(g + s, groups) * GROUP + p for s in range(1, groups)]
    zg = [lax.rem(g + s, groups) for s in range(1, groups)]
    return me, p, g, groups, zq, zg


def start_all(copies):
    for c in copies:
        c.start()
    return copies


def bring(pairs, sem):
    return start_all([pltpu.make_async_copy(a, b, sem.at[i]) for i, (a, b) in enumerate(pairs)])


def in_hbm(*arrays):
    return [pltpu.with_memory_space_constraint(a, pltpu.HBM) for a in arrays]


def wait_all(copies):
    for c in copies:
        c.wait()


class PlaneGather:
    COPIES = 14

    def __init__(self, me, p, src, dst, ss, rs, ls=None):
        sib, xn, yn = me ^ 1, me ^ 2, me ^ 4

        def cp(a, b, i, dev):
            return rcopy(a, b, ss.at[i], rs.at[i], dev)

        def own(i, dev):
            return [cp(src(h), dst(p, h), i + h, dev) for h in range(2)]

        def on(m, h, i, dev):
            return cp(dst(p ^ m, h), dst(p ^ m, h), i, dev)

        self.x, self.y, self.o = own(0, xn), own(2, yn), own(4, sib)
        self.r = [on(2, 0, 6, yn), on(4, 1, 7, xn)]
        self.fx = [on(2, h, 8 + h, sib) for h in range(2)]
        self.fy = [on(4, h, 10 + h, sib) for h in range(2)]
        self.fd = [on(6, h, 12 + h, sib) for h in range(2)]
        self.local = [] if ls is None else [
            pltpu.make_async_copy(src(h), dst(p, h), ls.at[h]) for h in range(2)
        ]

    def start(self):
        self.start_first()
        self.start_second()

    def start_first(self):
        start_all([self.x[0], self.y[1]] + self.o + self.local)

    def start_second(self):
        start_all([self.x[1], self.y[0]])

    def relay1(self):
        self.x[0].wait_recv()
        start_all([self.r[0], self.fx[0]])
        self.y[1].wait_recv()
        start_all([self.r[1], self.fy[1]])

    def relay2(self):
        self.x[1].wait_recv()
        self.fx[1].start()
        self.y[0].wait_recv()
        self.fy[0].start()

    def relay3(self):
        for h in range(2):
            self.r[h].wait_recv()
            self.fd[h].start()

    def arrive(self, copies):
        for c in copies:
            c.wait_recv()

    def sent(self):
        for c in self.x + self.y + self.r + self.o + self.fx + self.fy + self.fd:
            c.wait_send()
        wait_all(self.local)

    def finish(self):
        self.arrive(self.o + self.fx + self.fy + self.fd)
        self.sent()


class Ring:
    def __init__(self, n, p, g, src, dst, ss, rs, ls=None):
        groups = n // GROUP
        to = lambda s: lax.rem(g + s, groups) * GROUP + p
        at = lambda s: lax.rem(g + s, groups)

        def cp(a, b, i, dev):
            return rcopy(a, b, ss.at[i], rs.at[i], dev)

        self.relays = []
        if groups == 4:
            self.up = [cp(src(h), dst(g, h), h, to(1)) for h in range(2)]
            self.down = [cp(src(h), dst(g, h), 2 + h, to(3)) for h in range(2)]
            self.first = [self.up[0], self.down[1], self.up[1], self.down[0]]
            below, above = at(3), at(1)
            self.relays = [cp(dst(below, 0), dst(below, 0), 4, to(1)), cp(dst(above, 1), dst(above, 1), 5, to(3))]
        else:
            self.first = [cp(src(None), dst(g, None), s - 1, to(s)) for s in range(1, groups)]
        self.local = [] if ls is None else [pltpu.make_async_copy(src(None), dst(g, None), ls)]

    def start(self):
        start_all(self.first + self.local)

    def relay(self):
        if self.relays:
            self.up[0].wait_recv()
            self.relays[0].start()
            self.down[1].wait_recv()
            self.relays[1].start()

    def finish(self):
        if self.relays:
            self.up[1].wait_recv()
            self.down[0].wait_recv()
            for c in self.first:
                c.wait_send()
        else:
            wait_all(self.first)
        wait_all(self.relays + self.local)


def ring_count(n):
    return max(6, n // GROUP - 1)


def halves(length, base=0):
    cut = length // 2
    part = (pl.ds(base, cut), pl.ds(base + cut, length - cut))
    return lambda h: pl.ds(base, length) if h is None else part[h]


class RingReduce:
    def __init__(self, n, p, g, part, low, high, send, fin, ss, rs):
        groups = n // GROUP
        to = lambda s: lax.rem(g + s, groups) * GROUP + p
        at = lambda s: lax.rem(g + s, groups)
        hs = halves(part.shape[1])
        self.part, self.fin, self.send, self.g, self.hs = part, fin, send, g, hs

        def cp(a, b, i, dev):
            return rcopy(a, b, ss.at[i], rs.at[i], dev)

        self.ring = groups == 4
        if self.ring:
            self.above, self.below = at(1), at(3)
            self.low, self.high = low, high
            far = at(2)
            self.a = cp(part.at[far, hs(0)], low, 0, to(1))
            self.b = cp(part.at[far, hs(1)], high, 1, to(3))
            self.c = cp(part.at[self.above, hs(1)], fin.at[0, hs(1)], 2, to(1))
            self.d = cp(part.at[self.below, hs(0)], fin.at[1, hs(0)], 3, to(3))
            self.e = cp(send.at[hs(0)], fin.at[0, hs(0)], 4, to(1))
            self.f = cp(send.at[hs(1)], fin.at[1, hs(1)], 5, to(3))
            self.all = [self.a, self.b, self.c, self.d, self.e, self.f]
        else:
            self.all = [cp(part.at[at(s)], fin.at[s - 1], s - 1, to(s)) for s in range(1, groups)]
        self.count = groups - 1

    def start(self):
        start_all(self.all[:4] if self.ring else self.all)

    def relay(self):
        if self.ring:
            for got, buf, h, b, out in (
                (self.a, self.low, 0, self.above, self.e),
                (self.b, self.high, 1, self.below, self.f),
            ):
                got.wait_recv()
                at = self.hs(h)
                self.send[at] = (self.part[b, at].astype(F32) + buf[...].astype(F32)).astype(BF16)
                out.start()

    def finish(self):
        for c in self.all[2:] if self.ring else self.all:
            c.wait_recv()
        val = self.part[self.g].astype(F32)
        for s in range(2 if self.ring else self.count):
            val = val + self.fin[s].astype(F32)
        for c in self.all:
            c.wait_send()
        return val


def ring_scratch(n, shape):
    cut = shape[0] // 2
    groups = n // GROUP
    count = 2 if groups == 4 else groups - 1
    tail = tuple(shape[1:])
    vm = lambda s: pltpu.VMEM(s, BF16)
    return [
        vm((max(cut, 1),) + tail),
        vm((shape[0] - cut,) + tail),
        vm(tuple(shape)),
        vm((count,) + tuple(shape)),
        DMA((ring_count(n),)),
        DMA((ring_count(n),)),
    ]


class PlaneReduce:
    def __init__(self, me, part, sib, send, relay, fx, fy, ss, rs):
        p = lax.rem(me, GROUP)
        xn, yn = me ^ 2, me ^ 4
        hs = halves(sib.shape[1])
        self.hs, self.p, self.part = hs, p, part
        self.sib, self.send, self.relay, self.fx, self.fy = sib, send, relay, fx, fy

        def cp(a, b, i, dev):
            return rcopy(a, b, ss.at[i], rs.at[i], dev)

        self.first = [cp(part(p ^ (2 * i + 1)), sib.at[i], i, me ^ 1) for i in range(4)]
        self.diag = [cp(send.at[0, hs(0)], relay.at[0], 4, xn), cp(send.at[0, hs(1)], relay.at[1], 5, yn)]
        self.toy = [cp(send.at[2, hs(h)], fy.at[hs(h)], 6 + h, yn) for h in range(2)]
        self.tox = [cp(send.at[1, hs(h)], fx.at[hs(h)], 8 + h, xn) for h in range(2)]

    def start(self):
        start_all([self.first[i] for i in (3, 1, 2, 0)])

    def chip(self, i):
        self.first[i].wait_recv()
        return self.part(self.p ^ (2 * i))[...].astype(F32) + self.sib[i].astype(F32)

    def chip_d(self):
        self.send[0] = self.chip(3).astype(BF16)
        start_all(self.diag)

    def chip_x(self):
        self.send[1] = self.chip(1).astype(BF16)
        self.tox[0].start()

    def chip_y(self):
        self.send[2] = self.chip(2).astype(BF16)
        self.toy[1].start()

    def phase1(self):
        self.chip_d()
        self.chip_x()
        self.chip_y()

    def phase2(self):
        self.diag[0].wait_recv()
        at = self.hs(0)
        self.send[2, at] = (self.send[2, at].astype(F32) + self.relay[0].astype(F32)).astype(BF16)
        self.toy[0].start()
        self.diag[1].wait_recv()
        at = self.hs(1)
        self.send[1, at] = (self.send[1, at].astype(F32) + self.relay[1].astype(F32)).astype(BF16)
        self.tox[1].start()

    def phase3(self):
        own = self.chip(0)
        for c in self.toy + self.tox:
            c.wait_recv()
        own = own + self.fx[...].astype(F32) + self.fy[...].astype(F32)
        for c in self.first + self.diag + self.toy + self.tox:
            c.wait_send()
        return own


def plane_scratch(shape):
    tail = tuple(shape[1:])
    vm = lambda *s: pltpu.VMEM(s + tail, BF16)
    return [
        vm(4, shape[0]),
        vm(3, shape[0]),
        vm(2, shape[0] // 2),
        vm(shape[0]),
        vm(shape[0]),
        DMA((10,)),
        DMA((10,)),
    ]


def gather_kernel(n, len_ref, x_, wq_, wk_, wv_, wg_, wu_, wo_, wd_, gn_, xo, a1o, b1o, b2o, woo, wdo, gvec, ct, st, x, gn, wq, wk, wv, wo, wd, wg, wu, a1, b1, b2, gt, gto, fs, ls, xs, xr, ps, pr, zs, zr):
    me, p, g, groups, zq, zg = places(n)
    fetch = bring(
        (
            (x_, x),
            (gn_, gn),
            (wq_, wq),
            (wk_, wk),
            (wv_, wv),
            (wo_, wo),
            (wd_.at[pl.ds(0, wd.shape[0])], wd),
            (wg_, wg),
            (wu_, wu),
        ),
        fs,
    )
    share = gn.shape[1]
    ffc = wg.shape[1] // (groups * GROUP)
    big = 2 * ffc // 3
    barrier([me ^ m for m in range(1, GROUP)] + zq)
    hx = halves(BLOCK)
    xg = PlaneGather(me, p, lambda h: x.at[hx(h)], lambda b, h: xo.at[b, hx(h)], xs, xr, ls.at[pl.ds(5, 2)])
    fetch[0].wait()
    xg.start_first()

    def ring(k, src, dst, local=None):
        hk = halves(dst.shape[1])
        return Ring(n, p, g, lambda h: src.at[hk(h)], lambda b, h: dst.at[b, hk(h)], zs.at[k], zr.at[k], local)

    rings = [
        ring(0, a1o.at[g], a1o),
        ring(1, gto.at[g], gto),
        ring(2, wd, wdo, ls.at[3]),
        ring(3, wo, woo, ls.at[4]),
    ]
    pc = {}

    def exchange(k, src, dst):
        for m in range(1, GROUP):
            pc[k, m] = rcopy(src(p ^ m), dst, ps.at[k, m - 1], pr.at[k, m - 1], me ^ m)
            pc[k, m].start()

    fetch[1].wait()
    gt[...] = jnp.zeros_like(gt)
    gt[0:1, :share] = gn[...].astype(F32)
    exchange(1, lambda b: gt, gto.at[g, p])
    gto[g, p] = gt[...]
    wait_all(fetch[2:5])
    for b in range(GROUP):
        a1[b, :, :128] = wq[:, 128 * b : 128 * (b + 1)]
        at = slice(HEAD * b, HEAD * (b + 1))
        a1[b, :, 128:] = jnp.concatenate([wk[:, at], wv[:, at]], axis=1)
    exchange(0, lambda b: a1.at[b], a1o.at[g, p])
    wait_all(fetch[5:7])
    rings[3].start()
    rings[2].start()
    wait_all(fetch[7:])
    for buf, low, high in ((b1, 0, big), (b2, big, ffc)):
        for b in range(GROUP):
            at = [slice((GROUP * k + b) * ffc + low, (GROUP * k + b) * ffc + high) for k in range(groups)]
            buf[b] = jnp.concatenate([wg[:, k] for k in at] + [wu[:, k] for k in at], axis=1)
    exchange(2, lambda b: b1.at[b], b1o.at[p])
    exchange(3, lambda b: b2.at[b], b2o.at[p])
    xg.start_second()
    local = [
        pltpu.make_async_copy(a1.at[p], a1o.at[g, p], ls.at[0]),
        pltpu.make_async_copy(b1.at[p], b1o.at[p], ls.at[2]),
        pltpu.make_async_copy(b2.at[p], b2o.at[p], ls.at[1]),
    ]
    start_all(local)
    local[0].wait()
    for k in range(2):
        for m in range(1, GROUP):
            pc[k, m].wait_recv()
        rings[k].start()
    xg.relay1()
    row = lax.broadcasted_iota(jnp.int32, (1, ROWS), 1)
    position = (row - seq_start(row, len_ref, g)).astype(F32)
    index = lax.broadcasted_iota(jnp.int32, (HEAD // 2, 1), 0).astype(F32)
    angles = jnp.exp(index * (-2.0 * math.log(ROPE_THETA) / HEAD)) * position
    c, s = jnp.cos(angles).T, jnp.sin(angles).T
    ct[...] = jnp.concatenate([c, c, c, c], axis=1)
    st[...] = jnp.concatenate([-s, s, -s, s], axis=1)
    xg.relay2()
    for k in (3, 0, 1, 2):
        rings[k].relay()
    xg.relay3()
    for k in (2, 3):
        for m in range(1, GROUP):
            pc[k, m].wait_recv()
    wait_all(local[1:])
    for c in pc.values():
        c.wait_send()
    for k in range(4):
        rings[k].finish()
    gvec[...] = jnp.concatenate(
        [gto[k, b, 0:1, :share] for k in range(groups) for b in range(GROUP)], axis=1
    )
    xg.finish()


def gather_all(n, lengths, x, wq, wk, wv, wg, wu, wo, wd, gn):
    groups = n // GROUP
    r = wq.shape[0]
    wide = 2 * wg.shape[1] // GROUP
    wide1 = 2 * wide // 3
    wd1 = (2 * wd.shape[0] // 3,) + wd.shape[1:]
    return pl.pallas_call(
        functools.partial(gather_kernel, n),
        out_shape=(
            SDS((GROUP, BLOCK, D), BF16),
            SDS((groups, GROUP, r, QKV), BF16),
            SDS((GROUP, r, wide1), BF16),
            SDS((GROUP, r, wide - wide1), BF16),
            SDS((groups,) + wo.shape, BF16),
            SDS((groups,) + wd1, BF16),
            SDS((1, gn.shape[1] * n), F32),
            SDS((ROWS, 128), F32),
            SDS((ROWS, 128), F32),
        ),
        in_specs=[SM] + [HB] * 9,
        out_specs=(HB,) * 6 + (VM, VM, VM),
        scratch_shapes=[
            pltpu.VMEM(w, BF16)
            for w in (x.shape, gn.shape, wq.shape, wk.shape, wv.shape, wo.shape, wd1, wg.shape, wu.shape)
        ]
        + [
            pltpu.VMEM((GROUP, r, QKV), BF16),
            pltpu.VMEM((GROUP, r, wide1), BF16),
            pltpu.VMEM((GROUP, r, wide - wide1), BF16),
            pltpu.VMEM((8, 128), F32),
            pltpu.VMEM((groups, GROUP, 8, 128), F32),
            DMA((9,)),
            DMA((7,)),
            DMA((14,)),
            DMA((14,)),
            DMA((4, 7)),
            DMA((4, 7)),
            DMA((4, ring_count(n))),
            DMA((4, ring_count(n))),
        ],
        compiler_params=pltpu.CompilerParams(collective_id=1, has_side_effects=True, vmem_limit_bytes=VMEM_LIMIT),
        name="gather_all",
    )(lengths, x, wq, wk, wv, wg, wu, wo, wd, gn)


def swap_halves(v):
    lane = lax.broadcasted_iota(jnp.int32, v.shape, 1)
    low = lax.rem(lane, HEAD) < HEAD // 2
    width = v.shape[1]
    return jnp.where(low, pltpu.roll(v, width - HEAD // 2, 1), pltpu.roll(v, HEAD // 2, 1))


def head_mean(v):
    row = lax.broadcasted_iota(jnp.int32, (128, 128), 0)
    lane = lax.broadcasted_iota(jnp.int32, (128, 128), 1)
    same = jnp.where((row < HEAD) == (lane < HEAD), 1.0 / HEAD, 0.0).astype(BF16)
    high = v.astype(BF16)
    low = (v - high.astype(F32)).astype(BF16)
    return nn(high, same) + nn(low, same)


def head_gains(g_ref):
    t = g_ref[:, 2 * D :]
    t = jnp.broadcast_to(t, (8, 128))
    lane = lax.broadcasted_iota(jnp.int32, (8, 128), 1)
    other = pltpu.roll(t, HEAD, 1)
    return jnp.where(lane < HEAD, t, other)[0:1, :], jnp.where(lane < HEAD, other, t)[0:1, :]


def seq_start(row, len_ref, g):
    e1 = len_ref[g, 0]
    e2 = e1 + len_ref[g, 1]
    e3 = e2 + len_ref[g, 2]
    zero = row * 0
    s = jnp.where(row >= e1, zero + e1, zero)
    s = jnp.where(row >= e2, zero + e2, s)
    return jnp.where(row >= e3, zero + e3, s)


def windows(i, window):
    for low, high, count in ((0, 1, 2), (2, 3, 4), (4, 7, WINDOW + 1)):

        @pl.when((i >= low) & (i <= high))
        def _():
            window(jnp.maximum(i - WINDOW, 0), count)


def attn_fwd_kernel(n, len_ref, x_ref, w_ref, g_ref, ct_ref, st_ref, dy_, w2_, wo_, h_ref, raw_ref, q_ref, kv_ref, mixf_ref, lse_ref, mixo, dyo, w2o, woo, k_s, v_s, acc, dy, w2, wo, mixs, fs, ls, ds_, dr, os_, orr, zs, zr, ms, mr):
    i = pl.program_id(0)
    me, p, g, groups, zq, zg = places(n)
    hd, hw, ho = halves(BLOCK), halves(GROUP), halves(wo.shape[0])
    dg = PlaneGather(me, p, lambda h: dy.at[hd(h)], lambda b, h: dyo.at[b, hd(h)], ds_, dr, ls.at[pl.ds(0, 2)])
    og = PlaneGather(me, p, lambda h: wo.at[ho(h)], lambda b, h: woo.at[ho(h), b], os_, orr, ls.at[pl.ds(2, 2)])
    wring = Ring(n, p, g, lambda h: w2.at[hw(h)], lambda b, h: w2o.at[b, hw(h)], zs, zr, ls.at[5])
    fetch = [pltpu.make_async_copy(a, b, fs.at[k]) for k, (a, b) in enumerate(((dy_, dy), (wo_, wo), (w2_, w2)))]

    @pl.when(i == 0)
    def _():
        start_all(fetch)
        k_s[: WINDOW * BLOCK] = jnp.zeros((WINDOW * BLOCK, HEAD), BF16)
        v_s[: WINDOW * BLOCK] = jnp.zeros((WINDOW * BLOCK, 128), BF16)
        barrier([me ^ m for m in range(1, GROUP)] + zq)
        fetch[2].wait()
        wring.start()
        fetch[0].wait()
        dg.start_first()

    @pl.when(i == 2)
    def _():
        dg.start_second()

    @pl.when(i == 3)
    def _():
        dg.relay1()

    @pl.when(i == 4)
    def _():
        fetch[1].wait()
        og.start_first()

    @pl.when(i == 5)
    def _():
        dg.relay2()
        wring.relay()
        og.start_second()

    @pl.when(i == 6)
    def _():
        dg.relay3()
        og.relay1()

    @pl.when(i == 7)
    def _():
        og.relay2()

    xb = x_ref[0].astype(F32)
    r = lax.rsqrt(jnp.mean(xb * xb, axis=-1, keepdims=True) + EPSILON)
    h = (xb * r * g_ref[:, :D]).astype(BF16)
    gq, gk = head_gains(g_ref)
    h_ref[0] = h
    raw = nn(h, w_ref[...])
    raw_ref[0] = raw
    ct, st = ct_ref[...], st_ref[...]
    qraw, kvraw = raw[:, :128], raw[:, 128:]
    qn = qraw * lax.rsqrt(head_mean(qraw * qraw) + EPSILON) * gq
    q = (qn * ct + swap_halves(qn) * st).astype(BF16)
    kn = kvraw * lax.rsqrt(head_mean(kvraw * kvraw) + EPSILON) * gk
    k = (kn * ct + swap_halves(kn) * st).astype(BF16)
    lane = lax.broadcasted_iota(jnp.int32, (BLOCK, 128), 1)
    kv = jnp.where(lane < HEAD, k.astype(F32), kvraw).astype(BF16)
    q_ref[0] = q
    kv_ref[0] = kv
    k_s[pl.ds(i * BLOCK, BLOCK), :] = kv[:, :HEAD]
    v_s[pl.ds(i * BLOCK, BLOCK), :] = jnp.where(lane < HEAD, pltpu.roll(kvraw, HEAD, 1), 1.0).astype(BF16)
    q2 = jnp.concatenate([q[:, :HEAD], q[:, HEAD:]], axis=0)
    row = lax.broadcasted_iota(jnp.int32, (2 * BLOCK, 1), 0)
    qrow = i * BLOCK + jnp.where(row >= BLOCK, row - BLOCK, row)
    qstart = seq_start(qrow, len_ref, g)

    def window(first, count):
        at = pl.ds(pl.multiple_of(first * BLOCK, BLOCK), count * BLOCK)
        kc = lax.broadcasted_iota(jnp.int32, (2 * BLOCK, count * BLOCK), 1) + first * BLOCK
        ok = (kc >= qstart) & (kc <= qrow)
        e = jnp.where(ok, jnp.exp2(nt(q2, k_s[at, :]) * (SCALE * LOG2E)), 0.0).astype(BF16)
        acc[...] = nn(e, v_s[at, :])

    windows(i, window)
    total = acc[:, HEAD:]
    m = acc[:, :HEAD] / total
    both = jnp.concatenate([m[:BLOCK], m[BLOCK:]], axis=1)
    mixf_ref[0] = both
    mixs[i] = both.astype(BF16)

    @pl.when(i == p)
    def _():
        pltpu.make_async_copy(mixs.at[i], mixo.at[p], ls.at[4]).start()

    @pl.when(i != p)
    def _():
        rcopy(mixs.at[i], mixo.at[p], ms.at[p ^ i], mr.at[p ^ i], me ^ p ^ i).start()

    lse_ref[0] = jnp.log2(total.T)[:8, :]

    @pl.when(i == 7)
    def _():
        og.relay3()
        dg.finish()
        wring.finish()
        og.finish()
        for m in range(1, GROUP):
            rcopy(mixs.at[p ^ m], mixo.at[p], ms.at[m], mr.at[m], me ^ m).wait()
        pltpu.make_async_copy(mixs.at[p], mixo.at[p], ls.at[4]).wait()


def attn_fwd(n, lengths, x_all, wqkv, gvec, ct, st, dy, w2, wo):
    groups = n // GROUP
    blk = lambda c: pl.BlockSpec((1, BLOCK, c), lambda i: (i, 0, 0))
    whole = lambda s: pl.BlockSpec(s, lambda i: (0,) * len(s), pipeline_mode=pl.Buffered(1))
    nb = ROWS // BLOCK
    return pl.pallas_call(
        functools.partial(attn_fwd_kernel, n),
        grid=(nb,),
        in_specs=[
            SM,
            blk(D),
            whole((D, QKV)),
            whole(gvec.shape),
            pl.BlockSpec((BLOCK, 128), lambda i: (i, 0)),
            pl.BlockSpec((BLOCK, 128), lambda i: (i, 0)),
            HB,
            HB,
            HB,
        ],
        out_specs=(blk(D), blk(QKV), blk(128), blk(128), blk(128), pl.BlockSpec((1, 8, 2 * BLOCK), lambda i: (i, 0, 0)), HB, HB, HB, HB),
        out_shape=(
            SDS((nb, BLOCK, D), BF16),
            SDS((nb, BLOCK, QKV), F32),
            SDS((nb, BLOCK, 128), BF16),
            SDS((nb, BLOCK, 128), BF16),
            SDS((nb, BLOCK, 128), F32),
            SDS((nb, 8, 2 * BLOCK), F32),
            SDS((GROUP, BLOCK, 128), BF16),
            SDS((GROUP, BLOCK, D), BF16),
            SDS((groups,) + w2.shape, BF16),
            SDS((groups, GROUP) + wo.shape[1:], BF16),
        ),
        scratch_shapes=[
            pltpu.VMEM((ROWS, HEAD), BF16),
            pltpu.VMEM((ROWS, 128), BF16),
            pltpu.VMEM((2 * BLOCK, 128), F32),
            pltpu.VMEM(dy.shape, BF16),
            pltpu.VMEM(w2.shape, BF16),
            pltpu.VMEM(wo.shape, BF16),
            pltpu.VMEM((GROUP, BLOCK, 128), BF16),
            DMA((3,)),
            DMA((6,)),
            DMA((14,)),
            DMA((14,)),
            DMA((14,)),
            DMA((14,)),
            DMA((ring_count(n),)),
            DMA((ring_count(n),)),
            DMA((GROUP,)),
            DMA((GROUP,)),
        ],
        compiler_params=pltpu.CompilerParams(
            collective_id=5, has_side_effects=True, dimension_semantics=("arbitrary",), vmem_limit_bytes=VMEM_LIMIT
        ),
        cost_estimate=pl.CostEstimate(flops=4 * 10**9, bytes_accessed=16 << 20, transcendentals=4 * 10**6),
        name="attn_fwd",
    )(lengths, *in_hbm(x_all, wqkv, gvec, ct, st), dy, w2, wo)


def norm_back(dyv, xv, gain):
    r = lax.rsqrt(jnp.mean(xv * xv, axis=-1, keepdims=True) + EPSILON)
    xr = xv * r
    gy = dyv * gain
    dx = r * (gy - xr * jnp.mean(gy * xr, axis=-1, keepdims=True))
    return dx, jnp.sum(dyv * xr, axis=0, keepdims=True)


def unit_grads(h, dyb, wgu, wd):
    f = wd.shape[0]
    gu = nn(h, wgu)
    da = nt(dyb, wd)
    gp, up = gu[:, :f], gu[:, f:]
    sig = 1.0 / (1.0 + jnp.exp(-gp))
    sg = gp * sig
    dg = (da * up * (sig * (1.0 + gp * (1.0 - sig)))).astype(BF16)
    return (sg * up).astype(BF16), jnp.concatenate([dg, (da * sg).astype(BF16)], axis=1)


def ffn_block_kernel(n, order, mix_, x_, wo_, g_ref, w21_, w22_, wd1_, wd2_, dy_, res, gmid, dgf, dwo, dmh, po, t21, dw22, dwd, x, wo, w21, dy, fs, mbuf, h2, h2t, w2v, w22, wdv, wds, dys, acts, dgu1, dgu2, dw21, part, mown, stage, hs, hr, os_, qs, qr, zs, zr, *red_refs):
    me, p, g, groups, zq, zg = places(n)
    f1 = wd1_.shape[0]
    f2 = wds.shape[0] - f1
    fetch = bring(
        (
            (wd2_.at[pl.ds(wd2_.shape[0] - wdv.shape[1], wdv.shape[1])], wdv.at[g]),
            (w22_, w2v.at[g]),
            (mix_, mbuf),
            (x_, x),
            (wo_, wo),
            (w21_, w21),
            (wd1_, wds.at[pl.ds(0, f1)]),
            (dy_, dy),
        ),
        fs,
    )
    barrier([me ^ m for m in range(1, GROUP)] + zq)
    gf = g_ref.at[:, D : 2 * D]
    r = w2v.shape[2]

    def holder(q):
        s = 0
        for k in range(ROWS // SLOT):
            s = jnp.where(order[g, k] == q, k, s)
        return s

    hw, h8 = halves(wdv.shape[1]), halves(GROUP)
    wrings = [
        Ring(n, p, g, lambda h: w2v.at[g, h8(h)], lambda b, h: w2v.at[b, h8(h)], zs.at[0], zr.at[0]),
        Ring(n, p, g, lambda h: wdv.at[g, hw(h)], lambda b, h: wdv.at[b, hw(h)], zs.at[1], zr.at[1]),
    ]
    wait_all(fetch[:2])
    for c in wrings:
        c.start()
    wait_all(fetch[2:5])
    m = jnp.concatenate([mbuf[b] for b in range(GROUP)], axis=1)
    mown[...] = m
    z = x[...].astype(F32) + nn(m, wo[...])
    res[...] = z
    h2[p] = (z * lax.rsqrt(jnp.mean(z * z, axis=-1, keepdims=True) + EPSILON) * gf[...]).astype(BF16)
    hb = halves(BLOCK)
    hg = PlaneGather(me, p, lambda h: h2.at[p, hb(h)], lambda b, h: h2.at[b, hb(h)], hs, hr)
    red = PlaneReduce(me, lambda b: part.at[b], *red_refs[:7])
    ring21 = RingReduce(n, p, g, dw21, *red_refs[7:])
    hg.start_first()
    wait_all(fetch[5:])

    def first(t, carry):
        @pl.when(t == 1)
        def _():
            hg.start_second()
            hg.arrive(hg.o)

        @pl.when(t == 2)
        def _():
            hg.relay1()
            hg.relay2()

        @pl.when(t == 3)
        def _():
            hg.arrive(hg.fx)

        @pl.when(t == 4)
        def _():
            for c in wrings:
                c.relay()

        @pl.when(t == 5)
        def _():
            hg.arrive(hg.fy)

        @pl.when(t == 6)
        def _():
            hg.relay3()

        @pl.when(t == 7)
        def _():
            hg.arrive(hg.fd)

        b = p ^ t
        dys[b] = jnp.concatenate([dy[holder(2 * b)], dy[holder(2 * b + 1)]], axis=0)
        h2t[:, pl.ds(pl.multiple_of(b * BLOCK, BLOCK), BLOCK)] = h2[b].T
        acts[b, :, :f1], dgu1[b] = unit_grads(h2[b], dys[b], w21[...], wds[:f1])
        return carry

    lax.fori_loop(0, GROUP, first, 0)
    grad1 = nn(h2t[...], dgu1[...].reshape(ROWS, 2 * f1)).astype(BF16)
    for k in range(groups * GROUP):
        dw21[k // GROUP, k % GROUP] = grad1[k * r : (k + 1) * r]
    ring21.start()
    for c in wrings:
        c.finish()
    for k in range(groups * GROUP):
        w22[k * r : (k + 1) * r] = w2v[k // GROUP, k % GROUP]
    each = f2 // groups
    for k in range(groups):
        wds[f1 + k * each : f1 + (k + 1) * each] = wdv[k].reshape(each, D)

    def second(t, carry):
        @pl.when(t == 1)
        def _():
            red.first[3].start()

        @pl.when(t == 3)
        def _():
            red.first[2].start()
            red.chip_d()

        @pl.when(t == 5)
        def _():
            red.first[1].start()
            red.chip_y()

        @pl.when(t == 7)
        def _():
            red.first[0].start()
            red.chip_x()

        b = p ^ (GROUP - 1 - t)
        acts[b, :, f1:], dgu2[b] = unit_grads(h2[b], dys[b], w22[...], wds[f1:])
        part[b] = (nt(dgu1[b], w21[...]) + nt(dgu2[b], w22[...])).astype(BF16)
        return carry

    lax.fori_loop(0, GROUP, second, 0)
    dw = tn(acts[...].reshape(ROWS, f1 + f2), dys[...].reshape(ROWS, D)).astype(BF16)
    l1 = dwd.shape[1] - wdv.shape[1]
    e1 = f1 // groups
    for k in range(groups):
        dwd[k, :l1] = dw[k * e1 : (k + 1) * e1].reshape((l1,) + dwd.shape[2:])
        dwd[k, l1:] = dw[f1 + k * each : f1 + (k + 1) * each].reshape(wdv.shape[1:])
    red.phase2()
    ring21.relay()
    dw22[...] = nn(h2t[...], dgu2[...].reshape(ROWS, 2 * f2)).astype(BF16)
    dx, dgain = norm_back(red.phase3(), res[...], gf[...])
    gm = dys[p].astype(F32) + dx
    gmid[...] = gm
    dgf[...] = dgain
    gl = gm.astype(BF16)
    dm = nt(gl, wo[...]).astype(BF16)
    for b in range(GROUP):
        mbuf[b] = dm[:, 128 * b : 128 * (b + 1)]
    qc = start_all(
        [rcopy(mbuf.at[p ^ m], dmh.at[p], qs.at[m - 1], qr.at[m - 1], me ^ m) for m in range(1, GROUP)]
    )
    dmh[p] = mbuf[p]
    dwo[...] = tn(mown[...], gl).astype(BF16)

    def out(b, carry):
        slot = lax.rem(b, 2)

        @pl.when(b > 1)
        def _():
            pltpu.make_async_copy(stage.at[slot], po.at[b - 2], os_.at[slot]).wait()

        stage[slot] = nn(acts[b], wds[...]).astype(BF16)
        pltpu.make_async_copy(stage.at[slot], po.at[b], os_.at[slot]).start()
        return carry

    lax.fori_loop(0, GROUP, out, 0)
    for b in range(GROUP - 2, GROUP):
        pltpu.make_async_copy(stage.at[b % 2], po.at[b], os_.at[b % 2]).wait()
    wait_all(qc)
    hg.sent()
    t21[...] = ring21.finish().astype(BF16)


def ffn_block(n, order, mix, x, wo, gvec, w21, w22, wd1, wd, dy):
    groups = n // GROUP
    r = w22.shape[1]
    f1, f2 = w21.shape[1] // 2, w22.shape[2] // 2
    wd2 = (wd.shape[0] // 3,) + wd.shape[1:]
    blk = (GROUP, r, 2 * f1)
    vm = lambda *s: pltpu.VMEM(s, BF16)
    return pl.pallas_call(
        functools.partial(ffn_block_kernel, n),
        out_shape=(
            SDS((BLOCK, D), F32),
            SDS((BLOCK, D), F32),
            SDS((1, D), F32),
            SDS((D, D), BF16),
            SDS((GROUP, BLOCK, 128), BF16),
            SDS((GROUP, BLOCK, D), BF16),
            SDS(blk, BF16),
            SDS((D, 2 * f2), BF16),
            SDS((groups,) + wd.shape, BF16),
        ),
        in_specs=[SM, HB, HB, HB, VM, HB, HB, HB, HB, HB],
        out_specs=(VM, VM, VM, VM, VM, HB, VM, VM, VM),
        scratch_shapes=[
            vm(BLOCK, D),
            vm(D, D),
            vm(D, 2 * f1),
            vm(ROWS // SLOT, SLOT, D),
            DMA((8,)),
            vm(GROUP, BLOCK, 128),
            vm(GROUP, BLOCK, D),
            vm(D, ROWS),
            vm(groups, *w22.shape),
            vm(D, 2 * f2),
            vm(groups, *wd2),
            vm(f1 + f2, D),
            vm(GROUP, BLOCK, D),
            vm(GROUP, BLOCK, f1 + f2),
            vm(GROUP, BLOCK, 2 * f1),
            vm(GROUP, BLOCK, 2 * f2),
            vm(groups, *blk),
            vm(GROUP, BLOCK, D),
            vm(BLOCK, D),
            vm(2, BLOCK, D),
            DMA((14,)),
            DMA((14,)),
            DMA((2,)),
            DMA((7,)),
            DMA((7,)),
            DMA((2, ring_count(n))),
            DMA((2, ring_count(n))),
        ]
        + plane_scratch((BLOCK, D))
        + ring_scratch(n, blk),
        compiler_params=pltpu.CompilerParams(collective_id=2, has_side_effects=True, vmem_limit_bytes=VMEM_LIMIT),
        name="ffn_block",
    )(order, mix, x, wo, gvec, w21, w22, wd1, wd, dy.reshape(ROWS // SLOT, SLOT, D))


def attn_bwd_kernel(n, len_ref, dm_ref, q_ref, kvall_ref, lse_ref, mixf_ref, h_ref, raw_ref, w_ref, g_ref, ct_ref, st_ref, po_, res_, dwo_, dw2_, dwd_, t21_, dgf, dh_ref, dw_ref, gpart, result, two, t2, od, o21, k_s, v_s, dkv, dqt, dws, dg_ref, es, er, po, res, dwo, dw2, dwd, t21, fs, *rest):
    step_id = pl.program_id(0)
    nb = ROWS // BLOCK
    i = nb - 1 - step_id
    me, p, g, groups, zq, zg = places(n)
    ored = PlaneReduce(me, lambda b: po.at[b], *rest[:7])
    wred = PlaneReduce(me, lambda b: dwo.at[:, b], *rest[7:14])
    ring2 = RingReduce(n, p, g, dw2, *rest[14:20])
    ringd = RingReduce(n, p, g, dwd, *rest[20:26])
    fetch = [
        pltpu.make_async_copy(a, b, fs.at[k])
        for k, (a, b) in enumerate(
            ((dwd_, dwd), (dw2_, dw2), (po_, po), (dwo_, dwo), (t21_, t21), (res_, res))
        )
    ]
    ex = [rcopy(t21.at[p ^ m], o21.at[p], es.at[m - 1], er.at[m - 1], me ^ m) for m in range(1, GROUP)]
    own_copy = pltpu.make_async_copy(t21.at[p], o21.at[p], fs.at[6])

    @pl.when(step_id == 0)
    def _():
        start_all(fetch)
        barrier([me ^ m for m in range(1, GROUP)] + zq)

    @pl.when(step_id == 1)
    def _():
        ored.phase1()
        wred.phase1()

    @pl.when(step_id == 3)
    def _():
        ringd.relay()
        ring2.relay()
        ored.phase2()

    @pl.when(step_id == 4)
    def _():
        wred.phase2()


    @pl.when(step_id == 0)
    def _():
        dkv[...] = jnp.zeros_like(dkv)
        dws[...] = jnp.zeros_like(dws)
        dg_ref[...] = jnp.zeros_like(dg_ref)
        for b in range(ROWS // BLOCK):
            kvb = kvall_ref[b]
            k_s[pl.ds(b * BLOCK, BLOCK), :] = kvb[:, :HEAD]
            v_s[pl.ds(b * BLOCK, BLOCK), :] = kvb[:, HEAD:]

    q, do, mf = q_ref[0], dm_ref[0], mixf_ref[0]
    q2 = jnp.concatenate([q[:, :HEAD], q[:, HEAD:]], axis=0)
    do2 = jnp.concatenate([do[:, :HEAD], do[:, HEAD:]], axis=0)
    prod = (do.astype(F32) * mf).T
    delta = jnp.concatenate(
        [jnp.sum(prod[:HEAD], axis=0, keepdims=True), jnp.sum(prod[HEAD:], axis=0, keepdims=True)], axis=1
    )
    lse = lse_ref[0, 0:1, :]
    colq = lax.broadcasted_iota(jnp.int32, (1, 2 * BLOCK), 1)
    qrow = i * BLOCK + jnp.where(colq >= BLOCK, colq - BLOCK, colq)
    qstart = seq_start(qrow, len_ref, g)

    def window(first, count):
        at = pl.ds(pl.multiple_of(first * BLOCK, BLOCK), count * BLOCK)
        kb, vb = k_s[at, :], v_s[at, :]
        kc = lax.broadcasted_iota(jnp.int32, (count * BLOCK, 2 * BLOCK), 0) + first * BLOCK
        ok = (kc >= qstart) & (kc <= qrow)
        pr = jnp.where(ok, jnp.exp2(nt(kb, q2) * (SCALE * LOG2E) - lse), 0.0)
        dsc = (pr * (nt(vb, do2) - delta)).astype(BF16)
        dkv[at, :HEAD] += nn(dsc, q2)
        dkv[at, HEAD:] += nn(pr.astype(BF16), do2)
        dqt[...] = tn(dsc, kb)

    windows(i, window)
    ct, st = ct_ref[...], st_ref[...]
    raw = raw_ref[0]
    dq = jnp.concatenate([dqt[:BLOCK], dqt[BLOCK:]], axis=1) * SCALE
    dkvb = dkv[pl.ds(pl.multiple_of(i * BLOCK, BLOCK), BLOCK), :]
    lane = lax.broadcasted_iota(jnp.int32, (BLOCK, 128), 1)

    def pull(d, v, gain):
        dn = d * ct - swap_halves(d) * st
        r = lax.rsqrt(head_mean(v * v) + EPSILON)
        vr = v * r
        gy = dn * gain
        return r * (gy - vr * head_mean(gy * vr)), jnp.sum(dn * vr, axis=0, keepdims=True)

    gq, gk = head_gains(g_ref)
    dqr, dgq = pull(dq, raw[:, :128], gq)
    dkr, dgk = pull(dkvb * SCALE, raw[:, 128:], gk)
    dg_ref[0:1, :] += dgq
    dg_ref[1:2, :] += dgk
    dqkv = jnp.concatenate([dqr, jnp.where(lane < HEAD, dkr, dkvb)], axis=1).astype(BF16)
    dh_ref[0] = nt(dqkv, w_ref[...]).astype(BF16)
    dws[...] += tn(h_ref[0], dqkv)

    @pl.when(step_id == 0)
    def _():
        wait_all(fetch)
        ringd.start()
        ring2.start()
        ored.start()
        wred.start()
        start_all(ex + [own_copy])

    @pl.when(step_id == nb - 1)
    def _():
        dw_ref[...] = dws[...].astype(BF16)
        result[...] = (ored.phase3() + res[...]).astype(BF16)
        two[...] = wred.phase3().astype(BF16)
        t2[...] = ring2.finish().astype(BF16)
        od[...] = ringd.finish()
        wait_all(ex + [own_copy])
        dga = lax.dot_general(
            jnp.ones((8, QKV), F32),
            w_ref[...].astype(F32) * dws[...],
            (((1,), (1,)), ((), ())),
            precision=lax.Precision.HIGHEST,
            preferred_element_type=F32,
        )
        dga = dga[0:1, :] / g_ref[:, :D]
        gpart[...] = jnp.zeros_like(gpart)
        for b in range(8):
            gpart[b : b + 1, :] = dga[:, 128 * b : 128 * (b + 1)]
            gpart[8 + b : 9 + b, :] = dgf[:, 128 * b : 128 * (b + 1)]
        turned = pltpu.roll(dg_ref[...], HEAD, 1)
        low = lax.broadcasted_iota(jnp.int32, (1, 128), 1) < HEAD
        gpart[16:17, :] = jnp.where(low, dg_ref[0:1, :] + turned[0:1, :], turned[1:2, :])


def attn_bwd(n, lengths, dmh, q, kv, lse, mixf, h, raw, wqkv, gvec, ct, st, po, res, dwo, dw2, dwd, t21, dgf):
    nb = ROWS // BLOCK
    groups = n // GROUP
    blk = lambda c: pl.BlockSpec((1, BLOCK, c), lambda i: (nb - 1 - i, 0, 0))
    whole = lambda s: pl.BlockSpec(s, lambda i: (0,) * len(s), pipeline_mode=pl.Buffered(1))
    return pl.pallas_call(
        functools.partial(attn_bwd_kernel, n),
        grid=(nb,),
        in_specs=[
            SM,
            blk(128),
            blk(128),
            whole((nb, BLOCK, 128)),
            pl.BlockSpec((1, 8, 2 * BLOCK), lambda i: (nb - 1 - i, 0, 0)),
            blk(128),
            blk(D),
            blk(QKV),
            whole((D, QKV)),
            whole(gvec.shape),
            pl.BlockSpec((BLOCK, 128), lambda i: (nb - 1 - i, 0)),
            pl.BlockSpec((BLOCK, 128), lambda i: (nb - 1 - i, 0)),
            HB,
            HB,
            HB,
            HB,
            HB,
            HB,
            whole(dgf.shape),
        ],
        out_specs=(
            blk(D),
            whole((D, QKV)),
            whole((24, 128)),
            whole((BLOCK, D)),
            whole((groups,) + dwo.shape[2:]),
            whole(dw2.shape[1:]),
            whole(dwd.shape[1:]),
            HB,
        ),
        out_shape=(
            SDS((nb, BLOCK, D), BF16),
            SDS((D, QKV), BF16),
            SDS((24, 128), F32),
            SDS((BLOCK, D), BF16),
            SDS((groups,) + dwo.shape[2:], BF16),
            SDS(dw2.shape[1:], BF16),
            SDS(dwd.shape[1:], F32),
            SDS(t21.shape, BF16),
        ),
        scratch_shapes=[
            pltpu.VMEM((ROWS, HEAD), BF16),
            pltpu.VMEM((ROWS, HEAD), BF16),
            pltpu.VMEM((ROWS, 128), F32),
            pltpu.VMEM((2 * BLOCK, HEAD), F32),
            pltpu.VMEM((D, QKV), F32),
            pltpu.VMEM((8, 128), F32),
            DMA((7,)),
            DMA((7,)),
        ]
        + [pltpu.VMEM(a.shape, a.dtype) for a in (po, res, dwo, dw2, dwd, t21)]
        + [DMA((7,))]
        + plane_scratch((BLOCK, D))
        + plane_scratch((groups,) + dwo.shape[2:])
        + ring_scratch(n, dw2.shape[1:])
        + ring_scratch(n, dwd.shape[1:]),
        compiler_params=pltpu.CompilerParams(
            collective_id=6, has_side_effects=True, dimension_semantics=("arbitrary",), vmem_limit_bytes=VMEM_LIMIT
        ),
        cost_estimate=pl.CostEstimate(flops=8 * 10**9, bytes_accessed=16 << 20, transcendentals=4 * 10**6),
        name="attn_bwd",
    )(lengths, dmh, q, kv, lse, mixf, h, raw, wqkv, gvec, ct, st, po, res, dwo, dw2, dwd, t21, dgf)


def final_kernel(n, dh, x, gmid, g_ref, dw1, two, t2, gpart, gtok, o1, o2, oo, og, t1, gin, gsum, gz, ps, pr, gs, gr, *rest):
    me, p, g, groups, zq, zg = places(n)
    nz = groups - 1
    share = g_ref.shape[1] // n
    barrier([me ^ m for m in range(1, GROUP)] + zq)
    red = PlaneReduce(me, lambda b: dh.at[b], *rest[:7])
    ring1 = RingReduce(n, p, g, dw1, *rest[7:13])
    ringo = RingReduce(n, p, g, two, *rest[13:19])
    red.start()
    gc = start_all([rcopy(gpart, gin.at[m - 1], gs.at[m - 1], gr.at[m - 1], me ^ m) for m in range(1, GROUP)])
    ring1.start()
    ringo.start()
    pc = []

    def exchange(k, src, out):
        for m in range(1, GROUP):
            c = rcopy(src.at[p ^ m], out.at[p], ps.at[k, m - 1], pr.at[k, m - 1], me ^ m)
            c.start()
            pc.append(c)
        out[p] = src[p]

    red.phase1()
    exchange(1, t2, o2)
    tot = gpart[...]
    for m in range(1, GROUP):
        gc[m - 1].wait_recv()
        tot = tot + gin[m - 1]
    gsum[...] = tot
    gzc = start_all([rcopy(gsum, gz.at[s], gs.at[7 + s], gr.at[7 + s], zq[s]) for s in range(nz)])
    ring1.relay()
    ringo.relay()
    red.phase2()
    t1[...] = ring1.finish().astype(BF16)
    exchange(0, t1, o1)
    oo[...] = ringo.finish()
    for s in range(nz):
        gzc[s].wait_recv()
        tot = tot + gz[s]
    gsum_row = me * share
    for c in gzc:
        c.wait_send()
    gsum[...] = tot
    first = gsum_row // 128
    off = lax.rem(gsum_row, 128)
    lane = lax.broadcasted_iota(jnp.int32, (8, 128), 1)
    turn = lambda row: pltpu.roll(jnp.broadcast_to(gsum[pl.ds(row, 1), :], (8, 128)), lax.rem(128 - off, 128), 1)
    og[...] = jnp.where(lane < 128 - off, turn(first), turn(first + 1))
    dx, _ = norm_back(red.phase3(), x[...].astype(F32), g_ref[:, :D])
    gtok[...] = gmid[...] + dx
    wait_all(pc)
    for c in gc:
        c.wait_send()


def final(n, dh, x, gmid, gvec, dw1, two, t2, gpart):
    groups = n // GROUP
    nz = groups - 1
    return pl.pallas_call(
        functools.partial(final_kernel, n),
        out_shape=(
            SDS((BLOCK, D), F32),
            SDS(dw1.shape[1:], BF16),
            SDS(t2.shape, BF16),
            SDS(two.shape[1:], F32),
            SDS((8, 128), F32),
        ),
        in_specs=[VM] * 8,
        out_specs=(VM,) * 5,
        scratch_shapes=[
            pltpu.VMEM(dw1.shape[1:], BF16),
            pltpu.VMEM((7, 24, 128), F32),
            pltpu.VMEM((24, 128), F32),
            pltpu.VMEM((nz, 24, 128), F32),
            DMA((2, 7)),
            DMA((2, 7)),
            DMA((7 + nz,)),
            DMA((7 + nz,)),
        ]
        + plane_scratch((BLOCK, D))
        + ring_scratch(n, dw1.shape[1:])
        + ring_scratch(n, two.shape[1:]),
        compiler_params=pltpu.CompilerParams(collective_id=4, has_side_effects=True, vmem_limit_bytes=VMEM_LIMIT),
        name="final",
    )(dh, x, gmid, gvec, dw1, two, t2, gpart)


def unpack_kernel(groups, result, gtok, o1, o21, o22, oo, od, og, result_o, gtok_o, gq, gk, gv, go, gg, gu, gd, gn):
    result_o[...] = result[...]
    gtok_o[...] = gtok[...]
    go[...] = oo[...]
    gd[...] = od[...]
    gn[...] = og[0:1, : gn.shape[1]]
    for b in range(GROUP):
        gq[:, 128 * b : 128 * (b + 1)] = o1[b, :, :128].astype(F32)
    for out, at in ((gk, slice(128, 128 + HEAD)), (gv, slice(128 + HEAD, 256))):
        for c in range(GROUP // 2):
            pair = [o1[2 * c + k, :, at].astype(F32) for k in range(2)]
            out[:, 128 * c : 128 * (c + 1)] = jnp.concatenate(pair, axis=1)
    ffc = gg.shape[1] // (groups * GROUP)
    for k, out in enumerate((gg, gu)):
        big = 2 * ffc // 3
        piece = lambda src, b, c, w: src[b, :, (k * groups + c) * w : (k * groups + c + 1) * w].astype(F32)
        parts = [
            piece(src, b, c, w)
            for c in range(groups)
            for b in range(GROUP)
            for src, w in ((o21, big), (o22, ffc - big))
        ]
        out[...] = jnp.concatenate(parts, axis=1)


def unpack(n, result, gtok, o1, o21, o22, oo, od, og, share):
    r = oo.shape[0]
    return pl.pallas_call(
        functools.partial(unpack_kernel, n // GROUP),
        out_shape=(
            SDS(result.shape, BF16),
            SDS(gtok.shape, F32),
            SDS((r, D), F32),
            SDS((r, D // 2), F32),
            SDS((r, D // 2), F32),
            SDS((r, D), F32),
            SDS((r, FF), F32),
            SDS((r, FF), F32),
            SDS(od.shape, F32),
            SDS((1, share), F32),
        ),
        in_specs=[VM] * 8,
        out_specs=(VM,) * 10,
        compiler_params=pltpu.CompilerParams(vmem_limit_bytes=VMEM_LIMIT),
        name="unpack",
    )(result, gtok, o1, o21, o22, oo, od, og)


def body(n, tokens, w_query, key_weight, w_value, w_out, w_gate, w_up, w_down, norm_gains, seq_lengths, slot_order, out_grad):
    groups = n // GROUP
    r = w_query.shape[0]
    ffc = w_down.shape[0]
    share = norm_gains.shape[0]
    wok = r // 16 if r % 16 == 0 else 1
    wdk = 9 if ffc % 144 == 0 else 3
    wo_blk, wd_blk = (wok, r // wok, D), (wdk, ffc // wdk, D)
    x_all, w1, w21, w22, wo, wd1, gvec, ct, st = gather_all(
        n,
        seq_lengths,
        tokens,
        w_query,
        key_weight,
        w_value,
        w_gate,
        w_up,
        w_out.reshape(wo_blk),
        w_down.reshape(wd_blk),
        norm_gains.reshape(1, share),
    )
    wqkv = w1.reshape(D, QKV)
    h, raw, q, kv, mixf, lse, mix, dy_all, w21, wo = attn_fwd(
        n, seq_lengths, x_all, wqkv, gvec, ct, st, out_grad, w21, wo.reshape(groups, r, D)
    )
    res, gmid, dgf, dwo, dmh, po, t21, dw22, dwd = ffn_block(
        n,
        slot_order,
        mix,
        tokens,
        wo.reshape(D, D),
        gvec,
        w21.reshape(D, -1),
        w22,
        wd1.reshape(-1, D),
        w_down.reshape(wd_blk),
        dy_all,
    )
    dh1, dwqkv, gpart, result, two, t2, od, o21 = attn_bwd(
        n,
        seq_lengths,
        dmh,
        q,
        kv,
        lse,
        mixf,
        h,
        raw,
        wqkv,
        gvec,
        ct,
        st,
        po,
        res,
        dwo.reshape(groups, GROUP, r, D),
        dw22.reshape(groups, GROUP, r, -1),
        dwd,
        t21,
        dgf,
    )
    gtok, o1, o22, oo, og = final(
        n,
        dh1,
        tokens,
        gmid,
        gvec,
        dwqkv.reshape(groups, GROUP, r, QKV),
        two.reshape((groups,) + wo_blk),
        t2,
        gpart,
    )
    outs = unpack(n, result, gtok, o1, o21, o22, oo.reshape(r, D), od.reshape(ffc, D), og, share)
    return outs[:-1] + (outs[-1].reshape(share),)


def solution(mesh):
    n = mesh.shape["dp"]
    row = P("dp", None)
    return jax.shard_map(
        functools.partial(body, n),
        mesh=mesh,
        in_specs=(row,) * 8 + (P("dp"), P(), P(), row),
        out_specs=(row,) * 9 + (P("dp"),),
        check_vma=False,
    )
```

```python
import functools
import math

import jax
import jax.numpy as jnp
from jax import lax
from jax.experimental import pallas as pl
from jax.experimental.pallas import tpu as pltpu
from jax.sharding import PartitionSpec as P

D = 1024
FF = 4608
QUERY_HEADS = 16
KEY_VALUE_HEADS = 8
HEAD = 64
SLOT = 128
GROUP = 8
ROWS = 2048
BLOCK = 256
QKV = 256
WINDOW = 4
VMEM_LIMIT = 62 << 20
EPSILON = 1e-05
ROPE_THETA = 1000000.0
SCALE = 1.0 / math.sqrt(HEAD)
LOG2E = math.log2(math.e)
F32 = jnp.float32
BF16 = jnp.bfloat16
MESH = pl.DeviceIdType.MESH
DMA = pltpu.SemaphoreType.DMA
VM = pl.BlockSpec(memory_space=pltpu.VMEM)
ANY = pl.BlockSpec(memory_space=pl.ANY)
HB = pl.BlockSpec(memory_space=pltpu.HBM)
SM = pl.BlockSpec(memory_space=pltpu.SMEM)
SDS = jax.ShapeDtypeStruct


def nn(a, b):
    return lax.dot_general(a, b, (((1,), (0,)), ((), ())), preferred_element_type=F32)


def nt(a, b):
    return lax.dot_general(a, b, (((1,), (1,)), ((), ())), preferred_element_type=F32)


def tn(a, b):
    return lax.dot_general(a, b, (((0,), (0,)), ((), ())), preferred_element_type=F32)


def rcopy(src, dst, send, recv, dev):
    return pltpu.make_async_remote_copy(
        src_ref=src, dst_ref=dst, send_sem=send, recv_sem=recv, device_id=(dev,), device_id_type=MESH
    )


def barrier(peers):
    sem = pltpu.get_barrier_semaphore()
    for q in peers:
        pl.semaphore_signal(sem, inc=1, device_id=(q,), device_id_type=MESH)
    pl.semaphore_wait(sem, len(peers))


def places(n):
    me = lax.axis_index("dp")
    p = lax.rem(me, GROUP)
    g = me // GROUP
    groups = n // GROUP
    zq = [lax.rem(g + s, groups) * GROUP + p for s in range(1, groups)]
    zg = [lax.rem(g + s, groups) for s in range(1, groups)]
    return me, p, g, groups, zq, zg


def start_all(copies):
    for c in copies:
        c.start()
    return copies


def bring(pairs, sem):
    return start_all([pltpu.make_async_copy(a, b, sem.at[i]) for i, (a, b) in enumerate(pairs)])


def wait_all(copies):
    for c in copies:
        c.wait()


class PlaneGather:
    COPIES = 14

    def __init__(self, me, p, src, dst, ss, rs, ls=None):
        sib, xn, yn = me ^ 1, me ^ 2, me ^ 4

        def cp(a, b, i, dev):
            return rcopy(a, b, ss.at[i], rs.at[i], dev)

        def own(i, dev):
            return [cp(src(h), dst(p, h), i + h, dev) for h in range(2)]

        def on(m, h, i, dev):
            return cp(dst(p ^ m, h), dst(p ^ m, h), i, dev)

        self.x, self.y, self.o = own(0, xn), own(2, yn), own(4, sib)
        self.r = [on(2, 0, 6, yn), on(4, 1, 7, xn)]
        self.fx = [on(2, h, 8 + h, sib) for h in range(2)]
        self.fy = [on(4, h, 10 + h, sib) for h in range(2)]
        self.fd = [on(6, h, 12 + h, sib) for h in range(2)]
        self.local = [] if ls is None else [
            pltpu.make_async_copy(src(h), dst(p, h), ls.at[h]) for h in range(2)
        ]

    def start(self):
        self.start_first()
        self.start_second()

    def start_first(self):
        start_all([self.x[0], self.y[1]] + self.o + self.local)

    def start_second(self):
        start_all([self.x[1], self.y[0]])

    def relay1(self):
        self.x[0].wait_recv()
        start_all([self.r[0], self.fx[0]])
        self.y[1].wait_recv()
        start_all([self.r[1], self.fy[1]])

    def relay2(self):
        self.x[1].wait_recv()
        self.fx[1].start()
        self.y[0].wait_recv()
        self.fy[0].start()

    def relay3(self):
        for h in range(2):
            self.r[h].wait_recv()
            self.fd[h].start()

    def arrive(self, copies):
        for c in copies:
            c.wait_recv()

    def sent(self):
        for c in self.x + self.y + self.r + self.o + self.fx + self.fy + self.fd:
            c.wait_send()
        wait_all(self.local)

    def finish(self):
        self.arrive(self.o + self.fx + self.fy + self.fd)
        self.sent()


class Ring:
    def __init__(self, n, p, g, src, dst, ss, rs, ls=None):
        groups = n // GROUP
        to = lambda s: lax.rem(g + s, groups) * GROUP + p
        at = lambda s: lax.rem(g + s, groups)

        def cp(a, b, i, dev):
            return rcopy(a, b, ss.at[i], rs.at[i], dev)

        self.relays = []
        if groups == 4:
            self.up = [cp(src(h), dst(g, h), h, to(1)) for h in range(2)]
            self.down = [cp(src(h), dst(g, h), 2 + h, to(3)) for h in range(2)]
            self.first = [self.up[0], self.down[1], self.up[1], self.down[0]]
            below, above = at(3), at(1)
            self.relays = [cp(dst(below, 0), dst(below, 0), 4, to(1)), cp(dst(above, 1), dst(above, 1), 5, to(3))]
        else:
            self.first = [cp(src(None), dst(g, None), s - 1, to(s)) for s in range(1, groups)]
        self.local = [] if ls is None else [pltpu.make_async_copy(src(None), dst(g, None), ls)]

    def start(self):
        start_all(self.first + self.local)

    def relay(self):
        if self.relays:
            self.up[0].wait_recv()
            self.relays[0].start()
            self.down[1].wait_recv()
            self.relays[1].start()

    def finish(self):
        if self.relays:
            self.up[1].wait_recv()
            self.down[0].wait_recv()
            for c in self.first:
                c.wait_send()
        else:
            wait_all(self.first)
        wait_all(self.relays + self.local)


def ring_count(n):
    return max(6, n // GROUP - 1)


def halves(length, base=0):
    cut = length // 2
    part = (pl.ds(base, cut), pl.ds(base + cut, length - cut))
    return lambda h: pl.ds(base, length) if h is None else part[h]


class RingReduce:
    def __init__(self, n, p, g, part, low, high, send, fin, ss, rs):
        groups = n // GROUP
        to = lambda s: lax.rem(g + s, groups) * GROUP + p
        at = lambda s: lax.rem(g + s, groups)
        hs = halves(part.shape[1])
        self.part, self.fin, self.send, self.g, self.hs = part, fin, send, g, hs

        def cp(a, b, i, dev):
            return rcopy(a, b, ss.at[i], rs.at[i], dev)

        self.ring = groups == 4
        if self.ring:
            self.above, self.below = at(1), at(3)
            self.low, self.high = low, high
            far = at(2)
            self.a = cp(part.at[far, hs(0)], low, 0, to(1))
            self.b = cp(part.at[far, hs(1)], high, 1, to(3))
            self.c = cp(part.at[self.above, hs(1)], fin.at[0, hs(1)], 2, to(1))
            self.d = cp(part.at[self.below, hs(0)], fin.at[1, hs(0)], 3, to(3))
            self.e = cp(send.at[hs(0)], fin.at[0, hs(0)], 4, to(1))
            self.f = cp(send.at[hs(1)], fin.at[1, hs(1)], 5, to(3))
            self.all = [self.a, self.b, self.c, self.d, self.e, self.f]
        else:
            self.all = [cp(part.at[at(s)], fin.at[s - 1], s - 1, to(s)) for s in range(1, groups)]
        self.count = groups - 1

    def start(self):
        start_all(self.all[:4] if self.ring else self.all)

    def relay(self):
        if self.ring:
            for got, buf, h, b, out in (
                (self.a, self.low, 0, self.above, self.e),
                (self.b, self.high, 1, self.below, self.f),
            ):
                got.wait_recv()
                at = self.hs(h)
                self.send[at] = (self.part[b, at].astype(F32) + buf[...].astype(F32)).astype(BF16)
                out.start()

    def finish(self):
        for c in self.all[2:] if self.ring else self.all:
            c.wait_recv()
        val = self.part[self.g].astype(F32)
        for s in range(2 if self.ring else self.count):
            val = val + self.fin[s].astype(F32)
        for c in self.all:
            c.wait_send()
        return val


def ring_scratch(n, shape):
    cut = shape[0] // 2
    groups = n // GROUP
    count = 2 if groups == 4 else groups - 1
    tail = tuple(shape[1:])
    vm = lambda s: pltpu.VMEM(s, BF16)
    return [
        vm((max(cut, 1),) + tail),
        vm((shape[0] - cut,) + tail),
        vm(tuple(shape)),
        vm((count,) + tuple(shape)),
        DMA((ring_count(n),)),
        DMA((ring_count(n),)),
    ]


class PlaneReduce:
    def __init__(self, me, part, sib, send, relay, fx, fy, ss, rs, own=None):
        p = lax.rem(me, GROUP)
        self.own = own or (lambda i: part(p ^ (2 * i)))
        xn, yn = me ^ 2, me ^ 4
        hs = halves(sib.shape[1])
        self.hs, self.p, self.part = hs, p, part
        self.sib, self.send, self.relay, self.fx, self.fy = sib, send, relay, fx, fy

        def cp(a, b, i, dev):
            return rcopy(a, b, ss.at[i], rs.at[i], dev)

        self.first = [cp(part(p ^ (2 * i + 1)), sib.at[i], i, me ^ 1) for i in range(4)]
        self.diag = [cp(send.at[0, hs(0)], relay.at[0], 4, xn), cp(send.at[0, hs(1)], relay.at[1], 5, yn)]
        self.toy = [cp(send.at[2, hs(h)], fy.at[hs(h)], 6 + h, yn) for h in range(2)]
        self.tox = [cp(send.at[1, hs(h)], fx.at[hs(h)], 8 + h, xn) for h in range(2)]

    def start(self):
        start_all([self.first[i] for i in (3, 1, 2, 0)])

    def chip(self, i):
        self.first[i].wait_recv()
        return self.own(i)[...].astype(F32) + self.sib[i].astype(F32)

    def chip_d(self):
        self.send[0] = self.chip(3).astype(BF16)
        start_all(self.diag)

    def chip_x(self):
        self.send[1] = self.chip(1).astype(BF16)
        self.tox[0].start()

    def chip_y(self):
        self.send[2] = self.chip(2).astype(BF16)
        self.toy[1].start()

    def phase1(self):
        self.chip_d()
        self.chip_x()
        self.chip_y()

    def phase2(self):
        self.diag[0].wait_recv()
        at = self.hs(0)
        self.send[2, at] = (self.send[2, at].astype(F32) + self.relay[0].astype(F32)).astype(BF16)
        self.toy[0].start()
        self.diag[1].wait_recv()
        at = self.hs(1)
        self.send[1, at] = (self.send[1, at].astype(F32) + self.relay[1].astype(F32)).astype(BF16)
        self.tox[1].start()

    def phase3(self):
        own = self.chip(0)
        for c in self.toy + self.tox:
            c.wait_recv()
        own = own + self.fx[...].astype(F32) + self.fy[...].astype(F32)
        for c in self.first + self.diag + self.toy + self.tox:
            c.wait_send()
        return own


def plane_scratch(shape):
    tail = tuple(shape[1:])
    vm = lambda *s: pltpu.VMEM(s + tail, BF16)
    return [
        vm(4, shape[0]),
        vm(3, shape[0]),
        vm(2, shape[0] // 2),
        vm(shape[0]),
        vm(shape[0]),
        DMA((10,)),
        DMA((10,)),
    ]


def swap_halves(v):
    lane = lax.broadcasted_iota(jnp.int32, v.shape, 1)
    low = lax.rem(lane, HEAD) < HEAD // 2
    width = v.shape[1]
    return jnp.where(low, pltpu.roll(v, width - HEAD // 2, 1), pltpu.roll(v, HEAD // 2, 1))


def head_mean(v):
    row = lax.broadcasted_iota(jnp.int32, (128, 128), 0)
    lane = lax.broadcasted_iota(jnp.int32, (128, 128), 1)
    same = jnp.where((row < HEAD) == (lane < HEAD), 1.0 / HEAD, 0.0).astype(BF16)
    high = v.astype(BF16)
    low = (v - high.astype(F32)).astype(BF16)
    return nn(high, same) + nn(low, same)


def head_gains(g_ref):
    t = g_ref[:, 2 * D :]
    t = jnp.broadcast_to(t, (8, 128))
    lane = lax.broadcasted_iota(jnp.int32, (8, 128), 1)
    other = pltpu.roll(t, HEAD, 1)
    return jnp.where(lane < HEAD, t, other)[0:1, :], jnp.where(lane < HEAD, other, t)[0:1, :]


def seq_start(row, len_ref, g):
    e1 = len_ref[g, 0]
    e2 = e1 + len_ref[g, 1]
    e3 = e2 + len_ref[g, 2]
    zero = row * 0
    s = jnp.where(row >= e1, zero + e1, zero)
    s = jnp.where(row >= e2, zero + e2, s)
    return jnp.where(row >= e3, zero + e3, s)


def windows(i, window):
    for low, high, count in ((0, 1, 2), (2, 3, 4), (4, 7, WINDOW + 1)):

        @pl.when((i >= low) & (i <= high))
        def _():
            window(jnp.maximum(i - WINDOW, 0), count)


def front_kernel(n, len_ref, x_, wq_, wk_, wv_, wg_, wu_, wo_, wd_, gn_, dy_, h_o, raw_o, q_o, kv_o, mixf_o, lse_o, mixo, dyo, w21o, w22o, woo, wdo, wqkv_o, gvec, ct, st, xa, gn, wq, wk, wv, wo, wd, wg, wu, dy, a1, b1, b2, gt, gto, w1v, woz, wqkv, h_s, raw_s, q_s, kv_s, mixf_s, lse_s, mixs, k_s, v_s, acc, fs, ls, xs, xr, ds_, dr, os_, orr, ps, pr, zs, zr, ms, mr, outs):
    me, p, g, groups, zq, zg = places(n)
    fetch = bring(
        (
            (x_, xa.at[p]),
            (gn_, gn),
            (wq_, wq),
            (wk_, wk),
            (wv_, wv),
            (wo_, wo),
            (wd_.at[pl.ds(0, wd.shape[0])], wd),
            (wg_, wg),
            (wu_, wu),
            (dy_, dy),
        ),
        fs,
    )
    share = gn.shape[1]
    ffc = wg.shape[1] // (groups * GROUP)
    big = 2 * ffc // 3
    r = wq.shape[0]
    barrier([me ^ m for m in range(1, GROUP)] + zq)
    hx, ho = halves(BLOCK), halves(groups)
    xg = PlaneGather(me, p, lambda h: xa.at[p, hx(h)], lambda b, h: xa.at[b, hx(h)], xs, xr)
    dg = PlaneGather(me, p, lambda h: dy.at[hx(h)], lambda b, h: dyo.at[b, hx(h)], ds_, dr, ls.at[pl.ds(0, 2)])
    og = PlaneGather(me, p, lambda h: woz.at[ho(h)], lambda b, h: woo.at[ho(h), b], os_, orr, ls.at[pl.ds(2, 2)])
    fetch[0].wait()
    xg.start_first()

    def ring(k, src, dst, local=None):
        hk = halves(dst.shape[1])
        return Ring(n, p, g, lambda h: src.at[hk(h)], lambda b, h: dst.at[b, hk(h)], zs.at[k], zr.at[k], local)

    wring, gring = ring(0, w1v.at[g], w1v), ring(1, gto.at[g], gto)
    dring, oring = ring(2, wd, wdo, ls.at[4]), ring(3, wo, woz, ls.at[5])
    uring = ring(4, w21o.at[g], w21o)
    pc = {}

    def exchange(k, src, dst):
        for m in range(1, GROUP):
            pc[k, m] = rcopy(src(p ^ m), dst, ps.at[k, m - 1], pr.at[k, m - 1], me ^ m)
            pc[k, m].start()

    def arrived(k):
        for m in range(1, GROUP):
            pc[k, m].wait_recv()

    fetch[1].wait()
    gt[...] = jnp.zeros_like(gt)
    gt[0:1, :share] = gn[...].astype(F32)
    exchange(1, lambda b: gt, gto.at[g, p])
    gto[g, p] = gt[...]
    wait_all(fetch[2:5])
    for b in range(GROUP):
        a1[b, :, :128] = wq[:, 128 * b : 128 * (b + 1)]
        at = slice(HEAD * b, HEAD * (b + 1))
        a1[b, :, 128:] = jnp.concatenate([wk[:, at], wv[:, at]], axis=1)
    exchange(0, lambda b: a1.at[b], w1v.at[g, p])
    w1v[g, p] = a1[p]
    wait_all(fetch[5:7])
    oring.start()
    dring.start()
    wait_all(fetch[7:9])
    for buf, low, high in ((b1, 0, big), (b2, big, ffc)):
        for b in range(GROUP):
            at = [slice((GROUP * k + b) * ffc + low, (GROUP * k + b) * ffc + high) for k in range(groups)]
            buf[b] = jnp.concatenate([wg[:, k] for k in at] + [wu[:, k] for k in at], axis=1)
    exchange(2, lambda b: b1.at[b], w21o.at[g, p])
    exchange(3, lambda b: b2.at[b], w22o.at[p])
    xg.start_second()
    local = start_all(
        [
            pltpu.make_async_copy(b1.at[p], w21o.at[g, p], ls.at[6]),
            pltpu.make_async_copy(b2.at[p], w22o.at[p], ls.at[7]),
        ]
    )
    arrived(0)
    wring.start()
    arrived(1)
    gring.start()
    xg.relay1()
    arrived(2)
    wait_all(local)
    uring.start()
    row = lax.broadcasted_iota(jnp.int32, (1, ROWS), 1)
    position = (row - seq_start(row, len_ref, g)).astype(F32)
    index = lax.broadcasted_iota(jnp.int32, (HEAD // 2, 1), 0).astype(F32)
    angles = jnp.exp(index * (-2.0 * math.log(ROPE_THETA) / HEAD)) * position
    c, s = jnp.cos(angles).T, jnp.sin(angles).T
    ct[...] = jnp.concatenate([c, c, c, c], axis=1)
    st[...] = jnp.concatenate([-s, s, -s, s], axis=1)
    k_s[: WINDOW * BLOCK] = jnp.zeros((WINDOW * BLOCK, HEAD), BF16)
    v_s[: WINDOW * BLOCK] = jnp.zeros((WINDOW * BLOCK, 128), BF16)
    xg.relay2()
    fetch[9].wait()
    dg.start_first()
    for c in (oring, wring, gring):
        c.relay()
    xg.relay3()
    dg.start_second()
    dring.relay()
    wring.finish()
    gring.finish()
    for k in range(groups * GROUP):
        wqkv[k * r : (k + 1) * r] = w1v[k // GROUP, k % GROUP]
    gvec[...] = jnp.concatenate(
        [gto[k, b, 0:1, :share] for k in range(groups) for b in range(GROUP)], axis=1
    )
    xg.arrive(xg.o + xg.fx + xg.fy + xg.fd)
    gq, gk = head_gains(gvec)
    results = ((h_s, h_o), (raw_s, raw_o), (q_s, q_o), (kv_s, kv_o), (mixf_s, mixf_o), (lse_s, lse_o))

    def block(i, carry):
        @pl.when(i == 1)
        def _():
            oring.finish()
            og.start_first()

        @pl.when(i == 2)
        def _():
            dg.relay1()
            og.start_second()

        @pl.when(i == 4)
        def _():
            dg.relay2()
            uring.relay()

        @pl.when(i == 5)
        def _():
            og.relay1()

        @pl.when(i == 6)
        def _():
            dg.relay3()

        @pl.when(i == 7)
        def _():
            og.relay2()

        at = pl.ds(pl.multiple_of(i * BLOCK, BLOCK), BLOCK)
        xb = xa[i].astype(F32)
        h = (xb * lax.rsqrt(jnp.mean(xb * xb, axis=-1, keepdims=True) + EPSILON) * gvec[:, :D]).astype(BF16)
        h_s[i] = h
        raw = nn(h, wqkv[...])
        raw_s[i] = raw
        cb, sb = ct[at, :], st[at, :]
        qraw, kvraw = raw[:, :128], raw[:, 128:]
        qn = qraw * lax.rsqrt(head_mean(qraw * qraw) + EPSILON) * gq
        q = (qn * cb + swap_halves(qn) * sb).astype(BF16)
        kn = kvraw * lax.rsqrt(head_mean(kvraw * kvraw) + EPSILON) * gk
        k = (kn * cb + swap_halves(kn) * sb).astype(BF16)
        lane = lax.broadcasted_iota(jnp.int32, (BLOCK, 128), 1)
        kv = jnp.where(lane < HEAD, k.astype(F32), kvraw).astype(BF16)
        q_s[i] = q
        kv_s[i] = kv
        k_s[at, :] = kv[:, :HEAD]
        v_s[at, :] = jnp.where(lane < HEAD, pltpu.roll(kvraw, HEAD, 1), 1.0).astype(BF16)
        q2 = jnp.concatenate([q[:, :HEAD], q[:, HEAD:]], axis=0)
        rows = lax.broadcasted_iota(jnp.int32, (2 * BLOCK, 1), 0)
        qrow = i * BLOCK + jnp.where(rows >= BLOCK, rows - BLOCK, rows)
        qstart = seq_start(qrow, len_ref, g)

        def window(first, count):
            span = pl.ds(pl.multiple_of(first * BLOCK, BLOCK), count * BLOCK)
            kc = lax.broadcasted_iota(jnp.int32, (2 * BLOCK, count * BLOCK), 1) + first * BLOCK
            ok = (kc >= qstart) & (kc <= qrow)
            e = jnp.where(ok, jnp.exp2(nt(q2, k_s[span, :]) * (SCALE * LOG2E)), 0.0).astype(BF16)
            acc[...] = nn(e, v_s[span, :])

        windows(i, window)
        total = acc[:, HEAD:]
        m = acc[:, :HEAD] / total
        both = jnp.concatenate([m[:BLOCK], m[BLOCK:]], axis=1)
        mixf_s[i] = both
        lse_s[i] = jnp.log2(total.T)[:8, :]
        mixs[i] = both.astype(BF16)

        @pl.when(i == p)
        def _():
            pltpu.make_async_copy(mixs.at[i], mixo.at[p], ls.at[8]).start()

        @pl.when(i != p)
        def _():
            rcopy(mixs.at[i], mixo.at[p], ms.at[p ^ i], mr.at[p ^ i], me ^ p ^ i).start()

        for k, (a, b) in enumerate(results):
            pltpu.make_async_copy(a.at[i], b.at[i], outs.at[k, i]).start()
        return carry

    lax.fori_loop(0, GROUP, block, 0)
    wq_out = pltpu.make_async_copy(wqkv, wqkv_o, ls.at[9])
    wq_out.start()
    og.relay3()
    for c in pc.values():
        c.wait_send()
    arrived(3)
    for c in (dring, uring):
        c.finish()
    xg.sent()
    dg.finish()
    og.finish()
    for m in range(1, GROUP):
        rcopy(mixs.at[p ^ m], mixo.at[p], ms.at[m], mr.at[m], me ^ m).wait()
    pltpu.make_async_copy(mixs.at[p], mixo.at[p], ls.at[8]).wait()
    for k, (a, b) in enumerate(results):
        for i in range(GROUP):
            pltpu.make_async_copy(a.at[i], b.at[i], outs.at[k, i]).wait()
    wq_out.wait()


def front(n, lengths, x, wq, wk, wv, wg, wu, wo, wd, gn, dy):
    groups = n // GROUP
    r = wq.shape[0]
    wide = 2 * wg.shape[1] // GROUP
    wide1 = 2 * wide // 3
    wd1 = (2 * wd.shape[0] // 3,) + wd.shape[1:]
    vm = lambda *s: pltpu.VMEM(s, BF16)
    vf = lambda *s: pltpu.VMEM(s, F32)
    return pl.pallas_call(
        functools.partial(front_kernel, n),
        out_shape=(
            SDS((GROUP, BLOCK, D), BF16),
            SDS((GROUP, BLOCK, QKV), F32),
            SDS((GROUP, BLOCK, 128), BF16),
            SDS((GROUP, BLOCK, 128), BF16),
            SDS((GROUP, BLOCK, 128), F32),
            SDS((GROUP, 8, 2 * BLOCK), F32),
            SDS((GROUP, BLOCK, 128), BF16),
            SDS((GROUP, BLOCK, D), BF16),
            SDS((groups, GROUP, r, wide1), BF16),
            SDS((GROUP, r, wide - wide1), BF16),
            SDS((groups, GROUP) + wo.shape, BF16),
            SDS((groups,) + wd1, BF16),
            SDS((D, QKV), BF16),
            SDS((1, gn.shape[1] * n), F32),
            SDS((ROWS, 128), F32),
            SDS((ROWS, 128), F32),
        ),
        in_specs=[SM] + [HB] * 10,
        out_specs=(HB,) * 13 + (VM,) * 3,
        scratch_shapes=[vm(GROUP, BLOCK, D)]
        + [vm(*s) for s in (gn.shape, wq.shape, wk.shape, wv.shape, wo.shape, wd1, wg.shape, wu.shape, dy.shape)]
        + [
            vm(GROUP, r, QKV),
            vm(GROUP, r, wide1),
            vm(GROUP, r, wide - wide1),
            vf(8, 128),
            vf(groups, GROUP, 8, 128),
            vm(groups, GROUP, r, QKV),
            vm(groups, *wo.shape),
            vm(D, QKV),
            vm(GROUP, BLOCK, D),
            vf(GROUP, BLOCK, QKV),
            vm(GROUP, BLOCK, 128),
            vm(GROUP, BLOCK, 128),
            vf(GROUP, BLOCK, 128),
            vf(GROUP, 8, 2 * BLOCK),
            vm(GROUP, BLOCK, 128),
            vm(ROWS, HEAD),
            vm(ROWS, 128),
            vf(2 * BLOCK, 128),
            DMA((10,)),
            DMA((10,)),
            DMA((14,)),
            DMA((14,)),
            DMA((14,)),
            DMA((14,)),
            DMA((14,)),
            DMA((14,)),
            DMA((4, 7)),
            DMA((4, 7)),
            DMA((5, ring_count(n))),
            DMA((5, ring_count(n))),
            DMA((GROUP,)),
            DMA((GROUP,)),
            DMA((6, GROUP)),
        ],
        compiler_params=pltpu.CompilerParams(collective_id=1, has_side_effects=True, vmem_limit_bytes=VMEM_LIMIT),
        name="front",
    )(lengths, x, wq, wk, wv, wg, wu, wo, wd, gn, dy)


def norm_back(dyv, xv, gain):
    r = lax.rsqrt(jnp.mean(xv * xv, axis=-1, keepdims=True) + EPSILON)
    xr = xv * r
    gy = dyv * gain
    dx = r * (gy - xr * jnp.mean(gy * xr, axis=-1, keepdims=True))
    return dx, jnp.sum(dyv * xr, axis=0, keepdims=True)


def unit_grads(h, dyb, wgu, wd):
    f = wd.shape[0]
    gu = nn(h, wgu)
    da = nt(dyb, wd)
    gp, up = gu[:, :f], gu[:, f:]
    sig = 1.0 / (1.0 + jnp.exp(-gp))
    sg = gp * sig
    dg = (da * up * (sig * (1.0 + gp * (1.0 - sig)))).astype(BF16)
    return (sg * up).astype(BF16), jnp.concatenate([dg, (da * sg).astype(BF16)], axis=1)


def ffn_block_kernel(n, order, mix_, x_, wo_, g_ref, w21_, w22_, wd1_, wd2_, dy_, res, gmid, dgf, dwo, dmh, po, t21, dw22, dwd, x, wo, w21, dy, fs, mbuf, h2, h2t, w2v, w22, wdv, wds, dys, acts, dgu1, dgu2, dw21, part, mown, stage, hs, hr, os_, qs, qr, zs, zr, *red_refs):
    me, p, g, groups, zq, zg = places(n)
    f1 = wd1_.shape[0]
    f2 = wds.shape[0] - f1
    fetch = bring(
        (
            (wd2_.at[pl.ds(wd2_.shape[0] - wdv.shape[1], wdv.shape[1])], wdv.at[g]),
            (w22_, w2v.at[g]),
            (mix_, mbuf),
            (x_, x),
            (wo_, wo),
            (w21_, w21),
            (wd1_, wds.at[pl.ds(0, f1)]),
            (dy_, dy),
        ),
        fs,
    )
    barrier([me ^ m for m in range(1, GROUP)] + zq)
    gf = g_ref.at[:, D : 2 * D]
    r = w2v.shape[2]

    def holder(q):
        s = 0
        for k in range(ROWS // SLOT):
            s = jnp.where(order[g, k] == q, k, s)
        return s

    hw, h8 = halves(wdv.shape[1]), halves(GROUP)
    wrings = [
        Ring(n, p, g, lambda h: w2v.at[g, h8(h)], lambda b, h: w2v.at[b, h8(h)], zs.at[0], zr.at[0]),
        Ring(n, p, g, lambda h: wdv.at[g, hw(h)], lambda b, h: wdv.at[b, hw(h)], zs.at[1], zr.at[1]),
    ]
    wait_all(fetch[:2])
    for c in wrings:
        c.start()
    wait_all(fetch[2:5])
    m = jnp.concatenate([mbuf[b] for b in range(GROUP)], axis=1)
    mown[...] = m
    z = x[...].astype(F32) + nn(m, wo[...])
    res[...] = z
    h2[p] = (z * lax.rsqrt(jnp.mean(z * z, axis=-1, keepdims=True) + EPSILON) * gf[...]).astype(BF16)
    hb = halves(BLOCK)
    hg = PlaneGather(me, p, lambda h: h2.at[p, hb(h)], lambda b, h: h2.at[b, hb(h)], hs, hr)
    red = PlaneReduce(me, lambda b: part.at[b], *red_refs[:7])
    ring21 = RingReduce(n, p, g, dw21, *red_refs[7:])
    hg.start_first()
    wait_all(fetch[5:])

    def first(t, carry):
        @pl.when(t == 1)
        def _():
            hg.start_second()
            hg.arrive(hg.o)

        @pl.when(t == 2)
        def _():
            hg.relay1()
            hg.relay2()

        @pl.when(t == 3)
        def _():
            hg.arrive(hg.fx)

        @pl.when(t == 4)
        def _():
            for c in wrings:
                c.relay()

        @pl.when(t == 5)
        def _():
            hg.arrive(hg.fy)

        @pl.when(t == 6)
        def _():
            hg.relay3()

        @pl.when(t == 7)
        def _():
            hg.arrive(hg.fd)

        b = p ^ t
        dys[b] = jnp.concatenate([dy[holder(2 * b)], dy[holder(2 * b + 1)]], axis=0)
        h2t[:, pl.ds(pl.multiple_of(b * BLOCK, BLOCK), BLOCK)] = h2[b].T
        acts[b, :, :f1], dgu1[b] = unit_grads(h2[b], dys[b], w21[...], wds[:f1])
        part[b] = nt(dgu1[b], w21[...]).astype(BF16)
        return carry

    lax.fori_loop(0, GROUP, first, 0)
    grad1 = nn(h2t[...], dgu1[...].reshape(ROWS, 2 * f1)).astype(BF16)
    for k in range(groups * GROUP):
        dw21[k // GROUP, k % GROUP] = grad1[k * r : (k + 1) * r]
    ring21.start()
    for c in wrings:
        c.finish()
    for k in range(groups * GROUP):
        w22[k * r : (k + 1) * r] = w2v[k // GROUP, k % GROUP]
    each = f2 // groups
    for k in range(groups):
        wds[f1 + k * each : f1 + (k + 1) * each] = wdv[k].reshape(each, D)

    def second(t, carry):
        @pl.when(t == 1)
        def _():
            red.first[3].start()

        @pl.when(t == 3)
        def _():
            red.first[2].start()
            red.chip_d()

        @pl.when(t == 5)
        def _():
            red.first[1].start()
            red.chip_y()

        @pl.when(t == 7)
        def _():
            red.first[0].start()
            red.chip_x()

        b = p ^ (GROUP - 1 - t)
        acts[b, :, f1:], dgu2[b] = unit_grads(h2[b], dys[b], w22[...], wds[f1:])
        part[b] = (part[b].astype(F32) + nt(dgu2[b], w22[...])).astype(BF16)
        return carry

    lax.fori_loop(0, GROUP, second, 0)
    dw = tn(acts[...].reshape(ROWS, f1 + f2), dys[...].reshape(ROWS, D)).astype(BF16)
    l1 = dwd.shape[1] - wdv.shape[1]
    e1 = f1 // groups
    for k in range(groups):
        dwd[k, :l1] = dw[k * e1 : (k + 1) * e1].reshape((l1,) + dwd.shape[2:])
        dwd[k, l1:] = dw[f1 + k * each : f1 + (k + 1) * each].reshape(wdv.shape[1:])
    red.phase2()
    ring21.relay()
    dw22[...] = nn(h2t[...], dgu2[...].reshape(ROWS, 2 * f2)).astype(BF16)
    dx, dgain = norm_back(red.phase3(), res[...], gf[...])
    gm = dys[p].astype(F32) + dx
    gmid[...] = gm
    dgf[...] = dgain
    gl = gm.astype(BF16)
    dm = nt(gl, wo[...]).astype(BF16)
    for b in range(GROUP):
        mbuf[b] = dm[:, 128 * b : 128 * (b + 1)]
    qc = start_all(
        [rcopy(mbuf.at[p ^ m], dmh.at[p], qs.at[m - 1], qr.at[m - 1], me ^ m) for m in range(1, GROUP)]
    )
    dmh[p] = mbuf[p]
    dwo[...] = tn(mown[...], gl).astype(BF16)

    def out(b, carry):
        slot = lax.rem(b, 2)

        @pl.when(b > 1)
        def _():
            pltpu.make_async_copy(stage.at[slot], po.at[b - 2], os_.at[slot]).wait()

        stage[slot] = nn(acts[b], wds[...]).astype(BF16)
        pltpu.make_async_copy(stage.at[slot], po.at[b], os_.at[slot]).start()
        return carry

    lax.fori_loop(0, GROUP, out, 0)
    for b in range(GROUP - 2, GROUP):
        pltpu.make_async_copy(stage.at[b % 2], po.at[b], os_.at[b % 2]).wait()
    wait_all(qc)
    hg.sent()
    t21[...] = ring21.finish().astype(BF16)


def ffn_block(n, order, mix, x, wo, gvec, w21, w22, wd1, wd, dy):
    groups = n // GROUP
    r = w22.shape[1]
    f1, f2 = w21.shape[1] // 2, w22.shape[2] // 2
    wd2 = (wd.shape[0] // 3,) + wd.shape[1:]
    blk = (GROUP, r, 2 * f1)
    vm = lambda *s: pltpu.VMEM(s, BF16)
    return pl.pallas_call(
        functools.partial(ffn_block_kernel, n),
        out_shape=(
            SDS((BLOCK, D), F32),
            SDS((BLOCK, D), F32),
            SDS((1, D), F32),
            SDS((D, D), BF16),
            SDS((GROUP, BLOCK, 128), BF16),
            SDS((GROUP, BLOCK, D), BF16),
            SDS(blk, BF16),
            SDS((D, 2 * f2), BF16),
            SDS((groups,) + wd.shape, BF16),
        ),
        in_specs=[SM, HB, HB, HB, VM, HB, HB, HB, HB, HB],
        out_specs=(VM, VM, VM, VM, VM, HB, VM, VM, VM),
        scratch_shapes=[
            vm(BLOCK, D),
            vm(D, D),
            vm(D, 2 * f1),
            vm(ROWS // SLOT, SLOT, D),
            DMA((8,)),
            vm(GROUP, BLOCK, 128),
            vm(GROUP, BLOCK, D),
            vm(D, ROWS),
            vm(groups, *w22.shape),
            vm(D, 2 * f2),
            vm(groups, *wd2),
            vm(f1 + f2, D),
            vm(GROUP, BLOCK, D),
            vm(GROUP, BLOCK, f1 + f2),
            vm(GROUP, BLOCK, 2 * f1),
            vm(GROUP, BLOCK, 2 * f2),
            vm(groups, *blk),
            vm(GROUP, BLOCK, D),
            vm(BLOCK, D),
            vm(2, BLOCK, D),
            DMA((14,)),
            DMA((14,)),
            DMA((2,)),
            DMA((7,)),
            DMA((7,)),
            DMA((2, ring_count(n))),
            DMA((2, ring_count(n))),
        ]
        + plane_scratch((BLOCK, D))
        + ring_scratch(n, blk),
        compiler_params=pltpu.CompilerParams(collective_id=2, has_side_effects=True, vmem_limit_bytes=VMEM_LIMIT),
        name="ffn_block",
    )(order, mix, x, wo, gvec, w21, w22, wd1, wd, dy.reshape(ROWS // SLOT, SLOT, D))


def attn_bwd_kernel(n, len_ref, dm_ref, q_ref, kvall_ref, lse_ref, mixf_ref, h_ref, raw_ref, w_ref, g_ref, ct_ref, st_ref, po_, res_, dwo_, dw2_, dwd_, t21_, dgf, dh_ref, dw_ref, gpart, result, two, t2, od, o21, k_s, v_s, dkv, dqt, dws, dg_ref, es, er, po, res, dwo, dw2, dwd, t21, fs, *rest):
    step_id = pl.program_id(0)
    nb = ROWS // BLOCK
    i = nb - 1 - step_id
    me, p, g, groups, zq, zg = places(n)
    ored = PlaneReduce(me, lambda b: po.at[b], *rest[:7])
    wred = PlaneReduce(me, lambda b: dwo.at[:, b], *rest[7:14])
    ring2 = RingReduce(n, p, g, dw2, *rest[14:20])
    ringd = RingReduce(n, p, g, dwd, *rest[20:26])
    fetch = [
        pltpu.make_async_copy(a, b, fs.at[k])
        for k, (a, b) in enumerate(
            ((dwd_, dwd), (dw2_, dw2), (po_, po), (dwo_, dwo), (t21_, t21), (res_, res))
        )
    ]
    ex = [rcopy(t21.at[p ^ m], o21.at[p], es.at[m - 1], er.at[m - 1], me ^ m) for m in range(1, GROUP)]
    own_copy = pltpu.make_async_copy(t21.at[p], o21.at[p], fs.at[6])

    @pl.when(step_id == 0)
    def _():
        start_all(fetch)
        barrier([me ^ m for m in range(1, GROUP)] + zq)

    @pl.when(step_id == 1)
    def _():
        ored.phase1()
        wred.phase1()

    @pl.when(step_id == 3)
    def _():
        ringd.relay()
        ring2.relay()
        ored.phase2()

    @pl.when(step_id == 4)
    def _():
        wred.phase2()


    @pl.when(step_id == 0)
    def _():
        dkv[...] = jnp.zeros_like(dkv)
        dws[...] = jnp.zeros_like(dws)
        dg_ref[...] = jnp.zeros_like(dg_ref)
        for b in range(ROWS // BLOCK):
            kvb = kvall_ref[b]
            k_s[pl.ds(b * BLOCK, BLOCK), :] = kvb[:, :HEAD]
            v_s[pl.ds(b * BLOCK, BLOCK), :] = kvb[:, HEAD:]

    q, do, mf = q_ref[0], dm_ref[0], mixf_ref[0]
    q2 = jnp.concatenate([q[:, :HEAD], q[:, HEAD:]], axis=0)
    do2 = jnp.concatenate([do[:, :HEAD], do[:, HEAD:]], axis=0)
    prod = (do.astype(F32) * mf).T
    delta = jnp.concatenate(
        [jnp.sum(prod[:HEAD], axis=0, keepdims=True), jnp.sum(prod[HEAD:], axis=0, keepdims=True)], axis=1
    )
    lse = lse_ref[0, 0:1, :]
    colq = lax.broadcasted_iota(jnp.int32, (1, 2 * BLOCK), 1)
    qrow = i * BLOCK + jnp.where(colq >= BLOCK, colq - BLOCK, colq)
    qstart = seq_start(qrow, len_ref, g)

    def window(first, count):
        at = pl.ds(pl.multiple_of(first * BLOCK, BLOCK), count * BLOCK)
        kb, vb = k_s[at, :], v_s[at, :]
        kc = lax.broadcasted_iota(jnp.int32, (count * BLOCK, 2 * BLOCK), 0) + first * BLOCK
        ok = (kc >= qstart) & (kc <= qrow)
        pr = jnp.where(ok, jnp.exp2(nt(kb, q2) * (SCALE * LOG2E) - lse), 0.0)
        dsc = (pr * (nt(vb, do2) - delta)).astype(BF16)
        dkv[at, :HEAD] += nn(dsc, q2)
        dkv[at, HEAD:] += nn(pr.astype(BF16), do2)
        dqt[...] = tn(dsc, kb)

    windows(i, window)
    ct, st = ct_ref[...], st_ref[...]
    raw = raw_ref[0]
    dq = jnp.concatenate([dqt[:BLOCK], dqt[BLOCK:]], axis=1) * SCALE
    dkvb = dkv[pl.ds(pl.multiple_of(i * BLOCK, BLOCK), BLOCK), :]
    lane = lax.broadcasted_iota(jnp.int32, (BLOCK, 128), 1)

    def pull(d, v, gain):
        dn = d * ct - swap_halves(d) * st
        r = lax.rsqrt(head_mean(v * v) + EPSILON)
        vr = v * r
        gy = dn * gain
        return r * (gy - vr * head_mean(gy * vr)), jnp.sum(dn * vr, axis=0, keepdims=True)

    gq, gk = head_gains(g_ref)
    dqr, dgq = pull(dq, raw[:, :128], gq)
    dkr, dgk = pull(dkvb * SCALE, raw[:, 128:], gk)
    dg_ref[0:1, :] += dgq
    dg_ref[1:2, :] += dgk
    dqkv = jnp.concatenate([dqr, jnp.where(lane < HEAD, dkr, dkvb)], axis=1).astype(BF16)
    dh_ref[0] = nt(dqkv, w_ref[...]).astype(BF16)
    dws[...] += tn(h_ref[0], dqkv)

    @pl.when(step_id == 0)
    def _():
        wait_all(fetch)
        ringd.start()
        ring2.start()
        ored.start()
        wred.start()
        start_all(ex + [own_copy])

    @pl.when(step_id == nb - 1)
    def _():
        dw_ref[...] = dws[...].astype(BF16)
        result[...] = (ored.phase3() + res[...]).astype(BF16)
        two[...] = wred.phase3().astype(BF16)
        t2[...] = ring2.finish().astype(BF16)
        od[...] = ringd.finish()
        wait_all(ex + [own_copy])
        dga = lax.dot_general(
            jnp.ones((8, QKV), F32),
            w_ref[...].astype(F32) * dws[...],
            (((1,), (1,)), ((), ())),
            precision=lax.Precision.HIGHEST,
            preferred_element_type=F32,
        )
        dga = dga[0:1, :] / g_ref[:, :D]
        gpart[...] = jnp.zeros_like(gpart)
        for b in range(8):
            gpart[b : b + 1, :] = dga[:, 128 * b : 128 * (b + 1)]
            gpart[8 + b : 9 + b, :] = dgf[:, 128 * b : 128 * (b + 1)]
        turned = pltpu.roll(dg_ref[...], HEAD, 1)
        low = lax.broadcasted_iota(jnp.int32, (1, 128), 1) < HEAD
        gpart[16:17, :] = jnp.where(low, dg_ref[0:1, :] + turned[0:1, :], turned[1:2, :])


def attn_bwd(n, lengths, dmh, q, kv, lse, mixf, h, raw, wqkv, gvec, ct, st, po, res, dwo, dw2, dwd, t21, dgf):
    nb = ROWS // BLOCK
    groups = n // GROUP
    blk = lambda c: pl.BlockSpec((1, BLOCK, c), lambda i: (nb - 1 - i, 0, 0))
    whole = lambda s: pl.BlockSpec(s, lambda i: (0,) * len(s), pipeline_mode=pl.Buffered(1))
    return pl.pallas_call(
        functools.partial(attn_bwd_kernel, n),
        grid=(nb,),
        in_specs=[
            SM,
            blk(128),
            blk(128),
            whole((nb, BLOCK, 128)),
            pl.BlockSpec((1, 8, 2 * BLOCK), lambda i: (nb - 1 - i, 0, 0)),
            blk(128),
            blk(D),
            blk(QKV),
            whole((D, QKV)),
            whole(gvec.shape),
            pl.BlockSpec((BLOCK, 128), lambda i: (nb - 1 - i, 0)),
            pl.BlockSpec((BLOCK, 128), lambda i: (nb - 1 - i, 0)),
            HB,
            HB,
            HB,
            HB,
            HB,
            HB,
            whole(dgf.shape),
        ],
        out_specs=(
            blk(D),
            whole((D, QKV)),
            whole((24, 128)),
            whole((BLOCK, D)),
            whole((groups,) + dwo.shape[2:]),
            whole(dw2.shape[1:]),
            whole(dwd.shape[1:]),
            HB,
        ),
        out_shape=(
            SDS((nb, BLOCK, D), BF16),
            SDS((D, QKV), BF16),
            SDS((24, 128), F32),
            SDS((BLOCK, D), BF16),
            SDS((groups,) + dwo.shape[2:], BF16),
            SDS(dw2.shape[1:], BF16),
            SDS(dwd.shape[1:], F32),
            SDS(t21.shape, BF16),
        ),
        scratch_shapes=[
            pltpu.VMEM((ROWS, HEAD), BF16),
            pltpu.VMEM((ROWS, HEAD), BF16),
            pltpu.VMEM((ROWS, 128), F32),
            pltpu.VMEM((2 * BLOCK, HEAD), F32),
            pltpu.VMEM((D, QKV), F32),
            pltpu.VMEM((8, 128), F32),
            DMA((7,)),
            DMA((7,)),
        ]
        + [pltpu.VMEM(a.shape, a.dtype) for a in (po, res, dwo, dw2, dwd, t21)]
        + [DMA((7,))]
        + plane_scratch((BLOCK, D))
        + plane_scratch((groups,) + dwo.shape[2:])
        + ring_scratch(n, dw2.shape[1:])
        + ring_scratch(n, dwd.shape[1:]),
        compiler_params=pltpu.CompilerParams(
            collective_id=6, has_side_effects=True, dimension_semantics=("arbitrary",), vmem_limit_bytes=VMEM_LIMIT
        ),
        cost_estimate=pl.CostEstimate(flops=8 * 10**9, bytes_accessed=16 << 20, transcendentals=4 * 10**6),
        name="attn_bwd",
    )(lengths, dmh, q, kv, lse, mixf, h, raw, wqkv, gvec, ct, st, po, res, dwo, dw2, dwd, t21, dgf)


def final_kernel(n, dh, x_, gmid_, g_ref, dw1, two, t2, gpart, gtok, o1, o2, oo, og, mine, x, gmid, fs, t1, gin, gsum, gz, ps, pr, gs, gr, *rest):
    me, p, g, groups, zq, zg = places(n)
    nz = groups - 1
    share = g_ref.shape[1] // n
    fetch = bring([(dh.at[p ^ (2 * i)], mine.at[i]) for i in (3, 1, 2, 0)] + [(x_, x), (gmid_, gmid)], fs)
    barrier([me ^ m for m in range(1, GROUP)] + zq)
    red = PlaneReduce(me, lambda b: dh.at[b], *rest[:7], own=lambda i: mine.at[i])
    ring1 = RingReduce(n, p, g, dw1, *rest[7:13])
    ringo = RingReduce(n, p, g, two, *rest[13:19])
    red.start()
    gc = start_all([rcopy(gpart, gin.at[m - 1], gs.at[m - 1], gr.at[m - 1], me ^ m) for m in range(1, GROUP)])
    ring1.start()
    ringo.start()
    pc = []

    def exchange(k, src, out):
        for m in range(1, GROUP):
            c = rcopy(src.at[p ^ m], out.at[p], ps.at[k, m - 1], pr.at[k, m - 1], me ^ m)
            c.start()
            pc.append(c)
        out[p] = src[p]

    wait_all(fetch)
    red.phase1()
    exchange(1, t2, o2)
    tot = gpart[...]
    for m in range(1, GROUP):
        gc[m - 1].wait_recv()
        tot = tot + gin[m - 1]
    gsum[...] = tot
    gzc = start_all([rcopy(gsum, gz.at[s], gs.at[7 + s], gr.at[7 + s], zq[s]) for s in range(nz)])
    ring1.relay()
    ringo.relay()
    red.phase2()
    t1[...] = ring1.finish().astype(BF16)
    exchange(0, t1, o1)
    oo[...] = ringo.finish()
    for s in range(nz):
        gzc[s].wait_recv()
        tot = tot + gz[s]
    gsum_row = me * share
    for c in gzc:
        c.wait_send()
    gsum[...] = tot
    first = gsum_row // 128
    off = lax.rem(gsum_row, 128)
    lane = lax.broadcasted_iota(jnp.int32, (8, 128), 1)
    turn = lambda row: pltpu.roll(jnp.broadcast_to(gsum[pl.ds(row, 1), :], (8, 128)), lax.rem(128 - off, 128), 1)
    og[...] = jnp.where(lane < 128 - off, turn(first), turn(first + 1))
    dx, _ = norm_back(red.phase3(), x[...].astype(F32), g_ref[:, :D])
    gtok[...] = gmid[...] + dx
    wait_all(pc)
    for c in gc:
        c.wait_send()


def final(n, dh, x, gmid, gvec, dw1, two, t2, gpart):
    groups = n // GROUP
    nz = groups - 1
    return pl.pallas_call(
        functools.partial(final_kernel, n),
        out_shape=(
            SDS((BLOCK, D), F32),
            SDS(dw1.shape[1:], BF16),
            SDS(t2.shape, BF16),
            SDS(two.shape[1:], F32),
            SDS((8, 128), F32),
        ),
        in_specs=[HB, HB, HB] + [VM] * 5,
        out_specs=(VM,) * 5,
        scratch_shapes=[
            pltpu.VMEM((4, BLOCK, D), BF16),
            pltpu.VMEM(x.shape, BF16),
            pltpu.VMEM(gmid.shape, F32),
            DMA((6,)),
            pltpu.VMEM(dw1.shape[1:], BF16),
            pltpu.VMEM((7, 24, 128), F32),
            pltpu.VMEM((24, 128), F32),
            pltpu.VMEM((nz, 24, 128), F32),
            DMA((2, 7)),
            DMA((2, 7)),
            DMA((7 + nz,)),
            DMA((7 + nz,)),
        ]
        + plane_scratch((BLOCK, D))
        + ring_scratch(n, dw1.shape[1:])
        + ring_scratch(n, two.shape[1:]),
        compiler_params=pltpu.CompilerParams(collective_id=4, has_side_effects=True, vmem_limit_bytes=VMEM_LIMIT),
        name="final",
    )(dh, x, gmid, gvec, dw1, two, t2, gpart)


def unpack_kernel(groups, result, gtok, o1, o21, o22, oo, od, og, result_o, gtok_o, gq, gk, gv, go, gg, gu, gd, gn):
    result_o[...] = result[...]
    gtok_o[...] = gtok[...]
    go[...] = oo[...]
    gd[...] = od[...]
    gn[...] = og[0:1, : gn.shape[1]]
    for b in range(GROUP):
        gq[:, 128 * b : 128 * (b + 1)] = o1[b, :, :128].astype(F32)
    for out, at in ((gk, slice(128, 128 + HEAD)), (gv, slice(128 + HEAD, 256))):
        for c in range(GROUP // 2):
            pair = [o1[2 * c + k, :, at].astype(F32) for k in range(2)]
            out[:, 128 * c : 128 * (c + 1)] = jnp.concatenate(pair, axis=1)
    ffc = gg.shape[1] // (groups * GROUP)
    for k, out in enumerate((gg, gu)):
        big = 2 * ffc // 3
        piece = lambda src, b, c, w: src[b, :, (k * groups + c) * w : (k * groups + c + 1) * w].astype(F32)
        parts = [
            piece(src, b, c, w)
            for c in range(groups)
            for b in range(GROUP)
            for src, w in ((o21, big), (o22, ffc - big))
        ]
        out[...] = jnp.concatenate(parts, axis=1)


def unpack(n, result, gtok, o1, o21, o22, oo, od, og, share):
    r = oo.shape[0]
    return pl.pallas_call(
        functools.partial(unpack_kernel, n // GROUP),
        out_shape=(
            SDS(result.shape, BF16),
            SDS(gtok.shape, F32),
            SDS((r, D), F32),
            SDS((r, D // 2), F32),
            SDS((r, D // 2), F32),
            SDS((r, D), F32),
            SDS((r, FF), F32),
            SDS((r, FF), F32),
            SDS(od.shape, F32),
            SDS((1, share), F32),
        ),
        in_specs=[VM] * 8,
        out_specs=(VM,) * 10,
        compiler_params=pltpu.CompilerParams(vmem_limit_bytes=VMEM_LIMIT),
        name="unpack",
    )(result, gtok, o1, o21, o22, oo, od, og)


def body(n, tokens, w_query, key_weight, w_value, w_out, w_gate, w_up, w_down, norm_gains, seq_lengths, slot_order, out_grad):
    groups = n // GROUP
    r = w_query.shape[0]
    ffc = w_down.shape[0]
    share = norm_gains.shape[0]
    wok = r // 16 if r % 16 == 0 else 1
    wdk = 9 if ffc % 144 == 0 else 3
    wo_blk, wd_blk = (wok, r // wok, D), (wdk, ffc // wdk, D)
    h, raw, q, kv, mixf, lse, mix, dy_all, w21, w22, wo, wd1, wqkv, gvec, ct, st = front(
        n,
        seq_lengths,
        tokens,
        w_query,
        key_weight,
        w_value,
        w_gate,
        w_up,
        w_out.reshape(wo_blk),
        w_down.reshape(wd_blk),
        norm_gains.reshape(1, share),
        out_grad,
    )
    res, gmid, dgf, dwo, dmh, po, t21, dw22, dwd = ffn_block(
        n,
        slot_order,
        mix,
        tokens,
        wo.reshape(D, D),
        gvec,
        w21.reshape(D, -1),
        w22,
        wd1.reshape(-1, D),
        w_down.reshape(wd_blk),
        dy_all,
    )
    dh1, dwqkv, gpart, result, two, t2, od, o21 = attn_bwd(
        n,
        seq_lengths,
        dmh,
        q,
        kv,
        lse,
        mixf,
        h,
        raw,
        wqkv,
        gvec,
        ct,
        st,
        po,
        res,
        dwo.reshape(groups, GROUP, r, D),
        dw22.reshape(groups, GROUP, r, -1),
        dwd,
        t21,
        dgf,
    )
    gtok, o1, o22, oo, og = final(
        n,
        dh1,
        tokens,
        gmid,
        gvec,
        dwqkv.reshape(groups, GROUP, r, QKV),
        two.reshape((groups,) + wo_blk),
        t2,
        gpart,
    )
    outs = unpack(n, result, gtok, o1, o21, o22, oo.reshape(r, D), od.reshape(ffc, D), og, share)
    return outs[:-1] + (outs[-1].reshape(share),)


def solution(mesh):
    n = mesh.shape["dp"]
    row = P("dp", None)
    return jax.shard_map(
        functools.partial(body, n),
        mesh=mesh,
        in_specs=(row,) * 8 + (P("dp"), P(), P(), row),
        out_specs=(row,) * 9 + (P("dp"),),
        check_vma=False,
    )
```

```python
import functools
import math

import jax
import jax.numpy as jnp
from jax import lax
from jax.experimental import pallas as pl
from jax.experimental.pallas import tpu as pltpu
from jax.sharding import PartitionSpec as P

D = 1024
FF = 4608
QUERY_HEADS = 16
KEY_VALUE_HEADS = 8
HEAD = 64
SLOT = 128
GROUP = 8
ROWS = 2048
BLOCK = 256
QKV = 256
WINDOW = 4
VMEM_LIMIT = 62 << 20
EPSILON = 1e-05
ROPE_THETA = 1000000.0
SCALE = 1.0 / math.sqrt(HEAD)
LOG2E = math.log2(math.e)
F32 = jnp.float32
BF16 = jnp.bfloat16
MESH = pl.DeviceIdType.MESH
DMA = pltpu.SemaphoreType.DMA
VM = pl.BlockSpec(memory_space=pltpu.VMEM)
ANY = pl.BlockSpec(memory_space=pl.ANY)
HB = pl.BlockSpec(memory_space=pltpu.HBM)
SM = pl.BlockSpec(memory_space=pltpu.SMEM)
SDS = jax.ShapeDtypeStruct


def nn(a, b):
    return lax.dot_general(a, b, (((1,), (0,)), ((), ())), preferred_element_type=F32)


def nt(a, b):
    return lax.dot_general(a, b, (((1,), (1,)), ((), ())), preferred_element_type=F32)


def tn(a, b):
    return lax.dot_general(a, b, (((0,), (0,)), ((), ())), preferred_element_type=F32)


def rcopy(src, dst, send, recv, dev):
    return pltpu.make_async_remote_copy(
        src_ref=src, dst_ref=dst, send_sem=send, recv_sem=recv, device_id=(dev,), device_id_type=MESH
    )


def barrier(peers):
    sem = pltpu.get_barrier_semaphore()
    for q in peers:
        pl.semaphore_signal(sem, inc=1, device_id=(q,), device_id_type=MESH)
    pl.semaphore_wait(sem, len(peers))


def places(n):
    me = lax.axis_index("dp")
    p = lax.rem(me, GROUP)
    g = me // GROUP
    groups = n // GROUP
    zq = [lax.rem(g + s, groups) * GROUP + p for s in range(1, groups)]
    zg = [lax.rem(g + s, groups) for s in range(1, groups)]
    return me, p, g, groups, zq, zg


def start_all(copies):
    for c in copies:
        c.start()
    return copies


def bring(pairs, sem):
    return start_all([pltpu.make_async_copy(a, b, sem.at[i]) for i, (a, b) in enumerate(pairs)])


def wait_all(copies):
    for c in copies:
        c.wait()


class PlaneGather:
    COPIES = 14

    def __init__(self, me, p, src, dst, ss, rs, ls=None):
        sib, xn, yn = me ^ 1, me ^ 2, me ^ 4

        def cp(a, b, i, dev):
            return rcopy(a, b, ss.at[i], rs.at[i], dev)

        def own(i, dev):
            return [cp(src(h), dst(p, h), i + h, dev) for h in range(2)]

        def on(m, h, i, dev):
            return cp(dst(p ^ m, h), dst(p ^ m, h), i, dev)

        self.x, self.y, self.o = own(0, xn), own(2, yn), own(4, sib)
        self.r = [on(2, 0, 6, yn), on(4, 1, 7, xn)]
        self.fx = [on(2, h, 8 + h, sib) for h in range(2)]
        self.fy = [on(4, h, 10 + h, sib) for h in range(2)]
        self.fd = [on(6, h, 12 + h, sib) for h in range(2)]
        self.local = [] if ls is None else [
            pltpu.make_async_copy(src(h), dst(p, h), ls.at[h]) for h in range(2)
        ]

    def start(self):
        self.start_first()
        self.start_second()

    def start_first(self):
        start_all([self.x[0], self.y[1]] + self.o + self.local)

    def start_second(self):
        start_all([self.x[1], self.y[0]])

    def relay1(self):
        self.x[0].wait_recv()
        start_all([self.r[0], self.fx[0]])
        self.y[1].wait_recv()
        start_all([self.r[1], self.fy[1]])

    def relay2(self):
        self.x[1].wait_recv()
        self.fx[1].start()
        self.y[0].wait_recv()
        self.fy[0].start()

    def relay3(self):
        for h in range(2):
            self.r[h].wait_recv()
            self.fd[h].start()

    def arrive(self, copies):
        for c in copies:
            c.wait_recv()

    def sent(self):
        for c in self.x + self.y + self.r + self.o + self.fx + self.fy + self.fd:
            c.wait_send()
        wait_all(self.local)

    def finish(self):
        self.arrive(self.o + self.fx + self.fy + self.fd)
        self.sent()


class Ring:
    def __init__(self, n, p, g, src, dst, ss, rs, ls=None):
        groups = n // GROUP
        to = lambda s: lax.rem(g + s, groups) * GROUP + p
        at = lambda s: lax.rem(g + s, groups)

        def cp(a, b, i, dev):
            return rcopy(a, b, ss.at[i], rs.at[i], dev)

        self.relays = []
        if groups == 4:
            self.up = [cp(src(h), dst(g, h), h, to(1)) for h in range(2)]
            self.down = [cp(src(h), dst(g, h), 2 + h, to(3)) for h in range(2)]
            self.first = [self.up[0], self.down[1], self.up[1], self.down[0]]
            below, above = at(3), at(1)
            self.relays = [cp(dst(below, 0), dst(below, 0), 4, to(1)), cp(dst(above, 1), dst(above, 1), 5, to(3))]
        else:
            self.first = [cp(src(None), dst(g, None), s - 1, to(s)) for s in range(1, groups)]
        self.local = [] if ls is None else [pltpu.make_async_copy(src(None), dst(g, None), ls)]

    def start(self):
        start_all(self.first + self.local)

    def relay(self):
        if self.relays:
            self.up[0].wait_recv()
            self.relays[0].start()
            self.down[1].wait_recv()
            self.relays[1].start()

    def finish(self):
        if self.relays:
            self.up[1].wait_recv()
            self.down[0].wait_recv()
            for c in self.first:
                c.wait_send()
        else:
            wait_all(self.first)
        wait_all(self.relays + self.local)


def ring_count(n):
    return max(6, n // GROUP - 1)


def halves(length, base=0):
    cut = length // 2
    part = (pl.ds(base, cut), pl.ds(base + cut, length - cut))
    return lambda h: pl.ds(base, length) if h is None else part[h]


class RingReduce:
    def __init__(self, n, p, g, part, low, high, send, fin, ss, rs):
        groups = n // GROUP
        to = lambda s: lax.rem(g + s, groups) * GROUP + p
        at = lambda s: lax.rem(g + s, groups)
        hs = halves(part.shape[1])
        self.part, self.fin, self.send, self.g, self.hs = part, fin, send, g, hs

        def cp(a, b, i, dev):
            return rcopy(a, b, ss.at[i], rs.at[i], dev)

        self.ring = groups == 4
        if self.ring:
            self.above, self.below = at(1), at(3)
            self.low, self.high = low, high
            far = at(2)
            self.a = cp(part.at[far, hs(0)], low, 0, to(1))
            self.b = cp(part.at[far, hs(1)], high, 1, to(3))
            self.c = cp(part.at[self.above, hs(1)], fin.at[0, hs(1)], 2, to(1))
            self.d = cp(part.at[self.below, hs(0)], fin.at[1, hs(0)], 3, to(3))
            self.e = cp(send.at[hs(0)], fin.at[0, hs(0)], 4, to(1))
            self.f = cp(send.at[hs(1)], fin.at[1, hs(1)], 5, to(3))
            self.all = [self.a, self.b, self.c, self.d, self.e, self.f]
        else:
            self.all = [cp(part.at[at(s)], fin.at[s - 1], s - 1, to(s)) for s in range(1, groups)]
        self.count = groups - 1

    def start(self):
        start_all(self.all[:4] if self.ring else self.all)

    def relay(self):
        if self.ring:
            for got, buf, h, b, out in (
                (self.a, self.low, 0, self.above, self.e),
                (self.b, self.high, 1, self.below, self.f),
            ):
                got.wait_recv()
                at = self.hs(h)
                self.send[at] = (self.part[b, at].astype(F32) + buf[...].astype(F32)).astype(BF16)
                out.start()

    def finish(self):
        for c in self.all[2:] if self.ring else self.all:
            c.wait_recv()
        val = self.part[self.g].astype(F32)
        for s in range(2 if self.ring else self.count):
            val = val + self.fin[s].astype(F32)
        for c in self.all:
            c.wait_send()
        return val


def ring_scratch(n, shape):
    cut = shape[0] // 2
    groups = n // GROUP
    count = 2 if groups == 4 else groups - 1
    tail = tuple(shape[1:])
    vm = lambda s: pltpu.VMEM(s, BF16)
    return [
        vm((max(cut, 1),) + tail),
        vm((shape[0] - cut,) + tail),
        vm(tuple(shape)),
        vm((count,) + tuple(shape)),
        DMA((ring_count(n),)),
        DMA((ring_count(n),)),
    ]


class PlaneReduce:
    def __init__(self, me, part, sib, send, relay, fx, fy, ss, rs, own=None):
        p = lax.rem(me, GROUP)
        self.own = own or (lambda i: part(p ^ (2 * i)))
        xn, yn = me ^ 2, me ^ 4
        hs = halves(sib.shape[1])
        self.hs, self.p, self.part = hs, p, part
        self.sib, self.send, self.relay, self.fx, self.fy = sib, send, relay, fx, fy

        def cp(a, b, i, dev):
            return rcopy(a, b, ss.at[i], rs.at[i], dev)

        self.first = [cp(part(p ^ (2 * i + 1)), sib.at[i], i, me ^ 1) for i in range(4)]
        self.diag = [cp(send.at[0, hs(0)], relay.at[0], 4, xn), cp(send.at[0, hs(1)], relay.at[1], 5, yn)]
        self.toy = [cp(send.at[2, hs(h)], fy.at[hs(h)], 6 + h, yn) for h in range(2)]
        self.tox = [cp(send.at[1, hs(h)], fx.at[hs(h)], 8 + h, xn) for h in range(2)]

    def start(self):
        start_all([self.first[i] for i in (3, 1, 2, 0)])

    def chip(self, i):
        self.first[i].wait_recv()
        return self.own(i)[...].astype(F32) + self.sib[i].astype(F32)

    def chip_d(self):
        self.send[0] = self.chip(3).astype(BF16)
        start_all(self.diag)

    def chip_x(self):
        self.send[1] = self.chip(1).astype(BF16)
        self.tox[0].start()

    def chip_y(self):
        self.send[2] = self.chip(2).astype(BF16)
        self.toy[1].start()

    def phase1(self):
        self.chip_d()
        self.chip_x()
        self.chip_y()

    def phase2(self):
        self.diag[0].wait_recv()
        at = self.hs(0)
        self.send[2, at] = (self.send[2, at].astype(F32) + self.relay[0].astype(F32)).astype(BF16)
        self.toy[0].start()
        self.diag[1].wait_recv()
        at = self.hs(1)
        self.send[1, at] = (self.send[1, at].astype(F32) + self.relay[1].astype(F32)).astype(BF16)
        self.tox[1].start()

    def phase3(self):
        own = self.chip(0)
        for c in self.toy + self.tox:
            c.wait_recv()
        own = own + self.fx[...].astype(F32) + self.fy[...].astype(F32)
        for c in self.first + self.diag + self.toy + self.tox:
            c.wait_send()
        return own


def plane_scratch(shape):
    tail = tuple(shape[1:])
    vm = lambda *s: pltpu.VMEM(s + tail, BF16)
    return [
        vm(4, shape[0]),
        vm(3, shape[0]),
        vm(2, shape[0] // 2),
        vm(shape[0]),
        vm(shape[0]),
        DMA((10,)),
        DMA((10,)),
    ]


def swap_halves(v):
    lane = lax.broadcasted_iota(jnp.int32, v.shape, 1)
    low = lax.rem(lane, HEAD) < HEAD // 2
    width = v.shape[1]
    return jnp.where(low, pltpu.roll(v, width - HEAD // 2, 1), pltpu.roll(v, HEAD // 2, 1))


def head_mean(v):
    row = lax.broadcasted_iota(jnp.int32, (128, 128), 0)
    lane = lax.broadcasted_iota(jnp.int32, (128, 128), 1)
    same = jnp.where((row < HEAD) == (lane < HEAD), 1.0 / HEAD, 0.0).astype(BF16)
    high = v.astype(BF16)
    low = (v - high.astype(F32)).astype(BF16)
    return nn(high, same) + nn(low, same)


def head_gains(g_ref):
    t = g_ref[:, 2 * D :]
    t = jnp.broadcast_to(t, (8, 128))
    lane = lax.broadcasted_iota(jnp.int32, (8, 128), 1)
    other = pltpu.roll(t, HEAD, 1)
    return jnp.where(lane < HEAD, t, other)[0:1, :], jnp.where(lane < HEAD, other, t)[0:1, :]


def seq_start(row, len_ref, g):
    e1 = len_ref[g, 0]
    e2 = e1 + len_ref[g, 1]
    e3 = e2 + len_ref[g, 2]
    zero = row * 0
    s = jnp.where(row >= e1, zero + e1, zero)
    s = jnp.where(row >= e2, zero + e2, s)
    return jnp.where(row >= e3, zero + e3, s)


def windows(i, window):
    for low, high, count in ((0, 1, 2), (2, 3, 4), (4, 7, WINDOW + 1)):

        @pl.when((i >= low) & (i <= high))
        def _():
            window(jnp.maximum(i - WINDOW, 0), count)


def front_kernel(n, len_ref, x_, wq_, wk_, wv_, wg_, wu_, wo_, wd_, gn_, dy_, h_o, raw_o, q_o, kv_o, mixf_o, lse_o, mixo, dyo, w21o, w22o, woo, wdo, wqkv_o, gvec, ct, st, xa, gn, wq, wk, wv, wo, wd, wg, wu, dy, a1, b1, b2, gt, gto, w1v, woz, wqkv, h_s, raw_s, q_s, kv_s, mixf_s, lse_s, mixs, k_s, v_s, acc, fs, ls, xs, xr, ds_, dr, os_, orr, ps, pr, zs, zr, ms, mr, outs):
    me, p, g, groups, zq, zg = places(n)
    fetch = bring(
        (
            (x_, xa.at[p]),
            (gn_, gn),
            (wq_, wq),
            (wk_, wk),
            (wv_, wv),
            (wo_, wo),
            (wd_.at[pl.ds(0, wd.shape[0])], wd),
            (wg_, wg),
            (wu_, wu),
            (dy_, dy),
        ),
        fs,
    )
    share = gn.shape[1]
    ffc = wg.shape[1] // (groups * GROUP)
    big = 5 * ffc // 9
    r = wq.shape[0]
    barrier([me ^ m for m in range(1, GROUP)] + zq)
    hx, ho = halves(BLOCK), halves(groups)
    xg = PlaneGather(me, p, lambda h: xa.at[p, hx(h)], lambda b, h: xa.at[b, hx(h)], xs, xr)
    dg = PlaneGather(me, p, lambda h: dy.at[hx(h)], lambda b, h: dyo.at[b, hx(h)], ds_, dr, ls.at[pl.ds(0, 2)])
    og = PlaneGather(me, p, lambda h: woz.at[ho(h)], lambda b, h: woo.at[ho(h), b], os_, orr, ls.at[pl.ds(2, 2)])
    def ring(k, src, dst, local=None):
        hk = halves(dst.shape[1])
        return Ring(n, p, g, lambda h: src.at[hk(h)], lambda b, h: dst.at[b, hk(h)], zs.at[k], zr.at[k], local)

    wring, gring = ring(0, w1v.at[g], w1v), ring(1, gto.at[g], gto)
    dring, oring = ring(2, wd, wdo, ls.at[4]), ring(3, wo, woz, ls.at[5])
    uring = ring(4, w21o.at[g], w21o)
    pc = {}

    def exchange(k, src, dst):
        for m in range(1, GROUP):
            pc[k, m] = rcopy(src(p ^ m), dst, ps.at[k, m - 1], pr.at[k, m - 1], me ^ m)
            pc[k, m].start()

    def arrived(k):
        for m in range(1, GROUP):
            pc[k, m].wait_recv()


    def pack(buf, low, high):
        for b in range(GROUP):
            at = [slice((GROUP * k + b) * ffc + low, (GROUP * k + b) * ffc + high) for k in range(groups)]
            buf[b] = jnp.concatenate([wg[:, k] for k in at] + [wu[:, k] for k in at], axis=1)

    fetch[0].wait()
    xg.start_first()
    fetch[1].wait()
    gt[...] = jnp.zeros_like(gt)
    gt[0:1, :share] = gn[...].astype(F32)
    gto[g, p] = gt[...]
    exchange(1, lambda b: gt, gto.at[g, p])
    wait_all(fetch[2:5])
    for b in range(GROUP):
        a1[b, :, :128] = wq[:, 128 * b : 128 * (b + 1)]
        at = slice(HEAD * b, HEAD * (b + 1))
        a1[b, :, 128:] = jnp.concatenate([wk[:, at], wv[:, at]], axis=1)
    exchange(0, lambda b: a1.at[b], w1v.at[g, p])
    w1v[g, p] = a1[p]
    fetch[5].wait()
    oring.start()
    fetch[6].wait()
    dring.start()
    wait_all(fetch[7:9])
    pack(b1, 0, big)
    exchange(2, lambda b: b1.at[b], w21o.at[g, p])
    local = start_all([pltpu.make_async_copy(b1.at[p], w21o.at[g, p], ls.at[6])])
    pack(b2, big, ffc)
    exchange(3, lambda b: b2.at[b], w22o.at[p])
    local += start_all([pltpu.make_async_copy(b2.at[p], w22o.at[p], ls.at[7])])
    xg.start_second()
    arrived(0)
    wring.start()
    arrived(1)
    gring.start()
    arrived(2)
    local[0].wait()
    uring.start()
    xg.relay1()
    row = lax.broadcasted_iota(jnp.int32, (1, ROWS), 1)
    position = (row - seq_start(row, len_ref, g)).astype(F32)
    index = lax.broadcasted_iota(jnp.int32, (HEAD // 2, 1), 0).astype(F32)
    angles = jnp.exp(index * (-2.0 * math.log(ROPE_THETA) / HEAD)) * position
    c, s = jnp.cos(angles).T, jnp.sin(angles).T
    ct[...] = jnp.concatenate([c, c, c, c], axis=1)
    st[...] = jnp.concatenate([-s, s, -s, s], axis=1)
    k_s[: WINDOW * BLOCK] = jnp.zeros((WINDOW * BLOCK, HEAD), BF16)
    v_s[: WINDOW * BLOCK] = jnp.zeros((WINDOW * BLOCK, 128), BF16)
    xg.relay2()
    fetch[9].wait()
    dg.start_first()
    for c in (wring, gring):
        c.relay()
    xg.relay3()
    dg.start_second()
    wring.finish()
    gring.finish()
    for k in range(groups * GROUP):
        wqkv[k * r : (k + 1) * r] = w1v[k // GROUP, k % GROUP]
    gvec[...] = jnp.concatenate(
        [gto[k, b, 0:1, :share] for k in range(groups) for b in range(GROUP)], axis=1
    )
    xg.arrive(xg.o + xg.fx + xg.fy + xg.fd)
    gq, gk = head_gains(gvec)
    results = ((h_s, h_o), (raw_s, raw_o), (q_s, q_o), (kv_s, kv_o), (mixf_s, mixf_o), (lse_s, lse_o))

    def block(i, carry):
        @pl.when(i == 0)
        def _():
            oring.relay()

        @pl.when(i == 1)
        def _():
            oring.finish()
            og.start_first()

        @pl.when(i == 2)
        def _():
            dg.relay1()
            og.start_second()

        @pl.when(i == 3)
        def _():
            uring.relay()

        @pl.when(i == 4)
        def _():
            dg.relay2()

        @pl.when(i == 5)
        def _():
            og.relay1()

        @pl.when(i == 6)
        def _():
            dg.relay3()
            dring.relay()

        @pl.when(i == 7)
        def _():
            og.relay2()

        at = pl.ds(pl.multiple_of(i * BLOCK, BLOCK), BLOCK)
        xb = xa[i].astype(F32)
        h = (xb * lax.rsqrt(jnp.mean(xb * xb, axis=-1, keepdims=True) + EPSILON) * gvec[:, :D]).astype(BF16)
        h_s[i] = h
        raw = nn(h, wqkv[...])
        raw_s[i] = raw
        cb, sb = ct[at, :], st[at, :]
        qraw, kvraw = raw[:, :128], raw[:, 128:]
        qn = qraw * lax.rsqrt(head_mean(qraw * qraw) + EPSILON) * gq
        q = (qn * cb + swap_halves(qn) * sb).astype(BF16)
        kn = kvraw * lax.rsqrt(head_mean(kvraw * kvraw) + EPSILON) * gk
        k = (kn * cb + swap_halves(kn) * sb).astype(BF16)
        lane = lax.broadcasted_iota(jnp.int32, (BLOCK, 128), 1)
        kv = jnp.where(lane < HEAD, k.astype(F32), kvraw).astype(BF16)
        q_s[i] = q
        kv_s[i] = kv
        k_s[at, :] = kv[:, :HEAD]
        v_s[at, :] = jnp.where(lane < HEAD, pltpu.roll(kvraw, HEAD, 1), 1.0).astype(BF16)
        q2 = jnp.concatenate([q[:, :HEAD], q[:, HEAD:]], axis=0)
        rows = lax.broadcasted_iota(jnp.int32, (2 * BLOCK, 1), 0)
        qrow = i * BLOCK + jnp.where(rows >= BLOCK, rows - BLOCK, rows)
        qstart = seq_start(qrow, len_ref, g)

        def window(first, count):
            span = pl.ds(pl.multiple_of(first * BLOCK, BLOCK), count * BLOCK)
            kc = lax.broadcasted_iota(jnp.int32, (2 * BLOCK, count * BLOCK), 1) + first * BLOCK
            ok = (kc >= qstart) & (kc <= qrow)
            e = jnp.where(ok, jnp.exp2(nt(q2, k_s[span, :]) * (SCALE * LOG2E)), 0.0).astype(BF16)
            acc[...] = nn(e, v_s[span, :])

        windows(i, window)
        total = acc[:, HEAD:]
        m = acc[:, :HEAD] / total
        both = jnp.concatenate([m[:BLOCK], m[BLOCK:]], axis=1)
        mixf_s[i] = both
        lse_s[i] = jnp.log2(total.T)[:8, :]
        mixs[i] = both.astype(BF16)

        @pl.when(i == p)
        def _():
            pltpu.make_async_copy(mixs.at[i], mixo.at[p], ls.at[8]).start()

        @pl.when(i != p)
        def _():
            rcopy(mixs.at[i], mixo.at[p], ms.at[p ^ i], mr.at[p ^ i], me ^ p ^ i).start()

        for k, (a, b) in enumerate(results):
            pltpu.make_async_copy(a.at[i], b.at[i], outs.at[k, i]).start()
        return carry

    lax.fori_loop(0, GROUP, block, 0)
    wq_out = pltpu.make_async_copy(wqkv, wqkv_o, ls.at[9])
    wq_out.start()
    og.relay3()
    for c in pc.values():
        c.wait_send()
    arrived(3)
    local[1].wait()
    for c in (dring, uring):
        c.finish()
    xg.sent()
    dg.finish()
    og.finish()
    for m in range(1, GROUP):
        rcopy(mixs.at[p ^ m], mixo.at[p], ms.at[m], mr.at[m], me ^ m).wait()
    pltpu.make_async_copy(mixs.at[p], mixo.at[p], ls.at[8]).wait()
    for k, (a, b) in enumerate(results):
        for i in range(GROUP):
            pltpu.make_async_copy(a.at[i], b.at[i], outs.at[k, i]).wait()
    wq_out.wait()


def front(n, lengths, x, wq, wk, wv, wg, wu, wo, wd, gn, dy):
    groups = n // GROUP
    r = wq.shape[0]
    wide = 2 * wg.shape[1] // GROUP
    wide1 = 5 * wide // 9
    wd1 = (5 * wd.shape[0] // 9,) + wd.shape[1:]
    vm = lambda *s: pltpu.VMEM(s, BF16)
    vf = lambda *s: pltpu.VMEM(s, F32)
    return pl.pallas_call(
        functools.partial(front_kernel, n),
        out_shape=(
            SDS((GROUP, BLOCK, D), BF16),
            SDS((GROUP, BLOCK, QKV), F32),
            SDS((GROUP, BLOCK, 128), BF16),
            SDS((GROUP, BLOCK, 128), BF16),
            SDS((GROUP, BLOCK, 128), F32),
            SDS((GROUP, 8, 2 * BLOCK), F32),
            SDS((GROUP, BLOCK, 128), BF16),
            SDS((GROUP, BLOCK, D), BF16),
            SDS((groups, GROUP, r, wide1), BF16),
            SDS((GROUP, r, wide - wide1), BF16),
            SDS((groups, GROUP) + wo.shape, BF16),
            SDS((groups,) + wd1, BF16),
            SDS((D, QKV), BF16),
            SDS((1, gn.shape[1] * n), F32),
            SDS((ROWS, 128), F32),
            SDS((ROWS, 128), F32),
        ),
        in_specs=[SM] + [HB] * 10,
        out_specs=(HB,) * 13 + (VM,) * 3,
        scratch_shapes=[vm(GROUP, BLOCK, D)]
        + [vm(*s) for s in (gn.shape, wq.shape, wk.shape, wv.shape, wo.shape, wd1, wg.shape, wu.shape, dy.shape)]
        + [
            vm(GROUP, r, QKV),
            vm(GROUP, r, wide1),
            vm(GROUP, r, wide - wide1),
            vf(8, 128),
            vf(groups, GROUP, 8, 128),
            vm(groups, GROUP, r, QKV),
            vm(groups, *wo.shape),
            vm(D, QKV),
            vm(GROUP, BLOCK, D),
            vf(GROUP, BLOCK, QKV),
            vm(GROUP, BLOCK, 128),
            vm(GROUP, BLOCK, 128),
            vf(GROUP, BLOCK, 128),
            vf(GROUP, 8, 2 * BLOCK),
            vm(GROUP, BLOCK, 128),
            vm(ROWS, HEAD),
            vm(ROWS, 128),
            vf(2 * BLOCK, 128),
            DMA((10,)),
            DMA((10,)),
            DMA((14,)),
            DMA((14,)),
            DMA((14,)),
            DMA((14,)),
            DMA((14,)),
            DMA((14,)),
            DMA((4, 7)),
            DMA((4, 7)),
            DMA((5, ring_count(n))),
            DMA((5, ring_count(n))),
            DMA((GROUP,)),
            DMA((GROUP,)),
            DMA((6, GROUP)),
        ],
        compiler_params=pltpu.CompilerParams(collective_id=1, has_side_effects=True, vmem_limit_bytes=VMEM_LIMIT),
        name="front",
    )(lengths, x, wq, wk, wv, wg, wu, wo, wd, gn, dy)


def norm_back(dyv, xv, gain):
    r = lax.rsqrt(jnp.mean(xv * xv, axis=-1, keepdims=True) + EPSILON)
    xr = xv * r
    gy = dyv * gain
    dx = r * (gy - xr * jnp.mean(gy * xr, axis=-1, keepdims=True))
    return dx, jnp.sum(dyv * xr, axis=0, keepdims=True)


def unit_grads(h, dyb, wgu, wd):
    f = wd.shape[0]
    gu = nn(h, wgu)
    da = nt(dyb, wd)
    gp, up = gu[:, :f], gu[:, f:]
    sig = 1.0 / (1.0 + jnp.exp(-gp))
    sg = gp * sig
    dg = (da * up * (sig * (1.0 + gp * (1.0 - sig)))).astype(BF16)
    return (sg * up).astype(BF16), jnp.concatenate([dg, (da * sg).astype(BF16)], axis=1)


def ffn_block_kernel(n, order, mix_, x_, wo_, g_ref, w21_, w22_, wd1_, wd2_, dy_, res, gmid, dgf, dwo, dmh, po, t21, dw22, dwd1, dwd2, x, wo, w21, dy, fs, mbuf, h2, h2t, w2v, w22, wdv, wds, dys, acts1, acts2, dgu1, dgu2, dw21, part, mown, stage, hs, hr, os_, qs, qr, zs, zr, *red_refs):
    me, p, g, groups, zq, zg = places(n)
    f1 = wd1_.shape[0]
    f2 = wds.shape[0] - f1
    fetch = bring(
        (
            (wd2_.at[pl.ds(wd2_.shape[0] - wdv.shape[1], wdv.shape[1])], wdv.at[g]),
            (w22_, w2v.at[g]),
            (mix_, mbuf),
            (x_, x),
            (wo_, wo),
            (w21_, w21),
            (wd1_, wds.at[pl.ds(0, f1)]),
            (dy_, dy),
        ),
        fs,
    )
    barrier([me ^ m for m in range(1, GROUP)] + zq)
    gf = g_ref.at[:, D : 2 * D]
    r = w2v.shape[2]

    def holder(q):
        s = 0
        for k in range(ROWS // SLOT):
            s = jnp.where(order[g, k] == q, k, s)
        return s

    hw, h8 = halves(wdv.shape[1]), halves(GROUP)
    wrings = [
        Ring(n, p, g, lambda h: w2v.at[g, h8(h)], lambda b, h: w2v.at[b, h8(h)], zs.at[0], zr.at[0]),
        Ring(n, p, g, lambda h: wdv.at[g, hw(h)], lambda b, h: wdv.at[b, hw(h)], zs.at[1], zr.at[1]),
    ]
    wait_all(fetch[:2])
    for c in wrings:
        c.start()
    wait_all(fetch[2:5])
    m = jnp.concatenate([mbuf[b] for b in range(GROUP)], axis=1)
    mown[...] = m
    z = x[...].astype(F32) + nn(m, wo[...])
    res[...] = z
    h2[p] = (z * lax.rsqrt(jnp.mean(z * z, axis=-1, keepdims=True) + EPSILON) * gf[...]).astype(BF16)
    hb = halves(BLOCK)
    hg = PlaneGather(me, p, lambda h: h2.at[p, hb(h)], lambda b, h: h2.at[b, hb(h)], hs, hr)
    red = PlaneReduce(me, lambda b: part.at[b], *red_refs[:7])
    ring21 = RingReduce(n, p, g, dw21, *red_refs[7:])
    hg.start_first()
    wait_all(fetch[5:])

    def first(t, carry):
        @pl.when(t == 1)
        def _():
            hg.start_second()
            hg.arrive(hg.o)

        @pl.when(t == 2)
        def _():
            hg.relay1()
            hg.relay2()

        @pl.when(t == 3)
        def _():
            hg.arrive(hg.fx)

        @pl.when(t == 4)
        def _():
            for c in wrings:
                c.relay()

        @pl.when(t == 5)
        def _():
            hg.arrive(hg.fy)

        @pl.when(t == 6)
        def _():
            hg.relay3()

        @pl.when(t == 7)
        def _():
            hg.arrive(hg.fd)

        b = p ^ t
        dys[b] = jnp.concatenate([dy[holder(2 * b)], dy[holder(2 * b + 1)]], axis=0)
        h2t[:, pl.ds(pl.multiple_of(b * BLOCK, BLOCK), BLOCK)] = h2[b].T
        acts1[b], dgu1[b] = unit_grads(h2[b], dys[b], w21[...], wds[:f1])
        part[b] = nt(dgu1[b], w21[...]).astype(BF16)
        return carry

    lax.fori_loop(0, GROUP, first, 0)
    grad1 = nn(h2t[...], dgu1[...].reshape(ROWS, 2 * f1)).astype(BF16)
    for k in range(groups * GROUP):
        dw21[k // GROUP, k % GROUP] = grad1[k * r : (k + 1) * r]
    ring21.start()
    for c in wrings:
        c.finish()
    for k in range(groups * GROUP):
        w22[k * r : (k + 1) * r] = w2v[k // GROUP, k % GROUP]
    each = f2 // groups
    for k in range(groups):
        wds[f1 + k * each : f1 + (k + 1) * each] = wdv[k].reshape(each, D)

    def second(t, carry):
        @pl.when(t == 1)
        def _():
            red.first[3].start()

        @pl.when(t == 3)
        def _():
            red.first[2].start()
            red.chip_d()

        @pl.when(t == 5)
        def _():
            red.first[1].start()
            red.chip_y()

        @pl.when(t == 7)
        def _():
            red.first[0].start()
            red.chip_x()

        b = p ^ (GROUP - 1 - t)
        acts2[b], dgu2[b] = unit_grads(h2[b], dys[b], w22[...], wds[f1:])
        part[b] = (part[b].astype(F32) + nt(dgu2[b], w22[...])).astype(BF16)
        return carry

    lax.fori_loop(0, GROUP, second, 0)
    dy_rows = dys[...].reshape(ROWS, D)
    for acts, out, rows in ((acts1, dwd1, f1), (acts2, dwd2, f2)):
        dw = tn(acts[...].reshape(ROWS, rows), dy_rows).astype(BF16)
        part_rows = rows // groups
        for k in range(groups):
            out[k] = dw[k * part_rows : (k + 1) * part_rows].reshape(out.shape[1:])
    red.phase2()
    ring21.relay()
    dw22[...] = nn(h2t[...], dgu2[...].reshape(ROWS, 2 * f2)).astype(BF16)
    dx, dgain = norm_back(red.phase3(), res[...], gf[...])
    gm = dys[p].astype(F32) + dx
    gmid[...] = gm
    dgf[...] = dgain
    gl = gm.astype(BF16)
    dm = nt(gl, wo[...]).astype(BF16)
    for b in range(GROUP):
        mbuf[b] = dm[:, 128 * b : 128 * (b + 1)]
    qc = start_all(
        [rcopy(mbuf.at[p ^ m], dmh.at[p], qs.at[m - 1], qr.at[m - 1], me ^ m) for m in range(1, GROUP)]
    )
    dmh[p] = mbuf[p]
    dwo[...] = tn(mown[...], gl).astype(BF16)

    def out(b, carry):
        slot = lax.rem(b, 2)

        @pl.when(b > 1)
        def _():
            pltpu.make_async_copy(stage.at[slot], po.at[b - 2], os_.at[slot]).wait()

        stage[slot] = (nn(acts1[b], wds[:f1]) + nn(acts2[b], wds[f1:])).astype(BF16)
        pltpu.make_async_copy(stage.at[slot], po.at[b], os_.at[slot]).start()
        return carry

    lax.fori_loop(0, GROUP, out, 0)
    for b in range(GROUP - 2, GROUP):
        pltpu.make_async_copy(stage.at[b % 2], po.at[b], os_.at[b % 2]).wait()
    wait_all(qc)
    hg.sent()
    t21[...] = ring21.finish().astype(BF16)


def ffn_block(n, order, mix, x, wo, gvec, w21, w22, wd1, wd, dy):
    groups = n // GROUP
    r = w22.shape[1]
    f1, f2 = w21.shape[1] // 2, w22.shape[2] // 2
    wd2 = (4 * wd.shape[0] // 9,) + wd.shape[1:]
    wd1_blk = (5 * wd.shape[0] // 9,) + wd.shape[1:]
    blk = (GROUP, r, 2 * f1)
    vm = lambda *s: pltpu.VMEM(s, BF16)
    return pl.pallas_call(
        functools.partial(ffn_block_kernel, n),
        out_shape=(
            SDS((BLOCK, D), F32),
            SDS((BLOCK, D), F32),
            SDS((1, D), F32),
            SDS((D, D), BF16),
            SDS((GROUP, BLOCK, 128), BF16),
            SDS((GROUP, BLOCK, D), BF16),
            SDS(blk, BF16),
            SDS((D, 2 * f2), BF16),
            SDS((groups,) + wd1_blk, BF16),
            SDS((groups,) + wd2, BF16),
        ),
        in_specs=[SM, HB, HB, HB, VM, HB, HB, HB, HB, HB],
        out_specs=(VM, VM, VM, VM, VM, HB, VM, VM, VM, VM),
        scratch_shapes=[
            vm(BLOCK, D),
            vm(D, D),
            vm(D, 2 * f1),
            vm(ROWS // SLOT, SLOT, D),
            DMA((8,)),
            vm(GROUP, BLOCK, 128),
            vm(GROUP, BLOCK, D),
            vm(D, ROWS),
            vm(groups, *w22.shape),
            vm(D, 2 * f2),
            vm(groups, *wd2),
            vm(f1 + f2, D),
            vm(GROUP, BLOCK, D),
            vm(GROUP, BLOCK, f1),
            vm(GROUP, BLOCK, f2),
            vm(GROUP, BLOCK, 2 * f1),
            vm(GROUP, BLOCK, 2 * f2),
            vm(groups, *blk),
            vm(GROUP, BLOCK, D),
            vm(BLOCK, D),
            vm(2, BLOCK, D),
            DMA((14,)),
            DMA((14,)),
            DMA((2,)),
            DMA((7,)),
            DMA((7,)),
            DMA((2, ring_count(n))),
            DMA((2, ring_count(n))),
        ]
        + plane_scratch((BLOCK, D))
        + ring_scratch(n, blk),
        compiler_params=pltpu.CompilerParams(collective_id=2, has_side_effects=True, vmem_limit_bytes=VMEM_LIMIT),
        name="ffn_block",
    )(order, mix, x, wo, gvec, w21, w22, wd1, wd, dy.reshape(ROWS // SLOT, SLOT, D))


def attn_bwd_kernel(n, len_ref, dm_ref, q_ref, kvall_ref, lse_ref, mixf_ref, h_ref, raw_ref, w_ref, g_ref, ct_ref, st_ref, po_, res_, dwo_, dw2_, dwd_, t21_, dgf, dh_ref, dw_ref, gpart, result, two, t2, od, o21, k_s, v_s, dkv, dqt, dws, dg_ref, es, er, po, res, dwo, dw2, dwd, t21, fs, *rest):
    step_id = pl.program_id(0)
    nb = ROWS // BLOCK
    i = nb - 1 - step_id
    me, p, g, groups, zq, zg = places(n)
    ored = PlaneReduce(me, lambda b: po.at[b], *rest[:7])
    wred = PlaneReduce(me, lambda b: dwo.at[:, b], *rest[7:14])
    ring2 = RingReduce(n, p, g, dw2, *rest[14:20])
    ringd = RingReduce(n, p, g, dwd, *rest[20:26])
    fetch = [
        pltpu.make_async_copy(a, b, fs.at[k])
        for k, (a, b) in enumerate(
            ((dwd_, dwd), (dw2_, dw2), (po_, po), (dwo_, dwo), (t21_, t21), (res_, res))
        )
    ]
    ex = [rcopy(t21.at[p ^ m], o21.at[p], es.at[m - 1], er.at[m - 1], me ^ m) for m in range(1, GROUP)]
    own_copy = pltpu.make_async_copy(t21.at[p], o21.at[p], fs.at[6])

    @pl.when(step_id == 0)
    def _():
        start_all(fetch)
        barrier([me ^ m for m in range(1, GROUP)] + zq)

    @pl.when(step_id == 1)
    def _():
        ored.phase1()
        wred.phase1()

    @pl.when(step_id == 3)
    def _():
        ringd.relay()
        ring2.relay()
        ored.phase2()

    @pl.when(step_id == 4)
    def _():
        wred.phase2()


    @pl.when(step_id == 0)
    def _():
        dkv[...] = jnp.zeros_like(dkv)
        dws[...] = jnp.zeros_like(dws)
        dg_ref[...] = jnp.zeros_like(dg_ref)
        for b in range(ROWS // BLOCK):
            kvb = kvall_ref[b]
            k_s[pl.ds(b * BLOCK, BLOCK), :] = kvb[:, :HEAD]
            v_s[pl.ds(b * BLOCK, BLOCK), :] = kvb[:, HEAD:]

    q, do, mf = q_ref[0], dm_ref[0], mixf_ref[0]
    q2 = jnp.concatenate([q[:, :HEAD], q[:, HEAD:]], axis=0)
    do2 = jnp.concatenate([do[:, :HEAD], do[:, HEAD:]], axis=0)
    prod = (do.astype(F32) * mf).T
    delta = jnp.concatenate(
        [jnp.sum(prod[:HEAD], axis=0, keepdims=True), jnp.sum(prod[HEAD:], axis=0, keepdims=True)], axis=1
    )
    lse = lse_ref[0, 0:1, :]
    colq = lax.broadcasted_iota(jnp.int32, (1, 2 * BLOCK), 1)
    qrow = i * BLOCK + jnp.where(colq >= BLOCK, colq - BLOCK, colq)
    qstart = seq_start(qrow, len_ref, g)

    def window(first, count):
        at = pl.ds(pl.multiple_of(first * BLOCK, BLOCK), count * BLOCK)
        kb, vb = k_s[at, :], v_s[at, :]
        kc = lax.broadcasted_iota(jnp.int32, (count * BLOCK, 2 * BLOCK), 0) + first * BLOCK
        ok = (kc >= qstart) & (kc <= qrow)
        pr = jnp.where(ok, jnp.exp2(nt(kb, q2) * (SCALE * LOG2E) - lse), 0.0)
        dsc = (pr * (nt(vb, do2) - delta)).astype(BF16)
        dkv[at, :HEAD] += nn(dsc, q2)
        dkv[at, HEAD:] += nn(pr.astype(BF16), do2)
        dqt[...] = tn(dsc, kb)

    windows(i, window)
    ct, st = ct_ref[...], st_ref[...]
    raw = raw_ref[0]
    dq = jnp.concatenate([dqt[:BLOCK], dqt[BLOCK:]], axis=1) * SCALE
    dkvb = dkv[pl.ds(pl.multiple_of(i * BLOCK, BLOCK), BLOCK), :]
    lane = lax.broadcasted_iota(jnp.int32, (BLOCK, 128), 1)

    def pull(d, v, gain):
        dn = d * ct - swap_halves(d) * st
        r = lax.rsqrt(head_mean(v * v) + EPSILON)
        vr = v * r
        gy = dn * gain
        return r * (gy - vr * head_mean(gy * vr)), jnp.sum(dn * vr, axis=0, keepdims=True)

    gq, gk = head_gains(g_ref)
    dqr, dgq = pull(dq, raw[:, :128], gq)
    dkr, dgk = pull(dkvb * SCALE, raw[:, 128:], gk)
    dg_ref[0:1, :] += dgq
    dg_ref[1:2, :] += dgk
    dqkv = jnp.concatenate([dqr, jnp.where(lane < HEAD, dkr, dkvb)], axis=1).astype(BF16)
    dh_ref[0] = nt(dqkv, w_ref[...]).astype(BF16)
    dws[...] += tn(h_ref[0], dqkv)

    @pl.when(step_id == 0)
    def _():
        wait_all(fetch)
        ringd.start()
        ring2.start()
        ored.start()
        wred.start()
        start_all(ex + [own_copy])

    @pl.when(step_id == nb - 1)
    def _():
        dw_ref[...] = dws[...].astype(BF16)
        result[...] = (ored.phase3() + res[...]).astype(BF16)
        two[...] = wred.phase3().astype(BF16)
        t2[...] = ring2.finish().astype(BF16)
        od[...] = ringd.finish()
        wait_all(ex + [own_copy])
        dga = lax.dot_general(
            jnp.ones((8, QKV), F32),
            w_ref[...].astype(F32) * dws[...],
            (((1,), (1,)), ((), ())),
            precision=lax.Precision.HIGHEST,
            preferred_element_type=F32,
        )
        dga = dga[0:1, :] / g_ref[:, :D]
        gpart[...] = jnp.zeros_like(gpart)
        for b in range(8):
            gpart[b : b + 1, :] = dga[:, 128 * b : 128 * (b + 1)]
            gpart[8 + b : 9 + b, :] = dgf[:, 128 * b : 128 * (b + 1)]
        turned = pltpu.roll(dg_ref[...], HEAD, 1)
        low = lax.broadcasted_iota(jnp.int32, (1, 128), 1) < HEAD
        gpart[16:17, :] = jnp.where(low, dg_ref[0:1, :] + turned[0:1, :], turned[1:2, :])


def attn_bwd(n, lengths, dmh, q, kv, lse, mixf, h, raw, wqkv, gvec, ct, st, po, res, dwo, dw2, dwd, t21, dgf):
    nb = ROWS // BLOCK
    groups = n // GROUP
    blk = lambda c: pl.BlockSpec((1, BLOCK, c), lambda i: (nb - 1 - i, 0, 0))
    whole = lambda s: pl.BlockSpec(s, lambda i: (0,) * len(s), pipeline_mode=pl.Buffered(1))
    return pl.pallas_call(
        functools.partial(attn_bwd_kernel, n),
        grid=(nb,),
        in_specs=[
            SM,
            blk(128),
            blk(128),
            whole((nb, BLOCK, 128)),
            pl.BlockSpec((1, 8, 2 * BLOCK), lambda i: (nb - 1 - i, 0, 0)),
            blk(128),
            blk(D),
            blk(QKV),
            whole((D, QKV)),
            whole(gvec.shape),
            pl.BlockSpec((BLOCK, 128), lambda i: (nb - 1 - i, 0)),
            pl.BlockSpec((BLOCK, 128), lambda i: (nb - 1 - i, 0)),
            HB,
            HB,
            HB,
            HB,
            HB,
            HB,
            whole(dgf.shape),
        ],
        out_specs=(
            blk(D),
            whole((D, QKV)),
            whole((24, 128)),
            whole((BLOCK, D)),
            whole((groups,) + dwo.shape[2:]),
            whole(dw2.shape[1:]),
            whole(dwd.shape[1:]),
            HB,
        ),
        out_shape=(
            SDS((nb, BLOCK, D), BF16),
            SDS((D, QKV), BF16),
            SDS((24, 128), F32),
            SDS((BLOCK, D), BF16),
            SDS((groups,) + dwo.shape[2:], BF16),
            SDS(dw2.shape[1:], BF16),
            SDS(dwd.shape[1:], F32),
            SDS(t21.shape, BF16),
        ),
        scratch_shapes=[
            pltpu.VMEM((ROWS, HEAD), BF16),
            pltpu.VMEM((ROWS, HEAD), BF16),
            pltpu.VMEM((ROWS, 128), F32),
            pltpu.VMEM((2 * BLOCK, HEAD), F32),
            pltpu.VMEM((D, QKV), F32),
            pltpu.VMEM((8, 128), F32),
            DMA((7,)),
            DMA((7,)),
        ]
        + [pltpu.VMEM(a.shape, a.dtype) for a in (po, res, dwo, dw2, dwd, t21)]
        + [DMA((7,))]
        + plane_scratch((BLOCK, D))
        + plane_scratch((groups,) + dwo.shape[2:])
        + ring_scratch(n, dw2.shape[1:])
        + ring_scratch(n, dwd.shape[1:]),
        compiler_params=pltpu.CompilerParams(
            collective_id=6, has_side_effects=True, dimension_semantics=("arbitrary",), vmem_limit_bytes=VMEM_LIMIT
        ),
        cost_estimate=pl.CostEstimate(flops=8 * 10**9, bytes_accessed=16 << 20, transcendentals=4 * 10**6),
        name="attn_bwd",
    )(lengths, dmh, q, kv, lse, mixf, h, raw, wqkv, gvec, ct, st, po, res, dwo, dw2, dwd, t21, dgf)


def final_kernel(n, dh, x_, gmid_, g_ref, dw1, two, t2, gpart, dwd, gtok, o1, o2, oo, og, od, mine, x, gmid, fs, t1, gin, gsum, gz, ps, pr, gs, gr, *rest):
    me, p, g, groups, zq, zg = places(n)
    nz = groups - 1
    share = g_ref.shape[1] // n
    fetch = bring([(dh.at[p ^ (2 * i)], mine.at[i]) for i in (3, 1, 2, 0)] + [(x_, x), (gmid_, gmid)], fs)
    barrier([me ^ m for m in range(1, GROUP)] + zq)
    red = PlaneReduce(me, lambda b: dh.at[b], *rest[:7], own=lambda i: mine.at[i])
    ring1 = RingReduce(n, p, g, dw1, *rest[7:13])
    ringo = RingReduce(n, p, g, two, *rest[13:19])
    ringd = RingReduce(n, p, g, dwd, *rest[19:25])
    red.start()
    gc = start_all([rcopy(gpart, gin.at[m - 1], gs.at[m - 1], gr.at[m - 1], me ^ m) for m in range(1, GROUP)])
    ring1.start()
    ringo.start()
    ringd.start()
    pc = []

    def exchange(k, src, out):
        for m in range(1, GROUP):
            c = rcopy(src.at[p ^ m], out.at[p], ps.at[k, m - 1], pr.at[k, m - 1], me ^ m)
            c.start()
            pc.append(c)
        out[p] = src[p]

    wait_all(fetch)
    red.phase1()
    exchange(1, t2, o2)
    tot = gpart[...]
    for m in range(1, GROUP):
        gc[m - 1].wait_recv()
        tot = tot + gin[m - 1]
    gsum[...] = tot
    gzc = start_all([rcopy(gsum, gz.at[s], gs.at[7 + s], gr.at[7 + s], zq[s]) for s in range(nz)])
    ring1.relay()
    ringo.relay()
    red.phase2()
    t1[...] = ring1.finish().astype(BF16)
    exchange(0, t1, o1)
    oo[...] = ringo.finish()
    ringd.relay()
    for s in range(nz):
        gzc[s].wait_recv()
        tot = tot + gz[s]
    gsum_row = me * share
    for c in gzc:
        c.wait_send()
    gsum[...] = tot
    first = gsum_row // 128
    off = lax.rem(gsum_row, 128)
    lane = lax.broadcasted_iota(jnp.int32, (8, 128), 1)
    turn = lambda row: pltpu.roll(jnp.broadcast_to(gsum[pl.ds(row, 1), :], (8, 128)), lax.rem(128 - off, 128), 1)
    og[...] = jnp.where(lane < 128 - off, turn(first), turn(first + 1))
    dx, _ = norm_back(red.phase3(), x[...].astype(F32), g_ref[:, :D])
    gtok[...] = gmid[...] + dx
    od[...] = ringd.finish()
    wait_all(pc)
    for c in gc:
        c.wait_send()


def final(n, dh, x, gmid, gvec, dw1, two, t2, gpart, dwd):
    groups = n // GROUP
    nz = groups - 1
    return pl.pallas_call(
        functools.partial(final_kernel, n),
        out_shape=(
            SDS((BLOCK, D), F32),
            SDS(dw1.shape[1:], BF16),
            SDS(t2.shape, BF16),
            SDS(two.shape[1:], F32),
            SDS((8, 128), F32),
            SDS(dwd.shape[1:], F32),
        ),
        in_specs=[HB, HB, HB] + [VM] * 6,
        out_specs=(VM,) * 6,
        scratch_shapes=[
            pltpu.VMEM((4, BLOCK, D), BF16),
            pltpu.VMEM(x.shape, BF16),
            pltpu.VMEM(gmid.shape, F32),
            DMA((6,)),
            pltpu.VMEM(dw1.shape[1:], BF16),
            pltpu.VMEM((7, 24, 128), F32),
            pltpu.VMEM((24, 128), F32),
            pltpu.VMEM((nz, 24, 128), F32),
            DMA((2, 7)),
            DMA((2, 7)),
            DMA((7 + nz,)),
            DMA((7 + nz,)),
        ]
        + plane_scratch((BLOCK, D))
        + ring_scratch(n, dw1.shape[1:])
        + ring_scratch(n, two.shape[1:])
        + ring_scratch(n, dwd.shape[1:]),
        compiler_params=pltpu.CompilerParams(collective_id=4, has_side_effects=True, vmem_limit_bytes=VMEM_LIMIT),
        name="final",
    )(dh, x, gmid, gvec, dw1, two, t2, gpart, dwd)


def unpack_kernel(groups, result, gtok, o1, o21, o22, oo, od, od2, og, result_o, gtok_o, gq, gk, gv, go, gg, gu, gd, gn):
    result_o[...] = result[...]
    gtok_o[...] = gtok[...]
    go[...] = oo[...]
    gd[: od.shape[0]] = od[...]
    gd[od.shape[0] :] = od2[...]
    gn[...] = og[0:1, : gn.shape[1]]
    for b in range(GROUP):
        gq[:, 128 * b : 128 * (b + 1)] = o1[b, :, :128].astype(F32)
    for out, at in ((gk, slice(128, 128 + HEAD)), (gv, slice(128 + HEAD, 256))):
        for c in range(GROUP // 2):
            pair = [o1[2 * c + k, :, at].astype(F32) for k in range(2)]
            out[:, 128 * c : 128 * (c + 1)] = jnp.concatenate(pair, axis=1)
    ffc = gg.shape[1] // (groups * GROUP)
    for k, out in enumerate((gg, gu)):
        big = 5 * ffc // 9
        piece = lambda src, b, c, w: src[b, :, (k * groups + c) * w : (k * groups + c + 1) * w].astype(F32)
        parts = [
            piece(src, b, c, w)
            for c in range(groups)
            for b in range(GROUP)
            for src, w in ((o21, big), (o22, ffc - big))
        ]
        out[...] = jnp.concatenate(parts, axis=1)


def unpack(n, result, gtok, o1, o21, o22, oo, od, od2, og, share):
    r = oo.shape[0]
    return pl.pallas_call(
        functools.partial(unpack_kernel, n // GROUP),
        out_shape=(
            SDS(result.shape, BF16),
            SDS(gtok.shape, F32),
            SDS((r, D), F32),
            SDS((r, D // 2), F32),
            SDS((r, D // 2), F32),
            SDS((r, D), F32),
            SDS((r, FF), F32),
            SDS((r, FF), F32),
            SDS((od.shape[0] + od2.shape[0], D), F32),
            SDS((1, share), F32),
        ),
        in_specs=[VM] * 9,
        out_specs=(VM,) * 10,
        compiler_params=pltpu.CompilerParams(vmem_limit_bytes=VMEM_LIMIT),
        name="unpack",
    )(result, gtok, o1, o21, o22, oo, od, od2, og)


def body(n, tokens, w_query, key_weight, w_value, w_out, w_gate, w_up, w_down, norm_gains, seq_lengths, slot_order, out_grad):
    groups = n // GROUP
    r = w_query.shape[0]
    ffc = w_down.shape[0]
    share = norm_gains.shape[0]
    wok = r // 16 if r % 16 == 0 else 1
    wdk = 9
    wo_blk, wd_blk = (wok, r // wok, D), (wdk, ffc // wdk, D)
    h, raw, q, kv, mixf, lse, mix, dy_all, w21, w22, wo, wd1, wqkv, gvec, ct, st = front(
        n,
        seq_lengths,
        tokens,
        w_query,
        key_weight,
        w_value,
        w_gate,
        w_up,
        w_out.reshape(wo_blk),
        w_down.reshape(wd_blk),
        norm_gains.reshape(1, share),
        out_grad,
    )
    res, gmid, dgf, dwo, dmh, po, t21, dw22, dwd1, dwd2 = ffn_block(
        n,
        slot_order,
        mix,
        tokens,
        wo.reshape(D, D),
        gvec,
        w21.reshape(D, -1),
        w22,
        wd1.reshape(-1, D),
        w_down.reshape(wd_blk),
        dy_all,
    )
    dh1, dwqkv, gpart, result, two, t2, od, o21 = attn_bwd(
        n,
        seq_lengths,
        dmh,
        q,
        kv,
        lse,
        mixf,
        h,
        raw,
        wqkv,
        gvec,
        ct,
        st,
        po,
        res,
        dwo.reshape(groups, GROUP, r, D),
        dw22.reshape(groups, GROUP, r, -1),
        dwd1,
        t21,
        dgf,
    )
    gtok, o1, o22, oo, og, od2 = final(
        n,
        dh1,
        tokens,
        gmid,
        gvec,
        dwqkv.reshape(groups, GROUP, r, QKV),
        two.reshape((groups,) + wo_blk),
        t2,
        gpart,
        dwd2,
    )
    outs = unpack(n, result, gtok, o1, o21, o22, oo.reshape(r, D), od.reshape(-1, D), od2.reshape(-1, D), og, share)
    return outs[:-1] + (outs[-1].reshape(share),)


def solution(mesh):
    n = mesh.shape["dp"]
    row = P("dp", None)
    return jax.shard_map(
        functools.partial(body, n),
        mesh=mesh,
        in_specs=(row,) * 8 + (P("dp"), P(), P(), row),
        out_specs=(row,) * 9 + (P("dp"),),
        check_vma=False,
    )
```

```python
import functools
import math

import jax
import jax.numpy as jnp
from jax import lax
from jax.experimental import pallas as pl
from jax.experimental.pallas import tpu as pltpu
from jax.sharding import PartitionSpec as P

D = 1024
FF = 4608
QUERY_HEADS = 16
KEY_VALUE_HEADS = 8
HEAD = 64
SLOT = 128
GROUP = 8
ROWS = 2048
BLOCK = 256
QKV = 256
WINDOW = 4
VMEM_LIMIT = 62 << 20
EPSILON = 1e-05
ROPE_THETA = 1000000.0
SCALE = 1.0 / math.sqrt(HEAD)
LOG2E = math.log2(math.e)
F32 = jnp.float32
BF16 = jnp.bfloat16
MESH = pl.DeviceIdType.MESH
DMA = pltpu.SemaphoreType.DMA
VM = pl.BlockSpec(memory_space=pltpu.VMEM)
ANY = pl.BlockSpec(memory_space=pl.ANY)
HB = pl.BlockSpec(memory_space=pltpu.HBM)
SM = pl.BlockSpec(memory_space=pltpu.SMEM)
SDS = jax.ShapeDtypeStruct


def nn(a, b):
    return lax.dot_general(a, b, (((1,), (0,)), ((), ())), preferred_element_type=F32)


def nt(a, b):
    return lax.dot_general(a, b, (((1,), (1,)), ((), ())), preferred_element_type=F32)


def tn(a, b):
    return lax.dot_general(a, b, (((0,), (0,)), ((), ())), preferred_element_type=F32)


def rcopy(src, dst, send, recv, dev):
    return pltpu.make_async_remote_copy(
        src_ref=src, dst_ref=dst, send_sem=send, recv_sem=recv, device_id=(dev,), device_id_type=MESH
    )


def barrier(peers):
    sem = pltpu.get_barrier_semaphore()
    for q in peers:
        pl.semaphore_signal(sem, inc=1, device_id=(q,), device_id_type=MESH)
    pl.semaphore_wait(sem, len(peers))


def places(n):
    me = lax.axis_index("dp")
    p = lax.rem(me, GROUP)
    g = me // GROUP
    groups = n // GROUP
    zq = [lax.rem(g + s, groups) * GROUP + p for s in range(1, groups)]
    zg = [lax.rem(g + s, groups) for s in range(1, groups)]
    return me, p, g, groups, zq, zg


def start_all(copies):
    for c in copies:
        c.start()
    return copies


def bring(pairs, sem):
    return start_all([pltpu.make_async_copy(a, b, sem.at[i]) for i, (a, b) in enumerate(pairs)])


def wait_all(copies):
    for c in copies:
        c.wait()


class PlaneGather:
    COPIES = 14

    def __init__(self, me, p, src, dst, ss, rs, ls=None):
        sib, xn, yn = me ^ 1, me ^ 2, me ^ 4

        def cp(a, b, i, dev):
            return rcopy(a, b, ss.at[i], rs.at[i], dev)

        def own(i, dev):
            return [cp(src(h), dst(p, h), i + h, dev) for h in range(2)]

        def on(m, h, i, dev):
            return cp(dst(p ^ m, h), dst(p ^ m, h), i, dev)

        self.x, self.y, self.o = own(0, xn), own(2, yn), own(4, sib)
        self.r = [on(2, 0, 6, yn), on(4, 1, 7, xn)]
        self.fx = [on(2, h, 8 + h, sib) for h in range(2)]
        self.fy = [on(4, h, 10 + h, sib) for h in range(2)]
        self.fd = [on(6, h, 12 + h, sib) for h in range(2)]
        self.local = [] if ls is None else [
            pltpu.make_async_copy(src(h), dst(p, h), ls.at[h]) for h in range(2)
        ]

    def start(self):
        self.start_first()
        self.start_second()

    def start_first(self):
        start_all([self.x[0], self.y[1]] + self.o + self.local)

    def start_second(self):
        start_all([self.x[1], self.y[0]])

    def relay1(self):
        self.x[0].wait_recv()
        start_all([self.r[0], self.fx[0]])
        self.y[1].wait_recv()
        start_all([self.r[1], self.fy[1]])

    def relay2(self):
        self.x[1].wait_recv()
        self.fx[1].start()
        self.y[0].wait_recv()
        self.fy[0].start()

    def relay3(self):
        for h in range(2):
            self.r[h].wait_recv()
            self.fd[h].start()

    def arrive(self, copies):
        for c in copies:
            c.wait_recv()

    def sent(self):
        for c in self.x + self.y + self.r + self.o + self.fx + self.fy + self.fd:
            c.wait_send()
        wait_all(self.local)

    def finish(self):
        self.arrive(self.o + self.fx + self.fy + self.fd)
        self.sent()


class Ring:
    def __init__(self, n, p, g, src, dst, ss, rs, ls=None):
        groups = n // GROUP
        to = lambda s: lax.rem(g + s, groups) * GROUP + p
        at = lambda s: lax.rem(g + s, groups)

        def cp(a, b, i, dev):
            return rcopy(a, b, ss.at[i], rs.at[i], dev)

        self.relays = []
        if groups == 4:
            self.up = [cp(src(h), dst(g, h), h, to(1)) for h in range(2)]
            self.down = [cp(src(h), dst(g, h), 2 + h, to(3)) for h in range(2)]
            self.first = [self.up[0], self.down[1], self.up[1], self.down[0]]
            below, above = at(3), at(1)
            self.relays = [cp(dst(below, 0), dst(below, 0), 4, to(1)), cp(dst(above, 1), dst(above, 1), 5, to(3))]
        else:
            self.first = [cp(src(None), dst(g, None), s - 1, to(s)) for s in range(1, groups)]
        self.local = [] if ls is None else [pltpu.make_async_copy(src(None), dst(g, None), ls)]

    def start(self):
        start_all(self.first + self.local)

    def relay(self):
        if self.relays:
            self.up[0].wait_recv()
            self.relays[0].start()
            self.down[1].wait_recv()
            self.relays[1].start()

    def finish(self):
        if self.relays:
            self.up[1].wait_recv()
            self.down[0].wait_recv()
            for c in self.first:
                c.wait_send()
        else:
            wait_all(self.first)
        wait_all(self.relays + self.local)


def ring_count(n):
    return max(6, n // GROUP - 1)


def halves(length, base=0):
    cut = length // 2
    part = (pl.ds(base, cut), pl.ds(base + cut, length - cut))
    return lambda h: pl.ds(base, length) if h is None else part[h]


class RingReduce:
    def __init__(self, n, p, g, part, low, high, send, fin, ss, rs):
        groups = n // GROUP
        to = lambda s: lax.rem(g + s, groups) * GROUP + p
        at = lambda s: lax.rem(g + s, groups)
        hs = halves(part.shape[1])
        self.part, self.fin, self.send, self.g, self.hs = part, fin, send, g, hs

        def cp(a, b, i, dev):
            return rcopy(a, b, ss.at[i], rs.at[i], dev)

        self.ring = groups == 4
        if self.ring:
            self.above, self.below = at(1), at(3)
            self.low, self.high = low, high
            far = at(2)
            self.a = cp(part.at[far, hs(0)], low, 0, to(1))
            self.b = cp(part.at[far, hs(1)], high, 1, to(3))
            self.c = cp(part.at[self.above, hs(1)], fin.at[0, hs(1)], 2, to(1))
            self.d = cp(part.at[self.below, hs(0)], fin.at[1, hs(0)], 3, to(3))
            self.e = cp(send.at[hs(0)], fin.at[0, hs(0)], 4, to(1))
            self.f = cp(send.at[hs(1)], fin.at[1, hs(1)], 5, to(3))
            self.all = [self.a, self.b, self.c, self.d, self.e, self.f]
        else:
            self.all = [cp(part.at[at(s)], fin.at[s - 1], s - 1, to(s)) for s in range(1, groups)]
        self.count = groups - 1

    def start(self):
        start_all(self.all[:4] if self.ring else self.all)

    def relay(self):
        if self.ring:
            for got, buf, h, b, out in (
                (self.a, self.low, 0, self.above, self.e),
                (self.b, self.high, 1, self.below, self.f),
            ):
                got.wait_recv()
                at = self.hs(h)
                self.send[at] = (self.part[b, at].astype(F32) + buf[...].astype(F32)).astype(BF16)
                out.start()

    def finish(self):
        for c in self.all[2:] if self.ring else self.all:
            c.wait_recv()
        val = self.part[self.g].astype(F32)
        for s in range(2 if self.ring else self.count):
            val = val + self.fin[s].astype(F32)
        for c in self.all:
            c.wait_send()
        return val


def ring_scratch(n, shape):
    cut = shape[0] // 2
    groups = n // GROUP
    count = 2 if groups == 4 else groups - 1
    tail = tuple(shape[1:])
    vm = lambda s: pltpu.VMEM(s, BF16)
    return [
        vm((max(cut, 1),) + tail),
        vm((shape[0] - cut,) + tail),
        vm(tuple(shape)),
        vm((count,) + tuple(shape)),
        DMA((ring_count(n),)),
        DMA((ring_count(n),)),
    ]


class PlaneReduce:
    def __init__(self, me, part, sib, send, relay, fx, fy, ss, rs, own=None):
        p = lax.rem(me, GROUP)
        self.own = own or (lambda i: part(p ^ (2 * i)))
        xn, yn = me ^ 2, me ^ 4
        hs = halves(sib.shape[1])
        self.hs, self.p, self.part = hs, p, part
        self.sib, self.send, self.relay, self.fx, self.fy = sib, send, relay, fx, fy

        def cp(a, b, i, dev):
            return rcopy(a, b, ss.at[i], rs.at[i], dev)

        self.first = [cp(part(p ^ (2 * i + 1)), sib.at[i], i, me ^ 1) for i in range(4)]
        self.diag = [cp(send.at[0, hs(0)], relay.at[0], 4, xn), cp(send.at[0, hs(1)], relay.at[1], 5, yn)]
        self.toy = [cp(send.at[2, hs(h)], fy.at[hs(h)], 6 + h, yn) for h in range(2)]
        self.tox = [cp(send.at[1, hs(h)], fx.at[hs(h)], 8 + h, xn) for h in range(2)]

    def start(self):
        start_all([self.first[i] for i in (3, 1, 2, 0)])

    def chip(self, i):
        self.first[i].wait_recv()
        return self.own(i)[...].astype(F32) + self.sib[i].astype(F32)

    def chip_d(self):
        self.send[0] = self.chip(3).astype(BF16)
        start_all(self.diag)

    def chip_x(self):
        self.send[1] = self.chip(1).astype(BF16)
        self.tox[0].start()

    def chip_y(self):
        self.send[2] = self.chip(2).astype(BF16)
        self.toy[1].start()

    def phase1(self):
        self.chip_d()
        self.chip_x()
        self.chip_y()

    def phase2(self):
        self.diag[0].wait_recv()
        at = self.hs(0)
        self.send[2, at] = (self.send[2, at].astype(F32) + self.relay[0].astype(F32)).astype(BF16)
        self.toy[0].start()
        self.diag[1].wait_recv()
        at = self.hs(1)
        self.send[1, at] = (self.send[1, at].astype(F32) + self.relay[1].astype(F32)).astype(BF16)
        self.tox[1].start()

    def phase3(self):
        own = self.chip(0)
        for c in self.toy + self.tox:
            c.wait_recv()
        own = own + self.fx[...].astype(F32) + self.fy[...].astype(F32)
        for c in self.first + self.diag + self.toy + self.tox:
            c.wait_send()
        return own


def plane_scratch(shape):
    tail = tuple(shape[1:])
    vm = lambda *s: pltpu.VMEM(s + tail, BF16)
    return [
        vm(4, shape[0]),
        vm(3, shape[0]),
        vm(2, shape[0] // 2),
        vm(shape[0]),
        vm(shape[0]),
        DMA((10,)),
        DMA((10,)),
    ]


def swap_halves(v):
    lane = lax.broadcasted_iota(jnp.int32, v.shape, 1)
    low = lax.rem(lane, HEAD) < HEAD // 2
    width = v.shape[1]
    return jnp.where(low, pltpu.roll(v, width - HEAD // 2, 1), pltpu.roll(v, HEAD // 2, 1))


def head_mean(v):
    row = lax.broadcasted_iota(jnp.int32, (128, 128), 0)
    lane = lax.broadcasted_iota(jnp.int32, (128, 128), 1)
    same = jnp.where((row < HEAD) == (lane < HEAD), 1.0 / HEAD, 0.0).astype(BF16)
    high = v.astype(BF16)
    low = (v - high.astype(F32)).astype(BF16)
    return nn(high, same) + nn(low, same)


def head_gains(g_ref):
    t = g_ref[:, 2 * D :]
    t = jnp.broadcast_to(t, (8, 128))
    lane = lax.broadcasted_iota(jnp.int32, (8, 128), 1)
    other = pltpu.roll(t, HEAD, 1)
    return jnp.where(lane < HEAD, t, other)[0:1, :], jnp.where(lane < HEAD, other, t)[0:1, :]


def seq_start(row, len_ref, g):
    e1 = len_ref[g, 0]
    e2 = e1 + len_ref[g, 1]
    e3 = e2 + len_ref[g, 2]
    zero = row * 0
    s = jnp.where(row >= e1, zero + e1, zero)
    s = jnp.where(row >= e2, zero + e2, s)
    return jnp.where(row >= e3, zero + e3, s)


def windows(i, window):
    for low, high, count in ((0, 1, 2), (2, 3, 4), (4, 7, WINDOW + 1)):

        @pl.when((i >= low) & (i <= high))
        def _():
            window(jnp.maximum(i - WINDOW, 0), count)


def front_kernel(n, len_ref, x_, wq_, wk_, wv_, wg_, wu_, wo_, wd_, gn_, dy_, h_o, raw_o, q_o, kv_o, mixf_o, lse_o, mixo, dyo, w21o, w22o, woo, wdo, wqkv_o, gvec, ct, st, xa, gn, wq, wk, wv, wo, wd, wg, wu, dy, a1, b1, b2, gt, gto, w1v, woz, wqkv, h_s, raw_s, q_s, kv_s, mixf_s, lse_s, mixs, k_s, v_s, acc, fs, ls, xs, xr, ds_, dr, os_, orr, ps, pr, zs, zr, ms, mr, outs):
    me, p, g, groups, zq, zg = places(n)
    fetch = bring(
        (
            (x_, xa.at[p]),
            (gn_, gn),
            (wq_, wq),
            (wk_, wk),
            (wv_, wv),
            (wo_, wo),
            (wd_.at[pl.ds(0, wd.shape[0])], wd),
            (wg_, wg),
            (wu_, wu),
            (dy_, dy),
        ),
        fs,
    )
    share = gn.shape[1]
    ffc = wg.shape[1] // (groups * GROUP)
    big = 5 * ffc // 9
    r = wq.shape[0]
    barrier([me ^ m for m in range(1, GROUP)] + zq)
    hx, ho = halves(BLOCK), halves(groups)
    xg = PlaneGather(me, p, lambda h: xa.at[p, hx(h)], lambda b, h: xa.at[b, hx(h)], xs, xr)
    dg = PlaneGather(me, p, lambda h: dy.at[hx(h)], lambda b, h: dyo.at[b, hx(h)], ds_, dr, ls.at[pl.ds(0, 2)])
    og = PlaneGather(me, p, lambda h: woz.at[ho(h)], lambda b, h: woo.at[ho(h), b], os_, orr, ls.at[pl.ds(2, 2)])
    def ring(k, src, dst, local=None):
        hk = halves(dst.shape[1])
        return Ring(n, p, g, lambda h: src.at[hk(h)], lambda b, h: dst.at[b, hk(h)], zs.at[k], zr.at[k], local)

    wring, gring = ring(0, w1v.at[g], w1v), ring(1, gto.at[g], gto)
    dring, oring = ring(2, wd, wdo, ls.at[4]), ring(3, wo, woz, ls.at[5])
    uring = ring(4, w21o.at[g], w21o)
    pc = {}

    def exchange(k, src, dst):
        for m in range(1, GROUP):
            pc[k, m] = rcopy(src(p ^ m), dst, ps.at[k, m - 1], pr.at[k, m - 1], me ^ m)
            pc[k, m].start()

    def arrived(k):
        for m in range(1, GROUP):
            pc[k, m].wait_recv()


    def pack(buf, low, high):
        for b in range(GROUP):
            at = [slice((GROUP * k + b) * ffc + low, (GROUP * k + b) * ffc + high) for k in range(groups)]
            buf[b] = jnp.concatenate([wg[:, k] for k in at] + [wu[:, k] for k in at], axis=1)

    fetch[0].wait()
    xg.start_first()
    fetch[1].wait()
    gt[...] = jnp.zeros_like(gt)
    gt[0:1, :share] = gn[...].astype(F32)
    gto[g, p] = gt[...]
    exchange(1, lambda b: gt, gto.at[g, p])
    wait_all(fetch[2:5])
    for b in range(GROUP):
        a1[b, :, :128] = wq[:, 128 * b : 128 * (b + 1)]
        at = slice(HEAD * b, HEAD * (b + 1))
        a1[b, :, 128:] = jnp.concatenate([wk[:, at], wv[:, at]], axis=1)
    exchange(0, lambda b: a1.at[b], w1v.at[g, p])
    w1v[g, p] = a1[p]
    fetch[5].wait()
    oring.start()
    fetch[6].wait()
    dring.start()
    wait_all(fetch[7:9])
    pack(b1, 0, big)
    exchange(2, lambda b: b1.at[b], w21o.at[g, p])
    local = start_all([pltpu.make_async_copy(b1.at[p], w21o.at[g, p], ls.at[6])])
    pack(b2, big, ffc)
    exchange(3, lambda b: b2.at[b], w22o.at[p])
    local += start_all([pltpu.make_async_copy(b2.at[p], w22o.at[p], ls.at[7])])
    xg.start_second()
    arrived(0)
    wring.start()
    arrived(1)
    gring.start()
    arrived(2)
    local[0].wait()
    uring.start()
    xg.relay1()
    fetch[9].wait()
    dg.start_first()
    row = lax.broadcasted_iota(jnp.int32, (1, ROWS), 1)
    position = (row - seq_start(row, len_ref, g)).astype(F32)
    index = lax.broadcasted_iota(jnp.int32, (HEAD // 2, 1), 0).astype(F32)
    angles = jnp.exp(index * (-2.0 * math.log(ROPE_THETA) / HEAD)) * position
    c, s = jnp.cos(angles).T, jnp.sin(angles).T
    ct[...] = jnp.concatenate([c, c, c, c], axis=1)
    st[...] = jnp.concatenate([-s, s, -s, s], axis=1)
    k_s[: WINDOW * BLOCK] = jnp.zeros((WINDOW * BLOCK, HEAD), BF16)
    v_s[: WINDOW * BLOCK] = jnp.zeros((WINDOW * BLOCK, 128), BF16)
    xg.relay2()
    for c in (wring, gring):
        c.relay()
    xg.relay3()
    dg.start_second()
    wring.finish()
    gring.finish()
    for k in range(groups * GROUP):
        wqkv[k * r : (k + 1) * r] = w1v[k // GROUP, k % GROUP]
    gvec[...] = jnp.concatenate(
        [gto[k, b, 0:1, :share] for k in range(groups) for b in range(GROUP)], axis=1
    )
    xg.arrive(xg.o + xg.fx + xg.fy + xg.fd)
    gq, gk = head_gains(gvec)
    results = ((h_s, h_o), (raw_s, raw_o), (q_s, q_o), (kv_s, kv_o), (mixf_s, mixf_o), (lse_s, lse_o))

    def block(i, carry):
        @pl.when(i == 0)
        def _():
            oring.relay()
            dg.relay1()

        @pl.when(i == 1)
        def _():
            oring.finish()
            og.start_first()

        @pl.when(i == 2)
        def _():
            og.start_second()

        @pl.when(i == 3)
        def _():
            uring.relay()
            dg.relay2()

        @pl.when(i == 5)
        def _():
            og.relay1()
            dg.relay3()

        @pl.when(i == 6)
        def _():
            dring.relay()

        @pl.when(i == 7)
        def _():
            og.relay2()

        at = pl.ds(pl.multiple_of(i * BLOCK, BLOCK), BLOCK)
        xb = xa[i].astype(F32)
        h = (xb * lax.rsqrt(jnp.mean(xb * xb, axis=-1, keepdims=True) + EPSILON) * gvec[:, :D]).astype(BF16)
        h_s[i] = h
        raw = nn(h, wqkv[...])
        raw_s[i] = raw
        cb, sb = ct[at, :], st[at, :]
        qraw, kvraw = raw[:, :128], raw[:, 128:]
        qn = qraw * lax.rsqrt(head_mean(qraw * qraw) + EPSILON) * gq
        q = (qn * cb + swap_halves(qn) * sb).astype(BF16)
        kn = kvraw * lax.rsqrt(head_mean(kvraw * kvraw) + EPSILON) * gk
        k = (kn * cb + swap_halves(kn) * sb).astype(BF16)
        lane = lax.broadcasted_iota(jnp.int32, (BLOCK, 128), 1)
        kv = jnp.where(lane < HEAD, k.astype(F32), kvraw).astype(BF16)
        q_s[i] = q
        kv_s[i] = kv
        k_s[at, :] = kv[:, :HEAD]
        v_s[at, :] = jnp.where(lane < HEAD, pltpu.roll(kvraw, HEAD, 1), 1.0).astype(BF16)
        q2 = jnp.concatenate([q[:, :HEAD], q[:, HEAD:]], axis=0)
        rows = lax.broadcasted_iota(jnp.int32, (2 * BLOCK, 1), 0)
        qrow = i * BLOCK + jnp.where(rows >= BLOCK, rows - BLOCK, rows)
        qstart = seq_start(qrow, len_ref, g)

        def window(first, count):
            span = pl.ds(pl.multiple_of(first * BLOCK, BLOCK), count * BLOCK)
            kc = lax.broadcasted_iota(jnp.int32, (2 * BLOCK, count * BLOCK), 1) + first * BLOCK
            ok = (kc >= qstart) & (kc <= qrow)
            e = jnp.where(ok, jnp.exp2(nt(q2, k_s[span, :]) * (SCALE * LOG2E)), 0.0).astype(BF16)
            acc[...] = nn(e, v_s[span, :])

        windows(i, window)
        total = acc[:, HEAD:]
        m = acc[:, :HEAD] / total
        both = jnp.concatenate([m[:BLOCK], m[BLOCK:]], axis=1)
        mixf_s[i] = both
        lse_s[i] = jnp.log2(total.T)[:8, :]
        mixs[i] = both.astype(BF16)

        @pl.when(i == p)
        def _():
            pltpu.make_async_copy(mixs.at[i], mixo.at[p], ls.at[8]).start()

        @pl.when(i != p)
        def _():
            rcopy(mixs.at[i], mixo.at[p], ms.at[p ^ i], mr.at[p ^ i], me ^ p ^ i).start()

        for k, (a, b) in enumerate(results):
            pltpu.make_async_copy(a.at[i], b.at[i], outs.at[k, i]).start()
        return carry

    lax.fori_loop(0, GROUP, block, 0)
    wq_out = pltpu.make_async_copy(wqkv, wqkv_o, ls.at[9])
    wq_out.start()
    og.relay3()
    for c in pc.values():
        c.wait_send()
    arrived(3)
    local[1].wait()
    for c in (dring, uring):
        c.finish()
    xg.sent()
    dg.finish()
    og.finish()
    for m in range(1, GROUP):
        rcopy(mixs.at[p ^ m], mixo.at[p], ms.at[m], mr.at[m], me ^ m).wait()
    pltpu.make_async_copy(mixs.at[p], mixo.at[p], ls.at[8]).wait()
    for k, (a, b) in enumerate(results):
        for i in range(GROUP):
            pltpu.make_async_copy(a.at[i], b.at[i], outs.at[k, i]).wait()
    wq_out.wait()


def front(n, lengths, x, wq, wk, wv, wg, wu, wo, wd, gn, dy):
    groups = n // GROUP
    r = wq.shape[0]
    wide = 2 * wg.shape[1] // GROUP
    wide1 = 5 * wide // 9
    wd1 = (5 * wd.shape[0] // 9,) + wd.shape[1:]
    vm = lambda *s: pltpu.VMEM(s, BF16)
    vf = lambda *s: pltpu.VMEM(s, F32)
    return pl.pallas_call(
        functools.partial(front_kernel, n),
        out_shape=(
            SDS((GROUP, BLOCK, D), BF16),
            SDS((GROUP, BLOCK, QKV), F32),
            SDS((GROUP, BLOCK, 128), BF16),
            SDS((GROUP, BLOCK, 128), BF16),
            SDS((GROUP, BLOCK, 128), F32),
            SDS((GROUP, 8, 2 * BLOCK), F32),
            SDS((GROUP, BLOCK, 128), BF16),
            SDS((GROUP, BLOCK, D), BF16),
            SDS((groups, GROUP, r, wide1), BF16),
            SDS((GROUP, r, wide - wide1), BF16),
            SDS((groups, GROUP) + wo.shape, BF16),
            SDS((groups,) + wd1, BF16),
            SDS((D, QKV), BF16),
            SDS((1, gn.shape[1] * n), F32),
            SDS((ROWS, 128), F32),
            SDS((ROWS, 128), F32),
        ),
        in_specs=[SM] + [HB] * 10,
        out_specs=(HB,) * 13 + (VM,) * 3,
        scratch_shapes=[vm(GROUP, BLOCK, D)]
        + [vm(*s) for s in (gn.shape, wq.shape, wk.shape, wv.shape, wo.shape, wd1, wg.shape, wu.shape, dy.shape)]
        + [
            vm(GROUP, r, QKV),
            vm(GROUP, r, wide1),
            vm(GROUP, r, wide - wide1),
            vf(8, 128),
            vf(groups, GROUP, 8, 128),
            vm(groups, GROUP, r, QKV),
            vm(groups, *wo.shape),
            vm(D, QKV),
            vm(GROUP, BLOCK, D),
            vf(GROUP, BLOCK, QKV),
            vm(GROUP, BLOCK, 128),
            vm(GROUP, BLOCK, 128),
            vf(GROUP, BLOCK, 128),
            vf(GROUP, 8, 2 * BLOCK),
            vm(GROUP, BLOCK, 128),
            vm(ROWS, HEAD),
            vm(ROWS, 128),
            vf(2 * BLOCK, 128),
            DMA((10,)),
            DMA((10,)),
            DMA((14,)),
            DMA((14,)),
            DMA((14,)),
            DMA((14,)),
            DMA((14,)),
            DMA((14,)),
            DMA((4, 7)),
            DMA((4, 7)),
            DMA((5, ring_count(n))),
            DMA((5, ring_count(n))),
            DMA((GROUP,)),
            DMA((GROUP,)),
            DMA((6, GROUP)),
        ],
        compiler_params=pltpu.CompilerParams(collective_id=1, has_side_effects=True, vmem_limit_bytes=VMEM_LIMIT),
        name="front",
    )(lengths, x, wq, wk, wv, wg, wu, wo, wd, gn, dy)


def norm_back(dyv, xv, gain):
    r = lax.rsqrt(jnp.mean(xv * xv, axis=-1, keepdims=True) + EPSILON)
    xr = xv * r
    gy = dyv * gain
    dx = r * (gy - xr * jnp.mean(gy * xr, axis=-1, keepdims=True))
    return dx, jnp.sum(dyv * xr, axis=0, keepdims=True)


def unit_grads(h, dyb, wgu, wd):
    f = wd.shape[0]
    gu = nn(h, wgu)
    da = nt(dyb, wd)
    gp, up = gu[:, :f], gu[:, f:]
    sig = 1.0 / (1.0 + jnp.exp(-gp))
    sg = gp * sig
    dg = (da * up * (sig * (1.0 + gp * (1.0 - sig)))).astype(BF16)
    return (sg * up).astype(BF16), jnp.concatenate([dg, (da * sg).astype(BF16)], axis=1)


def ffn_block_kernel(n, order, mix_, x_, wo_, g_ref, w21_, w22_, wd1_, wd2_, dy_, res_o, gmid_o, dgf, dwo_o, dmh, po, t21, dw22_o, dwd1_o, dwd2_o, res, gmid, dwo, dw22, dwd1, dwd2, sent, x, wo, w21, dy, fs, mbuf, h2, h2t, w2v, w22, wdv, wds, dys, acts1, acts2, dgu1, dgu2, dw21, part, mown, stage, hs, hr, os_, qs, qr, zs, zr, *red_refs):
    me, p, g, groups, zq, zg = places(n)
    f1 = wd1_.shape[0]
    f2 = wds.shape[0] - f1
    fetch = bring(
        (
            (wd2_.at[pl.ds(wd2_.shape[0] - wdv.shape[1], wdv.shape[1])], wdv.at[g]),
            (w22_, w2v.at[g]),
            (mix_, mbuf),
            (x_, x),
            (wo_, wo),
            (w21_, w21),
            (wd1_, wds.at[pl.ds(0, f1)]),
            (dy_, dy),
        ),
        fs,
    )
    barrier([me ^ m for m in range(1, GROUP)] + zq)
    gf = g_ref.at[:, D : 2 * D]
    r = w2v.shape[2]
    away = [
        pltpu.make_async_copy(a, b, sent.at[k])
        for k, (a, b) in enumerate(
            ((res, res_o), (gmid, gmid_o), (dwo, dwo_o), (dw22, dw22_o), (dwd1, dwd1_o), (dwd2, dwd2_o))
        )
    ]

    def holder(q):
        s = 0
        for k in range(ROWS // SLOT):
            s = jnp.where(order[g, k] == q, k, s)
        return s

    hw, h8 = halves(wdv.shape[1]), halves(GROUP)
    wrings = [
        Ring(n, p, g, lambda h: w2v.at[g, h8(h)], lambda b, h: w2v.at[b, h8(h)], zs.at[0], zr.at[0]),
        Ring(n, p, g, lambda h: wdv.at[g, hw(h)], lambda b, h: wdv.at[b, hw(h)], zs.at[1], zr.at[1]),
    ]
    wait_all(fetch[:2])
    for c in wrings:
        c.start()
    wait_all(fetch[2:5])
    m = jnp.concatenate([mbuf[b] for b in range(GROUP)], axis=1)
    mown[...] = m
    z = x[...].astype(F32) + nn(m, wo[...])
    res[...] = z
    away[0].start()
    h2[p] = (z * lax.rsqrt(jnp.mean(z * z, axis=-1, keepdims=True) + EPSILON) * gf[...]).astype(BF16)
    hb = halves(BLOCK)
    hg = PlaneGather(me, p, lambda h: h2.at[p, hb(h)], lambda b, h: h2.at[b, hb(h)], hs, hr)
    red = PlaneReduce(me, lambda b: part.at[b], *red_refs[:7])
    ring21 = RingReduce(n, p, g, dw21, *red_refs[7:])
    hg.start_first()
    wait_all(fetch[5:])

    def first(t, carry):
        @pl.when(t == 1)
        def _():
            hg.start_second()
            hg.arrive(hg.o)

        @pl.when(t == 2)
        def _():
            hg.relay1()
            hg.relay2()

        @pl.when(t == 3)
        def _():
            hg.arrive(hg.fx)

        @pl.when(t == 4)
        def _():
            for c in wrings:
                c.relay()

        @pl.when(t == 5)
        def _():
            hg.arrive(hg.fy)

        @pl.when(t == 6)
        def _():
            hg.relay3()

        @pl.when(t == 7)
        def _():
            hg.arrive(hg.fd)

        b = p ^ t
        dys[b] = jnp.concatenate([dy[holder(2 * b)], dy[holder(2 * b + 1)]], axis=0)
        h2t[:, pl.ds(pl.multiple_of(b * BLOCK, BLOCK), BLOCK)] = h2[b].T
        acts1[b], dgu1[b] = unit_grads(h2[b], dys[b], w21[...], wds[:f1])
        part[b] = nt(dgu1[b], w21[...]).astype(BF16)
        return carry

    lax.fori_loop(0, GROUP, first, 0)
    grad1 = nn(h2t[...], dgu1[...].reshape(ROWS, 2 * f1)).astype(BF16)
    for k in range(groups * GROUP):
        dw21[k // GROUP, k % GROUP] = grad1[k * r : (k + 1) * r]
    ring21.start()
    for c in wrings:
        c.finish()
    for k in range(groups * GROUP):
        w22[k * r : (k + 1) * r] = w2v[k // GROUP, k % GROUP]
    each = f2 // groups
    for k in range(groups):
        wds[f1 + k * each : f1 + (k + 1) * each] = wdv[k].reshape(each, D)

    def second(t, carry):
        @pl.when(t == 1)
        def _():
            red.first[3].start()

        @pl.when(t == 3)
        def _():
            red.first[2].start()
            red.chip_d()

        @pl.when(t == 5)
        def _():
            red.first[1].start()
            red.chip_y()

        @pl.when(t == 7)
        def _():
            red.first[0].start()
            red.chip_x()

        b = p ^ (GROUP - 1 - t)
        acts2[b], dgu2[b] = unit_grads(h2[b], dys[b], w22[...], wds[f1:])
        part[b] = (part[b].astype(F32) + nt(dgu2[b], w22[...])).astype(BF16)
        return carry

    lax.fori_loop(0, GROUP, second, 0)
    dy_rows = dys[...].reshape(ROWS, D)
    for acts, out, rows in ((acts1, dwd1, f1), (acts2, dwd2, f2)):
        dw = tn(acts[...].reshape(ROWS, rows), dy_rows).astype(BF16)
        part_rows = rows // groups
        for k in range(groups):
            out[k] = dw[k * part_rows : (k + 1) * part_rows].reshape(out.shape[1:])
    start_all(away[4:])
    red.phase2()
    ring21.relay()
    dw22[...] = nn(h2t[...], dgu2[...].reshape(ROWS, 2 * f2)).astype(BF16)
    away[3].start()
    dx, dgain = norm_back(red.phase3(), res[...], gf[...])
    gm = dys[p].astype(F32) + dx
    gmid[...] = gm
    away[1].start()
    dgf[...] = dgain
    gl = gm.astype(BF16)
    dm = nt(gl, wo[...]).astype(BF16)
    for b in range(GROUP):
        mbuf[b] = dm[:, 128 * b : 128 * (b + 1)]
    qc = start_all(
        [rcopy(mbuf.at[p ^ m], dmh.at[p], qs.at[m - 1], qr.at[m - 1], me ^ m) for m in range(1, GROUP)]
    )
    dmh[p] = mbuf[p]
    dwo[...] = tn(mown[...], gl).astype(BF16)
    away[2].start()

    def out(b, carry):
        slot = lax.rem(b, 2)

        @pl.when(b > 1)
        def _():
            pltpu.make_async_copy(stage.at[slot], po.at[b - 2], os_.at[slot]).wait()

        stage[slot] = (nn(acts1[b], wds[:f1]) + nn(acts2[b], wds[f1:])).astype(BF16)
        pltpu.make_async_copy(stage.at[slot], po.at[b], os_.at[slot]).start()
        return carry

    lax.fori_loop(0, GROUP, out, 0)
    for b in range(GROUP - 2, GROUP):
        pltpu.make_async_copy(stage.at[b % 2], po.at[b], os_.at[b % 2]).wait()
    wait_all(qc)
    hg.sent()
    t21[...] = ring21.finish().astype(BF16)
    wait_all(away)


def ffn_block(n, order, mix, x, wo, gvec, w21, w22, wd1, wd, dy):
    groups = n // GROUP
    r = w22.shape[1]
    f1, f2 = w21.shape[1] // 2, w22.shape[2] // 2
    wd2 = (4 * wd.shape[0] // 9,) + wd.shape[1:]
    wd1_blk = (5 * wd.shape[0] // 9,) + wd.shape[1:]
    blk = (GROUP, r, 2 * f1)
    vm = lambda *s: pltpu.VMEM(s, BF16)
    return pl.pallas_call(
        functools.partial(ffn_block_kernel, n),
        out_shape=(
            SDS((BLOCK, D), F32),
            SDS((BLOCK, D), F32),
            SDS((1, D), F32),
            SDS((D, D), BF16),
            SDS((GROUP, BLOCK, 128), BF16),
            SDS((GROUP, BLOCK, D), BF16),
            SDS(blk, BF16),
            SDS((D, 2 * f2), BF16),
            SDS((groups,) + wd1_blk, BF16),
            SDS((groups,) + wd2, BF16),
        ),
        in_specs=[SM, HB, HB, HB, VM, HB, HB, HB, HB, HB],
        out_specs=(HB, HB, VM, HB, VM, HB, VM, HB, HB, HB),
        scratch_shapes=[
            pltpu.VMEM((BLOCK, D), F32),
            pltpu.VMEM((BLOCK, D), F32),
            vm(D, D),
            vm(D, 2 * f2),
            vm(groups, *wd1_blk),
            vm(groups, *wd2),
            DMA((6,)),
            vm(BLOCK, D),
            vm(D, D),
            vm(D, 2 * f1),
            vm(ROWS // SLOT, SLOT, D),
            DMA((8,)),
            vm(GROUP, BLOCK, 128),
            vm(GROUP, BLOCK, D),
            vm(D, ROWS),
            vm(groups, *w22.shape),
            vm(D, 2 * f2),
            vm(groups, *wd2),
            vm(f1 + f2, D),
            vm(GROUP, BLOCK, D),
            vm(GROUP, BLOCK, f1),
            vm(GROUP, BLOCK, f2),
            vm(GROUP, BLOCK, 2 * f1),
            vm(GROUP, BLOCK, 2 * f2),
            vm(groups, *blk),
            vm(GROUP, BLOCK, D),
            vm(BLOCK, D),
            vm(2, BLOCK, D),
            DMA((14,)),
            DMA((14,)),
            DMA((2,)),
            DMA((7,)),
            DMA((7,)),
            DMA((2, ring_count(n))),
            DMA((2, ring_count(n))),
        ]
        + plane_scratch((BLOCK, D))
        + ring_scratch(n, blk),
        compiler_params=pltpu.CompilerParams(collective_id=2, has_side_effects=True, vmem_limit_bytes=VMEM_LIMIT),
        name="ffn_block",
    )(order, mix, x, wo, gvec, w21, w22, wd1, wd, dy.reshape(ROWS // SLOT, SLOT, D))


def attn_bwd_kernel(n, len_ref, dm_ref, q_ref, kvall_ref, lse_ref, mixf_ref, h_ref, raw_ref, w_ref, g_ref, ct_ref, st_ref, po_, res_, dwo_, dw2_, dwd_, t21_, dgf, dh_ref, dw_ref, gpart, result, two, t2, od, o21, k_s, v_s, dk_s, dv_s, dqt, dws, dg_ref, es, er, po, res, dwo, dw2, dwd, t21, fs, *rest):
    step_id = pl.program_id(0)
    nb = ROWS // BLOCK
    i = nb - 1 - step_id
    me, p, g, groups, zq, zg = places(n)
    ored = PlaneReduce(me, lambda b: po.at[b], *rest[:7])
    wred = PlaneReduce(me, lambda b: dwo.at[:, b], *rest[7:14])
    ring2 = RingReduce(n, p, g, dw2, *rest[14:20])
    ringd = RingReduce(n, p, g, dwd, *rest[20:26])
    fetch = [
        pltpu.make_async_copy(a, b, fs.at[k])
        for k, (a, b) in enumerate(
            ((dwd_, dwd), (dw2_, dw2), (po_, po), (dwo_, dwo), (t21_, t21), (res_, res))
        )
    ]
    ex = [rcopy(t21.at[p ^ m], o21.at[p], es.at[m - 1], er.at[m - 1], me ^ m) for m in range(1, GROUP)]
    own_copy = pltpu.make_async_copy(t21.at[p], o21.at[p], fs.at[6])

    @pl.when(step_id == 0)
    def _():
        start_all(fetch)
        barrier([me ^ m for m in range(1, GROUP)] + zq)

    @pl.when(step_id == 1)
    def _():
        ored.phase1()
        wred.phase1()

    @pl.when(step_id == 3)
    def _():
        ringd.relay()
        ring2.relay()
        ored.phase2()

    @pl.when(step_id == 4)
    def _():
        wred.phase2()


    @pl.when(step_id == 0)
    def _():
        dk_s[...] = jnp.zeros_like(dk_s)
        dv_s[...] = jnp.zeros_like(dv_s)
        dws[...] = jnp.zeros_like(dws)
        dg_ref[...] = jnp.zeros_like(dg_ref)
        for b in range(ROWS // BLOCK):
            kvb = kvall_ref[b]
            k_s[pl.ds(b * BLOCK, BLOCK), :] = kvb[:, :HEAD]
            v_s[pl.ds(b * BLOCK, BLOCK), :] = kvb[:, HEAD:]

    q, do, mf = q_ref[0], dm_ref[0], mixf_ref[0]
    q2 = jnp.concatenate([q[:, :HEAD], q[:, HEAD:]], axis=0)
    do2 = jnp.concatenate([do[:, :HEAD], do[:, HEAD:]], axis=0)
    prod = (do.astype(F32) * mf).T
    delta = jnp.concatenate(
        [jnp.sum(prod[:HEAD], axis=0, keepdims=True), jnp.sum(prod[HEAD:], axis=0, keepdims=True)], axis=1
    )
    lse = lse_ref[0, 0:1, :]
    colq = lax.broadcasted_iota(jnp.int32, (1, 2 * BLOCK), 1)
    qrow = i * BLOCK + jnp.where(colq >= BLOCK, colq - BLOCK, colq)
    qstart = seq_start(qrow, len_ref, g)

    def window(first, count):
        at = pl.ds(pl.multiple_of(first * BLOCK, BLOCK), count * BLOCK)
        kb, vb = k_s[at, :], v_s[at, :]
        kc = lax.broadcasted_iota(jnp.int32, (count * BLOCK, 2 * BLOCK), 0) + first * BLOCK
        ok = (kc >= qstart) & (kc <= qrow)
        pr = jnp.where(ok, jnp.exp2(nt(kb, q2) * (SCALE * LOG2E) - lse), 0.0)
        dsc = (pr * (nt(vb, do2) - delta)).astype(BF16)
        dk_s[at, :] += nn(dsc, q2)
        dv_s[at, :] += nn(pr.astype(BF16), do2)
        dqt[...] = tn(dsc, kb)

    windows(i, window)
    ct, st = ct_ref[...], st_ref[...]
    raw = raw_ref[0]
    dq = jnp.concatenate([dqt[:BLOCK], dqt[BLOCK:]], axis=1) * SCALE
    here = pl.ds(pl.multiple_of(i * BLOCK, BLOCK), BLOCK)
    dkvb = jnp.concatenate([dk_s[here, :], dv_s[here, :]], axis=1)
    lane = lax.broadcasted_iota(jnp.int32, (BLOCK, 128), 1)

    def pull(d, v, gain):
        dn = d * ct - swap_halves(d) * st
        r = lax.rsqrt(head_mean(v * v) + EPSILON)
        vr = v * r
        gy = dn * gain
        return r * (gy - vr * head_mean(gy * vr)), jnp.sum(dn * vr, axis=0, keepdims=True)

    gq, gk = head_gains(g_ref)
    dqr, dgq = pull(dq, raw[:, :128], gq)
    dkr, dgk = pull(dkvb * SCALE, raw[:, 128:], gk)
    dg_ref[0:1, :] += dgq
    dg_ref[1:2, :] += dgk
    dqkv = jnp.concatenate([dqr, jnp.where(lane < HEAD, dkr, dkvb)], axis=1).astype(BF16)
    dh_ref[0] = nt(dqkv, w_ref[...]).astype(BF16)
    dws[...] += tn(h_ref[0], dqkv)

    @pl.when(step_id == 0)
    def _():
        wait_all(fetch)
        ringd.start()
        ring2.start()
        ored.start()
        wred.start()
        start_all(ex + [own_copy])

    @pl.when(step_id == nb - 1)
    def _():
        dw_ref[...] = dws[...].astype(BF16)
        result[...] = (ored.phase3() + res[...]).astype(BF16)
        two[...] = wred.phase3().astype(BF16)
        t2[...] = ring2.finish().astype(BF16)
        od[...] = ringd.finish()
        wait_all(ex + [own_copy])
        dga = lax.dot_general(
            jnp.ones((8, QKV), F32),
            w_ref[...].astype(F32) * dws[...],
            (((1,), (1,)), ((), ())),
            precision=lax.Precision.HIGHEST,
            preferred_element_type=F32,
        )
        dga = dga[0:1, :] / g_ref[:, :D]
        gpart[...] = jnp.zeros_like(gpart)
        for b in range(8):
            gpart[b : b + 1, :] = dga[:, 128 * b : 128 * (b + 1)]
            gpart[8 + b : 9 + b, :] = dgf[:, 128 * b : 128 * (b + 1)]
        turned = pltpu.roll(dg_ref[...], HEAD, 1)
        low = lax.broadcasted_iota(jnp.int32, (1, 128), 1) < HEAD
        gpart[16:17, :] = jnp.where(low, dg_ref[0:1, :] + turned[0:1, :], turned[1:2, :])


def attn_bwd(n, lengths, dmh, q, kv, lse, mixf, h, raw, wqkv, gvec, ct, st, po, res, dwo, dw2, dwd, t21, dgf):
    nb = ROWS // BLOCK
    groups = n // GROUP
    blk = lambda c: pl.BlockSpec((1, BLOCK, c), lambda i: (nb - 1 - i, 0, 0))
    whole = lambda s: pl.BlockSpec(s, lambda i: (0,) * len(s), pipeline_mode=pl.Buffered(1))
    return pl.pallas_call(
        functools.partial(attn_bwd_kernel, n),
        grid=(nb,),
        in_specs=[
            SM,
            blk(128),
            blk(128),
            whole((nb, BLOCK, 128)),
            pl.BlockSpec((1, 8, 2 * BLOCK), lambda i: (nb - 1 - i, 0, 0)),
            blk(128),
            blk(D),
            blk(QKV),
            whole((D, QKV)),
            whole(gvec.shape),
            pl.BlockSpec((BLOCK, 128), lambda i: (nb - 1 - i, 0)),
            pl.BlockSpec((BLOCK, 128), lambda i: (nb - 1 - i, 0)),
            HB,
            HB,
            HB,
            HB,
            HB,
            HB,
            whole(dgf.shape),
        ],
        out_specs=(
            blk(D),
            whole((D, QKV)),
            whole((24, 128)),
            whole((BLOCK, D)),
            whole((groups,) + dwo.shape[2:]),
            whole(dw2.shape[1:]),
            whole(dwd.shape[1:]),
            HB,
        ),
        out_shape=(
            SDS((nb, BLOCK, D), BF16),
            SDS((D, QKV), BF16),
            SDS((24, 128), F32),
            SDS((BLOCK, D), BF16),
            SDS((groups,) + dwo.shape[2:], BF16),
            SDS(dw2.shape[1:], BF16),
            SDS(dwd.shape[1:], F32),
            SDS(t21.shape, BF16),
        ),
        scratch_shapes=[
            pltpu.VMEM((ROWS, HEAD), BF16),
            pltpu.VMEM((ROWS, HEAD), BF16),
            pltpu.VMEM((ROWS, HEAD), F32),
            pltpu.VMEM((ROWS, HEAD), F32),
            pltpu.VMEM((2 * BLOCK, HEAD), F32),
            pltpu.VMEM((D, QKV), F32),
            pltpu.VMEM((8, 128), F32),
            DMA((7,)),
            DMA((7,)),
        ]
        + [pltpu.VMEM(a.shape, a.dtype) for a in (po, res, dwo, dw2, dwd, t21)]
        + [DMA((7,))]
        + plane_scratch((BLOCK, D))
        + plane_scratch((groups,) + dwo.shape[2:])
        + ring_scratch(n, dw2.shape[1:])
        + ring_scratch(n, dwd.shape[1:]),
        compiler_params=pltpu.CompilerParams(
            collective_id=6, has_side_effects=True, dimension_semantics=("arbitrary",), vmem_limit_bytes=VMEM_LIMIT
        ),
        cost_estimate=pl.CostEstimate(flops=8 * 10**9, bytes_accessed=16 << 20, transcendentals=4 * 10**6),
        name="attn_bwd",
    )(lengths, dmh, q, kv, lse, mixf, h, raw, wqkv, gvec, ct, st, po, res, dwo, dw2, dwd, t21, dgf)


def final_kernel(n, dh, x_, gmid_, g_ref, dw1, two, t2, gpart, dwd, gtok, o1, o2, oo, og, od, mine, x, gmid, fs, t1, gin, gsum, gz, ps, pr, gs, gr, *rest):
    me, p, g, groups, zq, zg = places(n)
    nz = groups - 1
    share = g_ref.shape[1] // n
    fetch = bring([(dh.at[p ^ (2 * i)], mine.at[i]) for i in (3, 1, 2, 0)] + [(x_, x), (gmid_, gmid)], fs)
    barrier([me ^ m for m in range(1, GROUP)] + zq)
    red = PlaneReduce(me, lambda b: dh.at[b], *rest[:7], own=lambda i: mine.at[i])
    ring1 = RingReduce(n, p, g, dw1, *rest[7:13])
    ringo = RingReduce(n, p, g, two, *rest[13:19])
    ringd = RingReduce(n, p, g, dwd, *rest[19:25])
    red.start()
    gc = start_all([rcopy(gpart, gin.at[m - 1], gs.at[m - 1], gr.at[m - 1], me ^ m) for m in range(1, GROUP)])
    ring1.start()
    ringo.start()
    ringd.start()
    pc = []

    def exchange(k, src, out):
        for m in range(1, GROUP):
            c = rcopy(src.at[p ^ m], out.at[p], ps.at[k, m - 1], pr.at[k, m - 1], me ^ m)
            c.start()
            pc.append(c)
        out[p] = src[p]

    wait_all(fetch)
    red.phase1()
    exchange(1, t2, o2)
    tot = gpart[...]
    for m in range(1, GROUP):
        gc[m - 1].wait_recv()
        tot = tot + gin[m - 1]
    gsum[...] = tot
    gzc = start_all([rcopy(gsum, gz.at[s], gs.at[7 + s], gr.at[7 + s], zq[s]) for s in range(nz)])
    ring1.relay()
    ringo.relay()
    red.phase2()
    t1[...] = ring1.finish().astype(BF16)
    exchange(0, t1, o1)
    oo[...] = ringo.finish()
    ringd.relay()
    for s in range(nz):
        gzc[s].wait_recv()
        tot = tot + gz[s]
    gsum_row = me * share
    for c in gzc:
        c.wait_send()
    gsum[...] = tot
    first = gsum_row // 128
    off = lax.rem(gsum_row, 128)
    lane = lax.broadcasted_iota(jnp.int32, (8, 128), 1)
    turn = lambda row: pltpu.roll(jnp.broadcast_to(gsum[pl.ds(row, 1), :], (8, 128)), lax.rem(128 - off, 128), 1)
    og[...] = jnp.where(lane < 128 - off, turn(first), turn(first + 1))
    dx, _ = norm_back(red.phase3(), x[...].astype(F32), g_ref[:, :D])
    gtok[...] = gmid[...] + dx
    od[...] = ringd.finish()
    wait_all(pc)
    for c in gc:
        c.wait_send()


def final(n, dh, x, gmid, gvec, dw1, two, t2, gpart, dwd):
    groups = n // GROUP
    nz = groups - 1
    return pl.pallas_call(
        functools.partial(final_kernel, n),
        out_shape=(
            SDS((BLOCK, D), F32),
            SDS(dw1.shape[1:], BF16),
            SDS(t2.shape, BF16),
            SDS(two.shape[1:], F32),
            SDS((8, 128), F32),
            SDS(dwd.shape[1:], F32),
        ),
        in_specs=[HB, HB, HB] + [VM] * 6,
        out_specs=(VM,) * 6,
        scratch_shapes=[
            pltpu.VMEM((4, BLOCK, D), BF16),
            pltpu.VMEM(x.shape, BF16),
            pltpu.VMEM(gmid.shape, F32),
            DMA((6,)),
            pltpu.VMEM(dw1.shape[1:], BF16),
            pltpu.VMEM((7, 24, 128), F32),
            pltpu.VMEM((24, 128), F32),
            pltpu.VMEM((nz, 24, 128), F32),
            DMA((2, 7)),
            DMA((2, 7)),
            DMA((7 + nz,)),
            DMA((7 + nz,)),
        ]
        + plane_scratch((BLOCK, D))
        + ring_scratch(n, dw1.shape[1:])
        + ring_scratch(n, two.shape[1:])
        + ring_scratch(n, dwd.shape[1:]),
        compiler_params=pltpu.CompilerParams(collective_id=4, has_side_effects=True, vmem_limit_bytes=VMEM_LIMIT),
        name="final",
    )(dh, x, gmid, gvec, dw1, two, t2, gpart, dwd)


def unpack_kernel(groups, result, gtok, o1, o21, o22, oo, od, od2, og, result_o, gtok_o, gq, gk, gv, go, gg, gu, gd, gn):
    result_o[...] = result[...]
    gtok_o[...] = gtok[...]
    go[...] = oo[...]
    gd[: od.shape[0]] = od[...]
    gd[od.shape[0] :] = od2[...]
    gn[...] = og[0:1, : gn.shape[1]]
    for b in range(GROUP):
        gq[:, 128 * b : 128 * (b + 1)] = o1[b, :, :128].astype(F32)
    for out, at in ((gk, slice(128, 128 + HEAD)), (gv, slice(128 + HEAD, 256))):
        for c in range(GROUP // 2):
            pair = [o1[2 * c + k, :, at].astype(F32) for k in range(2)]
            out[:, 128 * c : 128 * (c + 1)] = jnp.concatenate(pair, axis=1)
    ffc = gg.shape[1] // (groups * GROUP)
    for k, out in enumerate((gg, gu)):
        big = 5 * ffc // 9
        piece = lambda src, b, c, w: src[b, :, (k * groups + c) * w : (k * groups + c + 1) * w].astype(F32)
        parts = [
            piece(src, b, c, w)
            for c in range(groups)
            for b in range(GROUP)
            for src, w in ((o21, big), (o22, ffc - big))
        ]
        out[...] = jnp.concatenate(parts, axis=1)


def unpack(n, result, gtok, o1, o21, o22, oo, od, od2, og, share):
    r = oo.shape[0]
    return pl.pallas_call(
        functools.partial(unpack_kernel, n // GROUP),
        out_shape=(
            SDS(result.shape, BF16),
            SDS(gtok.shape, F32),
            SDS((r, D), F32),
            SDS((r, D // 2), F32),
            SDS((r, D // 2), F32),
            SDS((r, D), F32),
            SDS((r, FF), F32),
            SDS((r, FF), F32),
            SDS((od.shape[0] + od2.shape[0], D), F32),
            SDS((1, share), F32),
        ),
        in_specs=[VM] * 9,
        out_specs=(VM,) * 10,
        compiler_params=pltpu.CompilerParams(vmem_limit_bytes=VMEM_LIMIT),
        name="unpack",
    )(result, gtok, o1, o21, o22, oo, od, od2, og)


def body(n, tokens, w_query, key_weight, w_value, w_out, w_gate, w_up, w_down, norm_gains, seq_lengths, slot_order, out_grad):
    groups = n // GROUP
    r = w_query.shape[0]
    ffc = w_down.shape[0]
    share = norm_gains.shape[0]
    wok = r // 16 if r % 16 == 0 else 1
    wdk = 9
    wo_blk, wd_blk = (wok, r // wok, D), (wdk, ffc // wdk, D)
    h, raw, q, kv, mixf, lse, mix, dy_all, w21, w22, wo, wd1, wqkv, gvec, ct, st = front(
        n,
        seq_lengths,
        tokens,
        w_query,
        key_weight,
        w_value,
        w_gate,
        w_up,
        w_out.reshape(wo_blk),
        w_down.reshape(wd_blk),
        norm_gains.reshape(1, share),
        out_grad,
    )
    res, gmid, dgf, dwo, dmh, po, t21, dw22, dwd1, dwd2 = ffn_block(
        n,
        slot_order,
        mix,
        tokens,
        wo.reshape(D, D),
        gvec,
        w21.reshape(D, -1),
        w22,
        wd1.reshape(-1, D),
        w_down.reshape(wd_blk),
        dy_all,
    )
    dh1, dwqkv, gpart, result, two, t2, od, o21 = attn_bwd(
        n,
        seq_lengths,
        dmh,
        q,
        kv,
        lse,
        mixf,
        h,
        raw,
        wqkv,
        gvec,
        ct,
        st,
        po,
        res,
        dwo.reshape(groups, GROUP, r, D),
        dw22.reshape(groups, GROUP, r, -1),
        dwd1,
        t21,
        dgf,
    )
    gtok, o1, o22, oo, og, od2 = final(
        n,
        dh1,
        tokens,
        gmid,
        gvec,
        dwqkv.reshape(groups, GROUP, r, QKV),
        two.reshape((groups,) + wo_blk),
        t2,
        gpart,
        dwd2,
    )
    outs = unpack(n, result, gtok, o1, o21, o22, oo.reshape(r, D), od.reshape(-1, D), od2.reshape(-1, D), og, share)
    return outs[:-1] + (outs[-1].reshape(share),)


def solution(mesh):
    n = mesh.shape["dp"]
    row = P("dp", None)
    return jax.shard_map(
        functools.partial(body, n),
        mesh=mesh,
        in_specs=(row,) * 8 + (P("dp"), P(), P(), row),
        out_specs=(row,) * 9 + (P("dp"),),
        check_vma=False,
    )
```

```python
import functools
import math

import jax
import jax.numpy as jnp
from jax import lax
from jax.experimental import pallas as pl
from jax.experimental.pallas import tpu as pltpu
from jax.sharding import PartitionSpec as P

D = 1024
FF = 4608
QUERY_HEADS = 16
KEY_VALUE_HEADS = 8
HEAD = 64
SLOT = 128
GROUP = 8
ROWS = 2048
BLOCK = 256
QKV = 256
WINDOW = 4
VMEM_LIMIT = 62 << 20
EPSILON = 1e-05
ROPE_THETA = 1000000.0
SCALE = 1.0 / math.sqrt(HEAD)
LOG2E = math.log2(math.e)
F32 = jnp.float32
BF16 = jnp.bfloat16
MESH = pl.DeviceIdType.MESH
DMA = pltpu.SemaphoreType.DMA
VM = pl.BlockSpec(memory_space=pltpu.VMEM)
ANY = pl.BlockSpec(memory_space=pl.ANY)
HB = pl.BlockSpec(memory_space=pltpu.HBM)
SM = pl.BlockSpec(memory_space=pltpu.SMEM)
SDS = jax.ShapeDtypeStruct


def nn(a, b):
    return lax.dot_general(a, b, (((1,), (0,)), ((), ())), preferred_element_type=F32)


def nt(a, b):
    return lax.dot_general(a, b, (((1,), (1,)), ((), ())), preferred_element_type=F32)


def tn(a, b):
    return lax.dot_general(a, b, (((0,), (0,)), ((), ())), preferred_element_type=F32)


def rcopy(src, dst, send, recv, dev):
    return pltpu.make_async_remote_copy(
        src_ref=src, dst_ref=dst, send_sem=send, recv_sem=recv, device_id=(dev,), device_id_type=MESH
    )


def barrier(peers):
    sem = pltpu.get_barrier_semaphore()
    for q in peers:
        pl.semaphore_signal(sem, inc=1, device_id=(q,), device_id_type=MESH)
    pl.semaphore_wait(sem, len(peers))


def places(n):
    me = lax.axis_index("dp")
    p = lax.rem(me, GROUP)
    g = me // GROUP
    groups = n // GROUP
    zq = [lax.rem(g + s, groups) * GROUP + p for s in range(1, groups)]
    zg = [lax.rem(g + s, groups) for s in range(1, groups)]
    return me, p, g, groups, zq, zg


def start_all(copies):
    for c in copies:
        c.start()
    return copies


def bring(pairs, sem):
    return start_all([pltpu.make_async_copy(a, b, sem.at[i]) for i, (a, b) in enumerate(pairs)])


def wait_all(copies):
    for c in copies:
        c.wait()


class PlaneGather:
    COPIES = 14

    def __init__(self, me, p, src, dst, ss, rs, ls=None):
        sib, xn, yn = me ^ 1, me ^ 2, me ^ 4

        def cp(a, b, i, dev):
            return rcopy(a, b, ss.at[i], rs.at[i], dev)

        def own(i, dev):
            return [cp(src(h), dst(p, h), i + h, dev) for h in range(2)]

        def on(m, h, i, dev):
            return cp(dst(p ^ m, h), dst(p ^ m, h), i, dev)

        self.x, self.y, self.o = own(0, xn), own(2, yn), own(4, sib)
        self.r = [on(2, 0, 6, yn), on(4, 1, 7, xn)]
        self.fx = [on(2, h, 8 + h, sib) for h in range(2)]
        self.fy = [on(4, h, 10 + h, sib) for h in range(2)]
        self.fd = [on(6, h, 12 + h, sib) for h in range(2)]
        self.local = [] if ls is None else [
            pltpu.make_async_copy(src(h), dst(p, h), ls.at[h]) for h in range(2)
        ]

    def start(self):
        self.start_first()
        self.start_second()

    def start_first(self):
        start_all([self.x[0], self.y[1]] + self.o + self.local)

    def start_second(self):
        start_all([self.x[1], self.y[0]])

    def relay1(self):
        self.x[0].wait_recv()
        start_all([self.r[0], self.fx[0]])
        self.y[1].wait_recv()
        start_all([self.r[1], self.fy[1]])

    def relay2(self):
        self.x[1].wait_recv()
        self.fx[1].start()
        self.y[0].wait_recv()
        self.fy[0].start()

    def relay3(self):
        for h in range(2):
            self.r[h].wait_recv()
            self.fd[h].start()

    def arrive(self, copies):
        for c in copies:
            c.wait_recv()

    def sent(self):
        for c in self.x + self.y + self.r + self.o + self.fx + self.fy + self.fd:
            c.wait_send()
        wait_all(self.local)

    def finish(self):
        self.arrive(self.o + self.fx + self.fy + self.fd)
        self.sent()


class Ring:
    def __init__(self, n, p, g, src, dst, ss, rs, ls=None):
        groups = n // GROUP
        to = lambda s: lax.rem(g + s, groups) * GROUP + p
        at = lambda s: lax.rem(g + s, groups)

        def cp(a, b, i, dev):
            return rcopy(a, b, ss.at[i], rs.at[i], dev)

        self.relays = []
        if groups == 4:
            self.up = [cp(src(h), dst(g, h), h, to(1)) for h in range(2)]
            self.down = [cp(src(h), dst(g, h), 2 + h, to(3)) for h in range(2)]
            self.first = [self.up[0], self.down[1], self.up[1], self.down[0]]
            below, above = at(3), at(1)
            self.relays = [cp(dst(below, 0), dst(below, 0), 4, to(1)), cp(dst(above, 1), dst(above, 1), 5, to(3))]
        else:
            self.first = [cp(src(None), dst(g, None), s - 1, to(s)) for s in range(1, groups)]
        self.local = [] if ls is None else [pltpu.make_async_copy(src(None), dst(g, None), ls)]

    def start(self):
        start_all(self.first + self.local)

    def relay(self):
        if self.relays:
            self.up[0].wait_recv()
            self.relays[0].start()
            self.down[1].wait_recv()
            self.relays[1].start()

    def finish(self):
        if self.relays:
            self.up[1].wait_recv()
            self.down[0].wait_recv()
            for c in self.first:
                c.wait_send()
        else:
            wait_all(self.first)
        wait_all(self.relays + self.local)


def ring_count(n):
    return max(6, n // GROUP - 1)


def halves(length, base=0):
    cut = length // 2
    part = (pl.ds(base, cut), pl.ds(base + cut, length - cut))
    return lambda h: pl.ds(base, length) if h is None else part[h]


class RingReduce:
    def __init__(self, n, p, g, part, low, high, send, fin, ss, rs):
        groups = n // GROUP
        to = lambda s: lax.rem(g + s, groups) * GROUP + p
        at = lambda s: lax.rem(g + s, groups)
        hs = halves(part.shape[1])
        self.part, self.fin, self.send, self.g, self.hs = part, fin, send, g, hs

        def cp(a, b, i, dev):
            return rcopy(a, b, ss.at[i], rs.at[i], dev)

        self.ring = groups == 4
        if self.ring:
            self.above, self.below = at(1), at(3)
            self.low, self.high = low, high
            far = at(2)
            self.a = cp(part.at[far, hs(0)], low, 0, to(1))
            self.b = cp(part.at[far, hs(1)], high, 1, to(3))
            self.c = cp(part.at[self.above, hs(1)], fin.at[0, hs(1)], 2, to(1))
            self.d = cp(part.at[self.below, hs(0)], fin.at[1, hs(0)], 3, to(3))
            self.e = cp(send.at[hs(0)], fin.at[0, hs(0)], 4, to(1))
            self.f = cp(send.at[hs(1)], fin.at[1, hs(1)], 5, to(3))
            self.all = [self.a, self.b, self.c, self.d, self.e, self.f]
        else:
            self.all = [cp(part.at[at(s)], fin.at[s - 1], s - 1, to(s)) for s in range(1, groups)]
        self.count = groups - 1

    def start(self):
        start_all(self.all[:4] if self.ring else self.all)

    def relay(self):
        if self.ring:
            for got, buf, h, b, out in (
                (self.a, self.low, 0, self.above, self.e),
                (self.b, self.high, 1, self.below, self.f),
            ):
                got.wait_recv()
                at = self.hs(h)
                self.send[at] = (self.part[b, at].astype(F32) + buf[...].astype(F32)).astype(BF16)
                out.start()

    def finish(self):
        for c in self.all[2:] if self.ring else self.all:
            c.wait_recv()
        val = self.part[self.g].astype(F32)
        for s in range(2 if self.ring else self.count):
            val = val + self.fin[s].astype(F32)
        for c in self.all:
            c.wait_send()
        return val


def ring_scratch(n, shape):
    cut = shape[0] // 2
    groups = n // GROUP
    count = 2 if groups == 4 else groups - 1
    tail = tuple(shape[1:])
    vm = lambda s: pltpu.VMEM(s, BF16)
    return [
        vm((max(cut, 1),) + tail),
        vm((shape[0] - cut,) + tail),
        vm(tuple(shape)),
        vm((count,) + tuple(shape)),
        DMA((ring_count(n),)),
        DMA((ring_count(n),)),
    ]


class PlaneReduce:
    def __init__(self, me, part, sib, send, relay, fx, fy, ss, rs, own=None):
        p = lax.rem(me, GROUP)
        self.own = own or (lambda i: part(p ^ (2 * i)))
        xn, yn = me ^ 2, me ^ 4
        hs = halves(sib.shape[1])
        self.hs, self.p, self.part = hs, p, part
        self.sib, self.send, self.relay, self.fx, self.fy = sib, send, relay, fx, fy

        def cp(a, b, i, dev):
            return rcopy(a, b, ss.at[i], rs.at[i], dev)

        self.first = [cp(part(p ^ (2 * i + 1)), sib.at[i], i, me ^ 1) for i in range(4)]
        self.diag = [cp(send.at[0, hs(0)], relay.at[0], 4, xn), cp(send.at[0, hs(1)], relay.at[1], 5, yn)]
        self.toy = [cp(send.at[2, hs(h)], fy.at[hs(h)], 6 + h, yn) for h in range(2)]
        self.tox = [cp(send.at[1, hs(h)], fx.at[hs(h)], 8 + h, xn) for h in range(2)]

    def start(self):
        start_all([self.first[i] for i in (3, 1, 2, 0)])

    def chip(self, i):
        self.first[i].wait_recv()
        return self.own(i)[...].astype(F32) + self.sib[i].astype(F32)

    def chip_d(self):
        self.send[0] = self.chip(3).astype(BF16)
        start_all(self.diag)

    def chip_x(self):
        self.send[1] = self.chip(1).astype(BF16)
        self.tox[0].start()

    def chip_y(self):
        self.send[2] = self.chip(2).astype(BF16)
        self.toy[1].start()

    def phase1(self):
        self.chip_d()
        self.chip_x()
        self.chip_y()

    def phase2(self):
        self.diag[0].wait_recv()
        at = self.hs(0)
        self.send[2, at] = (self.send[2, at].astype(F32) + self.relay[0].astype(F32)).astype(BF16)
        self.toy[0].start()
        self.diag[1].wait_recv()
        at = self.hs(1)
        self.send[1, at] = (self.send[1, at].astype(F32) + self.relay[1].astype(F32)).astype(BF16)
        self.tox[1].start()

    def phase3(self):
        own = self.chip(0)
        for c in self.toy + self.tox:
            c.wait_recv()
        own = own + self.fx[...].astype(F32) + self.fy[...].astype(F32)
        for c in self.first + self.diag + self.toy + self.tox:
            c.wait_send()
        return own


def plane_scratch(shape):
    tail = tuple(shape[1:])
    vm = lambda *s: pltpu.VMEM(s + tail, BF16)
    return [
        vm(4, shape[0]),
        vm(3, shape[0]),
        vm(2, shape[0] // 2),
        vm(shape[0]),
        vm(shape[0]),
        DMA((10,)),
        DMA((10,)),
    ]


def swap_halves(v):
    lane = lax.broadcasted_iota(jnp.int32, v.shape, 1)
    low = lax.rem(lane, HEAD) < HEAD // 2
    width = v.shape[1]
    return jnp.where(low, pltpu.roll(v, width - HEAD // 2, 1), pltpu.roll(v, HEAD // 2, 1))


def head_mean(v):
    row = lax.broadcasted_iota(jnp.int32, (128, 128), 0)
    lane = lax.broadcasted_iota(jnp.int32, (128, 128), 1)
    same = jnp.where((row < HEAD) == (lane < HEAD), 1.0 / HEAD, 0.0).astype(BF16)
    high = v.astype(BF16)
    low = (v - high.astype(F32)).astype(BF16)
    return nn(high, same) + nn(low, same)


def head_gains(g_ref):
    t = g_ref[:, 2 * D :]
    t = jnp.broadcast_to(t, (8, 128))
    lane = lax.broadcasted_iota(jnp.int32, (8, 128), 1)
    other = pltpu.roll(t, HEAD, 1)
    return jnp.where(lane < HEAD, t, other)[0:1, :], jnp.where(lane < HEAD, other, t)[0:1, :]


def seq_start(row, len_ref, g):
    e1 = len_ref[g, 0]
    e2 = e1 + len_ref[g, 1]
    e3 = e2 + len_ref[g, 2]
    zero = row * 0
    s = jnp.where(row >= e1, zero + e1, zero)
    s = jnp.where(row >= e2, zero + e2, s)
    return jnp.where(row >= e3, zero + e3, s)


def windows(i, window):
    for low, high, count in ((0, 1, 2), (2, 3, 4), (4, 7, WINDOW + 1)):

        @pl.when((i >= low) & (i <= high))
        def _():
            window(jnp.maximum(i - WINDOW, 0), count)


def front_kernel(n, len_ref, x_, wq_, wk_, wv_, wg_, wu_, wo_, wd_, gn_, dy_, h_o, raw_o, q_o, kv_o, mixf_o, lse_o, mixo, dyo, w21o, w22o, woo, wdo, wqkv_o, gvec, ct, st, xa, gn, wq, wk, wv, wo, wd, wg, wu, dy, a1, b1, b2, gt, gto, w1v, woz, wqkv, h_s, raw_s, q_s, kv_s, mixf_s, lse_s, mixs, k_s, v_s, acc, fs, ls, xs, xr, ds_, dr, os_, orr, ps, pr, zs, zr, ms, mr, outs):
    me, p, g, groups, zq, zg = places(n)
    fetch = bring(
        (
            (x_, xa.at[p]),
            (gn_, gn),
            (wq_, wq),
            (wk_, wk),
            (wv_, wv),
            (wo_, wo),
            (wd_.at[pl.ds(0, wd.shape[0])], wd),
            (wg_, wg),
            (wu_, wu),
            (dy_, dy),
        ),
        fs,
    )
    share = gn.shape[1]
    ffc = wg.shape[1] // (groups * GROUP)
    big = 5 * ffc // 9
    r = wq.shape[0]
    barrier([me ^ m for m in range(1, GROUP)] + zq)
    hx, ho = halves(BLOCK), halves(groups)
    xg = PlaneGather(me, p, lambda h: xa.at[p, hx(h)], lambda b, h: xa.at[b, hx(h)], xs, xr)
    dg = PlaneGather(me, p, lambda h: dy.at[hx(h)], lambda b, h: dyo.at[b, hx(h)], ds_, dr, ls.at[pl.ds(0, 2)])
    og = PlaneGather(me, p, lambda h: woz.at[ho(h)], lambda b, h: woo.at[ho(h), b], os_, orr, ls.at[pl.ds(2, 2)])
    def ring(k, src, dst, local=None):
        hk = halves(dst.shape[1])
        return Ring(n, p, g, lambda h: src.at[hk(h)], lambda b, h: dst.at[b, hk(h)], zs.at[k], zr.at[k], local)

    wring, gring = ring(0, w1v.at[g], w1v), ring(1, gto.at[g], gto)
    dring, oring = ring(2, wd, wdo, ls.at[4]), ring(3, wo, woz, ls.at[5])
    uring = ring(4, w21o.at[g], w21o)
    pc = {}

    def exchange(k, src, dst):
        for m in range(1, GROUP):
            pc[k, m] = rcopy(src(p ^ m), dst, ps.at[k, m - 1], pr.at[k, m - 1], me ^ m)
            pc[k, m].start()

    def arrived(k):
        for m in range(1, GROUP):
            pc[k, m].wait_recv()


    def pack(buf, low, high):
        for b in range(GROUP):
            at = [slice((GROUP * k + b) * ffc + low, (GROUP * k + b) * ffc + high) for k in range(groups)]
            buf[b] = jnp.concatenate([wg[:, k] for k in at] + [wu[:, k] for k in at], axis=1)

    fetch[0].wait()
    xg.start_first()
    fetch[1].wait()
    gt[...] = jnp.zeros_like(gt)
    gt[0:1, :share] = gn[...].astype(F32)
    gto[g, p] = gt[...]
    exchange(1, lambda b: gt, gto.at[g, p])
    wait_all(fetch[2:5])
    for b in range(GROUP):
        a1[b, :, :128] = wq[:, 128 * b : 128 * (b + 1)]
        at = slice(HEAD * b, HEAD * (b + 1))
        a1[b, :, 128:] = jnp.concatenate([wk[:, at], wv[:, at]], axis=1)
    exchange(0, lambda b: a1.at[b], w1v.at[g, p])
    w1v[g, p] = a1[p]
    fetch[5].wait()
    oring.start()
    fetch[6].wait()
    dring.start()
    wait_all(fetch[7:9])
    pack(b1, 0, big)
    exchange(2, lambda b: b1.at[b], w21o.at[g, p])
    local = start_all([pltpu.make_async_copy(b1.at[p], w21o.at[g, p], ls.at[6])])
    pack(b2, big, ffc)
    exchange(3, lambda b: b2.at[b], w22o.at[p])
    local += start_all([pltpu.make_async_copy(b2.at[p], w22o.at[p], ls.at[7])])
    xg.start_second()
    arrived(0)
    wring.start()
    arrived(1)
    gring.start()
    arrived(2)
    local[0].wait()
    uring.start()
    xg.relay1()
    fetch[9].wait()
    dg.start_first()
    row = lax.broadcasted_iota(jnp.int32, (1, ROWS), 1)
    position = (row - seq_start(row, len_ref, g)).astype(F32)
    index = lax.broadcasted_iota(jnp.int32, (HEAD // 2, 1), 0).astype(F32)
    angles = jnp.exp(index * (-2.0 * math.log(ROPE_THETA) / HEAD)) * position
    c, s = jnp.cos(angles).T, jnp.sin(angles).T
    ct[...] = jnp.concatenate([c, c, c, c], axis=1)
    st[...] = jnp.concatenate([-s, s, -s, s], axis=1)
    k_s[: WINDOW * BLOCK] = jnp.zeros((WINDOW * BLOCK, HEAD), BF16)
    v_s[: WINDOW * BLOCK] = jnp.zeros((WINDOW * BLOCK, 128), BF16)
    xg.relay2()
    for c in (wring, gring):
        c.relay()
    xg.relay3()
    dg.start_second()
    wring.finish()
    gring.finish()
    for k in range(groups * GROUP):
        wqkv[k * r : (k + 1) * r] = w1v[k // GROUP, k % GROUP]
    gvec[...] = jnp.concatenate(
        [gto[k, b, 0:1, :share] for k in range(groups) for b in range(GROUP)], axis=1
    )
    xg.arrive(xg.o + xg.fx + xg.fy + xg.fd)
    gq, gk = head_gains(gvec)
    results = ((h_s, h_o), (raw_s, raw_o), (q_s, q_o), (kv_s, kv_o), (mixf_s, mixf_o), (lse_s, lse_o))

    def block(i, carry):
        @pl.when(i == 0)
        def _():
            oring.relay()
            dg.relay1()

        @pl.when(i == 1)
        def _():
            oring.finish()
            og.start_first()

        @pl.when(i == 2)
        def _():
            og.start_second()

        @pl.when(i == 3)
        def _():
            uring.relay()
            dg.relay2()

        @pl.when(i == 5)
        def _():
            og.relay1()
            dg.relay3()

        @pl.when(i == 6)
        def _():
            dring.relay()

        @pl.when(i == 7)
        def _():
            og.relay2()

        at = pl.ds(pl.multiple_of(i * BLOCK, BLOCK), BLOCK)
        xb = xa[i].astype(F32)
        h = (xb * lax.rsqrt(jnp.mean(xb * xb, axis=-1, keepdims=True) + EPSILON) * gvec[:, :D]).astype(BF16)
        h_s[i] = h
        raw = nn(h, wqkv[...])
        raw_s[i] = raw
        cb, sb = ct[at, :], st[at, :]
        qraw, kvraw = raw[:, :128], raw[:, 128:]
        qn = qraw * lax.rsqrt(head_mean(qraw * qraw) + EPSILON) * gq
        q = (qn * cb + swap_halves(qn) * sb).astype(BF16)
        kn = kvraw * lax.rsqrt(head_mean(kvraw * kvraw) + EPSILON) * gk
        k = (kn * cb + swap_halves(kn) * sb).astype(BF16)
        lane = lax.broadcasted_iota(jnp.int32, (BLOCK, 128), 1)
        kv = jnp.where(lane < HEAD, k.astype(F32), kvraw).astype(BF16)
        q_s[i] = q
        kv_s[i] = kv
        k_s[at, :] = kv[:, :HEAD]
        v_s[at, :] = jnp.where(lane < HEAD, pltpu.roll(kvraw, HEAD, 1), 1.0).astype(BF16)
        q2 = jnp.concatenate([q[:, :HEAD], q[:, HEAD:]], axis=0)
        rows = lax.broadcasted_iota(jnp.int32, (2 * BLOCK, 1), 0)
        qrow = i * BLOCK + jnp.where(rows >= BLOCK, rows - BLOCK, rows)
        qstart = seq_start(qrow, len_ref, g)

        def window(first, count):
            span = pl.ds(pl.multiple_of(first * BLOCK, BLOCK), count * BLOCK)
            kc = lax.broadcasted_iota(jnp.int32, (2 * BLOCK, count * BLOCK), 1) + first * BLOCK
            ok = (kc >= qstart) & (kc <= qrow)
            e = jnp.where(ok, jnp.exp2(nt(q2, k_s[span, :]) * (SCALE * LOG2E)), 0.0).astype(BF16)
            acc[...] = nn(e, v_s[span, :])

        windows(i, window)
        total = acc[:, HEAD:]
        m = acc[:, :HEAD] / total
        both = jnp.concatenate([m[:BLOCK], m[BLOCK:]], axis=1)
        mixf_s[i] = both
        lse_s[i] = jnp.log2(total.T)[:8, :]
        mixs[i] = both.astype(BF16)

        @pl.when(i == p)
        def _():
            pltpu.make_async_copy(mixs.at[i], mixo.at[p], ls.at[8]).start()

        @pl.when(i != p)
        def _():
            rcopy(mixs.at[i], mixo.at[p], ms.at[p ^ i], mr.at[p ^ i], me ^ p ^ i).start()

        for k, (a, b) in enumerate(results):
            pltpu.make_async_copy(a.at[i], b.at[i], outs.at[k, i]).start()
        return carry

    lax.fori_loop(0, GROUP, block, 0)
    wq_out = pltpu.make_async_copy(wqkv, wqkv_o, ls.at[9])
    wq_out.start()
    og.relay3()
    for c in pc.values():
        c.wait_send()
    arrived(3)
    local[1].wait()
    for c in (dring, uring):
        c.finish()
    xg.sent()
    dg.finish()
    og.finish()
    for m in range(1, GROUP):
        rcopy(mixs.at[p ^ m], mixo.at[p], ms.at[m], mr.at[m], me ^ m).wait()
    pltpu.make_async_copy(mixs.at[p], mixo.at[p], ls.at[8]).wait()
    for k, (a, b) in enumerate(results):
        for i in range(GROUP):
            pltpu.make_async_copy(a.at[i], b.at[i], outs.at[k, i]).wait()
    wq_out.wait()


def front(n, lengths, x, wq, wk, wv, wg, wu, wo, wd, gn, dy):
    groups = n // GROUP
    r = wq.shape[0]
    wide = 2 * wg.shape[1] // GROUP
    wide1 = 5 * wide // 9
    wd1 = (5 * wd.shape[0] // 9,) + wd.shape[1:]
    vm = lambda *s: pltpu.VMEM(s, BF16)
    vf = lambda *s: pltpu.VMEM(s, F32)
    return pl.pallas_call(
        functools.partial(front_kernel, n),
        out_shape=(
            SDS((GROUP, BLOCK, D), BF16),
            SDS((GROUP, BLOCK, QKV), F32),
            SDS((GROUP, BLOCK, 128), BF16),
            SDS((GROUP, BLOCK, 128), BF16),
            SDS((GROUP, BLOCK, 128), F32),
            SDS((GROUP, 8, 2 * BLOCK), F32),
            SDS((GROUP, BLOCK, 128), BF16),
            SDS((GROUP, BLOCK, D), BF16),
            SDS((groups, GROUP, r, wide1), BF16),
            SDS((GROUP, r, wide - wide1), BF16),
            SDS((groups, GROUP) + wo.shape, BF16),
            SDS((groups,) + wd1, BF16),
            SDS((D, QKV), BF16),
            SDS((1, gn.shape[1] * n), F32),
            SDS((ROWS, 128), F32),
            SDS((ROWS, 128), F32),
        ),
        in_specs=[SM] + [HB] * 10,
        out_specs=(HB,) * 13 + (VM,) * 3,
        scratch_shapes=[vm(GROUP, BLOCK, D)]
        + [vm(*s) for s in (gn.shape, wq.shape, wk.shape, wv.shape, wo.shape, wd1, wg.shape, wu.shape, dy.shape)]
        + [
            vm(GROUP, r, QKV),
            vm(GROUP, r, wide1),
            vm(GROUP, r, wide - wide1),
            vf(8, 128),
            vf(groups, GROUP, 8, 128),
            vm(groups, GROUP, r, QKV),
            vm(groups, *wo.shape),
            vm(D, QKV),
            vm(GROUP, BLOCK, D),
            vf(GROUP, BLOCK, QKV),
            vm(GROUP, BLOCK, 128),
            vm(GROUP, BLOCK, 128),
            vf(GROUP, BLOCK, 128),
            vf(GROUP, 8, 2 * BLOCK),
            vm(GROUP, BLOCK, 128),
            vm(ROWS, HEAD),
            vm(ROWS, 128),
            vf(2 * BLOCK, 128),
            DMA((10,)),
            DMA((10,)),
            DMA((14,)),
            DMA((14,)),
            DMA((14,)),
            DMA((14,)),
            DMA((14,)),
            DMA((14,)),
            DMA((4, 7)),
            DMA((4, 7)),
            DMA((5, ring_count(n))),
            DMA((5, ring_count(n))),
            DMA((GROUP,)),
            DMA((GROUP,)),
            DMA((6, GROUP)),
        ],
        compiler_params=pltpu.CompilerParams(collective_id=1, has_side_effects=True, vmem_limit_bytes=VMEM_LIMIT),
        name="front",
    )(lengths, x, wq, wk, wv, wg, wu, wo, wd, gn, dy)


def norm_back(dyv, xv, gain):
    r = lax.rsqrt(jnp.mean(xv * xv, axis=-1, keepdims=True) + EPSILON)
    xr = xv * r
    gy = dyv * gain
    dx = r * (gy - xr * jnp.mean(gy * xr, axis=-1, keepdims=True))
    return dx, jnp.sum(dyv * xr, axis=0, keepdims=True)


def unit_grads(h, dyb, wgu, wd):
    f = wd.shape[0]
    gu = nn(h, wgu)
    da = nt(dyb, wd)
    gp, up = gu[:, :f], gu[:, f:]
    sig = 1.0 / (1.0 + jnp.exp(-gp))
    sg = gp * sig
    dg = (da * up * (sig * (1.0 + gp * (1.0 - sig)))).astype(BF16)
    return (sg * up).astype(BF16), jnp.concatenate([dg, (da * sg).astype(BF16)], axis=1)


def ffn_block_kernel(n, order, mix_, x_, wo_, g_ref, w21_, w22_, wd1_, wd2_, dy_, res_o, gmid_o, dgf, dwo_o, dmh, po, t21, dw22_o, dwd1_o, dwd2_o, res, gmid, dwo, dw22, dwd1, dwd2, sent, x, wo, w21, dy, fs, mbuf, h2, h2t, w2v, w22, wdv, wds, dys, acts1, acts2, dgu1, dgu2, dw21, part, mown, stage, hs, hr, os_, qs, qr, zs, zr, *red_refs):
    me, p, g, groups, zq, zg = places(n)
    f1 = wd1_.shape[0]
    f2 = wds.shape[0] - f1
    fetch = bring(
        (
            (wd2_.at[pl.ds(wd2_.shape[0] - wdv.shape[1], wdv.shape[1])], wdv.at[g]),
            (w22_, w2v.at[g]),
            (mix_, mbuf),
            (x_, x),
            (wo_, wo),
            (w21_, w21),
            (wd1_, wds.at[pl.ds(0, f1)]),
            (dy_, dy),
        ),
        fs,
    )
    barrier([me ^ m for m in range(1, GROUP)] + zq)
    gf = g_ref.at[:, D : 2 * D]
    r = w2v.shape[2]
    away = [
        pltpu.make_async_copy(a, b, sent.at[k])
        for k, (a, b) in enumerate(
            ((res, res_o), (gmid, gmid_o), (dwo, dwo_o), (dw22, dw22_o), (dwd1, dwd1_o), (dwd2, dwd2_o))
        )
    ]

    def holder(q):
        s = 0
        for k in range(ROWS // SLOT):
            s = jnp.where(order[g, k] == q, k, s)
        return s

    hw, h8 = halves(wdv.shape[1]), halves(GROUP)
    wrings = [
        Ring(n, p, g, lambda h: w2v.at[g, h8(h)], lambda b, h: w2v.at[b, h8(h)], zs.at[0], zr.at[0]),
        Ring(n, p, g, lambda h: wdv.at[g, hw(h)], lambda b, h: wdv.at[b, hw(h)], zs.at[1], zr.at[1]),
    ]
    wait_all(fetch[:2])
    for c in wrings:
        c.start()
    wait_all(fetch[2:5])
    m = jnp.concatenate([mbuf[b] for b in range(GROUP)], axis=1)
    mown[...] = m
    z = x[...].astype(F32) + nn(m, wo[...])
    res[...] = z
    away[0].start()
    h2[p] = (z * lax.rsqrt(jnp.mean(z * z, axis=-1, keepdims=True) + EPSILON) * gf[...]).astype(BF16)
    hb = halves(BLOCK)
    hg = PlaneGather(me, p, lambda h: h2.at[p, hb(h)], lambda b, h: h2.at[b, hb(h)], hs, hr)
    red = PlaneReduce(me, lambda b: part.at[b], *red_refs[:7])
    ring21 = RingReduce(n, p, g, dw21, *red_refs[7:])
    hg.start_first()
    wait_all(fetch[5:])

    def first(t, carry):
        @pl.when(t == 1)
        def _():
            hg.start_second()
            hg.arrive(hg.o)

        @pl.when(t == 2)
        def _():
            hg.relay1()
            hg.relay2()

        @pl.when(t == 3)
        def _():
            hg.arrive(hg.fx)

        @pl.when(t == 3)
        def _():
            for c in wrings:
                c.relay()

        @pl.when(t == 5)
        def _():
            hg.arrive(hg.fy)

        @pl.when(t == 6)
        def _():
            hg.relay3()

        @pl.when(t == 7)
        def _():
            hg.arrive(hg.fd)

        b = p ^ t
        dys[b] = jnp.concatenate([dy[holder(2 * b)], dy[holder(2 * b + 1)]], axis=0)
        h2t[:, pl.ds(pl.multiple_of(b * BLOCK, BLOCK), BLOCK)] = h2[b].T
        acts1[b], dgu1[b] = unit_grads(h2[b], dys[b], w21[...], wds[:f1])
        part[b] = nt(dgu1[b], w21[...]).astype(BF16)
        return carry

    lax.fori_loop(0, GROUP, first, 0)
    grad1 = nn(h2t[...], dgu1[...].reshape(ROWS, 2 * f1)).astype(BF16)
    for k in range(groups * GROUP):
        dw21[k // GROUP, k % GROUP] = grad1[k * r : (k + 1) * r]
    ring21.start()
    for c in wrings:
        c.finish()
    for k in range(groups * GROUP):
        w22[k * r : (k + 1) * r] = w2v[k // GROUP, k % GROUP]
    each = f2 // groups
    for k in range(groups):
        wds[f1 + k * each : f1 + (k + 1) * each] = wdv[k].reshape(each, D)

    def second(t, carry):
        @pl.when(t == 1)
        def _():
            red.first[3].start()

        @pl.when(t == 3)
        def _():
            red.first[2].start()
            red.chip_d()

        @pl.when(t == 5)
        def _():
            red.first[1].start()
            red.chip_y()

        @pl.when(t == 7)
        def _():
            red.first[0].start()
            red.chip_x()

        b = p ^ (GROUP - 1 - t)
        acts2[b], dgu2[b] = unit_grads(h2[b], dys[b], w22[...], wds[f1:])
        part[b] = (part[b].astype(F32) + nt(dgu2[b], w22[...])).astype(BF16)
        return carry

    lax.fori_loop(0, GROUP, second, 0)
    dy_rows = dys[...].reshape(ROWS, D)
    for acts, out, rows in ((acts1, dwd1, f1), (acts2, dwd2, f2)):
        dw = tn(acts[...].reshape(ROWS, rows), dy_rows).astype(BF16)
        part_rows = rows // groups
        for k in range(groups):
            out[k] = dw[k * part_rows : (k + 1) * part_rows].reshape(out.shape[1:])
    start_all(away[4:])
    red.phase2()
    ring21.relay()
    dw22[...] = nn(h2t[...], dgu2[...].reshape(ROWS, 2 * f2)).astype(BF16)
    away[3].start()
    dx, dgain = norm_back(red.phase3(), res[...], gf[...])
    gm = dys[p].astype(F32) + dx
    gmid[...] = gm
    away[1].start()
    dgf[...] = dgain
    gl = gm.astype(BF16)
    dm = nt(gl, wo[...]).astype(BF16)
    for b in range(GROUP):
        mbuf[b] = dm[:, 128 * b : 128 * (b + 1)]
    qc = start_all(
        [rcopy(mbuf.at[p ^ m], dmh.at[p], qs.at[m - 1], qr.at[m - 1], me ^ m) for m in range(1, GROUP)]
    )
    dmh[p] = mbuf[p]
    dwo[...] = tn(mown[...], gl).astype(BF16)
    away[2].start()

    def out(b, carry):
        slot = lax.rem(b, 2)

        @pl.when(b > 1)
        def _():
            pltpu.make_async_copy(stage.at[slot], po.at[b - 2], os_.at[slot]).wait()

        stage[slot] = (nn(acts1[b], wds[:f1]) + nn(acts2[b], wds[f1:])).astype(BF16)
        pltpu.make_async_copy(stage.at[slot], po.at[b], os_.at[slot]).start()
        return carry

    lax.fori_loop(0, GROUP, out, 0)
    for b in range(GROUP - 2, GROUP):
        pltpu.make_async_copy(stage.at[b % 2], po.at[b], os_.at[b % 2]).wait()
    wait_all(qc)
    hg.sent()
    t21[...] = ring21.finish().astype(BF16)
    wait_all(away)


def ffn_block(n, order, mix, x, wo, gvec, w21, w22, wd1, wd, dy):
    groups = n // GROUP
    r = w22.shape[1]
    f1, f2 = w21.shape[1] // 2, w22.shape[2] // 2
    wd2 = (4 * wd.shape[0] // 9,) + wd.shape[1:]
    wd1_blk = (5 * wd.shape[0] // 9,) + wd.shape[1:]
    blk = (GROUP, r, 2 * f1)
    vm = lambda *s: pltpu.VMEM(s, BF16)
    return pl.pallas_call(
        functools.partial(ffn_block_kernel, n),
        out_shape=(
            SDS((BLOCK, D), F32),
            SDS((BLOCK, D), F32),
            SDS((1, D), F32),
            SDS((D, D), BF16),
            SDS((GROUP, BLOCK, 128), BF16),
            SDS((GROUP, BLOCK, D), BF16),
            SDS(blk, BF16),
            SDS((D, 2 * f2), BF16),
            SDS((groups,) + wd1_blk, BF16),
            SDS((groups,) + wd2, BF16),
        ),
        in_specs=[SM, HB, HB, HB, VM, HB, HB, HB, HB, HB],
        out_specs=(HB, HB, VM, HB, VM, HB, VM, HB, HB, HB),
        scratch_shapes=[
            pltpu.VMEM((BLOCK, D), F32),
            pltpu.VMEM((BLOCK, D), F32),
            vm(D, D),
            vm(D, 2 * f2),
            vm(groups, *wd1_blk),
            vm(groups, *wd2),
            DMA((6,)),
            vm(BLOCK, D),
            vm(D, D),
            vm(D, 2 * f1),
            vm(ROWS // SLOT, SLOT, D),
            DMA((8,)),
            vm(GROUP, BLOCK, 128),
            vm(GROUP, BLOCK, D),
            vm(D, ROWS),
            vm(groups, *w22.shape),
            vm(D, 2 * f2),
            vm(groups, *wd2),
            vm(f1 + f2, D),
            vm(GROUP, BLOCK, D),
            vm(GROUP, BLOCK, f1),
            vm(GROUP, BLOCK, f2),
            vm(GROUP, BLOCK, 2 * f1),
            vm(GROUP, BLOCK, 2 * f2),
            vm(groups, *blk),
            vm(GROUP, BLOCK, D),
            vm(BLOCK, D),
            vm(2, BLOCK, D),
            DMA((14,)),
            DMA((14,)),
            DMA((2,)),
            DMA((7,)),
            DMA((7,)),
            DMA((2, ring_count(n))),
            DMA((2, ring_count(n))),
        ]
        + plane_scratch((BLOCK, D))
        + ring_scratch(n, blk),
        compiler_params=pltpu.CompilerParams(collective_id=2, has_side_effects=True, vmem_limit_bytes=VMEM_LIMIT),
        name="ffn_block",
    )(order, mix, x, wo, gvec, w21, w22, wd1, wd, dy.reshape(ROWS // SLOT, SLOT, D))


def attn_bwd_kernel(n, len_ref, dm_ref, q_ref, kvall_ref, lse_ref, mixf_ref, h_ref, raw_ref, w_ref, g_ref, ct_ref, st_ref, po_, res_, dwo_, dw2_, dwd_, t21_, dgf, dh_ref, dw_ref, gpart, result, two, t2, od, o21, k_s, v_s, dk_s, dv_s, dqt, dws, dg_ref, es, er, po, res, dwo, dw2, dwd, t21, fs, *rest):
    step_id = pl.program_id(0)
    nb = ROWS // BLOCK
    i = nb - 1 - step_id
    me, p, g, groups, zq, zg = places(n)
    ored = PlaneReduce(me, lambda b: po.at[b], *rest[:7])
    wred = PlaneReduce(me, lambda b: dwo.at[:, b], *rest[7:14])
    ring2 = RingReduce(n, p, g, dw2, *rest[14:20])
    ringd = RingReduce(n, p, g, dwd, *rest[20:26])
    fetch = [
        pltpu.make_async_copy(a, b, fs.at[k])
        for k, (a, b) in enumerate(
            ((dwd_, dwd), (dw2_, dw2), (po_, po), (dwo_, dwo), (t21_, t21), (res_, res))
        )
    ]
    ex = [rcopy(t21.at[p ^ m], o21.at[p], es.at[m - 1], er.at[m - 1], me ^ m) for m in range(1, GROUP)]
    own_copy = pltpu.make_async_copy(t21.at[p], o21.at[p], fs.at[6])

    @pl.when(step_id == 0)
    def _():
        start_all(fetch)
        barrier([me ^ m for m in range(1, GROUP)] + zq)

    @pl.when(step_id == 1)
    def _():
        ored.phase1()
        wred.phase1()

    @pl.when(step_id == 3)
    def _():
        ringd.relay()
        ring2.relay()
        ored.phase2()

    @pl.when(step_id == 4)
    def _():
        wred.phase2()


    @pl.when(step_id == 0)
    def _():
        dk_s[...] = jnp.zeros_like(dk_s)
        dv_s[...] = jnp.zeros_like(dv_s)
        dws[...] = jnp.zeros_like(dws)
        dg_ref[...] = jnp.zeros_like(dg_ref)
        for b in range(ROWS // BLOCK):
            kvb = kvall_ref[b]
            k_s[pl.ds(b * BLOCK, BLOCK), :] = kvb[:, :HEAD]
            v_s[pl.ds(b * BLOCK, BLOCK), :] = kvb[:, HEAD:]

    q, do, mf = q_ref[0], dm_ref[0], mixf_ref[0]
    q2 = jnp.concatenate([q[:, :HEAD], q[:, HEAD:]], axis=0)
    do2 = jnp.concatenate([do[:, :HEAD], do[:, HEAD:]], axis=0)
    prod = (do.astype(F32) * mf).T
    delta = jnp.concatenate(
        [jnp.sum(prod[:HEAD], axis=0, keepdims=True), jnp.sum(prod[HEAD:], axis=0, keepdims=True)], axis=1
    )
    lse = lse_ref[0, 0:1, :]
    colq = lax.broadcasted_iota(jnp.int32, (1, 2 * BLOCK), 1)
    qrow = i * BLOCK + jnp.where(colq >= BLOCK, colq - BLOCK, colq)
    qstart = seq_start(qrow, len_ref, g)

    def window(first, count):
        at = pl.ds(pl.multiple_of(first * BLOCK, BLOCK), count * BLOCK)
        kb, vb = k_s[at, :], v_s[at, :]
        kc = lax.broadcasted_iota(jnp.int32, (count * BLOCK, 2 * BLOCK), 0) + first * BLOCK
        ok = (kc >= qstart) & (kc <= qrow)
        pr = jnp.where(ok, jnp.exp2(nt(kb, q2) * (SCALE * LOG2E) - lse), 0.0)
        dsc = (pr * (nt(vb, do2) - delta)).astype(BF16)
        dk_s[at, :] += nn(dsc, q2)
        dv_s[at, :] += nn(pr.astype(BF16), do2)
        dqt[...] = tn(dsc, kb)

    windows(i, window)
    ct, st = ct_ref[...], st_ref[...]
    raw = raw_ref[0]
    dq = jnp.concatenate([dqt[:BLOCK], dqt[BLOCK:]], axis=1) * SCALE
    here = pl.ds(pl.multiple_of(i * BLOCK, BLOCK), BLOCK)
    dkvb = jnp.concatenate([dk_s[here, :], dv_s[here, :]], axis=1)
    lane = lax.broadcasted_iota(jnp.int32, (BLOCK, 128), 1)

    def pull(d, v, gain):
        dn = d * ct - swap_halves(d) * st
        r = lax.rsqrt(head_mean(v * v) + EPSILON)
        vr = v * r
        gy = dn * gain
        return r * (gy - vr * head_mean(gy * vr)), jnp.sum(dn * vr, axis=0, keepdims=True)

    gq, gk = head_gains(g_ref)
    dqr, dgq = pull(dq, raw[:, :128], gq)
    dkr, dgk = pull(dkvb * SCALE, raw[:, 128:], gk)
    dg_ref[0:1, :] += dgq
    dg_ref[1:2, :] += dgk
    dqkv = jnp.concatenate([dqr, jnp.where(lane < HEAD, dkr, dkvb)], axis=1).astype(BF16)
    dh_ref[0] = nt(dqkv, w_ref[...]).astype(BF16)
    dws[...] += tn(h_ref[0], dqkv)

    @pl.when(step_id == 0)
    def _():
        wait_all(fetch)
        ringd.start()
        ring2.start()
        ored.start()
        wred.start()
        start_all(ex + [own_copy])

    @pl.when(step_id == nb - 1)
    def _():
        dw_ref[...] = dws[...].astype(BF16)
        result[...] = (ored.phase3() + res[...]).astype(BF16)
        two[...] = wred.phase3().astype(BF16)
        t2[...] = ring2.finish().astype(BF16)
        od[...] = ringd.finish()
        wait_all(ex + [own_copy])
        dga = lax.dot_general(
            jnp.ones((8, QKV), F32),
            w_ref[...].astype(F32) * dws[...],
            (((1,), (1,)), ((), ())),
            precision=lax.Precision.HIGHEST,
            preferred_element_type=F32,
        )
        dga = dga[0:1, :] / g_ref[:, :D]
        gpart[...] = jnp.zeros_like(gpart)
        for b in range(8):
            gpart[b : b + 1, :] = dga[:, 128 * b : 128 * (b + 1)]
            gpart[8 + b : 9 + b, :] = dgf[:, 128 * b : 128 * (b + 1)]
        turned = pltpu.roll(dg_ref[...], HEAD, 1)
        low = lax.broadcasted_iota(jnp.int32, (1, 128), 1) < HEAD
        gpart[16:17, :] = jnp.where(low, dg_ref[0:1, :] + turned[0:1, :], turned[1:2, :])


def attn_bwd(n, lengths, dmh, q, kv, lse, mixf, h, raw, wqkv, gvec, ct, st, po, res, dwo, dw2, dwd, t21, dgf):
    nb = ROWS // BLOCK
    groups = n // GROUP
    blk = lambda c: pl.BlockSpec((1, BLOCK, c), lambda i: (nb - 1 - i, 0, 0))
    whole = lambda s: pl.BlockSpec(s, lambda i: (0,) * len(s), pipeline_mode=pl.Buffered(1))
    return pl.pallas_call(
        functools.partial(attn_bwd_kernel, n),
        grid=(nb,),
        in_specs=[
            SM,
            blk(128),
            blk(128),
            whole((nb, BLOCK, 128)),
            pl.BlockSpec((1, 8, 2 * BLOCK), lambda i: (nb - 1 - i, 0, 0)),
            blk(128),
            blk(D),
            blk(QKV),
            whole((D, QKV)),
            whole(gvec.shape),
            pl.BlockSpec((BLOCK, 128), lambda i: (nb - 1 - i, 0)),
            pl.BlockSpec((BLOCK, 128), lambda i: (nb - 1 - i, 0)),
            HB,
            HB,
            HB,
            HB,
            HB,
            HB,
            whole(dgf.shape),
        ],
        out_specs=(
            blk(D),
            whole((D, QKV)),
            whole((24, 128)),
            whole((BLOCK, D)),
            whole((groups,) + dwo.shape[2:]),
            whole(dw2.shape[1:]),
            whole(dwd.shape[1:]),
            HB,
        ),
        out_shape=(
            SDS((nb, BLOCK, D), BF16),
            SDS((D, QKV), BF16),
            SDS((24, 128), F32),
            SDS((BLOCK, D), BF16),
            SDS((groups,) + dwo.shape[2:], BF16),
            SDS(dw2.shape[1:], BF16),
            SDS(dwd.shape[1:], F32),
            SDS(t21.shape, BF16),
        ),
        scratch_shapes=[
            pltpu.VMEM((ROWS, HEAD), BF16),
            pltpu.VMEM((ROWS, HEAD), BF16),
            pltpu.VMEM((ROWS, HEAD), F32),
            pltpu.VMEM((ROWS, HEAD), F32),
            pltpu.VMEM((2 * BLOCK, HEAD), F32),
            pltpu.VMEM((D, QKV), F32),
            pltpu.VMEM((8, 128), F32),
            DMA((7,)),
            DMA((7,)),
        ]
        + [pltpu.VMEM(a.shape, a.dtype) for a in (po, res, dwo, dw2, dwd, t21)]
        + [DMA((7,))]
        + plane_scratch((BLOCK, D))
        + plane_scratch((groups,) + dwo.shape[2:])
        + ring_scratch(n, dw2.shape[1:])
        + ring_scratch(n, dwd.shape[1:]),
        compiler_params=pltpu.CompilerParams(
            collective_id=6, has_side_effects=True, dimension_semantics=("arbitrary",), vmem_limit_bytes=VMEM_LIMIT
        ),
        cost_estimate=pl.CostEstimate(flops=8 * 10**9, bytes_accessed=16 << 20, transcendentals=4 * 10**6),
        name="attn_bwd",
    )(lengths, dmh, q, kv, lse, mixf, h, raw, wqkv, gvec, ct, st, po, res, dwo, dw2, dwd, t21, dgf)


def final_kernel(n, dh, x_, gmid_, g_ref, dw1, two, t2, gpart, dwd, gtok, o1, o2, oo, og, od, mine, x, gmid, fs, t1, gin, gsum, gz, ps, pr, gs, gr, *rest):
    me, p, g, groups, zq, zg = places(n)
    nz = groups - 1
    share = g_ref.shape[1] // n
    fetch = bring([(dh.at[p ^ (2 * i)], mine.at[i]) for i in (3, 1, 2, 0)] + [(x_, x), (gmid_, gmid)], fs)
    barrier([me ^ m for m in range(1, GROUP)] + zq)
    red = PlaneReduce(me, lambda b: dh.at[b], *rest[:7], own=lambda i: mine.at[i])
    ring1 = RingReduce(n, p, g, dw1, *rest[7:13])
    ringo = RingReduce(n, p, g, two, *rest[13:19])
    ringd = RingReduce(n, p, g, dwd, *rest[19:25])
    red.start()
    gc = start_all([rcopy(gpart, gin.at[m - 1], gs.at[m - 1], gr.at[m - 1], me ^ m) for m in range(1, GROUP)])
    ring1.start()
    ringo.start()
    ringd.start()
    pc = []

    def exchange(k, src, out):
        for m in range(1, GROUP):
            c = rcopy(src.at[p ^ m], out.at[p], ps.at[k, m - 1], pr.at[k, m - 1], me ^ m)
            c.start()
            pc.append(c)
        out[p] = src[p]

    wait_all(fetch)
    red.phase1()
    exchange(1, t2, o2)
    tot = gpart[...]
    for m in range(1, GROUP):
        gc[m - 1].wait_recv()
        tot = tot + gin[m - 1]
    gsum[...] = tot
    gzc = start_all([rcopy(gsum, gz.at[s], gs.at[7 + s], gr.at[7 + s], zq[s]) for s in range(nz)])
    ring1.relay()
    ringo.relay()
    red.phase2()
    t1[...] = ring1.finish().astype(BF16)
    exchange(0, t1, o1)
    oo[...] = ringo.finish()
    ringd.relay()
    for s in range(nz):
        gzc[s].wait_recv()
        tot = tot + gz[s]
    gsum_row = me * share
    for c in gzc:
        c.wait_send()
    gsum[...] = tot
    first = gsum_row // 128
    off = lax.rem(gsum_row, 128)
    lane = lax.broadcasted_iota(jnp.int32, (8, 128), 1)
    turn = lambda row: pltpu.roll(jnp.broadcast_to(gsum[pl.ds(row, 1), :], (8, 128)), lax.rem(128 - off, 128), 1)
    og[...] = jnp.where(lane < 128 - off, turn(first), turn(first + 1))
    dx, _ = norm_back(red.phase3(), x[...].astype(F32), g_ref[:, :D])
    gtok[...] = gmid[...] + dx
    od[...] = ringd.finish()
    wait_all(pc)
    for c in gc:
        c.wait_send()


def final(n, dh, x, gmid, gvec, dw1, two, t2, gpart, dwd):
    groups = n // GROUP
    nz = groups - 1
    return pl.pallas_call(
        functools.partial(final_kernel, n),
        out_shape=(
            SDS((BLOCK, D), F32),
            SDS(dw1.shape[1:], BF16),
            SDS(t2.shape, BF16),
            SDS(two.shape[1:], F32),
            SDS((8, 128), F32),
            SDS(dwd.shape[1:], F32),
        ),
        in_specs=[HB, HB, HB] + [VM] * 6,
        out_specs=(VM,) * 6,
        scratch_shapes=[
            pltpu.VMEM((4, BLOCK, D), BF16),
            pltpu.VMEM(x.shape, BF16),
            pltpu.VMEM(gmid.shape, F32),
            DMA((6,)),
            pltpu.VMEM(dw1.shape[1:], BF16),
            pltpu.VMEM((7, 24, 128), F32),
            pltpu.VMEM((24, 128), F32),
            pltpu.VMEM((nz, 24, 128), F32),
            DMA((2, 7)),
            DMA((2, 7)),
            DMA((7 + nz,)),
            DMA((7 + nz,)),
        ]
        + plane_scratch((BLOCK, D))
        + ring_scratch(n, dw1.shape[1:])
        + ring_scratch(n, two.shape[1:])
        + ring_scratch(n, dwd.shape[1:]),
        compiler_params=pltpu.CompilerParams(collective_id=4, has_side_effects=True, vmem_limit_bytes=VMEM_LIMIT),
        name="final",
    )(dh, x, gmid, gvec, dw1, two, t2, gpart, dwd)


def unpack_kernel(groups, result, gtok, o1, o21, o22, oo, od, od2, og, result_o, gtok_o, gq, gk, gv, go, gg, gu, gd, gn):
    result_o[...] = result[...]
    gtok_o[...] = gtok[...]
    go[...] = oo[...]
    gd[: od.shape[0]] = od[...]
    gd[od.shape[0] :] = od2[...]
    gn[...] = og[0:1, : gn.shape[1]]
    for b in range(GROUP):
        gq[:, 128 * b : 128 * (b + 1)] = o1[b, :, :128].astype(F32)
    for out, at in ((gk, slice(128, 128 + HEAD)), (gv, slice(128 + HEAD, 256))):
        for c in range(GROUP // 2):
            pair = [o1[2 * c + k, :, at].astype(F32) for k in range(2)]
            out[:, 128 * c : 128 * (c + 1)] = jnp.concatenate(pair, axis=1)
    ffc = gg.shape[1] // (groups * GROUP)
    for k, out in enumerate((gg, gu)):
        big = 5 * ffc // 9
        piece = lambda src, b, c, w: src[b, :, (k * groups + c) * w : (k * groups + c + 1) * w].astype(F32)
        parts = [
            piece(src, b, c, w)
            for c in range(groups)
            for b in range(GROUP)
            for src, w in ((o21, big), (o22, ffc - big))
        ]
        out[...] = jnp.concatenate(parts, axis=1)


def unpack(n, result, gtok, o1, o21, o22, oo, od, od2, og, share):
    r = oo.shape[0]
    return pl.pallas_call(
        functools.partial(unpack_kernel, n // GROUP),
        out_shape=(
            SDS(result.shape, BF16),
            SDS(gtok.shape, F32),
            SDS((r, D), F32),
            SDS((r, D // 2), F32),
            SDS((r, D // 2), F32),
            SDS((r, D), F32),
            SDS((r, FF), F32),
            SDS((r, FF), F32),
            SDS((od.shape[0] + od2.shape[0], D), F32),
            SDS((1, share), F32),
        ),
        in_specs=[VM] * 9,
        out_specs=(VM,) * 10,
        compiler_params=pltpu.CompilerParams(vmem_limit_bytes=VMEM_LIMIT),
        name="unpack",
    )(result, gtok, o1, o21, o22, oo, od, od2, og)


def body(n, tokens, w_query, key_weight, w_value, w_out, w_gate, w_up, w_down, norm_gains, seq_lengths, slot_order, out_grad):
    groups = n // GROUP
    r = w_query.shape[0]
    ffc = w_down.shape[0]
    share = norm_gains.shape[0]
    wok = r // 16 if r % 16 == 0 else 1
    wdk = 9
    wo_blk, wd_blk = (wok, r // wok, D), (wdk, ffc // wdk, D)
    h, raw, q, kv, mixf, lse, mix, dy_all, w21, w22, wo, wd1, wqkv, gvec, ct, st = front(
        n,
        seq_lengths,
        tokens,
        w_query,
        key_weight,
        w_value,
        w_gate,
        w_up,
        w_out.reshape(wo_blk),
        w_down.reshape(wd_blk),
        norm_gains.reshape(1, share),
        out_grad,
    )
    res, gmid, dgf, dwo, dmh, po, t21, dw22, dwd1, dwd2 = ffn_block(
        n,
        slot_order,
        mix,
        tokens,
        wo.reshape(D, D),
        gvec,
        w21.reshape(D, -1),
        w22,
        wd1.reshape(-1, D),
        w_down.reshape(wd_blk),
        dy_all,
    )
    dh1, dwqkv, gpart, result, two, t2, od, o21 = attn_bwd(
        n,
        seq_lengths,
        dmh,
        q,
        kv,
        lse,
        mixf,
        h,
        raw,
        wqkv,
        gvec,
        ct,
        st,
        po,
        res,
        dwo.reshape(groups, GROUP, r, D),
        dw22.reshape(groups, GROUP, r, -1),
        dwd1,
        t21,
        dgf,
    )
    gtok, o1, o22, oo, og, od2 = final(
        n,
        dh1,
        tokens,
        gmid,
        gvec,
        dwqkv.reshape(groups, GROUP, r, QKV),
        two.reshape((groups,) + wo_blk),
        t2,
        gpart,
        dwd2,
    )
    outs = unpack(n, result, gtok, o1, o21, o22, oo.reshape(r, D), od.reshape(-1, D), od2.reshape(-1, D), og, share)
    return outs[:-1] + (outs[-1].reshape(share),)


def solution(mesh):
    n = mesh.shape["dp"]
    row = P("dp", None)
    return jax.shard_map(
        functools.partial(body, n),
        mesh=mesh,
        in_specs=(row,) * 8 + (P("dp"), P(), P(), row),
        out_specs=(row,) * 9 + (P("dp"),),
        check_vma=False,
    )
```

```python
import functools
import math

import jax
import jax.numpy as jnp
from jax import lax
from jax.experimental import pallas as pl
from jax.experimental.pallas import tpu as pltpu
from jax.sharding import PartitionSpec as P

D = 1024
FF = 4608
QUERY_HEADS = 16
KEY_VALUE_HEADS = 8
HEAD = 64
SLOT = 128
GROUP = 8
ROWS = 2048
BLOCK = 256
QKV = 256
WINDOW = 4
VMEM_LIMIT = 62 << 20
EPSILON = 1e-05
ROPE_THETA = 1000000.0
SCALE = 1.0 / math.sqrt(HEAD)
LOG2E = math.log2(math.e)
F32 = jnp.float32
BF16 = jnp.bfloat16
MESH = pl.DeviceIdType.MESH
DMA = pltpu.SemaphoreType.DMA
VM = pl.BlockSpec(memory_space=pltpu.VMEM)
ANY = pl.BlockSpec(memory_space=pl.ANY)
HB = pl.BlockSpec(memory_space=pltpu.HBM)
SM = pl.BlockSpec(memory_space=pltpu.SMEM)
SDS = jax.ShapeDtypeStruct


def nn(a, b):
    return lax.dot_general(a, b, (((1,), (0,)), ((), ())), preferred_element_type=F32)


def nt(a, b):
    return lax.dot_general(a, b, (((1,), (1,)), ((), ())), preferred_element_type=F32)


def tn(a, b):
    return lax.dot_general(a, b, (((0,), (0,)), ((), ())), preferred_element_type=F32)


def rcopy(src, dst, send, recv, dev):
    return pltpu.make_async_remote_copy(
        src_ref=src, dst_ref=dst, send_sem=send, recv_sem=recv, device_id=(dev,), device_id_type=MESH
    )


def barrier(peers):
    sem = pltpu.get_barrier_semaphore()
    for q in peers:
        pl.semaphore_signal(sem, inc=1, device_id=(q,), device_id_type=MESH)
    pl.semaphore_wait(sem, len(peers))


def places(n):
    me = lax.axis_index("dp")
    p = lax.rem(me, GROUP)
    g = me // GROUP
    groups = n // GROUP
    zq = [lax.rem(g + s, groups) * GROUP + p for s in range(1, groups)]
    zg = [lax.rem(g + s, groups) for s in range(1, groups)]
    return me, p, g, groups, zq, zg


def start_all(copies):
    for c in copies:
        c.start()
    return copies


def bring(pairs, sem):
    return start_all([pltpu.make_async_copy(a, b, sem.at[i]) for i, (a, b) in enumerate(pairs)])


def wait_all(copies):
    for c in copies:
        c.wait()


class PlaneGather:
    COPIES = 14

    def __init__(self, me, p, src, dst, ss, rs, ls=None):
        sib, xn, yn = me ^ 1, me ^ 2, me ^ 4

        def cp(a, b, i, dev):
            return rcopy(a, b, ss.at[i], rs.at[i], dev)

        def own(i, dev):
            return [cp(src(h), dst(p, h), i + h, dev) for h in range(2)]

        def on(m, h, i, dev):
            return cp(dst(p ^ m, h), dst(p ^ m, h), i, dev)

        self.x, self.y, self.o = own(0, xn), own(2, yn), own(4, sib)
        self.r = [on(2, 0, 6, yn), on(4, 1, 7, xn)]
        self.fx = [on(2, h, 8 + h, sib) for h in range(2)]
        self.fy = [on(4, h, 10 + h, sib) for h in range(2)]
        self.fd = [on(6, h, 12 + h, sib) for h in range(2)]
        self.local = [] if ls is None else [
            pltpu.make_async_copy(src(h), dst(p, h), ls.at[h]) for h in range(2)
        ]

    def start(self):
        self.start_first()
        self.start_second()

    def start_first(self):
        start_all([self.x[0], self.y[1]] + self.o + self.local)

    def start_second(self):
        start_all([self.x[1], self.y[0]])

    def relay1(self):
        self.x[0].wait_recv()
        start_all([self.r[0], self.fx[0]])
        self.y[1].wait_recv()
        start_all([self.r[1], self.fy[1]])

    def relay2(self):
        self.x[1].wait_recv()
        self.fx[1].start()
        self.y[0].wait_recv()
        self.fy[0].start()

    def relay3(self):
        for h in range(2):
            self.r[h].wait_recv()
            self.fd[h].start()

    def arrive(self, copies):
        for c in copies:
            c.wait_recv()

    def sent(self):
        for c in self.x + self.y + self.r + self.o + self.fx + self.fy + self.fd:
            c.wait_send()
        wait_all(self.local)

    def finish(self):
        self.arrive(self.o + self.fx + self.fy + self.fd)
        self.sent()


class Ring:
    def __init__(self, n, p, g, src, dst, ss, rs, ls=None):
        groups = n // GROUP
        to = lambda s: lax.rem(g + s, groups) * GROUP + p
        at = lambda s: lax.rem(g + s, groups)

        def cp(a, b, i, dev):
            return rcopy(a, b, ss.at[i], rs.at[i], dev)

        self.relays = []
        if groups == 4:
            self.up = [cp(src(h), dst(g, h), h, to(1)) for h in range(2)]
            self.down = [cp(src(h), dst(g, h), 2 + h, to(3)) for h in range(2)]
            self.first = [self.up[0], self.down[1], self.up[1], self.down[0]]
            below, above = at(3), at(1)
            self.relays = [cp(dst(below, 0), dst(below, 0), 4, to(1)), cp(dst(above, 1), dst(above, 1), 5, to(3))]
        else:
            self.first = [cp(src(None), dst(g, None), s - 1, to(s)) for s in range(1, groups)]
        self.local = [] if ls is None else [pltpu.make_async_copy(src(None), dst(g, None), ls)]

    def start(self):
        start_all(self.first + self.local)

    def relay(self):
        if self.relays:
            self.up[0].wait_recv()
            self.relays[0].start()
            self.down[1].wait_recv()
            self.relays[1].start()

    def finish(self):
        if self.relays:
            self.up[1].wait_recv()
            self.down[0].wait_recv()
            for c in self.first:
                c.wait_send()
        else:
            wait_all(self.first)
        wait_all(self.relays + self.local)


def ring_count(n):
    return max(6, n // GROUP - 1)


def halves(length, base=0):
    cut = length // 2
    part = (pl.ds(base, cut), pl.ds(base + cut, length - cut))
    return lambda h: pl.ds(base, length) if h is None else part[h]


class RingReduce:
    def __init__(self, n, p, g, part, low, high, send, fin, ss, rs):
        groups = n // GROUP
        to = lambda s: lax.rem(g + s, groups) * GROUP + p
        at = lambda s: lax.rem(g + s, groups)
        hs = halves(part.shape[1])
        self.part, self.fin, self.send, self.g, self.hs = part, fin, send, g, hs

        def cp(a, b, i, dev):
            return rcopy(a, b, ss.at[i], rs.at[i], dev)

        self.ring = groups == 4
        if self.ring:
            self.above, self.below = at(1), at(3)
            self.low, self.high = low, high
            far = at(2)
            self.a = cp(part.at[far, hs(0)], low, 0, to(1))
            self.b = cp(part.at[far, hs(1)], high, 1, to(3))
            self.c = cp(part.at[self.above, hs(1)], fin.at[0, hs(1)], 2, to(1))
            self.d = cp(part.at[self.below, hs(0)], fin.at[1, hs(0)], 3, to(3))
            self.e = cp(send.at[hs(0)], fin.at[0, hs(0)], 4, to(1))
            self.f = cp(send.at[hs(1)], fin.at[1, hs(1)], 5, to(3))
            self.all = [self.a, self.b, self.c, self.d, self.e, self.f]
        else:
            self.all = [cp(part.at[at(s)], fin.at[s - 1], s - 1, to(s)) for s in range(1, groups)]
        self.count = groups - 1

    def start(self):
        start_all(self.all[:4] if self.ring else self.all)

    def relay(self):
        if self.ring:
            for got, buf, h, b, out in (
                (self.a, self.low, 0, self.above, self.e),
                (self.b, self.high, 1, self.below, self.f),
            ):
                got.wait_recv()
                at = self.hs(h)
                self.send[at] = (self.part[b, at].astype(F32) + buf[...].astype(F32)).astype(BF16)
                out.start()

    def finish(self):
        for c in self.all[2:] if self.ring else self.all:
            c.wait_recv()
        val = self.part[self.g].astype(F32)
        for s in range(2 if self.ring else self.count):
            val = val + self.fin[s].astype(F32)
        for c in self.all:
            c.wait_send()
        return val


def ring_scratch(n, shape):
    cut = shape[0] // 2
    groups = n // GROUP
    count = 2 if groups == 4 else groups - 1
    tail = tuple(shape[1:])
    vm = lambda s: pltpu.VMEM(s, BF16)
    return [
        vm((max(cut, 1),) + tail),
        vm((shape[0] - cut,) + tail),
        vm(tuple(shape)),
        vm((count,) + tuple(shape)),
        DMA((ring_count(n),)),
        DMA((ring_count(n),)),
    ]


class PlaneReduce:
    def __init__(self, me, part, sib, send, relay, fx, fy, ss, rs, own=None):
        p = lax.rem(me, GROUP)
        self.own = own or (lambda i: part(p ^ (2 * i)))
        xn, yn = me ^ 2, me ^ 4
        hs = halves(sib.shape[1])
        self.hs, self.p, self.part = hs, p, part
        self.sib, self.send, self.relay, self.fx, self.fy = sib, send, relay, fx, fy

        def cp(a, b, i, dev):
            return rcopy(a, b, ss.at[i], rs.at[i], dev)

        self.first = [cp(part(p ^ (2 * i + 1)), sib.at[i], i, me ^ 1) for i in range(4)]
        self.diag = [cp(send.at[0, hs(0)], relay.at[0], 4, xn), cp(send.at[0, hs(1)], relay.at[1], 5, yn)]
        self.toy = [cp(send.at[2, hs(h)], fy.at[hs(h)], 6 + h, yn) for h in range(2)]
        self.tox = [cp(send.at[1, hs(h)], fx.at[hs(h)], 8 + h, xn) for h in range(2)]

    def start(self):
        start_all([self.first[i] for i in (3, 1, 2, 0)])

    def chip(self, i):
        self.first[i].wait_recv()
        return self.own(i)[...].astype(F32) + self.sib[i].astype(F32)

    def chip_d(self):
        self.send[0] = self.chip(3).astype(BF16)
        start_all(self.diag)

    def chip_x(self):
        self.send[1] = self.chip(1).astype(BF16)
        self.tox[0].start()

    def chip_y(self):
        self.send[2] = self.chip(2).astype(BF16)
        self.toy[1].start()

    def phase1(self):
        self.chip_d()
        self.chip_x()
        self.chip_y()

    def phase2(self):
        self.diag[0].wait_recv()
        at = self.hs(0)
        self.send[2, at] = (self.send[2, at].astype(F32) + self.relay[0].astype(F32)).astype(BF16)
        self.toy[0].start()
        self.diag[1].wait_recv()
        at = self.hs(1)
        self.send[1, at] = (self.send[1, at].astype(F32) + self.relay[1].astype(F32)).astype(BF16)
        self.tox[1].start()

    def phase3(self):
        own = self.chip(0)
        for c in self.toy + self.tox:
            c.wait_recv()
        own = own + self.fx[...].astype(F32) + self.fy[...].astype(F32)
        for c in self.first + self.diag + self.toy + self.tox:
            c.wait_send()
        return own


def plane_scratch(shape):
    tail = tuple(shape[1:])
    vm = lambda *s: pltpu.VMEM(s + tail, BF16)
    return [
        vm(4, shape[0]),
        vm(3, shape[0]),
        vm(2, shape[0] // 2),
        vm(shape[0]),
        vm(shape[0]),
        DMA((10,)),
        DMA((10,)),
    ]


def swap_halves(v):
    lane = lax.broadcasted_iota(jnp.int32, v.shape, 1)
    low = lax.rem(lane, HEAD) < HEAD // 2
    width = v.shape[1]
    return jnp.where(low, pltpu.roll(v, width - HEAD // 2, 1), pltpu.roll(v, HEAD // 2, 1))


def head_mean(v):
    row = lax.broadcasted_iota(jnp.int32, (128, 128), 0)
    lane = lax.broadcasted_iota(jnp.int32, (128, 128), 1)
    same = jnp.where((row < HEAD) == (lane < HEAD), 1.0 / HEAD, 0.0).astype(BF16)
    high = v.astype(BF16)
    low = (v - high.astype(F32)).astype(BF16)
    return nn(high, same) + nn(low, same)


def head_gains(g_ref):
    t = g_ref[:, 2 * D :]
    t = jnp.broadcast_to(t, (8, 128))
    lane = lax.broadcasted_iota(jnp.int32, (8, 128), 1)
    other = pltpu.roll(t, HEAD, 1)
    return jnp.where(lane < HEAD, t, other)[0:1, :], jnp.where(lane < HEAD, other, t)[0:1, :]


def seq_start(row, len_ref, g):
    e1 = len_ref[g, 0]
    e2 = e1 + len_ref[g, 1]
    e3 = e2 + len_ref[g, 2]
    zero = row * 0
    s = jnp.where(row >= e1, zero + e1, zero)
    s = jnp.where(row >= e2, zero + e2, s)
    return jnp.where(row >= e3, zero + e3, s)


def windows(i, window):
    for low, high, count in ((0, 1, 2), (2, 3, 4), (4, 7, WINDOW + 1)):

        @pl.when((i >= low) & (i <= high))
        def _():
            window(jnp.maximum(i - WINDOW, 0), count)


def front_kernel(n, len_ref, x_, wq_, wk_, wv_, wg_, wu_, wo_, wd_, gn_, dy_, h_o, raw_o, q_o, kv_o, mixf_o, lse_o, mixo, dyo, w21o, w22o, woo, wdo, wqkv_o, gvec, ct, st, xa, gn, wq, wk, wv, wo, wd, wg, wu, dy, a1, b1, b2, gt, gto, w1v, woz, wqkv, h_s, raw_s, q_s, kv_s, mixf_s, lse_s, mixs, k_s, v_s, acc, fs, ls, xs, xr, ds_, dr, os_, orr, ps, pr, zs, zr, ms, mr, outs):
    me, p, g, groups, zq, zg = places(n)
    fetch = bring(
        (
            (x_, xa.at[p]),
            (gn_, gn),
            (wq_, wq),
            (wk_, wk),
            (wv_, wv),
            (wo_, wo),
            (wd_.at[pl.ds(0, wd.shape[0])], wd),
            (wg_, wg),
            (wu_, wu),
            (dy_, dy),
        ),
        fs,
    )
    share = gn.shape[1]
    ffc = wg.shape[1] // (groups * GROUP)
    big = 5 * ffc // 9
    r = wq.shape[0]
    barrier([me ^ m for m in range(1, GROUP)] + zq)
    hx, ho = halves(BLOCK), halves(groups)
    xg = PlaneGather(me, p, lambda h: xa.at[p, hx(h)], lambda b, h: xa.at[b, hx(h)], xs, xr)
    dg = PlaneGather(me, p, lambda h: dy.at[hx(h)], lambda b, h: dyo.at[b, hx(h)], ds_, dr, ls.at[pl.ds(0, 2)])
    og = PlaneGather(me, p, lambda h: woz.at[ho(h)], lambda b, h: woo.at[ho(h), b], os_, orr, ls.at[pl.ds(2, 2)])
    def ring(k, src, dst, local=None):
        hk = halves(dst.shape[1])
        return Ring(n, p, g, lambda h: src.at[hk(h)], lambda b, h: dst.at[b, hk(h)], zs.at[k], zr.at[k], local)

    wring, gring = ring(0, w1v.at[g], w1v), ring(1, gto.at[g], gto)
    dring, oring = ring(2, wd, wdo, ls.at[4]), ring(3, wo, woz, ls.at[5])
    uring = ring(4, w21o.at[g], w21o)
    pc = {}

    def exchange(k, src, dst):
        for m in range(1, GROUP):
            pc[k, m] = rcopy(src(p ^ m), dst, ps.at[k, m - 1], pr.at[k, m - 1], me ^ m)
            pc[k, m].start()

    def arrived(k):
        for m in range(1, GROUP):
            pc[k, m].wait_recv()


    def pack(buf, low, high):
        for b in range(GROUP):
            at = [slice((GROUP * k + b) * ffc + low, (GROUP * k + b) * ffc + high) for k in range(groups)]
            buf[b] = jnp.concatenate([wg[:, k] for k in at] + [wu[:, k] for k in at], axis=1)

    fetch[0].wait()
    xg.start_first()
    fetch[1].wait()
    gt[...] = jnp.zeros_like(gt)
    gt[0:1, :share] = gn[...].astype(F32)
    gto[g, p] = gt[...]
    exchange(1, lambda b: gt, gto.at[g, p])
    wait_all(fetch[2:5])
    for b in range(GROUP):
        a1[b, :, :128] = wq[:, 128 * b : 128 * (b + 1)]
        at = slice(HEAD * b, HEAD * (b + 1))
        a1[b, :, 128:] = jnp.concatenate([wk[:, at], wv[:, at]], axis=1)
    exchange(0, lambda b: a1.at[b], w1v.at[g, p])
    w1v[g, p] = a1[p]
    fetch[5].wait()
    oring.start()
    fetch[6].wait()
    dring.start()
    wait_all(fetch[7:9])
    pack(b1, 0, big)
    exchange(2, lambda b: b1.at[b], w21o.at[g, p])
    local = start_all([pltpu.make_async_copy(b1.at[p], w21o.at[g, p], ls.at[6])])
    pack(b2, big, ffc)
    exchange(3, lambda b: b2.at[b], w22o.at[p])
    local += start_all([pltpu.make_async_copy(b2.at[p], w22o.at[p], ls.at[7])])
    xg.start_second()
    arrived(0)
    wring.start()
    arrived(1)
    gring.start()
    arrived(2)
    local[0].wait()
    uring.start()
    xg.relay1()
    fetch[9].wait()
    dg.start_first()
    row = lax.broadcasted_iota(jnp.int32, (1, ROWS), 1)
    position = (row - seq_start(row, len_ref, g)).astype(F32)
    index = lax.broadcasted_iota(jnp.int32, (HEAD // 2, 1), 0).astype(F32)
    angles = jnp.exp(index * (-2.0 * math.log(ROPE_THETA) / HEAD)) * position
    c, s = jnp.cos(angles).T, jnp.sin(angles).T
    ct[...] = jnp.concatenate([c, c, c, c], axis=1)
    st[...] = jnp.concatenate([-s, s, -s, s], axis=1)
    k_s[: WINDOW * BLOCK] = jnp.zeros((WINDOW * BLOCK, HEAD), BF16)
    v_s[: WINDOW * BLOCK] = jnp.zeros((WINDOW * BLOCK, 128), BF16)
    xg.relay2()
    for c in (wring, gring):
        c.relay()
    xg.relay3()
    dg.start_second()
    wring.finish()
    gring.finish()
    for k in range(groups * GROUP):
        wqkv[k * r : (k + 1) * r] = w1v[k // GROUP, k % GROUP]
    gvec[...] = jnp.concatenate(
        [gto[k, b, 0:1, :share] for k in range(groups) for b in range(GROUP)], axis=1
    )
    xg.arrive(xg.o + xg.fx + xg.fy + xg.fd)
    gq, gk = head_gains(gvec)
    results = ((h_s, h_o), (raw_s, raw_o), (q_s, q_o), (kv_s, kv_o), (mixf_s, mixf_o), (lse_s, lse_o))

    def block(i, carry):
        @pl.when(i == 0)
        def _():
            oring.relay()
            dg.relay1()

        @pl.when(i == 1)
        def _():
            oring.finish()
            og.start_first()

        @pl.when(i == 2)
        def _():
            og.start_second()

        @pl.when(i == 3)
        def _():
            uring.relay()
            dg.relay2()

        @pl.when(i == 5)
        def _():
            og.relay1()
            dg.relay3()

        @pl.when(i == 6)
        def _():
            dring.relay()

        @pl.when(i == 7)
        def _():
            og.relay2()

        at = pl.ds(pl.multiple_of(i * BLOCK, BLOCK), BLOCK)
        xb = xa[i].astype(F32)
        h = (xb * lax.rsqrt(jnp.mean(xb * xb, axis=-1, keepdims=True) + EPSILON) * gvec[:, :D]).astype(BF16)
        h_s[i] = h
        raw = nn(h, wqkv[...])
        raw_s[i] = raw
        cb, sb = ct[at, :], st[at, :]
        qraw, kvraw = raw[:, :128], raw[:, 128:]
        qn = qraw * lax.rsqrt(head_mean(qraw * qraw) + EPSILON) * gq
        q = (qn * cb + swap_halves(qn) * sb).astype(BF16)
        kn = kvraw * lax.rsqrt(head_mean(kvraw * kvraw) + EPSILON) * gk
        k = (kn * cb + swap_halves(kn) * sb).astype(BF16)
        lane = lax.broadcasted_iota(jnp.int32, (BLOCK, 128), 1)
        kv = jnp.where(lane < HEAD, k.astype(F32), kvraw).astype(BF16)
        q_s[i] = q
        kv_s[i] = kv
        k_s[at, :] = kv[:, :HEAD]
        v_s[at, :] = jnp.where(lane < HEAD, pltpu.roll(kvraw, HEAD, 1), 1.0).astype(BF16)
        q2 = jnp.concatenate([q[:, :HEAD], q[:, HEAD:]], axis=0)
        rows = lax.broadcasted_iota(jnp.int32, (2 * BLOCK, 1), 0)
        qrow = i * BLOCK + jnp.where(rows >= BLOCK, rows - BLOCK, rows)
        qstart = seq_start(qrow, len_ref, g)

        def window(first, count):
            span = pl.ds(pl.multiple_of(first * BLOCK, BLOCK), count * BLOCK)
            kc = lax.broadcasted_iota(jnp.int32, (2 * BLOCK, count * BLOCK), 1) + first * BLOCK
            ok = (kc >= qstart) & (kc <= qrow)
            e = jnp.where(ok, jnp.exp2(nt(q2, k_s[span, :]) * (SCALE * LOG2E)), 0.0).astype(BF16)
            acc[...] = nn(e, v_s[span, :])

        windows(i, window)
        total = acc[:, HEAD:]
        m = acc[:, :HEAD] / total
        both = jnp.concatenate([m[:BLOCK], m[BLOCK:]], axis=1)
        mixf_s[i] = both
        lse_s[i] = jnp.log2(total.T)[:8, :]
        mixs[i] = both.astype(BF16)

        @pl.when(i == p)
        def _():
            pltpu.make_async_copy(mixs.at[i], mixo.at[p], ls.at[8]).start()

        @pl.when(i != p)
        def _():
            rcopy(mixs.at[i], mixo.at[p], ms.at[p ^ i], mr.at[p ^ i], me ^ p ^ i).start()

        for k, (a, b) in enumerate(results):
            pltpu.make_async_copy(a.at[i], b.at[i], outs.at[k, i]).start()
        return carry

    lax.fori_loop(0, GROUP, block, 0)
    wq_out = pltpu.make_async_copy(wqkv, wqkv_o, ls.at[9])
    wq_out.start()
    og.relay3()
    for c in pc.values():
        c.wait_send()
    arrived(3)
    local[1].wait()
    for c in (dring, uring):
        c.finish()
    xg.sent()
    dg.finish()
    og.finish()
    for m in range(1, GROUP):
        rcopy(mixs.at[p ^ m], mixo.at[p], ms.at[m], mr.at[m], me ^ m).wait()
    pltpu.make_async_copy(mixs.at[p], mixo.at[p], ls.at[8]).wait()
    for k, (a, b) in enumerate(results):
        for i in range(GROUP):
            pltpu.make_async_copy(a.at[i], b.at[i], outs.at[k, i]).wait()
    wq_out.wait()


def front(n, lengths, x, wq, wk, wv, wg, wu, wo, wd, gn, dy):
    groups = n // GROUP
    r = wq.shape[0]
    wide = 2 * wg.shape[1] // GROUP
    wide1 = 5 * wide // 9
    wd1 = (5 * wd.shape[0] // 9,) + wd.shape[1:]
    vm = lambda *s: pltpu.VMEM(s, BF16)
    vf = lambda *s: pltpu.VMEM(s, F32)
    return pl.pallas_call(
        functools.partial(front_kernel, n),
        out_shape=(
            SDS((GROUP, BLOCK, D), BF16),
            SDS((GROUP, BLOCK, QKV), F32),
            SDS((GROUP, BLOCK, 128), BF16),
            SDS((GROUP, BLOCK, 128), BF16),
            SDS((GROUP, BLOCK, 128), F32),
            SDS((GROUP, 8, 2 * BLOCK), F32),
            SDS((GROUP, BLOCK, 128), BF16),
            SDS((GROUP, BLOCK, D), BF16),
            SDS((groups, GROUP, r, wide1), BF16),
            SDS((GROUP, r, wide - wide1), BF16),
            SDS((groups, GROUP) + wo.shape, BF16),
            SDS((groups,) + wd1, BF16),
            SDS((D, QKV), BF16),
            SDS((1, gn.shape[1] * n), F32),
            SDS((ROWS, 128), F32),
            SDS((ROWS, 128), F32),
        ),
        in_specs=[SM] + [HB] * 10,
        out_specs=(HB,) * 13 + (VM,) * 3,
        scratch_shapes=[vm(GROUP, BLOCK, D)]
        + [vm(*s) for s in (gn.shape, wq.shape, wk.shape, wv.shape, wo.shape, wd1, wg.shape, wu.shape, dy.shape)]
        + [
            vm(GROUP, r, QKV),
            vm(GROUP, r, wide1),
            vm(GROUP, r, wide - wide1),
            vf(8, 128),
            vf(groups, GROUP, 8, 128),
            vm(groups, GROUP, r, QKV),
            vm(groups, *wo.shape),
            vm(D, QKV),
            vm(GROUP, BLOCK, D),
            vf(GROUP, BLOCK, QKV),
            vm(GROUP, BLOCK, 128),
            vm(GROUP, BLOCK, 128),
            vf(GROUP, BLOCK, 128),
            vf(GROUP, 8, 2 * BLOCK),
            vm(GROUP, BLOCK, 128),
            vm(ROWS, HEAD),
            vm(ROWS, 128),
            vf(2 * BLOCK, 128),
            DMA((10,)),
            DMA((10,)),
            DMA((14,)),
            DMA((14,)),
            DMA((14,)),
            DMA((14,)),
            DMA((14,)),
            DMA((14,)),
            DMA((4, 7)),
            DMA((4, 7)),
            DMA((5, ring_count(n))),
            DMA((5, ring_count(n))),
            DMA((GROUP,)),
            DMA((GROUP,)),
            DMA((6, GROUP)),
        ],
        compiler_params=pltpu.CompilerParams(collective_id=1, has_side_effects=True, vmem_limit_bytes=VMEM_LIMIT),
        name="front",
    )(lengths, x, wq, wk, wv, wg, wu, wo, wd, gn, dy)


def norm_back(dyv, xv, gain):
    r = lax.rsqrt(jnp.mean(xv * xv, axis=-1, keepdims=True) + EPSILON)
    xr = xv * r
    gy = dyv * gain
    dx = r * (gy - xr * jnp.mean(gy * xr, axis=-1, keepdims=True))
    return dx, jnp.sum(dyv * xr, axis=0, keepdims=True)


def unit_grads(h, dyb, wgu, wd):
    f = wd.shape[0]
    gu = nn(h, wgu)
    da = nt(dyb, wd)
    gp, up = gu[:, :f], gu[:, f:]
    sig = 1.0 / (1.0 + jnp.exp(-gp))
    sg = gp * sig
    dg = (da * up * (sig * (1.0 + gp * (1.0 - sig)))).astype(BF16)
    return (sg * up).astype(BF16), jnp.concatenate([dg, (da * sg).astype(BF16)], axis=1)


def ffn_block_kernel(n, order, mix_, x_, wo_, g_ref, w21_, w22_, wd1_, wd2_, dy_, res_o, gmid_o, dgf, dwo_o, dmh, po, t21, dw22_o, dwd1_o, dwd2_o, res, gmid, dwo, dw22, dwd1, dwd2, sent, x, wo, w21, dy, fs, mbuf, h2, h2t, w2v, w22, wdv, wds, dys, acts1, acts2, dgu1, dgu2, dw21, part, mown, stage, hs, hr, os_, qs, qr, zs, zr, *red_refs):
    me, p, g, groups, zq, zg = places(n)
    f1 = wd1_.shape[0]
    f2 = wds.shape[0] - f1
    fetch = bring(
        (
            (wd2_.at[pl.ds(wd2_.shape[0] - wdv.shape[1], wdv.shape[1])], wdv.at[g]),
            (w22_, w2v.at[g]),
            (mix_, mbuf),
            (x_, x),
            (wo_, wo),
            (w21_, w21),
            (wd1_, wds.at[pl.ds(0, f1)]),
            (dy_, dy),
        ),
        fs,
    )
    barrier([me ^ m for m in range(1, GROUP)] + zq)
    gf = g_ref.at[:, D : 2 * D]
    r = w2v.shape[2]
    away = [
        pltpu.make_async_copy(a, b, sent.at[k])
        for k, (a, b) in enumerate(
            ((res, res_o), (gmid, gmid_o), (dwo, dwo_o), (dw22, dw22_o), (dwd1, dwd1_o), (dwd2, dwd2_o))
        )
    ]

    def holder(q):
        s = 0
        for k in range(ROWS // SLOT):
            s = jnp.where(order[g, k] == q, k, s)
        return s

    hw, h8 = halves(wdv.shape[1]), halves(GROUP)
    wrings = [
        Ring(n, p, g, lambda h: w2v.at[g, h8(h)], lambda b, h: w2v.at[b, h8(h)], zs.at[0], zr.at[0]),
        Ring(n, p, g, lambda h: wdv.at[g, hw(h)], lambda b, h: wdv.at[b, hw(h)], zs.at[1], zr.at[1]),
    ]
    wait_all(fetch[:2])
    for c in wrings:
        c.start()
    wait_all(fetch[2:5])
    m = jnp.concatenate([mbuf[b] for b in range(GROUP)], axis=1)
    mown[...] = m
    z = x[...].astype(F32) + nn(m, wo[...])
    res[...] = z
    away[0].start()
    h2[p] = (z * lax.rsqrt(jnp.mean(z * z, axis=-1, keepdims=True) + EPSILON) * gf[...]).astype(BF16)
    hb = halves(BLOCK)
    hg = PlaneGather(me, p, lambda h: h2.at[p, hb(h)], lambda b, h: h2.at[b, hb(h)], hs, hr)
    red = PlaneReduce(me, lambda b: part.at[b], *red_refs[:7])
    ring21 = RingReduce(n, p, g, dw21, *red_refs[7:])
    hg.start()
    wait_all(fetch[5:])

    def first(t, carry):
        @pl.when(t == 1)
        def _():
            hg.arrive(hg.o)

        @pl.when(t == 2)
        def _():
            hg.relay1()
            hg.relay2()

        @pl.when(t == 3)
        def _():
            hg.arrive(hg.fx)

        @pl.when(t == 3)
        def _():
            for c in wrings:
                c.relay()

        @pl.when(t == 5)
        def _():
            hg.arrive(hg.fy)

        @pl.when(t == 6)
        def _():
            hg.relay3()

        @pl.when(t == 7)
        def _():
            hg.arrive(hg.fd)

        b = p ^ t
        dys[b] = jnp.concatenate([dy[holder(2 * b)], dy[holder(2 * b + 1)]], axis=0)
        h2t[:, pl.ds(pl.multiple_of(b * BLOCK, BLOCK), BLOCK)] = h2[b].T
        acts1[b], dgu1[b] = unit_grads(h2[b], dys[b], w21[...], wds[:f1])
        part[b] = nt(dgu1[b], w21[...]).astype(BF16)
        return carry

    lax.fori_loop(0, GROUP, first, 0)
    grad1 = nn(h2t[...], dgu1[...].reshape(ROWS, 2 * f1)).astype(BF16)
    for k in range(groups * GROUP):
        dw21[k // GROUP, k % GROUP] = grad1[k * r : (k + 1) * r]
    ring21.start()
    for c in wrings:
        c.finish()
    for k in range(groups * GROUP):
        w22[k * r : (k + 1) * r] = w2v[k // GROUP, k % GROUP]
    each = f2 // groups
    for k in range(groups):
        wds[f1 + k * each : f1 + (k + 1) * each] = wdv[k].reshape(each, D)

    def second(t, carry):
        @pl.when(t == 1)
        def _():
            red.first[3].start()

        @pl.when(t == 3)
        def _():
            red.first[2].start()
            red.chip_d()

        @pl.when(t == 5)
        def _():
            red.first[1].start()
            red.chip_y()

        @pl.when(t == 7)
        def _():
            red.first[0].start()
            red.chip_x()

        b = p ^ (GROUP - 1 - t)
        acts2[b], dgu2[b] = unit_grads(h2[b], dys[b], w22[...], wds[f1:])
        part[b] = (part[b].astype(F32) + nt(dgu2[b], w22[...])).astype(BF16)
        return carry

    lax.fori_loop(0, GROUP, second, 0)
    dy_rows = dys[...].reshape(ROWS, D)
    for acts, out, rows in ((acts1, dwd1, f1), (acts2, dwd2, f2)):
        dw = tn(acts[...].reshape(ROWS, rows), dy_rows).astype(BF16)
        part_rows = rows // groups
        for k in range(groups):
            out[k] = dw[k * part_rows : (k + 1) * part_rows].reshape(out.shape[1:])
    start_all(away[4:])
    red.phase2()
    ring21.relay()
    dw22[...] = nn(h2t[...], dgu2[...].reshape(ROWS, 2 * f2)).astype(BF16)
    away[3].start()
    dx, dgain = norm_back(red.phase3(), res[...], gf[...])
    gm = dys[p].astype(F32) + dx
    gmid[...] = gm
    away[1].start()
    dgf[...] = dgain
    gl = gm.astype(BF16)
    dm = nt(gl, wo[...]).astype(BF16)
    for b in range(GROUP):
        mbuf[b] = dm[:, 128 * b : 128 * (b + 1)]
    qc = start_all(
        [rcopy(mbuf.at[p ^ m], dmh.at[p], qs.at[m - 1], qr.at[m - 1], me ^ m) for m in range(1, GROUP)]
    )
    dmh[p] = mbuf[p]
    dwo[...] = tn(mown[...], gl).astype(BF16)
    away[2].start()

    def out(b, carry):
        slot = lax.rem(b, 2)

        @pl.when(b > 1)
        def _():
            pltpu.make_async_copy(stage.at[slot], po.at[b - 2], os_.at[slot]).wait()

        stage[slot] = (nn(acts1[b], wds[:f1]) + nn(acts2[b], wds[f1:])).astype(BF16)
        pltpu.make_async_copy(stage.at[slot], po.at[b], os_.at[slot]).start()
        return carry

    lax.fori_loop(0, GROUP, out, 0)
    for b in range(GROUP - 2, GROUP):
        pltpu.make_async_copy(stage.at[b % 2], po.at[b], os_.at[b % 2]).wait()
    wait_all(qc)
    hg.sent()
    t21[...] = ring21.finish().astype(BF16)
    wait_all(away)


def ffn_block(n, order, mix, x, wo, gvec, w21, w22, wd1, wd, dy):
    groups = n // GROUP
    r = w22.shape[1]
    f1, f2 = w21.shape[1] // 2, w22.shape[2] // 2
    wd2 = (4 * wd.shape[0] // 9,) + wd.shape[1:]
    wd1_blk = (5 * wd.shape[0] // 9,) + wd.shape[1:]
    blk = (GROUP, r, 2 * f1)
    vm = lambda *s: pltpu.VMEM(s, BF16)
    return pl.pallas_call(
        functools.partial(ffn_block_kernel, n),
        out_shape=(
            SDS((BLOCK, D), F32),
            SDS((BLOCK, D), F32),
            SDS((1, D), F32),
            SDS((D, D), BF16),
            SDS((GROUP, BLOCK, 128), BF16),
            SDS((GROUP, BLOCK, D), BF16),
            SDS(blk, BF16),
            SDS((D, 2 * f2), BF16),
            SDS((groups,) + wd1_blk, BF16),
            SDS((groups,) + wd2, BF16),
        ),
        in_specs=[SM, HB, HB, HB, VM, HB, HB, HB, HB, HB],
        out_specs=(HB, HB, VM, HB, VM, HB, VM, HB, HB, HB),
        scratch_shapes=[
            pltpu.VMEM((BLOCK, D), F32),
            pltpu.VMEM((BLOCK, D), F32),
            vm(D, D),
            vm(D, 2 * f2),
            vm(groups, *wd1_blk),
            vm(groups, *wd2),
            DMA((6,)),
            vm(BLOCK, D),
            vm(D, D),
            vm(D, 2 * f1),
            vm(ROWS // SLOT, SLOT, D),
            DMA((8,)),
            vm(GROUP, BLOCK, 128),
            vm(GROUP, BLOCK, D),
            vm(D, ROWS),
            vm(groups, *w22.shape),
            vm(D, 2 * f2),
            vm(groups, *wd2),
            vm(f1 + f2, D),
            vm(GROUP, BLOCK, D),
            vm(GROUP, BLOCK, f1),
            vm(GROUP, BLOCK, f2),
            vm(GROUP, BLOCK, 2 * f1),
            vm(GROUP, BLOCK, 2 * f2),
            vm(groups, *blk),
            vm(GROUP, BLOCK, D),
            vm(BLOCK, D),
            vm(2, BLOCK, D),
            DMA((14,)),
            DMA((14,)),
            DMA((2,)),
            DMA((7,)),
            DMA((7,)),
            DMA((2, ring_count(n))),
            DMA((2, ring_count(n))),
        ]
        + plane_scratch((BLOCK, D))
        + ring_scratch(n, blk),
        compiler_params=pltpu.CompilerParams(collective_id=2, has_side_effects=True, vmem_limit_bytes=VMEM_LIMIT),
        name="ffn_block",
    )(order, mix, x, wo, gvec, w21, w22, wd1, wd, dy.reshape(ROWS // SLOT, SLOT, D))


def attn_bwd_kernel(n, len_ref, dm_ref, q_ref, kvall_ref, lse_ref, mixf_ref, h_ref, raw_ref, w_ref, g_ref, ct_ref, st_ref, po_, res_, dwo_, dw2_, dwd_, t21_, dgf, dh_ref, dw_ref, gpart, result, two, t2, od, o21, k_s, v_s, dk_s, dv_s, dqt, dws, dg_ref, es, er, po, res, dwo, dw2, dwd, t21, fs, *rest):
    step_id = pl.program_id(0)
    nb = ROWS // BLOCK
    i = nb - 1 - step_id
    me, p, g, groups, zq, zg = places(n)
    ored = PlaneReduce(me, lambda b: po.at[b], *rest[:7])
    wred = PlaneReduce(me, lambda b: dwo.at[:, b], *rest[7:14])
    ring2 = RingReduce(n, p, g, dw2, *rest[14:20])
    ringd = RingReduce(n, p, g, dwd, *rest[20:26])
    fetch = [
        pltpu.make_async_copy(a, b, fs.at[k])
        for k, (a, b) in enumerate(
            ((dwd_, dwd), (dw2_, dw2), (po_, po), (dwo_, dwo), (t21_, t21), (res_, res))
        )
    ]
    ex = [rcopy(t21.at[p ^ m], o21.at[p], es.at[m - 1], er.at[m - 1], me ^ m) for m in range(1, GROUP)]
    own_copy = pltpu.make_async_copy(t21.at[p], o21.at[p], fs.at[6])

    @pl.when(step_id == 0)
    def _():
        start_all(fetch)
        barrier([me ^ m for m in range(1, GROUP)] + zq)

    @pl.when(step_id == 1)
    def _():
        ored.phase1()
        wred.phase1()

    @pl.when(step_id == 3)
    def _():
        ringd.relay()
        ring2.relay()
        ored.phase2()

    @pl.when(step_id == 4)
    def _():
        wred.phase2()


    @pl.when(step_id == 0)
    def _():
        dk_s[...] = jnp.zeros_like(dk_s)
        dv_s[...] = jnp.zeros_like(dv_s)
        dws[...] = jnp.zeros_like(dws)
        dg_ref[...] = jnp.zeros_like(dg_ref)
        for b in range(ROWS // BLOCK):
            kvb = kvall_ref[b]
            k_s[pl.ds(b * BLOCK, BLOCK), :] = kvb[:, :HEAD]
            v_s[pl.ds(b * BLOCK, BLOCK), :] = kvb[:, HEAD:]

    q, do, mf = q_ref[0], dm_ref[0], mixf_ref[0]
    q2 = jnp.concatenate([q[:, :HEAD], q[:, HEAD:]], axis=0)
    do2 = jnp.concatenate([do[:, :HEAD], do[:, HEAD:]], axis=0)
    prod = (do.astype(F32) * mf).T
    delta = jnp.concatenate(
        [jnp.sum(prod[:HEAD], axis=0, keepdims=True), jnp.sum(prod[HEAD:], axis=0, keepdims=True)], axis=1
    )
    lse = lse_ref[0, 0:1, :]
    colq = lax.broadcasted_iota(jnp.int32, (1, 2 * BLOCK), 1)
    qrow = i * BLOCK + jnp.where(colq >= BLOCK, colq - BLOCK, colq)
    qstart = seq_start(qrow, len_ref, g)

    def window(first, count):
        at = pl.ds(pl.multiple_of(first * BLOCK, BLOCK), count * BLOCK)
        kb, vb = k_s[at, :], v_s[at, :]
        kc = lax.broadcasted_iota(jnp.int32, (count * BLOCK, 2 * BLOCK), 0) + first * BLOCK
        ok = (kc >= qstart) & (kc <= qrow)
        pr = jnp.where(ok, jnp.exp2(nt(kb, q2) * (SCALE * LOG2E) - lse), 0.0)
        dsc = (pr * (nt(vb, do2) - delta)).astype(BF16)
        dk_s[at, :] += nn(dsc, q2)
        dv_s[at, :] += nn(pr.astype(BF16), do2)
        dqt[...] = tn(dsc, kb)

    windows(i, window)
    ct, st = ct_ref[...], st_ref[...]
    raw = raw_ref[0]
    dq = jnp.concatenate([dqt[:BLOCK], dqt[BLOCK:]], axis=1) * SCALE
    here = pl.ds(pl.multiple_of(i * BLOCK, BLOCK), BLOCK)
    dkvb = jnp.concatenate([dk_s[here, :], dv_s[here, :]], axis=1)
    lane = lax.broadcasted_iota(jnp.int32, (BLOCK, 128), 1)

    def pull(d, v, gain):
        dn = d * ct - swap_halves(d) * st
        r = lax.rsqrt(head_mean(v * v) + EPSILON)
        vr = v * r
        gy = dn * gain
        return r * (gy - vr * head_mean(gy * vr)), jnp.sum(dn * vr, axis=0, keepdims=True)

    gq, gk = head_gains(g_ref)
    dqr, dgq = pull(dq, raw[:, :128], gq)
    dkr, dgk = pull(dkvb * SCALE, raw[:, 128:], gk)
    dg_ref[0:1, :] += dgq
    dg_ref[1:2, :] += dgk
    dqkv = jnp.concatenate([dqr, jnp.where(lane < HEAD, dkr, dkvb)], axis=1).astype(BF16)
    dh_ref[0] = nt(dqkv, w_ref[...]).astype(BF16)
    dws[...] += tn(h_ref[0], dqkv)

    @pl.when(step_id == 0)
    def _():
        wait_all(fetch)
        ringd.start()
        ring2.start()
        ored.start()
        wred.start()
        start_all(ex + [own_copy])

    @pl.when(step_id == nb - 1)
    def _():
        dw_ref[...] = dws[...].astype(BF16)
        result[...] = (ored.phase3() + res[...]).astype(BF16)
        two[...] = wred.phase3().astype(BF16)
        t2[...] = ring2.finish().astype(BF16)
        od[...] = ringd.finish()
        wait_all(ex + [own_copy])
        dga = lax.dot_general(
            jnp.ones((8, QKV), F32),
            w_ref[...].astype(F32) * dws[...],
            (((1,), (1,)), ((), ())),
            precision=lax.Precision.HIGHEST,
            preferred_element_type=F32,
        )
        dga = dga[0:1, :] / g_ref[:, :D]
        gpart[...] = jnp.zeros_like(gpart)
        for b in range(8):
            gpart[b : b + 1, :] = dga[:, 128 * b : 128 * (b + 1)]
            gpart[8 + b : 9 + b, :] = dgf[:, 128 * b : 128 * (b + 1)]
        turned = pltpu.roll(dg_ref[...], HEAD, 1)
        low = lax.broadcasted_iota(jnp.int32, (1, 128), 1) < HEAD
        gpart[16:17, :] = jnp.where(low, dg_ref[0:1, :] + turned[0:1, :], turned[1:2, :])


def attn_bwd(n, lengths, dmh, q, kv, lse, mixf, h, raw, wqkv, gvec, ct, st, po, res, dwo, dw2, dwd, t21, dgf):
    nb = ROWS // BLOCK
    groups = n // GROUP
    blk = lambda c: pl.BlockSpec((1, BLOCK, c), lambda i: (nb - 1 - i, 0, 0))
    whole = lambda s: pl.BlockSpec(s, lambda i: (0,) * len(s), pipeline_mode=pl.Buffered(1))
    return pl.pallas_call(
        functools.partial(attn_bwd_kernel, n),
        grid=(nb,),
        in_specs=[
            SM,
            blk(128),
            blk(128),
            whole((nb, BLOCK, 128)),
            pl.BlockSpec((1, 8, 2 * BLOCK), lambda i: (nb - 1 - i, 0, 0)),
            blk(128),
            blk(D),
            blk(QKV),
            whole((D, QKV)),
            whole(gvec.shape),
            pl.BlockSpec((BLOCK, 128), lambda i: (nb - 1 - i, 0)),
            pl.BlockSpec((BLOCK, 128), lambda i: (nb - 1 - i, 0)),
            HB,
            HB,
            HB,
            HB,
            HB,
            HB,
            whole(dgf.shape),
        ],
        out_specs=(
            blk(D),
            whole((D, QKV)),
            whole((24, 128)),
            whole((BLOCK, D)),
            whole((groups,) + dwo.shape[2:]),
            whole(dw2.shape[1:]),
            whole(dwd.shape[1:]),
            HB,
        ),
        out_shape=(
            SDS((nb, BLOCK, D), BF16),
            SDS((D, QKV), BF16),
            SDS((24, 128), F32),
            SDS((BLOCK, D), BF16),
            SDS((groups,) + dwo.shape[2:], BF16),
            SDS(dw2.shape[1:], BF16),
            SDS(dwd.shape[1:], F32),
            SDS(t21.shape, BF16),
        ),
        scratch_shapes=[
            pltpu.VMEM((ROWS, HEAD), BF16),
            pltpu.VMEM((ROWS, HEAD), BF16),
            pltpu.VMEM((ROWS, HEAD), F32),
            pltpu.VMEM((ROWS, HEAD), F32),
            pltpu.VMEM((2 * BLOCK, HEAD), F32),
            pltpu.VMEM((D, QKV), F32),
            pltpu.VMEM((8, 128), F32),
            DMA((7,)),
            DMA((7,)),
        ]
        + [pltpu.VMEM(a.shape, a.dtype) for a in (po, res, dwo, dw2, dwd, t21)]
        + [DMA((7,))]
        + plane_scratch((BLOCK, D))
        + plane_scratch((groups,) + dwo.shape[2:])
        + ring_scratch(n, dw2.shape[1:])
        + ring_scratch(n, dwd.shape[1:]),
        compiler_params=pltpu.CompilerParams(
            collective_id=6, has_side_effects=True, dimension_semantics=("arbitrary",), vmem_limit_bytes=VMEM_LIMIT
        ),
        cost_estimate=pl.CostEstimate(flops=8 * 10**9, bytes_accessed=16 << 20, transcendentals=4 * 10**6),
        name="attn_bwd",
    )(lengths, dmh, q, kv, lse, mixf, h, raw, wqkv, gvec, ct, st, po, res, dwo, dw2, dwd, t21, dgf)


def final_kernel(n, dh, x_, gmid_, g_ref, dw1, two, t2, gpart, dwd, gtok, o1, o2, oo, og, od, mine, x, gmid, fs, t1, gin, gsum, gz, ps, pr, gs, gr, *rest):
    me, p, g, groups, zq, zg = places(n)
    nz = groups - 1
    share = g_ref.shape[1] // n
    fetch = bring([(dh.at[p ^ (2 * i)], mine.at[i]) for i in (3, 1, 2, 0)] + [(x_, x), (gmid_, gmid)], fs)
    barrier([me ^ m for m in range(1, GROUP)] + zq)
    red = PlaneReduce(me, lambda b: dh.at[b], *rest[:7], own=lambda i: mine.at[i])
    ring1 = RingReduce(n, p, g, dw1, *rest[7:13])
    ringo = RingReduce(n, p, g, two, *rest[13:19])
    ringd = RingReduce(n, p, g, dwd, *rest[19:25])
    red.start()
    gc = start_all([rcopy(gpart, gin.at[m - 1], gs.at[m - 1], gr.at[m - 1], me ^ m) for m in range(1, GROUP)])
    ring1.start()
    ringo.start()
    ringd.start()
    pc = []

    def exchange(k, src, out):
        for m in range(1, GROUP):
            c = rcopy(src.at[p ^ m], out.at[p], ps.at[k, m - 1], pr.at[k, m - 1], me ^ m)
            c.start()
            pc.append(c)
        out[p] = src[p]

    exchange(1, t2, o2)
    wait_all(fetch)
    red.phase1()
    tot = gpart[...]
    for m in range(1, GROUP):
        gc[m - 1].wait_recv()
        tot = tot + gin[m - 1]
    gsum[...] = tot
    gzc = start_all([rcopy(gsum, gz.at[s], gs.at[7 + s], gr.at[7 + s], zq[s]) for s in range(nz)])
    ring1.relay()
    ringo.relay()
    red.phase2()
    t1[...] = ring1.finish().astype(BF16)
    exchange(0, t1, o1)
    oo[...] = ringo.finish()
    ringd.relay()
    for s in range(nz):
        gzc[s].wait_recv()
        tot = tot + gz[s]
    gsum_row = me * share
    for c in gzc:
        c.wait_send()
    gsum[...] = tot
    first = gsum_row // 128
    off = lax.rem(gsum_row, 128)
    lane = lax.broadcasted_iota(jnp.int32, (8, 128), 1)
    turn = lambda row: pltpu.roll(jnp.broadcast_to(gsum[pl.ds(row, 1), :], (8, 128)), lax.rem(128 - off, 128), 1)
    og[...] = jnp.where(lane < 128 - off, turn(first), turn(first + 1))
    dx, _ = norm_back(red.phase3(), x[...].astype(F32), g_ref[:, :D])
    gtok[...] = gmid[...] + dx
    od[...] = ringd.finish()
    wait_all(pc)
    for c in gc:
        c.wait_send()


def final(n, dh, x, gmid, gvec, dw1, two, t2, gpart, dwd):
    groups = n // GROUP
    nz = groups - 1
    return pl.pallas_call(
        functools.partial(final_kernel, n),
        out_shape=(
            SDS((BLOCK, D), F32),
            SDS(dw1.shape[1:], BF16),
            SDS(t2.shape, BF16),
            SDS(two.shape[1:], F32),
            SDS((8, 128), F32),
            SDS(dwd.shape[1:], F32),
        ),
        in_specs=[HB, HB, HB] + [VM] * 6,
        out_specs=(VM,) * 6,
        scratch_shapes=[
            pltpu.VMEM((4, BLOCK, D), BF16),
            pltpu.VMEM(x.shape, BF16),
            pltpu.VMEM(gmid.shape, F32),
            DMA((6,)),
            pltpu.VMEM(dw1.shape[1:], BF16),
            pltpu.VMEM((7, 24, 128), F32),
            pltpu.VMEM((24, 128), F32),
            pltpu.VMEM((nz, 24, 128), F32),
            DMA((2, 7)),
            DMA((2, 7)),
            DMA((7 + nz,)),
            DMA((7 + nz,)),
        ]
        + plane_scratch((BLOCK, D))
        + ring_scratch(n, dw1.shape[1:])
        + ring_scratch(n, two.shape[1:])
        + ring_scratch(n, dwd.shape[1:]),
        compiler_params=pltpu.CompilerParams(collective_id=4, has_side_effects=True, vmem_limit_bytes=VMEM_LIMIT),
        name="final",
    )(dh, x, gmid, gvec, dw1, two, t2, gpart, dwd)


def unpack_kernel(groups, result, gtok, o1, o21, o22, oo, od, od2, og, result_o, gtok_o, gq, gk, gv, go, gg, gu, gd, gn):
    result_o[...] = result[...]
    gtok_o[...] = gtok[...]
    go[...] = oo[...]
    gd[: od.shape[0]] = od[...]
    gd[od.shape[0] :] = od2[...]
    gn[...] = og[0:1, : gn.shape[1]]
    for b in range(GROUP):
        gq[:, 128 * b : 128 * (b + 1)] = o1[b, :, :128].astype(F32)
    for out, at in ((gk, slice(128, 128 + HEAD)), (gv, slice(128 + HEAD, 256))):
        for c in range(GROUP // 2):
            pair = [o1[2 * c + k, :, at].astype(F32) for k in range(2)]
            out[:, 128 * c : 128 * (c + 1)] = jnp.concatenate(pair, axis=1)
    ffc = gg.shape[1] // (groups * GROUP)
    for k, out in enumerate((gg, gu)):
        big = 5 * ffc // 9
        piece = lambda src, b, c, w: src[b, :, (k * groups + c) * w : (k * groups + c + 1) * w].astype(F32)
        parts = [
            piece(src, b, c, w)
            for c in range(groups)
            for b in range(GROUP)
            for src, w in ((o21, big), (o22, ffc - big))
        ]
        out[...] = jnp.concatenate(parts, axis=1)


def unpack(n, result, gtok, o1, o21, o22, oo, od, od2, og, share):
    r = oo.shape[0]
    return pl.pallas_call(
        functools.partial(unpack_kernel, n // GROUP),
        out_shape=(
            SDS(result.shape, BF16),
            SDS(gtok.shape, F32),
            SDS((r, D), F32),
            SDS((r, D // 2), F32),
            SDS((r, D // 2), F32),
            SDS((r, D), F32),
            SDS((r, FF), F32),
            SDS((r, FF), F32),
            SDS((od.shape[0] + od2.shape[0], D), F32),
            SDS((1, share), F32),
        ),
        in_specs=[VM] * 9,
        out_specs=(VM,) * 10,
        compiler_params=pltpu.CompilerParams(vmem_limit_bytes=VMEM_LIMIT),
        name="unpack",
    )(result, gtok, o1, o21, o22, oo, od, od2, og)


def body(n, tokens, w_query, key_weight, w_value, w_out, w_gate, w_up, w_down, norm_gains, seq_lengths, slot_order, out_grad):
    groups = n // GROUP
    r = w_query.shape[0]
    ffc = w_down.shape[0]
    share = norm_gains.shape[0]
    wok = r // 16 if r % 16 == 0 else 1
    wdk = 9
    wo_blk, wd_blk = (wok, r // wok, D), (wdk, ffc // wdk, D)
    h, raw, q, kv, mixf, lse, mix, dy_all, w21, w22, wo, wd1, wqkv, gvec, ct, st = front(
        n,
        seq_lengths,
        tokens,
        w_query,
        key_weight,
        w_value,
        w_gate,
        w_up,
        w_out.reshape(wo_blk),
        w_down.reshape(wd_blk),
        norm_gains.reshape(1, share),
        out_grad,
    )
    res, gmid, dgf, dwo, dmh, po, t21, dw22, dwd1, dwd2 = ffn_block(
        n,
        slot_order,
        mix,
        tokens,
        wo.reshape(D, D),
        gvec,
        w21.reshape(D, -1),
        w22,
        wd1.reshape(-1, D),
        w_down.reshape(wd_blk),
        dy_all,
    )
    dh1, dwqkv, gpart, result, two, t2, od, o21 = attn_bwd(
        n,
        seq_lengths,
        dmh,
        q,
        kv,
        lse,
        mixf,
        h,
        raw,
        wqkv,
        gvec,
        ct,
        st,
        po,
        res,
        dwo.reshape(groups, GROUP, r, D),
        dw22.reshape(groups, GROUP, r, -1),
        dwd1,
        t21,
        dgf,
    )
    gtok, o1, o22, oo, og, od2 = final(
        n,
        dh1,
        tokens,
        gmid,
        gvec,
        dwqkv.reshape(groups, GROUP, r, QKV),
        two.reshape((groups,) + wo_blk),
        t2,
        gpart,
        dwd2,
    )
    outs = unpack(n, result, gtok, o1, o21, o22, oo.reshape(r, D), od.reshape(-1, D), od2.reshape(-1, D), og, share)
    return outs[:-1] + (outs[-1].reshape(share),)


def solution(mesh):
    n = mesh.shape["dp"]
    row = P("dp", None)
    return jax.shard_map(
        functools.partial(body, n),
        mesh=mesh,
        in_specs=(row,) * 8 + (P("dp"), P(), P(), row),
        out_specs=(row,) * 9 + (P("dp"),),
        check_vma=False,
    )
```
